32 devices in a mesh: ctx: 4 (over z), fsdp: 8 (over y, x, core).
Axes of the slice: x: 2, y: 2, z: 4, core: 2. Of those that a mesh axis runs over, the one named last changes fastest.
Arguments:
- tokens: bfloat16 [8, 1024, 2048], P('fsdp', 'ctx'), may hold values from -6 to 6
- attn_gain: bfloat16 [2048], P('fsdp'), may hold values from 0.25 to 1.75
- w_query: bfloat16 [2048, 2048], P('fsdp'), may hold values from -1.2374369 to 1.2374369
- w_key: bfloat16 [2048, 256], P('fsdp'), may hold values from -0.13258252 to 0.13258252
- w_value: bfloat16 [2048, 256], P('fsdp'), may hold values from -0.125 to 0.125
- w_out: bfloat16 [2048, 2048], P('fsdp'), may hold values from -1.5 to 1.5
- ffn_gain: bfloat16 [2048], P('fsdp'), may hold values from 0.25 to 1.75
- w_gate: bfloat16 [2048, 5632], P('fsdp'), may hold values from -0.125 to 0.125
- w_up: bfloat16 [2048, 5632], P('fsdp'), may hold values from -0.125 to 0.125
- w_down: bfloat16 [5632, 2048], P('fsdp'), may hold values from -0.078125 to 0.078125
- block_table: int32 [4, 2], replicated, may hold values from 0 to 7, as said below
- positions: int32 [8, 1024], P('fsdp', 'ctx'), may hold values from 0 to 5118, as said below
- out_grad: bfloat16 [8, 1024, 2048], P('fsdp', 'ctx'), may hold values from -6 to 6
Outputs:
- layer_out: bfloat16 [8, 1024, 2048], P('fsdp', 'ctx')
- tokens_grad: float32 [8, 1024, 2048], P('fsdp', 'ctx')
- attn_gain_grad: float32 [2048], P('fsdp')
- w_query_grad: float32 [2048, 2048], P('fsdp')
- w_key_grad: float32 [2048, 256], P('fsdp')
- w_value_grad: float32 [2048, 256], P('fsdp')
- w_out_grad: float32 [2048, 2048], P('fsdp')
- ffn_gain_grad: float32 [2048], P('fsdp')
- w_gate_grad: float32 [2048, 5632], P('fsdp')
- w_up_grad: float32 [2048, 5632], P('fsdp')
- w_down_grad: float32 [5632, 2048], P('fsdp')
The draws below stay inside these ranges and needn't reach their ends.
Inputs may be any that keep to these rules, and one draw needn't show every extreme that they name: `block_table`: row c holds a block p and its mirror 8 - 1 - p; every block of 0 to 7 stands once in the table. positions[s, r] is an offset of sequence s plus idx of stored row r, so positions rise by one along a sequence.
All inputs are finite; a program needn't handle non-finite values.
Results may differ from the reference program's by a relative error of at most 0.014.
Values may be sent and summed in bfloat16 or wider, within the bound.
A program may use at most 512 MiB of HBM per device.

```python
import math
import jax
import jax.numpy as jnp
from jax import lax

D = 2048
HEADS = 32
KV_HEADS = 4
HEAD_DIM = 64
FF = 5632
SEQ = 1024
SEQS = 8
BLOCK = 128
BLOCKS = 8


def pair_order(key):
    return jax.random.permutation(jax.random.fold_in(key, 7), BLOCKS // 2).astype(jnp.int32)


def key_matrix(key):
    raw = jnp.clip(jax.random.normal(jax.random.fold_in(key, 11), (D, KV_HEADS * HEAD_DIM), jnp.float32), -6.0, 6.0)
    return raw / math.sqrt(D)


def draw_block_table(key, part):
    first = pair_order(key)
    return jnp.stack([first, BLOCKS - 1 - first], axis=1).astype(jnp.int32)


def draw_positions(key, part):
    first = pair_order(key)
    table = jnp.stack([first, BLOCKS - 1 - first], axis=1)
    order = (table[:, :, None] * BLOCK + jnp.arange(BLOCK, dtype=jnp.int32)[None, None, :]).reshape(-1)
    offsets = jax.random.randint(jax.random.fold_in(key, 8), (SEQS,), 0, 4096)
    chosen = jax.random.randint(jax.random.fold_in(key, 9), (), 0, SEQS)
    offsets = jnp.where(jnp.arange(SEQS) == chosen, 4095, offsets)
    return (offsets[:, None] + order[None, :]).astype(jnp.int32)


def draw_w_key(key, part):
    return key_matrix(key).astype(jnp.bfloat16)


def draw_w_query(key, part):
    noise = jnp.clip(jax.random.normal(jax.random.fold_in(key, 12), (D, HEADS * HEAD_DIM), jnp.float32), -6.0, 6.0) / math.sqrt(D)
    return noise.astype(jnp.bfloat16)


def level_of(rng, dims, pieces, low, largest):
    def one(axis_at, shards_of):
        heights = jax.random.uniform(jax.random.fold_in(jax.random.fold_in(rng, 6), axis_at), (shards_of,), jnp.float32, low / len(pieces), largest / len(pieces))
        return jnp.repeat(jnp.exp(heights), dims[axis_at] // shards_of).reshape((-1,) + (1,) * (len(dims) - axis_at - 1))

    loudness = one(*pieces[0])
    for cut in pieces[1:]:
        loudness = loudness * one(*cut)
    return loudness


def gaussian(own_key, shape, spread, limit, pieces=(), kind=jnp.bfloat16):
    entries = jax.random.normal(own_key, shape, jnp.float32) * spread
    if len(pieces) > 0:
        entries = level_of(own_key, shape, pieces, -0.22, 0.18) * entries
    return jnp.clip(entries, min=-limit, max=limit).astype(kind)


def setup_inputs(seed: int = 0) -> dict:
    splits = jax.random.split(jax.random.key(seed), 14)
    return {
        "tokens": gaussian(splits[0], (SEQS, SEQ, D), 1.0, 6.0, ((0, 8), (1, 4))),
        "attn_gain": jnp.clip(1.0 + 0.15 * jax.random.normal(splits[1], (D,), jnp.float32), 0.25, 1.75).astype(jnp.bfloat16),
        "w_query": draw_w_query(jax.random.fold_in(splits[13], 71), 0),
        "w_key": draw_w_key(jax.random.fold_in(splits[13], 71), 0),
        "w_value": gaussian(splits[4], (D, KV_HEADS * HEAD_DIM), D ** -0.5, 0.125, ((0, 8),)),
        "w_out": gaussian(splits[5], (HEADS * HEAD_DIM, D), (max(1, HEADS * HEAD_DIM * 8 // SEQ)) ** -0.5, 1.5, ((0, 8),)),
        "ffn_gain": jnp.clip(1.0 + 0.15 * jax.random.normal(splits[6], (D,), jnp.float32), 0.25, 1.75).astype(jnp.bfloat16),
        "w_gate": gaussian(splits[7], (D, FF), D ** -0.5, 0.125, ((0, 8),)),
        "w_up": gaussian(splits[8], (D, FF), D ** -0.5, 0.125, ((0, 8),)),
        "w_down": gaussian(splits[9], (FF, D), FF ** -0.5, 0.078125, ((0, 8),)),
        "block_table": draw_block_table(jax.random.fold_in(splits[13], 71), 0),
        "positions": draw_positions(jax.random.fold_in(splits[13], 71), 0),
        "out_grad": gaussian(splits[12], (SEQS, SEQ, D), 1.0, 6.0, ((0, 8), (1, 4))),
    }


@jax.custom_vjp
def low(v):
    return lax.optimization_barrier(v.astype(jnp.bfloat16)).astype(jnp.float32)

@jax.custom_vjp
def low_back(v):
    return v

def low_keep(v):
    return (low(v), None)

def low_pass(kept, grad):
    return (grad,)

def back_keep(v):
    return (v, None)

def back_low(kept, grad):
    return (low(grad),)
low.defvjp(low_keep, low_pass)
low_back.defvjp(back_keep, back_low)
EPS = 1e-05
THETA = 10000.0
HIGH = lax.Precision.HIGHEST

def rope_tables(positions):
    half_dim = HEAD_DIM // 2
    frequency = THETA ** (-jnp.arange(half_dim, dtype=jnp.float32) * (2.0 / HEAD_DIM))
    angle = positions.astype(jnp.float32)[:, None] * frequency[None, :]
    return (jnp.cos(angle)[:, None, :], jnp.sin(angle)[:, None, :])

def rotate(values, cosine, sine):
    half_dim = HEAD_DIM // 2
    first = values[..., :half_dim]
    second = values[..., half_dim:]
    return jnp.concatenate([first * cosine - second * sine, second * cosine + first * sine], axis=-1)

def normalize(values):
    return values * lax.rsqrt(lax.optimization_barrier(jnp.mean(values * values, axis=1, keepdims=True)) + EPS)

def layer(inputs, attn_gain, w_query, w_key, w_value, w_out, ffn_gain, w_gate, w_up, w_down, cosine, sine, allowed):
    length = inputs.shape[0]
    group_size = HEADS // KV_HEADS
    score_scale = HEAD_DIM ** (-0.5)
    normed = low(normalize(inputs) * attn_gain[None, :])
    queries = low_back(jnp.dot(normed, w_query, precision=HIGH)).reshape(length, HEADS, HEAD_DIM)
    keys = low_back(jnp.dot(normed, w_key, precision=HIGH)).reshape(length, KV_HEADS, HEAD_DIM)
    values = low(low_back(jnp.dot(normed, w_value, precision=HIGH))).reshape(length, KV_HEADS, HEAD_DIM)
    queries = low(rotate(queries, cosine, sine))
    keys = low(rotate(keys, cosine, sine))
    query_heads = queries.reshape(length, KV_HEADS, group_size, HEAD_DIM).transpose(1, 2, 0, 3)
    key_heads = keys.transpose(1, 0, 2)
    value_heads = values.transpose(1, 0, 2)

    def head_block(operands):
        query_block, key_block, value_block = operands
        scores = low_back(jnp.einsum('gqd,kd->gqk', query_block, key_block, precision=HIGH) * score_scale)
        scores = jnp.where(allowed[None], scores, -1e+30)
        softmaxed = low(jax.nn.softmax(scores, axis=-1))
        return jnp.einsum('gqk,kd->gqd', softmaxed, value_block, precision=HIGH)
    mixed = lax.map(jax.checkpoint(head_block), (query_heads, key_heads, value_heads))
    attended = low(low_back(mixed.transpose(2, 0, 1, 3).reshape(length, HEADS * HEAD_DIM)))
    hidden = inputs + low_back(jnp.dot(attended, w_out, precision=HIGH))
    normed_two = low(normalize(hidden) * ffn_gain[None, :])
    gate = low_back(jnp.dot(normed_two, w_gate, precision=HIGH))
    up_branch = low_back(jnp.dot(normed_two, w_up, precision=HIGH))
    activated = low(jax.nn.silu(gate) * up_branch)
    return hidden + low_back(jnp.dot(activated, w_down, precision=HIGH))

def reference(tokens, attn_gain, w_query, w_key, w_value, w_out, ffn_gain, w_gate, w_up, w_down, block_table, positions, out_grad):
    params = tuple((w.astype(jnp.float32) for w in (attn_gain, w_query, w_key, w_value, w_out, ffn_gain, w_gate, w_up, w_down)))
    table = block_table.astype(jnp.int32)
    seq_index = (table[:, :, None] * BLOCK + jnp.arange(BLOCK, dtype=jnp.int32)[None, None, :]).reshape(-1)
    allowed = seq_index[None, :] <= seq_index[:, None]

    def one_sequence(totals, item):
        seq_tokens, seq_positions, seq_grad = item
        cosine, sine = rope_tables(seq_positions)

        def forward(inputs, *weights):
            return layer(inputs, *weights, cosine, sine, allowed)
        result, pull = jax.vjp(forward, seq_tokens.astype(jnp.float32), *params)
        grads = pull(seq_grad.astype(jnp.float32))
        totals = tuple((a + b for a, b in zip(totals, grads[1:])))
        return (totals, (result.astype(jnp.bfloat16), grads[0]))
    zeros = tuple((jnp.zeros_like(p) for p in params))
    totals, (outputs, input_grads) = lax.scan(one_sequence, zeros, (tokens, positions, out_grad))
    return (outputs, input_grads, totals[0], totals[1], totals[2], totals[3], totals[4], totals[5], totals[6], totals[7], totals[8])
```

```python
import functools

import jax
import jax.numpy as jnp
from jax import lax
from jax.experimental import pallas as pl
from jax.experimental.pallas import tpu as pltpu
from jax.sharding import PartitionSpec as P

HEADS = 32
KV_HEADS = 4
HEAD_DIM = 64
GROUP = HEADS // KV_HEADS
PAIRS = GROUP // 2
LANES = 2 * HEAD_DIM
STACK = PAIRS * LANES

EPS = 1e-05
THETA = 10000.0
NEG = -1e30
FLIGHT = 2
BF = jnp.bfloat16
F32 = jnp.float32


def dot(left, right, contract, out=F32):
    return lax.dot_general(
        left, right, ((contract[:1], contract[1:]), ((), ())), preferred_element_type=out
    )


def swap_halves(z):
    lane = lax.broadcasted_iota(jnp.int32, z.shape, 1)
    first = (lane % HEAD_DIM) < (HEAD_DIM // 2)
    return jnp.where(
        first,
        pltpu.roll(z, LANES - HEAD_DIM // 2, 1),
        pltpu.roll(z, HEAD_DIM // 2, 1),
    )


def split_heads(rows):
    lane = lax.broadcasted_iota(jnp.int32, rows.shape, 1)
    zero = jnp.zeros_like(rows)
    return jnp.concatenate(
        [jnp.where(lane < HEAD_DIM, rows, zero), jnp.where(lane >= HEAD_DIM, rows, zero)], axis=0
    )


def join_heads(columns):
    half = columns.shape[1] // 2
    sub = lax.broadcasted_iota(jnp.int32, (LANES, half), 0)
    return jnp.where(sub < HEAD_DIM, columns[:, :half], columns[:, half:]).T


def stack_pairs(ref, rows):
    return jnp.concatenate([ref[rows, p * LANES : (p + 1) * LANES] for p in range(PAIRS)], axis=0)


def two_blocks(ref, table, j, block):
    parts = [
        ref[pl.ds(pl.multiple_of(table[2 + 2 * j + i] * block, block), block), :] for i in range(2)
    ]
    return jnp.concatenate(parts, axis=0)


def causal(scores, j, own, block):
    key = lax.broadcasted_iota(jnp.int32, scores.shape, 0) + j * (2 * block)
    query = lax.broadcasted_iota(jnp.int32, scores.shape, 1) % block + own * block
    return jnp.where(key <= query, scores, NEG)


def head_twice(pair, group):
    wide = pair.astype(F32)
    lane = lax.broadcasted_iota(jnp.int32, wide.shape, 1)
    keep = (lane < HEAD_DIM) == (group % 2 == 0)
    return jnp.where(keep, wide, pltpu.roll(wide, HEAD_DIM, 1)).astype(BF)


def attention_forward_kernel(
    table,
    q_ref,
    cos_ref,
    sin_ref,
    k_pair,
    v_pair,
    qr_ref,
    o_ref,
    ob_ref,
    lse_ref,
    qm,
    m,
    l,
    acc,
    k_ref,
    v_ref,
):
    block = q_ref.shape[0] // 2
    group = pl.program_id(0)
    k_ref[...] = head_twice(k_pair[...], group)
    v_ref[...] = head_twice(v_pair[...], group)
    for h in range(2):
        rows = slice(h * block, (h + 1) * block)
        cosine, sine = cos_ref[rows, :], sin_ref[rows, :]
        for p in range(PAIRS):
            lanes = slice(p * LANES, (p + 1) * LANES)
            z = q_ref[rows, lanes]
            qr_ref[rows, lanes] = (z * cosine + swap_halves(z) * sine).astype(BF)
        scaled = stack_pairs(qr_ref, rows).astype(F32) * (HEAD_DIM**-0.5)
        qm[...] = split_heads(scaled).astype(BF)
        m[...] = jnp.full_like(m, NEG)
        l[...] = jnp.zeros_like(l)
        acc[...] = jnp.zeros_like(acc)
        own = table[h]

        def step(j, masked):
            keys = two_blocks(k_ref, table, j, block)
            values = two_blocks(v_ref, table, j, block)
            s = dot(keys, qm[...], (1, 1))
            if masked:
                s = causal(s, j, own, block)
            before = m[...]
            now = jnp.maximum(before, jnp.max(s, axis=0, keepdims=True))
            p = jnp.exp(s - now)
            decay = jnp.exp(before - now)
            l[...] = l[...] * decay + jnp.sum(p, axis=0, keepdims=True)
            acc[...] = acc[...] * decay + dot(values, p.astype(BF), (0, 0))
            m[...] = now

        last = own // 2

        @pl.loop(0, last)
        def _(j):
            step(j, False)

        step(last, True)
        lse_ref[0, h : h + 1, :] = m[...] + jnp.log(l[...])
        o = join_heads(acc[...] / l[...])
        for p in range(PAIRS):
            lanes = slice(p * LANES, (p + 1) * LANES)
            piece = o[p * block : (p + 1) * block, :]
            o_ref[rows, lanes] = piece
            ob_ref[rows, lanes] = piece.astype(BF)


def attention_forward(table, q, cosine, sine, kv):
    rows, length = q.shape[0], kv.shape[0]
    query_width = HEADS * HEAD_DIM
    columns = pl.BlockSpec((rows, STACK), lambda g, t: (0, g))
    whole = pl.BlockSpec((rows, LANES), lambda g, t: (0, 0))
    key_pair = pl.BlockSpec((length, LANES), lambda g, t: (0, g // 2))
    value_pair = pl.BlockSpec((length, LANES), lambda g, t: (0, KV_HEADS // 2 + g // 2))
    wide = GROUP * (rows // 2)
    return pl.pallas_call(
        attention_forward_kernel,
        grid_spec=pltpu.PrefetchScalarGridSpec(
            num_scalar_prefetch=1,
            grid=(KV_HEADS,),
            in_specs=[columns, whole, whole, key_pair, value_pair],
            out_specs=[
                columns,
                columns,
                columns,
                pl.BlockSpec((1, 2, wide), lambda g, t: (g, 0, 0)),
            ],
            scratch_shapes=[
                pltpu.VMEM((wide, LANES), BF),
                pltpu.VMEM((1, wide), F32),
                pltpu.VMEM((1, wide), F32),
                pltpu.VMEM((LANES, wide), F32),
                pltpu.VMEM((length, LANES), BF),
                pltpu.VMEM((length, LANES), BF),
            ],
        ),
        out_shape=[
            jax.ShapeDtypeStruct((rows, query_width), BF),
            jax.ShapeDtypeStruct((rows, query_width), F32),
            jax.ShapeDtypeStruct((rows, query_width), BF),
            jax.ShapeDtypeStruct((KV_HEADS, 2, wide), F32),
        ],
        compiler_params=pltpu.CompilerParams(vmem_limit_bytes=32 << 20),
        cost_estimate=pl.CostEstimate(
            flops=8 * HEADS * rows * length * HEAD_DIM,
            bytes_accessed=16 * rows * HEADS * HEAD_DIM,
            transcendentals=HEADS * rows * length,
        ),
        name="attention_forward",
    )(table, q, cosine, sine, kv, kv)


def attention_backward_kernel(
    table,
    qr_ref,
    do_ref,
    o_ref,
    lse_ref,
    k_pair,
    v_pair,
    cos_ref,
    sin_ref,
    dq_ref,
    dkv_ref,
    qm,
    dom,
    dqt,
    k_ref,
    v_ref,
    dk_ref,
    dv_ref,
):
    block = qr_ref.shape[0] // 2
    group = pl.program_id(0)
    k_ref[...] = head_twice(k_pair[...], group)
    v_ref[...] = head_twice(v_pair[...], group)
    dk_ref[...] = jnp.zeros_like(dk_ref)
    dv_ref[...] = jnp.zeros_like(dv_ref)
    for h in range(2):
        rows = slice(h * block, (h + 1) * block)
        scaled = stack_pairs(qr_ref, rows).astype(F32) * (HEAD_DIM**-0.5)
        qm[...] = split_heads(scaled).astype(BF)
        grads = stack_pairs(do_ref, rows).astype(F32)
        dom[...] = split_heads(grads).astype(BF)
        product = (grads * stack_pairs(o_ref, rows)).T
        inner = jnp.concatenate(
            [
                jnp.sum(product[:HEAD_DIM], axis=0, keepdims=True),
                jnp.sum(product[HEAD_DIM:], axis=0, keepdims=True),
            ],
            axis=1,
        )
        lse = lse_ref[0, h : h + 1, :]
        dqt[...] = jnp.zeros_like(dqt)
        own = table[h]

        def step(j, masked):
            keys = two_blocks(k_ref, table, j, block)
            values = two_blocks(v_ref, table, j, block)
            s = dot(keys, qm[...], (1, 1))
            if masked:
                s = causal(s, j, own, block)
            p = jnp.exp(s - lse)
            dp = dot(values, dom[...], (1, 1))
            ds = (p * (dp - inner)).astype(BF)
            dv = dot(p.astype(BF), dom[...], (1, 0))
            dk = dot(ds, qm[...], (1, 0))
            dqt[...] += dot(keys, ds, (0, 0))
            for i in range(2):
                at = pl.ds(pl.multiple_of(table[2 + 2 * j + i] * block, block), block)
                dk_ref[at, :] += dk[i * block : (i + 1) * block]
                dv_ref[at, :] += dv[i * block : (i + 1) * block]

        last = own // 2

        @pl.loop(0, last)
        def _(j):
            step(j, False)

        step(last, True)
        cosine, sine = cos_ref[rows, :], sin_ref[rows, :]
        dq = join_heads(dqt[...] * (HEAD_DIM**-0.5))
        for p in range(PAIRS):
            z = dq[p * block : (p + 1) * block, :]
            dq_ref[rows, p * LANES : (p + 1) * LANES] = (
                z * cosine - swap_halves(z) * sine
            ).astype(BF)
    lane = lax.broadcasted_iota(jnp.int32, dk_ref.shape, 1)
    keep = (lane < HEAD_DIM) == (group % 2 == 0)
    for i, ref in enumerate((dk_ref, dv_ref)):
        both = ref[...] + pltpu.roll(ref[...], HEAD_DIM, 1)
        dkv_ref[i] = jnp.where(keep, both, dkv_ref[i].astype(F32)).astype(BF)


def attention_backward(table, qr, grads, o, lse, kv, cosine, sine):
    rows, length = qr.shape[0], kv.shape[0]
    columns = pl.BlockSpec((rows, STACK), lambda g, t: (0, g))
    whole = pl.BlockSpec((rows, LANES), lambda g, t: (0, 0))
    key_pair = pl.BlockSpec((length, LANES), lambda g, t: (0, g // 2))
    value_pair = pl.BlockSpec((length, LANES), lambda g, t: (0, KV_HEADS // 2 + g // 2))
    wide = GROUP * (rows // 2)
    return pl.pallas_call(
        attention_backward_kernel,
        grid_spec=pltpu.PrefetchScalarGridSpec(
            num_scalar_prefetch=1,
            grid=(KV_HEADS,),
            in_specs=[
                columns,
                columns,
                columns,
                pl.BlockSpec((1, 2, wide), lambda g, t: (g, 0, 0)),
                key_pair,
                value_pair,
                whole,
                whole,
            ],
            out_specs=[columns, pl.BlockSpec((2, length, LANES), lambda g, t: (0, 0, g // 2))],
            scratch_shapes=[
                pltpu.VMEM((wide, LANES), BF),
                pltpu.VMEM((wide, LANES), BF),
                pltpu.VMEM((LANES, wide), F32),
                pltpu.VMEM((length, LANES), BF),
                pltpu.VMEM((length, LANES), BF),
                pltpu.VMEM((length, LANES), F32),
                pltpu.VMEM((length, LANES), F32),
            ],
        ),
        out_shape=[
            jax.ShapeDtypeStruct(qr.shape, BF),
            jax.ShapeDtypeStruct((2, length, KV_HEADS * HEAD_DIM), BF),
        ],
        compiler_params=pltpu.CompilerParams(vmem_limit_bytes=32 << 20),
        cost_estimate=pl.CostEstimate(
            flops=20 * HEADS * rows * length * HEAD_DIM,
            bytes_accessed=16 * rows * HEADS * HEAD_DIM,
            transcendentals=HEADS * rows * length,
        ),
        name="attention_backward",
    )(table, qr, grads, o, lse, kv, kv, cosine, sine)


def own_keys_kernel(k_ref, v_ref, cos_ref, sin_ref, kv_ref):
    width = k_ref.shape[1]
    for p in range(width // LANES):
        lanes = slice(p * LANES, (p + 1) * LANES)
        z = k_ref[:, lanes]
        kv_ref[:, lanes] = (z * cos_ref[...] + swap_halves(z) * sin_ref[...]).astype(BF)
    kv_ref[:, width:] = v_ref[...].astype(BF)


def own_keys(qkv, cosine, sine):
    rows, width = qkv.shape[0], KV_HEADS * HEAD_DIM
    at = HEADS * HEAD_DIM // width
    whole = pl.BlockSpec((rows, LANES), lambda i: (0, 0))
    return pl.pallas_call(
        own_keys_kernel,
        grid=(1,),
        in_specs=[
            pl.BlockSpec((rows, width), lambda i: (0, at)),
            pl.BlockSpec((rows, width), lambda i: (0, at + 1)),
            whole,
            whole,
        ],
        out_specs=pl.BlockSpec((rows, 2 * width), lambda i: (0, 0)),
        out_shape=jax.ShapeDtypeStruct((rows, 2 * width), BF),
        name="own_keys",
    )(qkv, qkv, cosine, sine)


def own_key_grads_kernel(*refs):
    *pieces, cos_ref, sin_ref, out_ref = refs
    width = out_ref.shape[1] // 2

    def total(i, lanes):
        return sum(piece[i, :, lanes].astype(F32) for piece in pieces)

    for p in range(width // LANES):
        lanes = slice(p * LANES, (p + 1) * LANES)
        z = total(0, lanes)
        out_ref[:, lanes] = (z * cos_ref[...] - swap_halves(z) * sin_ref[...]).astype(BF)
        out_ref[:, width + p * LANES : width + (p + 1) * LANES] = total(1, lanes).astype(BF)


def own_key_grads(pieces, cosine, sine):
    rows, width = pieces[0].shape[1], pieces[0].shape[2]
    return pl.pallas_call(
        own_key_grads_kernel,
        out_shape=jax.ShapeDtypeStruct((rows, 2 * width), BF),
        name="own_key_grads",
    )(*pieces, cosine, sine)


def pick_columns_kernel(order, gate_ref, up_ref, out_ref):
    part = gate_ref.shape[1]
    out_ref[0, :, :part] = gate_ref[...]
    out_ref[0, :, part:] = up_ref[...]


def pick_columns(order, share, shares, w_gate, w_up):
    rows, hidden = w_gate.shape[0] // shares, w_gate.shape[1]
    parts = order.shape[0]
    part = hidden // parts
    if part % 128:
        both = [
            lax.dynamic_slice_in_dim(w, share * rows, rows).reshape(rows, parts, part)
            for w in (w_gate, w_up)
        ]
        return jnp.take(jnp.concatenate(both, axis=2).transpose(1, 0, 2), order, axis=0)
    columns = pl.BlockSpec((rows, part), lambda k, t: (t[parts], t[k]))
    return pl.pallas_call(
        pick_columns_kernel,
        grid_spec=pltpu.PrefetchScalarGridSpec(
            num_scalar_prefetch=1,
            grid=(parts,),
            in_specs=[columns, columns],
            out_specs=pl.BlockSpec((1, rows, 2 * part), lambda k, t: (k, 0, 0)),
        ),
        out_shape=jax.ShapeDtypeStruct((parts, rows, 2 * part), BF),
        name="pick_columns",
    )(jnp.concatenate([order, share[None]]), w_gate, w_up)


def assemble_kernel(nc, *refs):
    *pieces, out, sems = refs
    chips = pieces[0].shape[0]
    place, here = lax.axis_index("fsdp"), lax.axis_index("ctx")
    chip, core = place // 2, place % 2

    def copies(ref, other, share, at, go):
        for k in range(chips):
            owner = 2 * (chip ^ k) + (core ^ other)
            copy = pltpu.make_async_copy(
                ref.at[k], out.at[owner, share], sems.at[other, at, k]
            )
            if go:
                copy.start()
            else:
                copy.wait()

    for go in (True, False):
        for other in range(2):
            mine = pieces[other * (2 * nc - 1) : (other + 1) * (2 * nc - 1)]
            copies(mine[0], other, here, 0, go)
            for d in range(1, nc):

                @pl.when(here >= d)
                def _():
                    copies(mine[d], other, here - d, d, go)

                @pl.when(here + d < nc)
                def _():
                    copies(mine[nc - 1 + d], other, here + d, nc - 1 + d, go)


def assemble(nf, nc, pieces):
    chips, rows, columns = pieces[0].shape
    anywhere = pl.BlockSpec(memory_space=pl.ANY)
    return pl.pallas_call(
        functools.partial(assemble_kernel, nc),
        in_specs=[anywhere] * len(pieces),
        out_specs=pl.BlockSpec(memory_space=pltpu.VMEM),
        out_shape=jax.ShapeDtypeStruct((nf, nc, rows, columns), BF),
        scratch_shapes=[pltpu.SemaphoreType.DMA((2, 2 * nc - 1, chips))],
        compiler_params=pltpu.CompilerParams(vmem_limit_bytes=24 << 20),
        name="assemble",
    )(*pieces)


def place_columns_kernel(order, both_ref, gate_ref, up_ref):
    part = gate_ref.shape[1]
    gate_ref[...] = both_ref[0, :, :part].astype(F32)
    up_ref[...] = both_ref[0, :, part:].astype(F32)


def place_columns(order, both):
    parts, shard, part = both.shape[0], both.shape[1], both.shape[2] // 2
    out = jax.ShapeDtypeStruct((shard, parts * part), F32)
    if part % 128:
        both = jnp.take(both, order, axis=0).transpose(1, 0, 2).astype(F32)
        return [both[:, :, i * part : (i + 1) * part].reshape(out.shape) for i in range(2)]
    columns = pl.BlockSpec((shard, part), lambda k, t: (0, t[k]))
    return pl.pallas_call(
        place_columns_kernel,
        grid_spec=pltpu.PrefetchScalarGridSpec(
            num_scalar_prefetch=1,
            grid=(parts,),
            in_specs=[pl.BlockSpec((1, shard, 2 * part), lambda k, t: (k, 0, 0))],
            out_specs=[columns, columns],
        ),
        out_shape=[out, out],
        name="place_columns",
    )(order, both)


def chunk_rows(rows):
    return max(r for r in range(16, 65, 16) if rows % r == 0)


def finish_kernel(nf, nc, *refs):
    sources, outs, owns, ins, xs = (refs[i : i + 5] for i in range(0, 25, 5))
    plane_send, plane_recv, local, in_sem, x_sem, first_send, second_send, out_sem = refs[25:]
    chips = nf // 2
    place, here = lax.axis_index("fsdp"), lax.axis_index("ctx")
    chip = place // 2
    lower = here < nc // 2
    depth = jnp.where(lower, here, nc - 1 - here)
    inner = jnp.where(lower, here + 1, here - 1)
    outer = jnp.where(lower, here - 1, here + 1)
    mesh_id = pl.DeviceIdType.MESH

    barrier = pltpu.get_barrier_semaphore()
    for k in range(1, chips):
        pl.semaphore_signal(
            barrier, inc=1, device_id={"fsdp": place ^ (2 * k)}, device_id_type=mesh_id
        )
    pl.semaphore_signal(barrier, inc=1, device_id={"ctx": inner}, device_id_type=mesh_id)

    @pl.when(depth > 0)
    def _():
        pl.semaphore_signal(barrier, inc=1, device_id={"ctx": outer}, device_id_type=mesh_id)
        pl.semaphore_wait(barrier, chips + 1)

    @pl.when(depth == 0)
    def _():
        pl.semaphore_wait(barrier, chips)

    def plane_copy(u, k):
        return pltpu.make_async_remote_copy(
            src_ref=sources[u].at[chip ^ k],
            dst_ref=owns[u].at[k],
            send_sem=plane_send.at[u, k],
            recv_sem=plane_recv.at[u, k],
            device_id={"fsdp": place ^ (2 * k)},
            device_id_type=mesh_id,
        )

    def local_copy(u):
        if u == 0:
            return pltpu.make_async_copy(sources[0], owns[0], local.at[0])
        return pltpu.make_async_copy(sources[u].at[chip], owns[u].at[0], local.at[u])

    for u in range(5):
        local_copy(u).start()
    for u in range(1, 5):
        for k in range(1, chips):
            plane_copy(u, k).start()

    units = [(0, None)] + [(1, k) for k in range(chips)] + [(u, None) for u in (2, 3, 4)]
    chunks = []
    for u, k in units:
        total = outs[u].shape[-2]
        size = chunk_rows(total)
        chunks += [(u, k, r, size) for r in range(0, total, size)]

    def views(c):
        u, k, r, size = chunks[c]
        rows = pl.ds(r, size)
        own = owns[u].at[rows] if u == 0 else owns[u].at[k or 0, rows]
        return [own] + [
            ref.at[rows] if k is None else ref.at[k, rows] for ref in (ins[u], xs[u], outs[u])
        ]

    def first_copy(c, across):
        own, arriving, x, _ = views(c)
        return pltpu.make_async_remote_copy(
            src_ref=own,
            dst_ref=x if across else arriving,
            send_sem=first_send.at[c],
            recv_sem=(x_sem if across else in_sem).at[c],
            device_id={"ctx": inner},
            device_id_type=mesh_id,
        )

    def second_copy(c, across):
        _, arriving, x, _ = views(c)
        return pltpu.make_async_remote_copy(
            src_ref=arriving if across else x,
            dst_ref=x,
            send_sem=second_send.at[c],
            recv_sem=x_sem.at[c],
            device_id={"ctx": outer},
            device_id_type=mesh_id,
        )

    def out_copy(c, across):
        _, arriving, x, out = views(c)
        return pltpu.make_async_copy(arriving if across else x, out, out_sem.at[c])

    def add_into(target, terms, size):
        @pl.loop(0, size // 16)
        def _(i):
            strip = pl.ds(pl.multiple_of(i * 16, 16), 16)
            target[strip, :] = sum(term[strip, :].astype(F32) for term in terms).astype(BF)

    def inward(c, level):
        u, k, r, size = chunks[c]
        own, arriving, _, _ = views(c)
        terms = [own]
        if r == 0:
            if not k:
                local_copy(u).wait()
            else:
                plane_copy(u, k).wait_recv()
            if u >= 2:
                for j in range(1, chips):
                    plane_copy(u, j).wait_recv()
        if u >= 2:
            terms += [owns[u].at[j, pl.ds(r, size)] for j in range(1, chips)]
        if level > 0:
            first_copy(c, False).wait_recv()
            terms.append(arriving)
        if len(terms) > 1:
            add_into(own, terms, size)
        if c >= FLIGHT:
            first_copy(c - FLIGHT, False).wait_send()
        first_copy(c, level == top).start()

    def outward(c, level):
        size = chunks[c][3]
        own, arriving, x, _ = views(c)
        first_copy(c, True).wait_recv()
        if level == top:
            add_into(arriving, [own, x], size)
        out_copy(c, level == top).start()
        if level > 0:
            if c >= FLIGHT:
                second_copy(c - FLIGHT, False).wait_send()
            second_copy(c, level == top).start()

    top = nc // 2 - 1
    count = len(chunks)
    for level in range(top + 1):

        @pl.when(depth == level)
        def _():
            lag = 1 + 2 * (top - level)
            for t in range(count + lag):
                if t < count:
                    inward(t, level)
                if t >= lag:
                    outward(t - lag, level)
            for c in range(max(0, count - FLIGHT), count):
                first_copy(c, False).wait_send()
                if level > 0:
                    second_copy(c, False).wait_send()
            for c in range(count):
                out_copy(c, False).wait()

    for u in range(1, 5):
        for k in range(1, chips):
            plane_copy(u, k).wait_send()


def finish(nf, nc, down, gate_up, *sums):
    chips = nf // 2
    arrays = (down, gate_up) + sums
    shapes = [down.shape, gate_up.shape] + [x.shape[1:] for x in sums]
    count = sum(
        (shape[0] if len(shape) == 3 else 1) * (shape[-2] // chunk_rows(shape[-2]))
        for shape in shapes
    )
    anywhere = pl.BlockSpec(memory_space=pl.ANY)
    dma = pltpu.SemaphoreType.DMA
    return pl.pallas_call(
        functools.partial(finish_kernel, nf, nc),
        in_specs=[anywhere] * 5,
        out_specs=[anywhere] * 5,
        out_shape=[jax.ShapeDtypeStruct(shape, BF) for shape in shapes],
        scratch_shapes=[pltpu.VMEM(x.shape, BF) for x in arrays]
        + [pltpu.VMEM(shape, BF) for shape in shapes]
        + [pltpu.VMEM(shape, BF) for shape in shapes]
        + [dma((5, chips)), dma((5, chips)), dma((5,))]
        + [dma((count,))] * 5,
        compiler_params=pltpu.CompilerParams(
            collective_id=0, has_side_effects=True, vmem_limit_bytes=56 << 20
        ),
        name="finish",
    )(*arrays)


def solution(mesh):
    nf, nc = mesh.shape["fsdp"], mesh.shape["ctx"]
    chips = nf // 2

    def swap(x, k):
        return lax.ppermute(x, "fsdp", [(i, i ^ k) for i in range(nf)])

    def cross(x, k):
        return lax.ppermute(x, "ctx", [(i, i ^ k) for i in range(nc)])

    def shards(
        tokens,
        attn_gain,
        w_query,
        w_key,
        w_value,
        w_out,
        ffn_gain,
        w_gate,
        w_up,
        w_down,
        block_table,
        positions,
        out_grad,
    ):
        place = lax.axis_index("fsdp")
        chip, core = place // 2, place % 2
        x = tokens[0].astype(F32)
        gb = out_grad[0]
        rows, width = x.shape
        hidden = w_gate.shape[1]
        part = hidden // chips
        shard = w_gate.shape[0]
        key_width = KV_HEADS * HEAD_DIM

        def core_sum(x):
            other = lax.dynamic_index_in_dim(x, 1 - core, 1, keepdims=False)
            mine = lax.dynamic_index_in_dim(x, core, 1, keepdims=False)
            return (mine.astype(F32) + swap(other, 1).astype(F32)).astype(BF)

        def rows_grad(left, right):
            columns = [left[:, i * shard : (i + 1) * shard] for i in range(nf)]
            even = jnp.concatenate(columns[::2], axis=1)
            odd = jnp.concatenate(columns[1::2], axis=1)
            mine = jnp.where(core == 0, even, odd)
            other = jnp.where(core == 0, odd, even)
            left = jnp.concatenate([mine, swap(other, 1)], axis=0)
            right = jnp.concatenate([right, swap(right, 1)], axis=0)
            return dot(left, right, (0, 0)).astype(BF).reshape(chips, shard, right.shape[1])

        gains = lax.all_gather(jnp.stack([attn_gain, ffn_gain]), "fsdp", axis=1, tiled=True)
        gains = gains.astype(F32)
        w_qkv = lax.all_gather(
            jnp.concatenate([w_query, w_key, w_value], axis=1), "fsdp", axis=0, tiled=True
        )
        w_o = lax.all_gather(w_out, "fsdp", axis=0, tiled=True)

        order = chip ^ jnp.arange(chips, dtype=jnp.int32)
        w_gate, w_up, gains = lax.optimization_barrier((w_gate, w_up, gains))
        gate_up = pick_columns(order, lax.axis_index("ctx"), nc, w_gate, w_up)
        first = jnp.stack([swap(gate_up[k], 2 * k) if k else gate_up[k] for k in range(chips)])
        upward = [(i, i + 1) for i in range(nc - 1)]
        downward = [(i + 1, i) for i in range(nc - 1)]
        below, above = [first], [first]
        for _ in range(nc - 2):
            below.append(lax.ppermute(below[-1], "ctx", upward))
            above.append(lax.ppermute(above[-1], "ctx", downward))
        w_d = jnp.zeros((2,) + w_down.shape, BF)
        w_d = lax.dynamic_update_index_in_dim(w_d, w_down, core, 0)
        w_d = lax.dynamic_update_index_in_dim(w_d, swap(w_down, 1), 1 - core, 0)
        w_d = w_d.reshape(part, width)

        half = HEAD_DIM // 2
        frequency = THETA ** (-jnp.arange(half, dtype=F32) * (2.0 / HEAD_DIM))
        angle = positions[0].astype(F32)[:, None] * frequency[None, :]
        cosine, sine = jnp.cos(angle), jnp.sin(angle)
        cos_lanes = jnp.tile(cosine, (1, 4))
        sin_lanes = jnp.tile(jnp.concatenate([-sine, sine], axis=1), (1, 2))
        blocks = 2 * nc
        stored = block_table.reshape(-1)
        number = jnp.arange(blocks, dtype=jnp.int32)
        where = jnp.sum(
            jnp.where(stored[None, :] == number[:, None], number[None, :], 0), axis=1
        )
        here = lax.axis_index("ctx")
        own = lax.dynamic_slice_in_dim(stored, 2 * here, 2)
        where = 2 * ((where // 2) ^ here) + where % 2
        table = jnp.concatenate([own, where]).astype(jnp.int32)

        inverse_one = lax.rsqrt(jnp.mean(x * x, axis=1, keepdims=True) + EPS)
        unit_one = x * inverse_one
        xn = (unit_one * gains[0][None, :]).astype(BF)
        qkv = dot(xn, w_qkv, (1, 0))
        kv = own_keys(qkv, cos_lanes, sin_lanes)
        sent, _ = lax.optimization_barrier((gb, kv))
        gb_of = [swap(sent, k) if k else gb for k in range(0, nf, 2)]
        _, below[-1], above[-1] = lax.optimization_barrier((kv, below[-1], above[-1]))
        below.append(lax.ppermute(below[-1], "ctx", upward))
        above.append(lax.ppermute(above[-1], "ctx", downward))
        kv = jnp.concatenate([cross(kv, k) if k else kv for k in range(nc)], axis=0)
        qr, o, ob, lse = attention_forward(table, qkv, cos_lanes, sin_lanes, kv)
        h1 = x + dot(ob, w_o, (1, 0))
        inverse_two = lax.rsqrt(jnp.mean(h1 * h1, axis=1, keepdims=True) + EPS)
        unit_two = h1 * inverse_two
        hn = (unit_two * gains[1][None, :]).astype(BF)

        pieces = [first] + below[1:] + above[1:]
        hn, gb_of, pieces = lax.optimization_barrier((hn, gb_of, pieces))
        w_gu = assemble(nf, nc, pieces + [swap(piece, 1) for piece in pieces])
        w_gu = w_gu.reshape(width, 2 * part)

        outs, dhns = [], []
        hn_of, act_of, dgu_of = [], [], []
        for k in range(0, nf, 2):
            hn_k = swap(hn, k) if k else hn
            gu = dot(hn_k, w_gu, (1, 0))
            dact = dot(gb_of[k // 2], w_d, (1, 1))
            gate, up = gu[:, :part], gu[:, part:]
            sg = jax.nn.sigmoid(gate)
            silu = gate * sg
            act = (silu * up).astype(BF)
            dgate = (dact * up * sg * (1.0 + gate * (1.0 - sg))).astype(BF)
            dgu = jnp.concatenate([dgate, (dact * silu).astype(BF)], axis=1)
            out_k = dot(act, w_d, (1, 0))
            dhn_k = dot(dgu, w_gu, (1, 1))
            outs.append(out_k.astype(BF) if k else out_k)
            dhns.append(dhn_k.astype(BF) if k else dhn_k)
            hn_of.append(hn_k)
            act_of.append(act)
            dgu_of.append(dgu)
        got = [swap(dhns[k], 2 * k) for k in range(1, chips)]
        act_of, dgu_of, got[:-1], _ = lax.optimization_barrier(
            (act_of, dgu_of, got[:-1], dhns[1:])
        )
        grad_hn = dhns[0]
        for piece in got:
            grad_hn = grad_hn + piece.astype(F32)

        gb_all = jnp.concatenate(gb_of, axis=0)
        down = dot(jnp.concatenate(act_of, axis=0), gb_all, (0, 0)).astype(BF)
        wide = rows_grad(jnp.concatenate(hn_of, axis=0), jnp.concatenate(dgu_of, axis=0))
        down_sum = core_sum(down.reshape((1, 2) + w_down.shape))[0]
        down_sum, wide, grad_hn = lax.optimization_barrier((down_sum, wide, grad_hn))
        branch = h1 + outs[0]
        for k in range(1, chips):
            branch = branch + swap(outs[k], 2 * k).astype(F32)
        layer_out = branch.astype(BF)

        gain_two_grad = jnp.sum(grad_hn * unit_two, axis=0)
        grad_unit = grad_hn * gains[1][None, :]
        dh1 = gb.astype(F32) + inverse_two * (
            grad_unit - unit_two * jnp.mean(grad_unit * unit_two, axis=1, keepdims=True)
        )
        dab = dh1.astype(BF)
        dob = dot(dab, w_o, (1, 1)).astype(BF)
        out_term = rows_grad(ob, dab)
        dq, dkv = attention_backward(table, qr, dob, o, lse, kv, cos_lanes, sin_lanes)
        pieces = [dkv[:, k * rows : (k + 1) * rows] for k in range(nc)]
        pieces = [cross(piece, k) if k else piece for k, piece in enumerate(pieces)]
        dqkv = jnp.concatenate([dq, own_key_grads(pieces, cos_lanes, sin_lanes)], axis=1)
        grad_xn = dot(dqkv, w_qkv, (1, 1))
        gain_one_grad = jnp.sum(grad_xn * unit_one, axis=0)
        grad_unit = grad_xn * gains[0][None, :]
        tokens_grad = dh1 + inverse_one * (
            grad_unit - unit_one * jnp.mean(grad_unit * unit_one, axis=1, keepdims=True)
        )
        qkv_term = rows_grad(xn, dqkv)

        gains_of = jnp.stack([gain_one_grad, gain_two_grad]).reshape(2, chips, 2, shard)
        other = lax.dynamic_index_in_dim(gains_of, 1 - core, 2, keepdims=False)
        mine = lax.dynamic_index_in_dim(gains_of, core, 2, keepdims=False)
        gains_of = (mine + swap(other, 1)).transpose(1, 0, 2).reshape(chips, 1, 2 * shard)
        gains_of = jnp.pad(gains_of.astype(BF), ((0, 0), (0, 15), (0, 0)))
        down_sum, gu_sum, out_sum, qkv_sum, gain_sum = finish(
            nf, nc, down_sum, wide, out_term, qkv_term, gains_of
        )
        qkv_sum = qkv_sum.astype(F32)
        gain_sum = gain_sum[0].reshape(2, shard).astype(F32)
        gate_grad, up_grad = place_columns(order, gu_sum)
        query_width = HEADS * HEAD_DIM
        return (
            layer_out.reshape(1, rows, width),
            tokens_grad.reshape(1, rows, width),
            gain_sum[0],
            qkv_sum[:, :query_width],
            qkv_sum[:, query_width : query_width + key_width],
            qkv_sum[:, query_width + key_width :],
            out_sum.astype(F32),
            gain_sum[1],
            gate_grad,
            up_grad,
            down_sum.astype(F32),
        )

    weight = P("fsdp", None)
    activation = P("fsdp", "ctx", None)
    return jax.shard_map(
        shards,
        mesh=mesh,
        in_specs=(
            activation,
            P("fsdp"),
            weight,
            weight,
            weight,
            weight,
            P("fsdp"),
            weight,
            weight,
            weight,
            P(),
            P("fsdp", "ctx"),
            activation,
        ),
        out_specs=(
            activation,
            activation,
            P("fsdp"),
            weight,
            weight,
            weight,
            weight,
            P("fsdp"),
            weight,
            weight,
            weight,
        ),
        check_vma=False,
    )
```

```python
import functools

import jax
import jax.numpy as jnp
from jax import lax
from jax.experimental import pallas as pl
from jax.experimental.pallas import tpu as pltpu
from jax.sharding import PartitionSpec as P

HEADS = 32
KV_HEADS = 4
HEAD_DIM = 64
GROUP = HEADS // KV_HEADS
PAIRS = GROUP // 2
LANES = 2 * HEAD_DIM
STACK = PAIRS * LANES

EPS = 1e-05
THETA = 10000.0
NEG = -1e30
FLIGHT = 2
BF = jnp.bfloat16
F32 = jnp.float32


def dot(left, right, contract, out=F32):
    return lax.dot_general(
        left, right, ((contract[:1], contract[1:]), ((), ())), preferred_element_type=out
    )


def swap_halves(z):
    lane = lax.broadcasted_iota(jnp.int32, z.shape, 1)
    first = (lane % HEAD_DIM) < (HEAD_DIM // 2)
    return jnp.where(
        first,
        pltpu.roll(z, LANES - HEAD_DIM // 2, 1),
        pltpu.roll(z, HEAD_DIM // 2, 1),
    )


def split_heads(rows):
    lane = lax.broadcasted_iota(jnp.int32, rows.shape, 1)
    zero = jnp.zeros_like(rows)
    return jnp.concatenate(
        [jnp.where(lane < HEAD_DIM, rows, zero), jnp.where(lane >= HEAD_DIM, rows, zero)], axis=0
    )


def join_heads(columns):
    half = columns.shape[1] // 2
    sub = lax.broadcasted_iota(jnp.int32, (LANES, half), 0)
    return jnp.where(sub < HEAD_DIM, columns[:, :half], columns[:, half:]).T


def stack_pairs(ref, rows):
    return jnp.concatenate([ref[rows, p * LANES : (p + 1) * LANES] for p in range(PAIRS)], axis=0)


def two_blocks(ref, table, j, block):
    parts = [
        ref[pl.ds(pl.multiple_of(table[2 + 2 * j + i] * block, block), block), :] for i in range(2)
    ]
    return jnp.concatenate(parts, axis=0)


def causal(scores, j, own, block):
    key = lax.broadcasted_iota(jnp.int32, scores.shape, 0) + j * (2 * block)
    query = lax.broadcasted_iota(jnp.int32, scores.shape, 1) % block + own * block
    return jnp.where(key <= query, scores, NEG)


def head_twice(pair, group):
    wide = pair.astype(F32)
    lane = lax.broadcasted_iota(jnp.int32, wide.shape, 1)
    keep = (lane < HEAD_DIM) == (group % 2 == 0)
    return jnp.where(keep, wide, pltpu.roll(wide, HEAD_DIM, 1)).astype(BF)


def attention_forward_kernel(
    table,
    q_ref,
    cos_ref,
    sin_ref,
    k_pair,
    v_pair,
    qr_ref,
    o_ref,
    ob_ref,
    lse_ref,
    qm,
    m,
    l,
    acc,
    k_ref,
    v_ref,
):
    block = q_ref.shape[0] // 2
    group = pl.program_id(0)
    k_ref[...] = head_twice(k_pair[...], group)
    v_ref[...] = head_twice(v_pair[...], group)
    for h in range(2):
        rows = slice(h * block, (h + 1) * block)
        cosine, sine = cos_ref[rows, :], sin_ref[rows, :]
        for p in range(PAIRS):
            lanes = slice(p * LANES, (p + 1) * LANES)
            z = q_ref[rows, lanes]
            qr_ref[rows, lanes] = (z * cosine + swap_halves(z) * sine).astype(BF)
        scaled = stack_pairs(qr_ref, rows).astype(F32) * (HEAD_DIM**-0.5)
        qm[...] = split_heads(scaled).astype(BF)
        m[...] = jnp.full_like(m, NEG)
        l[...] = jnp.zeros_like(l)
        acc[...] = jnp.zeros_like(acc)
        own = table[h]

        def step(j, masked):
            keys = two_blocks(k_ref, table, j, block)
            values = two_blocks(v_ref, table, j, block)
            s = dot(keys, qm[...], (1, 1))
            if masked:
                s = causal(s, j, own, block)
            before = m[...]
            now = jnp.maximum(before, jnp.max(s, axis=0, keepdims=True))
            p = jnp.exp(s - now)
            decay = jnp.exp(before - now)
            l[...] = l[...] * decay + jnp.sum(p, axis=0, keepdims=True)
            acc[...] = acc[...] * decay + dot(values, p.astype(BF), (0, 0))
            m[...] = now

        last = own // 2

        @pl.loop(0, last)
        def _(j):
            step(j, False)

        step(last, True)
        lse_ref[0, h : h + 1, :] = m[...] + jnp.log(l[...])
        o = join_heads(acc[...] / l[...])
        for p in range(PAIRS):
            lanes = slice(p * LANES, (p + 1) * LANES)
            piece = o[p * block : (p + 1) * block, :]
            o_ref[rows, lanes] = piece
            ob_ref[rows, lanes] = piece.astype(BF)


def attention_forward(table, q, cosine, sine, kv):
    rows, length = q.shape[0], kv.shape[0]
    query_width = HEADS * HEAD_DIM
    columns = pl.BlockSpec((rows, STACK), lambda g, t: (0, g))
    whole = pl.BlockSpec((rows, LANES), lambda g, t: (0, 0))
    key_pair = pl.BlockSpec((length, LANES), lambda g, t: (0, g // 2))
    value_pair = pl.BlockSpec((length, LANES), lambda g, t: (0, KV_HEADS // 2 + g // 2))
    wide = GROUP * (rows // 2)
    return pl.pallas_call(
        attention_forward_kernel,
        grid_spec=pltpu.PrefetchScalarGridSpec(
            num_scalar_prefetch=1,
            grid=(KV_HEADS,),
            in_specs=[columns, whole, whole, key_pair, value_pair],
            out_specs=[
                columns,
                columns,
                columns,
                pl.BlockSpec((1, 2, wide), lambda g, t: (g, 0, 0)),
            ],
            scratch_shapes=[
                pltpu.VMEM((wide, LANES), BF),
                pltpu.VMEM((1, wide), F32),
                pltpu.VMEM((1, wide), F32),
                pltpu.VMEM((LANES, wide), F32),
                pltpu.VMEM((length, LANES), BF),
                pltpu.VMEM((length, LANES), BF),
            ],
        ),
        out_shape=[
            jax.ShapeDtypeStruct((rows, query_width), BF),
            jax.ShapeDtypeStruct((rows, query_width), F32),
            jax.ShapeDtypeStruct((rows, query_width), BF),
            jax.ShapeDtypeStruct((KV_HEADS, 2, wide), F32),
        ],
        compiler_params=pltpu.CompilerParams(vmem_limit_bytes=32 << 20),
        cost_estimate=pl.CostEstimate(
            flops=8 * HEADS * rows * length * HEAD_DIM,
            bytes_accessed=16 * rows * HEADS * HEAD_DIM,
            transcendentals=HEADS * rows * length,
        ),
        name="attention_forward",
    )(table, q, cosine, sine, kv, kv)


def attention_backward_kernel(
    table,
    qr_ref,
    do_ref,
    o_ref,
    lse_ref,
    k_pair,
    v_pair,
    cos_ref,
    sin_ref,
    dq_ref,
    dkv_ref,
    qm,
    dom,
    dqt,
    k_ref,
    v_ref,
    dk_ref,
    dv_ref,
):
    block = qr_ref.shape[0] // 2
    group = pl.program_id(0)
    k_ref[...] = head_twice(k_pair[...], group)
    v_ref[...] = head_twice(v_pair[...], group)
    dk_ref[...] = jnp.zeros_like(dk_ref)
    dv_ref[...] = jnp.zeros_like(dv_ref)
    for h in range(2):
        rows = slice(h * block, (h + 1) * block)
        scaled = stack_pairs(qr_ref, rows).astype(F32) * (HEAD_DIM**-0.5)
        qm[...] = split_heads(scaled).astype(BF)
        grads = stack_pairs(do_ref, rows).astype(F32)
        dom[...] = split_heads(grads).astype(BF)
        product = (grads * stack_pairs(o_ref, rows)).T
        inner = jnp.concatenate(
            [
                jnp.sum(product[:HEAD_DIM], axis=0, keepdims=True),
                jnp.sum(product[HEAD_DIM:], axis=0, keepdims=True),
            ],
            axis=1,
        )
        lse = lse_ref[0, h : h + 1, :]
        dqt[...] = jnp.zeros_like(dqt)
        own = table[h]

        def step(j, masked):
            keys = two_blocks(k_ref, table, j, block)
            values = two_blocks(v_ref, table, j, block)
            s = dot(keys, qm[...], (1, 1))
            if masked:
                s = causal(s, j, own, block)
            p = jnp.exp(s - lse)
            dp = dot(values, dom[...], (1, 1))
            ds = (p * (dp - inner)).astype(BF)
            dv = dot(p.astype(BF), dom[...], (1, 0))
            dk = dot(ds, qm[...], (1, 0))
            dqt[...] += dot(keys, ds, (0, 0))
            for i in range(2):
                at = pl.ds(pl.multiple_of(table[2 + 2 * j + i] * block, block), block)
                dk_ref[at, :] += dk[i * block : (i + 1) * block]
                dv_ref[at, :] += dv[i * block : (i + 1) * block]

        last = own // 2

        @pl.loop(0, last)
        def _(j):
            step(j, False)

        step(last, True)
        cosine, sine = cos_ref[rows, :], sin_ref[rows, :]
        dq = join_heads(dqt[...] * (HEAD_DIM**-0.5))
        for p in range(PAIRS):
            z = dq[p * block : (p + 1) * block, :]
            dq_ref[rows, p * LANES : (p + 1) * LANES] = (
                z * cosine - swap_halves(z) * sine
            ).astype(BF)
    lane = lax.broadcasted_iota(jnp.int32, dk_ref.shape, 1)
    keep = (lane < HEAD_DIM) == (group % 2 == 0)
    for i, ref in enumerate((dk_ref, dv_ref)):
        both = ref[...] + pltpu.roll(ref[...], HEAD_DIM, 1)
        dkv_ref[i] = jnp.where(keep, both, dkv_ref[i].astype(F32)).astype(BF)


def attention_backward(table, qr, grads, o, lse, kv, cosine, sine):
    rows, length = qr.shape[0], kv.shape[0]
    columns = pl.BlockSpec((rows, STACK), lambda g, t: (0, g))
    whole = pl.BlockSpec((rows, LANES), lambda g, t: (0, 0))
    key_pair = pl.BlockSpec((length, LANES), lambda g, t: (0, g // 2))
    value_pair = pl.BlockSpec((length, LANES), lambda g, t: (0, KV_HEADS // 2 + g // 2))
    wide = GROUP * (rows // 2)
    return pl.pallas_call(
        attention_backward_kernel,
        grid_spec=pltpu.PrefetchScalarGridSpec(
            num_scalar_prefetch=1,
            grid=(KV_HEADS,),
            in_specs=[
                columns,
                columns,
                columns,
                pl.BlockSpec((1, 2, wide), lambda g, t: (g, 0, 0)),
                key_pair,
                value_pair,
                whole,
                whole,
            ],
            out_specs=[columns, pl.BlockSpec((2, length, LANES), lambda g, t: (0, 0, g // 2))],
            scratch_shapes=[
                pltpu.VMEM((wide, LANES), BF),
                pltpu.VMEM((wide, LANES), BF),
                pltpu.VMEM((LANES, wide), F32),
                pltpu.VMEM((length, LANES), BF),
                pltpu.VMEM((length, LANES), BF),
                pltpu.VMEM((length, LANES), F32),
                pltpu.VMEM((length, LANES), F32),
            ],
        ),
        out_shape=[
            jax.ShapeDtypeStruct(qr.shape, BF),
            jax.ShapeDtypeStruct((2, length, KV_HEADS * HEAD_DIM), BF),
        ],
        compiler_params=pltpu.CompilerParams(vmem_limit_bytes=32 << 20),
        cost_estimate=pl.CostEstimate(
            flops=20 * HEADS * rows * length * HEAD_DIM,
            bytes_accessed=16 * rows * HEADS * HEAD_DIM,
            transcendentals=HEADS * rows * length,
        ),
        name="attention_backward",
    )(table, qr, grads, o, lse, kv, kv, cosine, sine)


def own_keys_kernel(k_ref, v_ref, cos_ref, sin_ref, kv_ref):
    width = k_ref.shape[1]
    for p in range(width // LANES):
        lanes = slice(p * LANES, (p + 1) * LANES)
        z = k_ref[:, lanes]
        kv_ref[:, lanes] = (z * cos_ref[...] + swap_halves(z) * sin_ref[...]).astype(BF)
    kv_ref[:, width:] = v_ref[...].astype(BF)


def own_keys(qkv, cosine, sine):
    rows, width = qkv.shape[0], KV_HEADS * HEAD_DIM
    at = HEADS * HEAD_DIM // width
    whole = pl.BlockSpec((rows, LANES), lambda i: (0, 0))
    return pl.pallas_call(
        own_keys_kernel,
        grid=(1,),
        in_specs=[
            pl.BlockSpec((rows, width), lambda i: (0, at)),
            pl.BlockSpec((rows, width), lambda i: (0, at + 1)),
            whole,
            whole,
        ],
        out_specs=pl.BlockSpec((rows, 2 * width), lambda i: (0, 0)),
        out_shape=jax.ShapeDtypeStruct((rows, 2 * width), BF),
        name="own_keys",
    )(qkv, qkv, cosine, sine)


def own_key_grads_kernel(*refs):
    *pieces, cos_ref, sin_ref, out_ref = refs
    width = out_ref.shape[1] // 2

    def total(i, lanes):
        return sum(piece[i, :, lanes].astype(F32) for piece in pieces)

    for p in range(width // LANES):
        lanes = slice(p * LANES, (p + 1) * LANES)
        z = total(0, lanes)
        out_ref[:, lanes] = (z * cos_ref[...] - swap_halves(z) * sin_ref[...]).astype(BF)
        out_ref[:, width + p * LANES : width + (p + 1) * LANES] = total(1, lanes).astype(BF)


def own_key_grads(pieces, cosine, sine):
    rows, width = pieces[0].shape[1], pieces[0].shape[2]
    return pl.pallas_call(
        own_key_grads_kernel,
        out_shape=jax.ShapeDtypeStruct((rows, 2 * width), BF),
        name="own_key_grads",
    )(*pieces, cosine, sine)


def pick_columns_kernel(order, gate_ref, up_ref, out_ref):
    part = gate_ref.shape[1]
    out_ref[0, :, :part] = gate_ref[...]
    out_ref[0, :, part:] = up_ref[...]


def pick_columns(order, w_gate, w_up):
    shard, hidden = w_gate.shape
    parts = order.shape[0]
    part = hidden // parts
    if part % 128:
        both = [w.reshape(shard, parts, part).transpose(1, 0, 2) for w in (w_gate, w_up)]
        return jnp.take(jnp.concatenate(both, axis=2), order, axis=0)
    columns = pl.BlockSpec((shard, part), lambda k, t: (0, t[k]))
    return pl.pallas_call(
        pick_columns_kernel,
        grid_spec=pltpu.PrefetchScalarGridSpec(
            num_scalar_prefetch=1,
            grid=(parts,),
            in_specs=[columns, columns],
            out_specs=pl.BlockSpec((1, shard, 2 * part), lambda k, t: (k, 0, 0)),
        ),
        out_shape=jax.ShapeDtypeStruct((parts, shard, 2 * part), BF),
        name="pick_columns",
    )(order, w_gate, w_up)


def share_kernel(nf, nc, low, size, *refs):
    (qkv, picked, down, gains, wqkv, wide, downs, all_gains) = refs[:8]
    (qkv_own, wide_own, down_own, gains_own) = refs[8:12]
    (local, plane_send, plane_recv, along_send, along_recv, core_send, core_recv) = refs[12:19]
    (gain_send, gain_recv, down_sem, qkv_send, qkv_recv, qkv_core) = refs[19:]
    chips = nf // 2
    place, here = lax.axis_index("fsdp"), lax.axis_index("ctx")
    core = place % 2
    mesh_id = pl.DeviceIdType.MESH

    barrier = pltpu.get_barrier_semaphore()

    def greet(target):
        pl.semaphore_signal(barrier, inc=1, device_id=target, device_id_type=mesh_id)

    for j in range(1, nf):
        greet({"fsdp": place ^ j})
    for pos in range(nc):

        @pl.when(here == pos)
        def _():
            near = [i for i in (pos - 1, pos + 1) if 0 <= i < nc]
            for i in near:
                greet({"ctx": i})
            pl.semaphore_wait(barrier, nf - 1 + len(near))

    def remote(source, target, sends, recvs, where):
        return pltpu.make_async_remote_copy(
            src_ref=source,
            dst_ref=target,
            send_sem=sends,
            recv_sem=recvs,
            device_id=where,
            device_id_type=mesh_id,
        )

    def rows_of(share):
        return pl.ds(low + share * size, size)

    def plane_copy(k, kind):
        rows = rows_of(here) if kind else pl.ds(0, low)
        return remote(
            picked.at[k, rows],
            wide.at[place, rows],
            plane_send.at[kind, k],
            plane_recv.at[kind, k],
            {"fsdp": place ^ (2 * k)},
        )

    def along_copy(k, share, up, target):
        block = wide.at[place ^ (2 * k), rows_of(share)]
        return remote(
            block, block, along_send.at[up, share, k], along_recv.at[share, k], {"ctx": target}
        )

    def core_copy(k, share):
        rows = rows_of(share) if share < nc else pl.ds(0, low)
        block = wide.at[place ^ (2 * k), rows] if k else wide.at[place]
        source = block if k else picked.at[0]
        return remote(
            source, block, core_send.at[k, share], core_recv.at[k, share], {"fsdp": place ^ 1}
        )

    half = qkv.shape[0] // 2
    relayed = chips == 4

    def qkv_copy(k, part=0):
        if part == 0:
            source, owner, rows = qkv, place, pl.ds(0, 2 * half)
        else:
            owner, rows = place ^ (2 * (3 - k)), pl.ds((2 - k) * half, half)
            source = wqkv.at[owner, rows]
        at = 2 * k + part
        return remote(
            source,
            wqkv.at[owner, rows],
            qkv_send.at[at],
            qkv_recv.at[at],
            {"fsdp": place ^ (2 * k)},
        )

    def qkv_core_copy(k):
        block = wqkv.at[place ^ (2 * k)]
        return remote(
            block if k else qkv, block, qkv_core.at[0, k], qkv_core.at[1, k], {"fsdp": place ^ 1}
        )

    def down_copy():
        return remote(down, downs.at[core], down_sem.at[0], down_sem.at[1], {"fsdp": place ^ 1})

    def gain_copy(j):
        return remote(
            gains, all_gains.at[place], gain_send.at[j], gain_recv.at[j], {"fsdp": place ^ j}
        )

    direct = (1, 2) if relayed else tuple(range(1, chips))
    for k in range(1, chips):
        plane_copy(k, 1).start()
    for j in range(1, nf):
        gain_copy(j).start()
    core_copy(0, nc).start()
    qkv_core_copy(0).start()
    down_copy().start()
    own = (
        (qkv, qkv_own, wqkv.at[place]),
        (picked.at[0], wide_own, wide.at[place]),
        (down, down_own, downs.at[core]),
        (gains, gains_own, all_gains.at[place]),
    )
    for i, (source, stage, _) in enumerate(own):
        pltpu.make_async_copy(source, stage, local.at[0, i]).start()
    for i, (source, stage, target) in enumerate(own):
        pltpu.make_async_copy(source, stage, local.at[0, i]).wait()
        pltpu.make_async_copy(stage, target, local.at[1, i]).start()

    for k in range(1, chips):
        plane_copy(k, 1).wait_send()
    for k in direct:
        qkv_copy(k).start()

    for pos in range(nc):

        @pl.when(here == pos)
        def _():
            def pass_on(k, share):
                if share <= pos < nc - 1:
                    along_copy(k, share, 1, pos + 1).start()
                if share >= pos > 0:
                    along_copy(k, share, 0, pos - 1).start()
                core_copy(k, share).start()

            for k in range(1, chips):
                plane_copy(k, 1).wait_recv()
                pass_on(k, pos)
            if low:
                for k in range(1, chips):
                    plane_copy(k, 0).start()
            for k in direct:
                qkv_copy(k).wait_recv()
                if relayed:
                    qkv_copy(3 - k, 1).start()
                qkv_core_copy(k).start()
            for d in range(1, nc):
                for share in (pos - d, pos + d):
                    if 0 <= share < nc:
                        for k in range(1, chips):
                            along_copy(k, share, 0, 0).wait_recv()
                            pass_on(k, share)
            if low:
                for k in range(1, chips):
                    plane_copy(k, 0).wait_recv()
                    core_copy(k, nc).start()
            if relayed:
                for k in direct:
                    qkv_copy(k, 1).wait_recv()
                qkv_core_copy(3).start()
            for k in range(1, chips):
                for share in range(nc):
                    if share <= pos < nc - 1:
                        along_copy(k, share, 1, pos + 1).wait_send()
                    if share >= pos > 0:
                        along_copy(k, share, 0, pos - 1).wait_send()

    for k in range(chips):
        for share in range(nc + 1):
            if (share < nc and k) or (share == nc and (low or not k)):
                core_copy(k, share).wait_send()
                core_copy(k, share).wait_recv()
    if low:
        for k in range(1, chips):
            plane_copy(k, 0).wait_send()
    for j in range(1, nf):
        gain_copy(j).wait()
    for k in direct:
        qkv_copy(k).wait_send()
        if relayed:
            qkv_copy(k, 1).wait_send()
    for k in range(chips):
        qkv_core_copy(k).wait()
    down_copy().wait()
    for i, (_, stage, target) in enumerate(own):
        pltpu.make_async_copy(stage, target, local.at[1, i]).wait()


def share_weights(nf, nc, qkv, picked, down, gains):
    chips, shard, columns = picked.shape
    size = 16 * max(1, (shard * 3 // 4) // (16 * nc))
    low = shard - nc * size
    anywhere = pl.BlockSpec(memory_space=pl.ANY)
    dma = pltpu.SemaphoreType.DMA
    return pl.pallas_call(
        functools.partial(share_kernel, nf, nc, low, size),
        in_specs=[anywhere] * 4,
        out_specs=[anywhere] * 4,
        out_shape=[
            jax.ShapeDtypeStruct((nf,) + qkv.shape, BF),
            jax.ShapeDtypeStruct((nf, shard, columns), BF),
            jax.ShapeDtypeStruct((2,) + down.shape, BF),
            jax.ShapeDtypeStruct((nf,) + gains.shape, BF),
        ],
        scratch_shapes=[
            pltpu.VMEM(qkv.shape, BF),
            pltpu.VMEM((shard, columns), BF),
            pltpu.VMEM(down.shape, BF),
            pltpu.VMEM(gains.shape, BF),
            dma((2, 4)),
            dma((2, chips)),
            dma((2, chips)),
            dma((2, nc, chips)),
            dma((nc, chips)),
            dma((chips, nc + 1)),
            dma((chips, nc + 1)),
            dma((nf,)),
            dma((nf,)),
            dma((2,)),
            dma((2 * chips,)),
            dma((2 * chips,)),
            dma((2, chips)),
        ],
        compiler_params=pltpu.CompilerParams(
            collective_id=1, has_side_effects=True, vmem_limit_bytes=56 << 20
        ),
        name="share_weights",
    )(qkv, picked, down, gains)


def place_columns_kernel(order, both_ref, gate_ref, up_ref):
    part = gate_ref.shape[1]
    gate_ref[...] = both_ref[0, :, :part].astype(F32)
    up_ref[...] = both_ref[0, :, part:].astype(F32)


def place_columns(order, both):
    parts, shard, part = both.shape[0], both.shape[1], both.shape[2] // 2
    out = jax.ShapeDtypeStruct((shard, parts * part), F32)
    if part % 128:
        both = jnp.take(both, order, axis=0).transpose(1, 0, 2).astype(F32)
        return [both[:, :, i * part : (i + 1) * part].reshape(out.shape) for i in range(2)]
    columns = pl.BlockSpec((shard, part), lambda k, t: (0, t[k]))
    return pl.pallas_call(
        place_columns_kernel,
        grid_spec=pltpu.PrefetchScalarGridSpec(
            num_scalar_prefetch=1,
            grid=(parts,),
            in_specs=[pl.BlockSpec((1, shard, 2 * part), lambda k, t: (k, 0, 0))],
            out_specs=[columns, columns],
        ),
        out_shape=[out, out],
        name="place_columns",
    )(order, both)


def chunk_rows(rows):
    return max(r for r in range(16, 65, 16) if rows % r == 0)


def finish_kernel(nf, nc, *refs):
    pieces, refs = refs[: nf // 2], refs[nf // 2 - 1 :]
    sources, (outs, owns, ins, xs) = refs[:4], (refs[i : i + 4] for i in range(4, 20, 4))
    plane_send, plane_recv, local, in_sem, x_sem, first_send, second_send, out_sem = refs[20:]
    chips = nf // 2
    place, here = lax.axis_index("fsdp"), lax.axis_index("ctx")
    chip = place // 2
    lower = here < nc // 2
    depth = jnp.where(lower, here, nc - 1 - here)
    inner = jnp.where(lower, here + 1, here - 1)
    outer = jnp.where(lower, here - 1, here + 1)
    mesh_id = pl.DeviceIdType.MESH

    barrier = pltpu.get_barrier_semaphore()
    for k in range(1, chips):
        pl.semaphore_signal(
            barrier, inc=1, device_id={"fsdp": place ^ (2 * k)}, device_id_type=mesh_id
        )
    pl.semaphore_signal(barrier, inc=1, device_id={"ctx": inner}, device_id_type=mesh_id)

    @pl.when(depth > 0)
    def _():
        pl.semaphore_signal(barrier, inc=1, device_id={"ctx": outer}, device_id_type=mesh_id)
        pl.semaphore_wait(barrier, chips + 1)

    @pl.when(depth == 0)
    def _():
        pl.semaphore_wait(barrier, chips)

    def plane_copy(u, k):
        return pltpu.make_async_remote_copy(
            src_ref=sources[u].at[chip ^ k],
            dst_ref=owns[u].at[k],
            send_sem=plane_send.at[u, k],
            recv_sem=plane_recv.at[u, k],
            device_id={"fsdp": place ^ (2 * k)},
            device_id_type=mesh_id,
        )

    def local_copy(u, k):
        source = sources[u].at[chip] if u else pieces[k]
        return pltpu.make_async_copy(source, owns[u].at[k], local.at[u, k])

    for u in range(4):
        for k in range(chips):
            if u == 0 or k == 0:
                local_copy(u, k).start()
            else:
                plane_copy(u, k).start()

    units = [(0, k) for k in range(chips)] + [(u, None) for u in (1, 2, 3)]
    chunks = []
    for u, k in units:
        total = outs[u].shape[-2]
        size = chunk_rows(total)
        chunks += [(u, k, r, size) for r in range(0, total, size)]

    def views(c):
        u, k, r, size = chunks[c]
        rows = pl.ds(r, size)
        return [owns[u].at[k or 0, rows]] + [
            ref.at[rows] if k is None else ref.at[k, rows] for ref in (ins[u], xs[u], outs[u])
        ]

    def first_copy(c, across):
        own, arriving, x, _ = views(c)
        return pltpu.make_async_remote_copy(
            src_ref=own,
            dst_ref=x if across else arriving,
            send_sem=first_send.at[c],
            recv_sem=(x_sem if across else in_sem).at[c],
            device_id={"ctx": inner},
            device_id_type=mesh_id,
        )

    def second_copy(c, across):
        _, arriving, x, _ = views(c)
        return pltpu.make_async_remote_copy(
            src_ref=arriving if across else x,
            dst_ref=x,
            send_sem=second_send.at[c],
            recv_sem=x_sem.at[c],
            device_id={"ctx": outer},
            device_id_type=mesh_id,
        )

    def out_copy(c, across):
        _, arriving, x, out = views(c)
        return pltpu.make_async_copy(arriving if across else x, out, out_sem.at[c])

    def add_into(target, terms, size):
        @pl.loop(0, size // 16)
        def _(i):
            strip = pl.ds(pl.multiple_of(i * 16, 16), 16)
            target[strip, :] = sum(term[strip, :].astype(F32) for term in terms).astype(BF)

    def inward(c, level):
        u, k, r, size = chunks[c]
        own, arriving, _, _ = views(c)
        terms = [own]
        if r == 0:
            local_copy(u, k or 0).wait()
            if u >= 1:
                for j in range(1, chips):
                    plane_copy(u, j).wait_recv()
        if u >= 1:
            terms += [owns[u].at[j, pl.ds(r, size)] for j in range(1, chips)]
        if level > 0:
            first_copy(c, False).wait_recv()
            terms.append(arriving)
        if len(terms) > 1:
            add_into(own, terms, size)
        if c >= FLIGHT:
            first_copy(c - FLIGHT, False).wait_send()
        first_copy(c, level == top).start()

    def outward(c, level):
        size = chunks[c][3]
        own, arriving, x, _ = views(c)
        first_copy(c, True).wait_recv()
        if level == top:
            add_into(arriving, [own, x], size)
        out_copy(c, level == top).start()
        if level > 0:
            if c >= FLIGHT:
                second_copy(c - FLIGHT, False).wait_send()
            second_copy(c, level == top).start()

    top = nc // 2 - 1
    count = len(chunks)
    for level in range(top + 1):

        @pl.when(depth == level)
        def _():
            lag = 1 + 2 * (top - level)
            for t in range(count + lag):
                if t < count:
                    inward(t, level)
                if t >= lag:
                    outward(t - lag, level)
            for c in range(max(0, count - FLIGHT), count):
                first_copy(c, False).wait_send()
                if level > 0:
                    second_copy(c, False).wait_send()
            for c in range(count):
                out_copy(c, False).wait()

    for u in range(1, 4):
        for k in range(1, chips):
            plane_copy(u, k).wait_send()


def finish(nf, nc, pieces, sums):
    chips = nf // 2
    pieces_shape = (chips,) + pieces[0].shape
    shapes = [pieces_shape] + [x.shape[1:] for x in sums]
    count = sum(
        (shape[0] if len(shape) == 3 else 1) * (shape[-2] // chunk_rows(shape[-2]))
        for shape in shapes
    )
    anywhere = pl.BlockSpec(memory_space=pl.ANY)
    dma = pltpu.SemaphoreType.DMA
    return pl.pallas_call(
        functools.partial(finish_kernel, nf, nc),
        in_specs=[anywhere] * (chips + 3),
        out_specs=[anywhere] * 4,
        out_shape=[jax.ShapeDtypeStruct(shape, BF) for shape in shapes],
        scratch_shapes=[pltpu.VMEM(x, BF) for x in [pieces_shape] + [x.shape for x in sums]]
        + [pltpu.VMEM(shape, BF) for shape in shapes]
        + [pltpu.VMEM(shape, BF) for shape in shapes]
        + [dma((4, chips)), dma((4, chips)), dma((4, chips))]
        + [dma((count,))] * 5,
        compiler_params=pltpu.CompilerParams(
            collective_id=0, has_side_effects=True, vmem_limit_bytes=48 << 20
        ),
        cost_estimate=pl.CostEstimate(
            flops=200_000_000_000, bytes_accessed=60_000_000, transcendentals=0
        ),
        name="finish",
    )(*pieces, *sums)


def solution(mesh):
    nf, nc = mesh.shape["fsdp"], mesh.shape["ctx"]
    chips = nf // 2

    def swap(x, k):
        return lax.ppermute(x, "fsdp", [(i, i ^ k) for i in range(nf)])

    def plane_gather(x):
        if chips != 4:
            return [swap(x, 2 * k) for k in range(1, chips)]
        one, two = swap(x, 2), swap(x, 4)
        half = x.shape[0] // 2
        return [one, two, jnp.concatenate([swap(one[:half], 4), swap(two[half:], 2)], axis=0)]

    def cross(x, k):
        return lax.ppermute(x, "ctx", [(i, i ^ k) for i in range(nc)])

    def shards(
        tokens,
        attn_gain,
        w_query,
        w_key,
        w_value,
        w_out,
        ffn_gain,
        w_gate,
        w_up,
        w_down,
        block_table,
        positions,
        out_grad,
    ):
        place = lax.axis_index("fsdp")
        chip, core = place // 2, place % 2
        x = tokens[0].astype(F32)
        gb = out_grad[0]
        rows, width = x.shape
        hidden = w_gate.shape[1]
        part = hidden // chips
        shard = w_gate.shape[0]
        key_width = KV_HEADS * HEAD_DIM

        def core_sum(x):
            other = lax.dynamic_index_in_dim(x, 1 - core, 1, keepdims=False)
            mine = lax.dynamic_index_in_dim(x, core, 1, keepdims=False)
            return (mine.astype(F32) + swap(other, 1).astype(F32)).astype(BF)

        def rows_grad(left, right):
            columns = [left[:, i * shard : (i + 1) * shard] for i in range(nf)]
            even = jnp.concatenate(columns[::2], axis=1)
            odd = jnp.concatenate(columns[1::2], axis=1)
            mine = jnp.where(core == 0, even, odd)
            other = jnp.where(core == 0, odd, even)
            left = jnp.concatenate([mine, swap(other, 1)], axis=0)
            right = jnp.concatenate([right, swap(right, 1)], axis=0)
            return dot(left, right, (0, 0)).astype(BF).reshape(chips, shard, right.shape[1])


        order = chip ^ jnp.arange(chips, dtype=jnp.int32)
        both_gains = jnp.pad(jnp.stack([attn_gain, ffn_gain]), ((0, 14), (0, 0)))
        w_qkv, w_gu, w_d, gains = share_weights(
            nf,
            nc,
            jnp.concatenate([w_query, w_key, w_value], axis=1),
            pick_columns(order, w_gate, w_up),
            w_down,
            both_gains,
        )
        w_out, w_qkv = lax.optimization_barrier((w_out, w_qkv))
        w_o = lax.all_gather(w_out, "fsdp", axis=0, tiled=True)
        w_qkv = w_qkv.reshape(width, -1)
        w_gu = w_gu.reshape(width, 2 * part)
        w_d = w_d.reshape(part, width)
        gains = gains[:, :2].astype(F32).transpose(1, 0, 2).reshape(2, width)

        half = HEAD_DIM // 2
        frequency = THETA ** (-jnp.arange(half, dtype=F32) * (2.0 / HEAD_DIM))
        angle = positions[0].astype(F32)[:, None] * frequency[None, :]
        cosine, sine = jnp.cos(angle), jnp.sin(angle)
        cos_lanes = jnp.tile(cosine, (1, 4))
        sin_lanes = jnp.tile(jnp.concatenate([-sine, sine], axis=1), (1, 2))
        blocks = 2 * nc
        stored = block_table.reshape(-1)
        number = jnp.arange(blocks, dtype=jnp.int32)
        where = jnp.sum(
            jnp.where(stored[None, :] == number[:, None], number[None, :], 0), axis=1
        )
        here = lax.axis_index("ctx")
        own = lax.dynamic_slice_in_dim(stored, 2 * here, 2)
        where = 2 * ((where // 2) ^ here) + where % 2
        table = jnp.concatenate([own, where]).astype(jnp.int32)

        inverse_one = lax.rsqrt(jnp.mean(x * x, axis=1, keepdims=True) + EPS)
        unit_one = x * inverse_one
        xn = (unit_one * gains[0][None, :]).astype(BF)
        qkv = dot(xn, w_qkv, (1, 0))
        kv = own_keys(qkv, cos_lanes, sin_lanes)
        sent, _ = lax.optimization_barrier((gb, qkv))
        gb_of = [gb] + plane_gather(sent)
        kv = jnp.concatenate([cross(kv, k) if k else kv for k in range(nc)], axis=0)
        qr, o, ob, lse = attention_forward(table, qkv, cos_lanes, sin_lanes, kv)
        h1 = x + dot(ob, w_o, (1, 0))
        inverse_two = lax.rsqrt(jnp.mean(h1 * h1, axis=1, keepdims=True) + EPS)
        unit_two = h1 * inverse_two
        hn = (unit_two * gains[1][None, :]).astype(BF)

        hn, gb_of = lax.optimization_barrier((hn, gb_of))

        dhns = []
        hn_of, act_of, dgu_of = [], [], []
        for k, hn_k in enumerate([hn] + plane_gather(hn)):
            gu = dot(hn_k, w_gu, (1, 0))
            dact = dot(gb_of[k], w_d, (1, 1))
            gate, up = gu[:, :part], gu[:, part:]
            sg = jax.nn.sigmoid(gate)
            silu = gate * sg
            act = (silu * up).astype(BF)
            dgate = (dact * up * sg * (1.0 + gate * (1.0 - sg))).astype(BF)
            dgu = jnp.concatenate([dgate, (dact * silu).astype(BF)], axis=1)
            dhn_k = dot(dgu, w_gu, (1, 1))
            dhns.append(dhn_k.astype(BF) if k else dhn_k)
            hn_of.append(hn_k)
            act_of.append(act)
            dgu_of.append(dgu)
        got = [swap(dhns[k], 2 * k) for k in range(1, chips)]
        act_of, dgu_of, got[:-1], _ = lax.optimization_barrier(
            (act_of, dgu_of, got[:-1], dhns[1:])
        )
        grad_hn = dhns[0]
        for piece in got:
            grad_hn = grad_hn + piece.astype(F32)

        gb_all = jnp.concatenate(gb_of, axis=0)
        down = dot(jnp.concatenate(act_of, axis=0), gb_all, (0, 0)).astype(BF)
        down_sum = core_sum(down.reshape((1, 2) + w_down.shape))[0]
        down_sum, grad_hn = lax.optimization_barrier((down_sum, grad_hn))
        down_sum = lax.psum_scatter(down_sum, "ctx", scatter_dimension=0, tiled=True)
        hn_all, dgu_all = jnp.concatenate(hn_of, axis=0), jnp.concatenate(dgu_of, axis=0)

        gain_two_grad = jnp.sum(grad_hn * unit_two, axis=0)
        grad_unit = grad_hn * gains[1][None, :]
        dh1 = gb.astype(F32) + inverse_two * (
            grad_unit - unit_two * jnp.mean(grad_unit * unit_two, axis=1, keepdims=True)
        )
        dab = dh1.astype(BF)
        dob = dot(dab, w_o, (1, 1)).astype(BF)
        dq, dkv = attention_backward(table, qr, dob, o, lse, kv, cos_lanes, sin_lanes)
        act_of, xn, ob, dab, hn_all, dgu_all, _ = lax.optimization_barrier(
            (act_of, xn, ob, dab, hn_all, dgu_all, dq)
        )
        down_sum, hn_all, dgu_all = lax.optimization_barrier((down_sum, hn_all, dgu_all))
        down_sum = lax.all_gather(down_sum, "ctx", axis=0, tiled=True)
        wide = rows_grad(hn_all, dgu_all)
        wide = [
            lax.dynamic_index_in_dim(wide, chip ^ k, 0, keepdims=False) for k in range(chips)
        ]
        act_of, _ = lax.optimization_barrier((act_of, wide))
        wide = [swap(piece, 2 * k) if k else piece for k, piece in enumerate(wide)]
        outs = [dot(act, w_d, (1, 0)) for act in act_of]
        sent = [out.astype(BF) for out in outs[1:]]
        pieces = [dkv[:, k * rows : (k + 1) * rows] for k in range(nc)]
        pieces = [cross(piece, k) if k else piece for k, piece in enumerate(pieces)]
        out_term = rows_grad(ob, dab)
        pieces, outs[0], sent, out_term = lax.optimization_barrier(
            (pieces, outs[0], sent, out_term)
        )
        own = own_key_grads(pieces, cos_lanes, sin_lanes)
        dqkv = jnp.concatenate([dq, own], axis=1)
        grad_xn = dot(dqkv, w_qkv, (1, 1))
        gain_one_grad = jnp.sum(grad_xn * unit_one, axis=0)
        grad_unit = grad_xn * gains[0][None, :]
        tokens_grad = dh1 + inverse_one * (
            grad_unit - unit_one * jnp.mean(grad_unit * unit_one, axis=1, keepdims=True)
        )
        qkv_term = rows_grad(xn, dqkv)

        gains_of = jnp.stack([gain_one_grad, gain_two_grad]).reshape(2, chips, 2, shard)
        other = lax.dynamic_index_in_dim(gains_of, 1 - core, 2, keepdims=False)
        mine = lax.dynamic_index_in_dim(gains_of, core, 2, keepdims=False)
        gains_of = (mine + swap(other, 1)).transpose(1, 0, 2).reshape(chips, 1, 2 * shard)
        gains_of = jnp.pad(gains_of.astype(BF), ((0, 0), (0, 15), (0, 0)))
        wide, down_sum, out_term, qkv_term, outs[0], sent = lax.optimization_barrier(
            (wide, down_sum, out_term, qkv_term, outs[0], sent)
        )
        gu_sum, out_sum, qkv_sum, gain_sum = finish(
            nf, nc, wide, [out_term, qkv_term, gains_of]
        )
        h1, gain_sum = lax.optimization_barrier((h1, gain_sum))
        branch = h1 + outs[0]
        for k in range(1, chips):
            branch = branch + swap(sent[k - 1], 2 * k).astype(F32)
        layer_out = branch.astype(BF)
        qkv_sum = qkv_sum.astype(F32)
        gain_sum = gain_sum[0].reshape(2, shard).astype(F32)
        gate_grad, up_grad = place_columns(order, gu_sum)
        query_width = HEADS * HEAD_DIM
        return (
            layer_out.reshape(1, rows, width),
            tokens_grad.reshape(1, rows, width),
            gain_sum[0],
            qkv_sum[:, :query_width],
            qkv_sum[:, query_width : query_width + key_width],
            qkv_sum[:, query_width + key_width :],
            out_sum.astype(F32),
            gain_sum[1],
            gate_grad,
            up_grad,
            down_sum.astype(F32),
        )

    weight = P("fsdp", None)
    activation = P("fsdp", "ctx", None)
    return jax.shard_map(
        shards,
        mesh=mesh,
        in_specs=(
            activation,
            P("fsdp"),
            weight,
            weight,
            weight,
            weight,
            P("fsdp"),
            weight,
            weight,
            weight,
            P(),
            P("fsdp", "ctx"),
            activation,
        ),
        out_specs=(
            activation,
            activation,
            P("fsdp"),
            weight,
            weight,
            weight,
            weight,
            P("fsdp"),
            weight,
            weight,
            weight,
        ),
        check_vma=False,
    )
```

```python
import functools

import jax
import jax.numpy as jnp
from jax import lax
from jax.experimental import pallas as pl
from jax.experimental.pallas import tpu as pltpu
from jax.sharding import PartitionSpec as P

HEADS = 32
KV_HEADS = 4
HEAD_DIM = 64
GROUP = HEADS // KV_HEADS
PAIRS = GROUP // 2
LANES = 2 * HEAD_DIM
STACK = PAIRS * LANES

EPS = 1e-05
THETA = 10000.0
NEG = -1e30
FLIGHT = 2
USED = (0, 1, 2, 3)
BF = jnp.bfloat16
F32 = jnp.float32


def dot(left, right, contract, out=F32):
    return lax.dot_general(
        left, right, ((contract[:1], contract[1:]), ((), ())), preferred_element_type=out
    )


def swap_halves(z):
    lane = lax.broadcasted_iota(jnp.int32, z.shape, 1)
    first = (lane % HEAD_DIM) < (HEAD_DIM // 2)
    return jnp.where(
        first,
        pltpu.roll(z, LANES - HEAD_DIM // 2, 1),
        pltpu.roll(z, HEAD_DIM // 2, 1),
    )


def split_heads(rows):
    lane = lax.broadcasted_iota(jnp.int32, rows.shape, 1)
    zero = jnp.zeros_like(rows)
    return jnp.concatenate(
        [jnp.where(lane < HEAD_DIM, rows, zero), jnp.where(lane >= HEAD_DIM, rows, zero)], axis=0
    )


def join_heads(columns):
    half = columns.shape[1] // 2
    sub = lax.broadcasted_iota(jnp.int32, (LANES, half), 0)
    return jnp.where(sub < HEAD_DIM, columns[:, :half], columns[:, half:]).T


def stack_pairs(ref, rows):
    return jnp.concatenate([ref[rows, p * LANES : (p + 1) * LANES] for p in range(PAIRS)], axis=0)


def two_blocks(ref, table, j, block):
    parts = [
        ref[pl.ds(pl.multiple_of(table[2 + 2 * j + i] * block, block), block), :] for i in range(2)
    ]
    return jnp.concatenate(parts, axis=0)


def causal(scores, j, own, block):
    key = lax.broadcasted_iota(jnp.int32, scores.shape, 0) + j * (2 * block)
    query = lax.broadcasted_iota(jnp.int32, scores.shape, 1) % block + own * block
    return jnp.where(key <= query, scores, NEG)


def head_twice(pair, group):
    wide = pair.astype(F32)
    lane = lax.broadcasted_iota(jnp.int32, wide.shape, 1)
    keep = (lane < HEAD_DIM) == (group % 2 == 0)
    return jnp.where(keep, wide, pltpu.roll(wide, HEAD_DIM, 1)).astype(BF)


def attention_forward_kernel(
    table,
    q_ref,
    cos_ref,
    sin_ref,
    k_pair,
    v_pair,
    qr_ref,
    o_ref,
    ob_ref,
    lse_ref,
    qm,
    m,
    l,
    acc,
    k_ref,
    v_ref,
):
    block = q_ref.shape[0] // 2
    group = pl.program_id(0)
    k_ref[...] = head_twice(k_pair[...], group)
    v_ref[...] = head_twice(v_pair[...], group)
    for h in range(2):
        rows = slice(h * block, (h + 1) * block)
        cosine, sine = cos_ref[rows, :], sin_ref[rows, :]
        for p in range(PAIRS):
            lanes = slice(p * LANES, (p + 1) * LANES)
            z = q_ref[rows, lanes]
            qr_ref[rows, lanes] = (z * cosine + swap_halves(z) * sine).astype(BF)
        scaled = stack_pairs(qr_ref, rows).astype(F32) * (HEAD_DIM**-0.5)
        qm[...] = split_heads(scaled).astype(BF)
        m[...] = jnp.full_like(m, NEG)
        l[...] = jnp.zeros_like(l)
        acc[...] = jnp.zeros_like(acc)
        own = table[h]

        def step(j, masked):
            keys = two_blocks(k_ref, table, j, block)
            values = two_blocks(v_ref, table, j, block)
            s = dot(keys, qm[...], (1, 1))
            if masked:
                s = causal(s, j, own, block)
            before = m[...]
            now = jnp.maximum(before, jnp.max(s, axis=0, keepdims=True))
            p = jnp.exp(s - now)
            decay = jnp.exp(before - now)
            l[...] = l[...] * decay + jnp.sum(p, axis=0, keepdims=True)
            acc[...] = acc[...] * decay + dot(values, p.astype(BF), (0, 0))
            m[...] = now

        last = own // 2

        @pl.loop(0, last)
        def _(j):
            step(j, False)

        step(last, True)
        lse_ref[0, h : h + 1, :] = m[...] + jnp.log(l[...])
        o = join_heads(acc[...] / l[...])
        for p in range(PAIRS):
            lanes = slice(p * LANES, (p + 1) * LANES)
            piece = o[p * block : (p + 1) * block, :]
            o_ref[rows, lanes] = piece
            ob_ref[rows, lanes] = piece.astype(BF)


def attention_forward(table, q, cosine, sine, kv):
    rows, length = q.shape[0], kv.shape[0]
    query_width = HEADS * HEAD_DIM
    columns = pl.BlockSpec((rows, STACK), lambda g, t: (0, g))
    whole = pl.BlockSpec((rows, LANES), lambda g, t: (0, 0))
    key_pair = pl.BlockSpec((length, LANES), lambda g, t: (0, g // 2))
    value_pair = pl.BlockSpec((length, LANES), lambda g, t: (0, KV_HEADS // 2 + g // 2))
    wide = GROUP * (rows // 2)
    return pl.pallas_call(
        attention_forward_kernel,
        grid_spec=pltpu.PrefetchScalarGridSpec(
            num_scalar_prefetch=1,
            grid=(KV_HEADS,),
            in_specs=[columns, whole, whole, key_pair, value_pair],
            out_specs=[
                columns,
                columns,
                columns,
                pl.BlockSpec((1, 2, wide), lambda g, t: (g, 0, 0)),
            ],
            scratch_shapes=[
                pltpu.VMEM((wide, LANES), BF),
                pltpu.VMEM((1, wide), F32),
                pltpu.VMEM((1, wide), F32),
                pltpu.VMEM((LANES, wide), F32),
                pltpu.VMEM((length, LANES), BF),
                pltpu.VMEM((length, LANES), BF),
            ],
        ),
        out_shape=[
            jax.ShapeDtypeStruct((rows, query_width), BF),
            jax.ShapeDtypeStruct((rows, query_width), F32),
            jax.ShapeDtypeStruct((rows, query_width), BF),
            jax.ShapeDtypeStruct((KV_HEADS, 2, wide), F32),
        ],
        compiler_params=pltpu.CompilerParams(vmem_limit_bytes=32 << 20),
        cost_estimate=pl.CostEstimate(
            flops=8 * HEADS * rows * length * HEAD_DIM,
            bytes_accessed=16 * rows * HEADS * HEAD_DIM,
            transcendentals=HEADS * rows * length,
        ),
        name="attention_forward",
    )(table, q, cosine, sine, kv, kv)


def attention_backward_kernel(
    table,
    qr_ref,
    do_ref,
    o_ref,
    lse_ref,
    k_pair,
    v_pair,
    cos_ref,
    sin_ref,
    dq_ref,
    dkv_ref,
    qm,
    dom,
    dqt,
    k_ref,
    v_ref,
    dk_ref,
    dv_ref,
):
    block = qr_ref.shape[0] // 2
    group = pl.program_id(0)
    k_ref[...] = head_twice(k_pair[...], group)
    v_ref[...] = head_twice(v_pair[...], group)
    dk_ref[...] = jnp.zeros_like(dk_ref)
    dv_ref[...] = jnp.zeros_like(dv_ref)
    for h in range(2):
        rows = slice(h * block, (h + 1) * block)
        scaled = stack_pairs(qr_ref, rows).astype(F32) * (HEAD_DIM**-0.5)
        qm[...] = split_heads(scaled).astype(BF)
        grads = stack_pairs(do_ref, rows).astype(F32)
        dom[...] = split_heads(grads).astype(BF)
        product = (grads * stack_pairs(o_ref, rows)).T
        inner = jnp.concatenate(
            [
                jnp.sum(product[:HEAD_DIM], axis=0, keepdims=True),
                jnp.sum(product[HEAD_DIM:], axis=0, keepdims=True),
            ],
            axis=1,
        )
        lse = lse_ref[0, h : h + 1, :]
        dqt[...] = jnp.zeros_like(dqt)
        own = table[h]

        def step(j, masked):
            keys = two_blocks(k_ref, table, j, block)
            values = two_blocks(v_ref, table, j, block)
            s = dot(keys, qm[...], (1, 1))
            if masked:
                s = causal(s, j, own, block)
            p = jnp.exp(s - lse)
            dp = dot(values, dom[...], (1, 1))
            ds = (p * (dp - inner)).astype(BF)
            dv = dot(p.astype(BF), dom[...], (1, 0))
            dk = dot(ds, qm[...], (1, 0))
            dqt[...] += dot(keys, ds, (0, 0))
            for i in range(2):
                at = pl.ds(pl.multiple_of(table[2 + 2 * j + i] * block, block), block)
                dk_ref[at, :] += dk[i * block : (i + 1) * block]
                dv_ref[at, :] += dv[i * block : (i + 1) * block]

        last = own // 2

        @pl.loop(0, last)
        def _(j):
            step(j, False)

        step(last, True)
        cosine, sine = cos_ref[rows, :], sin_ref[rows, :]
        dq = join_heads(dqt[...] * (HEAD_DIM**-0.5))
        for p in range(PAIRS):
            z = dq[p * block : (p + 1) * block, :]
            dq_ref[rows, p * LANES : (p + 1) * LANES] = (
                z * cosine - swap_halves(z) * sine
            ).astype(BF)
    lane = lax.broadcasted_iota(jnp.int32, dk_ref.shape, 1)
    keep = (lane < HEAD_DIM) == (group % 2 == 0)
    for i, ref in enumerate((dk_ref, dv_ref)):
        both = ref[...] + pltpu.roll(ref[...], HEAD_DIM, 1)
        dkv_ref[i] = jnp.where(keep, both, dkv_ref[i].astype(F32)).astype(BF)


def attention_backward(table, qr, grads, o, lse, kv, cosine, sine):
    rows, length = qr.shape[0], kv.shape[0]
    columns = pl.BlockSpec((rows, STACK), lambda g, t: (0, g))
    whole = pl.BlockSpec((rows, LANES), lambda g, t: (0, 0))
    key_pair = pl.BlockSpec((length, LANES), lambda g, t: (0, g // 2))
    value_pair = pl.BlockSpec((length, LANES), lambda g, t: (0, KV_HEADS // 2 + g // 2))
    wide = GROUP * (rows // 2)
    return pl.pallas_call(
        attention_backward_kernel,
        grid_spec=pltpu.PrefetchScalarGridSpec(
            num_scalar_prefetch=1,
            grid=(KV_HEADS,),
            in_specs=[
                columns,
                columns,
                columns,
                pl.BlockSpec((1, 2, wide), lambda g, t: (g, 0, 0)),
                key_pair,
                value_pair,
                whole,
                whole,
            ],
            out_specs=[columns, pl.BlockSpec((2, length, LANES), lambda g, t: (0, 0, g // 2))],
            scratch_shapes=[
                pltpu.VMEM((wide, LANES), BF),
                pltpu.VMEM((wide, LANES), BF),
                pltpu.VMEM((LANES, wide), F32),
                pltpu.VMEM((length, LANES), BF),
                pltpu.VMEM((length, LANES), BF),
                pltpu.VMEM((length, LANES), F32),
                pltpu.VMEM((length, LANES), F32),
            ],
        ),
        out_shape=[
            jax.ShapeDtypeStruct(qr.shape, BF),
            jax.ShapeDtypeStruct((2, length, KV_HEADS * HEAD_DIM), BF),
        ],
        compiler_params=pltpu.CompilerParams(vmem_limit_bytes=32 << 20),
        cost_estimate=pl.CostEstimate(
            flops=20 * HEADS * rows * length * HEAD_DIM,
            bytes_accessed=16 * rows * HEADS * HEAD_DIM,
            transcendentals=HEADS * rows * length,
        ),
        name="attention_backward",
    )(table, qr, grads, o, lse, kv, kv, cosine, sine)


def own_keys_kernel(k_ref, v_ref, cos_ref, sin_ref, kv_ref):
    width = k_ref.shape[1]
    for p in range(width // LANES):
        lanes = slice(p * LANES, (p + 1) * LANES)
        z = k_ref[:, lanes]
        kv_ref[:, lanes] = (z * cos_ref[...] + swap_halves(z) * sin_ref[...]).astype(BF)
    kv_ref[:, width:] = v_ref[...].astype(BF)


def own_keys(kv, cosine, sine):
    rows, width = kv.shape[0], KV_HEADS * HEAD_DIM
    whole = pl.BlockSpec((rows, LANES), lambda i: (0, 0))
    return pl.pallas_call(
        own_keys_kernel,
        grid=(1,),
        in_specs=[
            pl.BlockSpec((rows, width), lambda i: (0, 0)),
            pl.BlockSpec((rows, width), lambda i: (0, 1)),
            whole,
            whole,
        ],
        out_specs=pl.BlockSpec((rows, 2 * width), lambda i: (0, 0)),
        out_shape=jax.ShapeDtypeStruct((rows, 2 * width), BF),
        name="own_keys",
    )(kv, kv, cosine, sine)


def own_key_grads_kernel(nc, dkv_ref, cos_ref, sin_ref, out_ref, got, send_sem, recv_sem):
    rows, width = out_ref.shape[0], out_ref.shape[1] // 2
    here = lax.axis_index("ctx")
    mesh_id = pl.DeviceIdType.MESH
    barrier = pltpu.get_barrier_semaphore()
    for k in range(1, nc):
        pl.semaphore_signal(barrier, inc=1, device_id={"ctx": here ^ k}, device_id_type=mesh_id)
    pl.semaphore_wait(barrier, nc - 1)

    def copy(k):
        source = dkv_ref.at[:, pl.ds(k * rows, rows)]
        if k == 0:
            return pltpu.make_async_copy(source, got.at[0], recv_sem.at[0])
        return pltpu.make_async_remote_copy(
            src_ref=source,
            dst_ref=got.at[k],
            send_sem=send_sem.at[k],
            recv_sem=recv_sem.at[k],
            device_id={"ctx": here ^ k},
            device_id_type=mesh_id,
        )

    for k in reversed(range(nc)):
        copy(k).start()
    for k in range(nc):
        copy(k).wait()

    def total(i, lanes):
        return sum(got[k, i, :, lanes].astype(F32) for k in range(nc))

    for p in range(width // LANES):
        lanes = slice(p * LANES, (p + 1) * LANES)
        z = total(0, lanes)
        out_ref[:, lanes] = (z * cos_ref[...] - swap_halves(z) * sin_ref[...]).astype(BF)
        out_ref[:, width + p * LANES : width + (p + 1) * LANES] = total(1, lanes).astype(BF)


def own_key_grads(nc, dkv, cosine, sine):
    rows, width = dkv.shape[1] // nc, dkv.shape[2]
    vmem = pl.BlockSpec(memory_space=pltpu.VMEM)
    return pl.pallas_call(
        functools.partial(own_key_grads_kernel, nc),
        in_specs=[pl.BlockSpec(memory_space=pl.ANY), vmem, vmem],
        out_specs=vmem,
        out_shape=jax.ShapeDtypeStruct((rows, 2 * width), BF),
        scratch_shapes=[
            pltpu.VMEM((nc, 2, rows, width), BF),
            pltpu.SemaphoreType.DMA((nc,)),
            pltpu.SemaphoreType.DMA((nc,)),
        ],
        compiler_params=pltpu.CompilerParams(collective_id=2, has_side_effects=True),
        name="own_key_grads",
    )(dkv, cosine, sine)


def share_kernel(nf, nc, low, size, raw, *refs):
    w_query, w_key, w_value, w_out, *halves, down, gains = refs[: 8 if raw else 7]
    refs = refs[8 if raw else 7 :]
    query, key_value, out, wide, downs, all_gains = refs[:6]
    query_own, key_value_own, out_own, wide_own, down_own, gains_own = refs[6:12]
    (local, plane_send, plane_recv, along_send, along_recv, core_send, core_recv) = refs[12:19]
    (gain_send, gain_recv, down_sem, gather_send, gather_recv, gather_core) = refs[19:]
    chips = nf // 2
    place, here = lax.axis_index("fsdp"), lax.axis_index("ctx")
    chip, core = place // 2, place % 2
    mesh_id = pl.DeviceIdType.MESH
    shard, columns = wide.shape[1:]
    part = columns // 2
    count = len(halves)
    key_width = w_key.shape[1]
    gathered = [
        (w_query, query, query_own, pl.ds(0, w_query.shape[1])),
        (w_key, key_value, key_value_own, pl.ds(0, key_width)),
        (w_value, key_value, key_value_own, pl.ds(key_width, key_width)),
        (w_out, out, out_own, pl.ds(0, w_out.shape[1])),
    ]

    barrier = pltpu.get_barrier_semaphore()

    def greet(target):
        pl.semaphore_signal(barrier, inc=1, device_id=target, device_id_type=mesh_id)

    for j in range(1, nf):
        greet({"fsdp": place ^ j})
    for pos in range(nc):

        @pl.when(here == pos)
        def _():
            near = [i for i in (pos - 1, pos + 1) if 0 <= i < nc]
            for i in near:
                greet({"ctx": i})
            pl.semaphore_wait(barrier, nf - 1 + len(near))

    def remote(source, target, sends, recvs, where):
        return pltpu.make_async_remote_copy(
            src_ref=source,
            dst_ref=target,
            send_sem=sends,
            recv_sem=recvs,
            device_id=where,
            device_id_type=mesh_id,
        )

    def piece(k, h, rows):
        if raw:
            at = pl.ds(pl.multiple_of((chip ^ k) * part, 128), part)
            return halves[h].at[rows, at]
        return halves[0].at[k, rows]

    def side(h):
        return pl.ds(h * part, part) if raw else pl.ds(0, columns)

    def rows_of(share):
        return pl.ds(low + share * size, size)

    def plane_copy(k, kind, h):
        rows = rows_of(here) if kind else pl.ds(0, low)
        return remote(
            piece(k, h, rows),
            wide.at[place, rows, side(h)],
            plane_send.at[kind, k, h],
            plane_recv.at[kind, k, h],
            {"fsdp": place ^ (2 * k)},
        )

    def along_copy(k, share, up, target):
        block = wide.at[place ^ (2 * k), rows_of(share)]
        return remote(
            block, block, along_send.at[up, share, k], along_recv.at[share, k], {"ctx": target}
        )

    def core_copy(k, share):
        rows = rows_of(share) if share < nc else pl.ds(0, low)
        block = wide.at[place ^ (2 * k), rows]
        return remote(
            block, block, core_send.at[k, share], core_recv.at[k, share], {"fsdp": place ^ 1}
        )

    def own_core_copy(h):
        return remote(
            piece(0, h, pl.ds(0, shard)),
            wide.at[place, :, side(h)],
            core_send.at[0, h],
            core_recv.at[0, h],
            {"fsdp": place ^ 1},
        )

    half = shard // 2
    relayed = chips == 4

    def gather_copy(u, k, relay=0):
        source, target, _, at = gathered[u]
        if relay:
            owner, rows = place ^ (2 * (3 - k)), pl.ds((2 - k) * half, half)
            source = target.at[owner, rows, at]
        else:
            owner, rows = place, pl.ds(0, shard)
        number = 2 * k + relay
        return remote(
            source,
            target.at[owner, rows, at],
            gather_send.at[u, number],
            gather_recv.at[u, number],
            {"fsdp": place ^ (2 * k)},
        )

    def gather_core_copy(u, k):
        source, target, _, at = gathered[u]
        block = target.at[place ^ (2 * k), :, at]
        return remote(
            block if k else source,
            block,
            gather_core.at[0, u, k],
            gather_core.at[1, u, k],
            {"fsdp": place ^ 1},
        )

    def down_copy():
        return remote(down, downs.at[core], down_sem.at[0], down_sem.at[1], {"fsdp": place ^ 1})

    def gain_copy(j):
        return remote(
            gains, all_gains.at[place], gain_send.at[j], gain_recv.at[j], {"fsdp": place ^ j}
        )

    direct = (1, 2) if relayed else tuple(range(1, chips))
    for k in range(1, chips):
        for h in range(count):
            plane_copy(k, 1, h).start()
    for j in range(1, nf):
        gain_copy(j).start()
    for h in range(count):
        own_core_copy(h).start()
    for u in USED:
        gather_core_copy(u, 0).start()
    down_copy().start()
    own = [(source, stage.at[:, at], None) for source, _, stage, at in (gathered[u] for u in USED)]
    own += [(piece(0, h, pl.ds(0, shard)), wide_own.at[:, side(h)], None) for h in range(count)]
    own += [(down, down_own, downs.at[core]), (gains, gains_own, all_gains.at[place])]
    back = [(query_own, query.at[place]), (key_value_own, key_value.at[place])]
    if 3 in USED:
        back.append((out_own, out.at[place]))
    back += [
        (wide_own, wide.at[place]),
        (down_own, downs.at[core]),
        (gains_own, all_gains.at[place]),
    ]
    for i, (source, stage, _) in enumerate(own):
        pltpu.make_async_copy(source, stage, local.at[0, i]).start()
    for i, (source, stage, _) in enumerate(own):
        pltpu.make_async_copy(source, stage, local.at[0, i]).wait()
    for i, (stage, target) in enumerate(back):
        pltpu.make_async_copy(stage, target, local.at[1, i]).start()

    for k in range(1, chips):
        for h in range(count):
            plane_copy(k, 1, h).wait_send()
    for u in USED:
        for k in direct:
            gather_copy(u, k).start()

    for pos in range(nc):

        @pl.when(here == pos)
        def _():
            def pass_on(k, share):
                if share <= pos < nc - 1:
                    along_copy(k, share, 1, pos + 1).start()
                if share >= pos > 0:
                    along_copy(k, share, 0, pos - 1).start()
                core_copy(k, share).start()

            for k in range(1, chips):
                for h in range(count):
                    plane_copy(k, 1, h).wait_recv()
                pass_on(k, pos)
            if low:
                for k in range(1, chips):
                    for h in range(count):
                        plane_copy(k, 0, h).start()
            for u in USED:
                for k in direct:
                    gather_copy(u, k).wait_recv()
                    if relayed:
                        gather_copy(u, 3 - k, 1).start()
                    gather_core_copy(u, k).start()
            for d in range(1, nc):
                for share in (pos - d, pos + d):
                    if 0 <= share < nc:
                        for k in range(1, chips):
                            along_copy(k, share, 0, 0).wait_recv()
                            pass_on(k, share)
            if low:
                for k in range(1, chips):
                    for h in range(count):
                        plane_copy(k, 0, h).wait_recv()
                    core_copy(k, nc).start()
            if relayed:
                for u in USED:
                    for k in direct:
                        gather_copy(u, k, 1).wait_recv()
                    gather_core_copy(u, 3).start()
            for k in range(1, chips):
                for share in range(nc):
                    if share <= pos < nc - 1:
                        along_copy(k, share, 1, pos + 1).wait_send()
                    if share >= pos > 0:
                        along_copy(k, share, 0, pos - 1).wait_send()

    for h in range(count):
        own_core_copy(h).wait()
    for k in range(1, chips):
        for share in range(nc + 1 if low else nc):
            core_copy(k, share).wait()
        if low:
            for h in range(count):
                plane_copy(k, 0, h).wait_send()
    for j in range(1, nf):
        gain_copy(j).wait()
    for u in USED:
        for k in direct:
            gather_copy(u, k).wait_send()
            if relayed:
                gather_copy(u, k, 1).wait_send()
        for k in range(chips):
            gather_core_copy(u, k).wait()
    down_copy().wait()
    for i, (stage, target) in enumerate(back):
        pltpu.make_async_copy(stage, target, local.at[1, i]).wait()


def share_weights(nf, nc, w_query, w_key, w_value, w_out, w_gate, w_up, order, down, gains):
    chips = nf // 2
    shard, hidden = w_gate.shape
    part = hidden // chips
    size = 16 * max(1, (shard * 3 // 4) // (16 * nc))
    low = shard - nc * size
    raw = part % 128 == 0
    halves = [w_gate, w_up]
    if not raw:
        both = [w.reshape(shard, chips, part).transpose(1, 0, 2) for w in halves]
        halves = [jnp.take(jnp.concatenate(both, axis=2), order, axis=0)]
    anywhere = pl.BlockSpec(memory_space=pl.ANY)
    dma = pltpu.SemaphoreType.DMA
    widths = [w_query.shape[1], 2 * w_key.shape[1], w_out.shape[1], 2 * part]
    return pl.pallas_call(
        functools.partial(share_kernel, nf, nc, low, size, raw),
        in_specs=[anywhere] * (6 + len(halves)),
        out_specs=[anywhere] * 6,
        out_shape=[jax.ShapeDtypeStruct((nf, shard, width), BF) for width in widths]
        + [
            jax.ShapeDtypeStruct((2,) + down.shape, BF),
            jax.ShapeDtypeStruct((nf,) + gains.shape, BF),
        ],
        scratch_shapes=[pltpu.VMEM((shard, width), BF) for width in widths]
        + [
            pltpu.VMEM(down.shape, BF),
            pltpu.VMEM(gains.shape, BF),
            dma((2, 8)),
            dma((2, chips, 2)),
            dma((2, chips, 2)),
            dma((2, nc, chips)),
            dma((nc, chips)),
            dma((chips, nc + 1)),
            dma((chips, nc + 1)),
            dma((nf,)),
            dma((nf,)),
            dma((2,)),
            dma((4, 2 * chips)),
            dma((4, 2 * chips)),
            dma((2, 4, chips)),
        ],
        compiler_params=pltpu.CompilerParams(
            collective_id=1, has_side_effects=True, vmem_limit_bytes=56 << 20
        ),
        name="share_weights",
    )(w_query, w_key, w_value, w_out, *halves, down, gains)


def place_columns_kernel(order, both_ref, gate_ref, up_ref):
    part = gate_ref.shape[1]
    gate_ref[...] = both_ref[0, :, :part].astype(F32)
    up_ref[...] = both_ref[0, :, part:].astype(F32)


def place_columns(order, both):
    parts, shard, part = both.shape[0], both.shape[1], both.shape[2] // 2
    out = jax.ShapeDtypeStruct((shard, parts * part), F32)
    if part % 128:
        both = jnp.take(both, order, axis=0).transpose(1, 0, 2).astype(F32)
        return [both[:, :, i * part : (i + 1) * part].reshape(out.shape) for i in range(2)]
    columns = pl.BlockSpec((shard, part), lambda k, t: (0, t[k]))
    return pl.pallas_call(
        place_columns_kernel,
        grid_spec=pltpu.PrefetchScalarGridSpec(
            num_scalar_prefetch=1,
            grid=(parts,),
            in_specs=[pl.BlockSpec((1, shard, 2 * part), lambda k, t: (k, 0, 0))],
            out_specs=[columns, columns],
        ),
        out_shape=[out, out],
        name="place_columns",
    )(order, both)


def feed_forward_kernel(nf, *refs):
    chips = nf // 2
    hn, *gbs, w_gu, w_d, grad, left, right, downs, outs = refs[: chips + 8]
    w_gu_v, w_d_v, hn_v, gb_v, dact_v, act_v, dgu_v, sent, got, outs_v = refs[chips + 8 : chips + 18]
    tiles, *sems = refs[chips + 18 :]
    load, load_gb, hn_send, hn_recv, dhn_send, dhn_recv, store = sems[:7]
    left_local, left_send, left_recv, right_local, right_send, right_recv = sems[7:13]
    down_local, down_send, down_recv = sems[13:]
    place = lax.axis_index("fsdp")
    core = place % 2
    rows, width = hn.shape
    part = w_d.shape[0]
    shard = width // nf
    half = rows // 2
    relayed = chips == 4
    direct = (1, 2) if relayed else tuple(range(1, chips))
    mesh_id = pl.DeviceIdType.MESH

    barrier = pltpu.get_barrier_semaphore()
    for j in [1] + [2 * k for k in range(1, chips)]:
        pl.semaphore_signal(
            barrier, inc=1, device_id={"fsdp": place ^ j}, device_id_type=mesh_id
        )
    pl.semaphore_wait(barrier, chips)

    def remote(source, target, sends, recvs, step):
        return pltpu.make_async_remote_copy(
            src_ref=source,
            dst_ref=target,
            send_sem=sends,
            recv_sem=recvs,
            device_id={"fsdp": place ^ step},
            device_id_type=mesh_id,
        )

    def hn_copy(k, relay=0):
        at = 2 * k + relay
        if relay:
            lines = pl.ds((2 - k) * half, half)
            source, target = hn_v.at[3 - k, lines], hn_v.at[3, lines]
        else:
            source, target = hn, hn_v.at[k]
        return remote(source, target, hn_send.at[at], hn_recv.at[at], 2 * k)

    def dhn_copy(k):
        return remote(sent.at[k - 1], got.at[k - 1], dhn_send.at[k], dhn_recv.at[k], 2 * k)

    def left_copy(k, j, other):
        number = 1 - core if other else core
        columns = pl.ds(pl.multiple_of((2 * j + number) * shard, shard), shard)
        source = hn_v.at[k, :, columns]
        target = left.at[other, k, :, pl.ds(j * shard, shard)]
        if other:
            return remote(source, target, left_send.at[k, j], left_recv.at[k, j], 1)
        return pltpu.make_async_copy(source, target, left_local.at[k, j])

    def right_copy(k, other):
        if other:
            return remote(dgu_v.at[k], right.at[1, k], right_send.at[k], right_recv.at[k], 1)
        return pltpu.make_async_copy(dgu_v.at[k], right.at[0, k], right_local.at[k])

    loads = [
        pltpu.make_async_copy(w_d, w_d_v, load.at[0]),
        pltpu.make_async_copy(hn, hn_v.at[0], load.at[1]),
        pltpu.make_async_copy(w_gu, w_gu_v, load.at[2]),
    ]
    gb_loads = [
        pltpu.make_async_copy(gb, gb_v.at[k], load_gb.at[k]) for k, gb in enumerate(gbs)
    ]
    store_outs = pltpu.make_async_copy(outs_v, outs, store.at[0])
    for k in direct:
        hn_copy(k).start()
    for copy in loads[:1] + gb_loads + loads[1:]:
        copy.start()

    for copy in loads[:1] + gb_loads:
        copy.wait()

    def dact_tile(start, size):
        tile = w_d_v[pl.ds(start, size), :]
        for k in range(chips):
            dact_v[k, :, pl.ds(start, size)] = dot(gb_v[k], tile, (1, 1))

    @pl.loop(0, part // 256)
    def _(i):
        dact_tile(pl.multiple_of(i * 256, 256), 256)

    if part % 256:
        dact_tile(part - 128, 128)

    def forward(k):
        for j in range(chips):
            left_copy(k, j, 1).start()
            left_copy(k, j, 0).start()

        def tile(start, size):
            one, two = pl.ds(start, size), pl.ds(pl.multiple_of(part + start, 128), size)
            gate = dot(hn_v[k], w_gu_v[:, one], (1, 0))
            up = dot(hn_v[k], w_gu_v[:, two], (1, 0))
            dact = dact_v[k, :, one]
            sg = jax.nn.sigmoid(gate)
            silu = gate * sg
            act_v[k, :, one] = (silu * up).astype(BF)
            dgu_v[k, :, one] = (dact * up * sg * (1.0 + gate * (1.0 - sg))).astype(BF)
            dgu_v[k, :, two] = (dact * silu).astype(BF)

        @pl.loop(0, part // 256)
        def _(i):
            tile(pl.multiple_of(i * 256, 256), 256)

        if part % 256:
            tile(part - 128, 128)

        right_copy(k, 1).start()
        right_copy(k, 0).start()

    def backward(k):
        @pl.loop(0, width // 256)
        def _(i):
            lines = pl.ds(pl.multiple_of(i * 256, 256), 256)
            dhn = dot(dgu_v[k], w_gu_v[lines, :], (1, 1))
            if k:
                sent[k - 1, :, lines] = dhn.astype(BF)
            else:
                grad[:, lines] = dhn

        if k:
            dhn_copy(k).start()

    for copy in loads[1:]:
        copy.wait()
    forward(0)
    for k in direct:
        hn_copy(k).wait_recv()
        if relayed:
            hn_copy(3 - k, 1).start()
    for k in range(1, chips):
        if relayed and k == 3:
            for i in direct:
                hn_copy(i, 1).wait_recv()
        forward(k)
        backward(k)
    backward(0)

    @pl.loop(0, width // 256)
    def _(i):
        columns = pl.ds(pl.multiple_of(i * 256, 256), 256)
        for k in range(chips):
            outs_v[k, :, columns] = dot(act_v[k], w_d_v[:, columns], (1, 0)).astype(BF)

    store_outs.start()

    lower = part // 2
    spans = []
    for start in range(0, part, 128):
        cuts = sorted({start, min(max(lower, start), start + 128), start + 128})
        spans += [(start, a, b) for a, b in zip(cuts, cuts[1:])]

    def span_copies(n):
        start, a, b = spans[n]
        number = int(a >= lower)
        source = tiles.at[(start // 128) % 2, pl.ds(a - start, b - a)]
        at = pl.ds(a - number * lower, b - a)

        def keep():
            return pltpu.make_async_copy(source, downs.at[0, at], down_local.at[n])

        def send():
            return remote(source, downs.at[1, at], down_send.at[n], down_recv.at[n], 1)

        return number, keep, send

    def each_span(chosen, go):
        for n in chosen:
            number, keep, send = span_copies(n)

            @pl.when(core == number)
            def _():
                keep().start() if go else keep().wait()

            @pl.when(core != number)
            def _():
                send().start() if go else send().wait_send()

    for start in range(0, part, 128):
        before = [n for n, span in enumerate(spans) if span[0] == start - 256]
        each_span(before, False)
        tile = sum(
            dot(act_v[k, :, start : start + 128], gb_v[k], (0, 0)) for k in range(chips)
        )
        tiles[(start // 128) % 2] = tile.astype(BF)
        each_span([n for n, span in enumerate(spans) if span[0] == start], True)
    each_span([n for n, span in enumerate(spans) if span[0] >= part - 256], False)
    for n in range(len(spans)):
        number, _, send = span_copies(n)

        @pl.when(core == number)
        def _():
            send().wait_recv()

    for k in range(1, chips):
        dhn_copy(k).wait_recv()

    @pl.loop(0, rows // 16)
    def _(i):
        lines = pl.ds(pl.multiple_of(i * 16, 16), 16)
        grad[lines, :] += sum(got[k, lines, :].astype(F32) for k in range(chips - 1))

    store_outs.wait()
    for k in range(chips):
        for j in range(chips):
            left_copy(k, j, 0).wait()
            left_copy(k, j, 1).wait()
        right_copy(k, 0).wait()
        right_copy(k, 1).wait()
        if k:
            dhn_copy(k).wait_send()
    for k in direct:
        hn_copy(k).wait_send()
        if relayed:
            hn_copy(k, 1).wait_send()


def feed_forward(nf, hn, gbs, w_gu, w_d):
    chips = nf // 2
    rows, width = hn.shape
    part = w_d.shape[0]
    anywhere = pl.BlockSpec(memory_space=pl.ANY)
    dma = pltpu.SemaphoreType.DMA
    shape = jax.ShapeDtypeStruct
    return pl.pallas_call(
        functools.partial(feed_forward_kernel, nf),
        in_specs=[anywhere] * (chips + 3),
        out_specs=[pl.BlockSpec(memory_space=pltpu.VMEM)] + [anywhere] * 4,
        out_shape=[
            shape((rows, width), F32),
            shape((2, chips, rows, width // 2), BF),
            shape((2, chips, rows, 2 * part), BF),
            shape((2, part // 2, width), BF),
            shape((chips, rows, width), BF),
        ],
        scratch_shapes=[
            pltpu.VMEM((width, 2 * part), BF),
            pltpu.VMEM((part, width), BF),
            pltpu.VMEM((chips, rows, width), BF),
            pltpu.VMEM((chips, rows, width), BF),
            pltpu.VMEM((chips, rows, part), F32),
            pltpu.VMEM((chips, rows, part), BF),
            pltpu.VMEM((chips, rows, 2 * part), BF),
            pltpu.VMEM((chips - 1, rows, width), BF),
            pltpu.VMEM((chips - 1, rows, width), BF),
            pltpu.VMEM((chips, rows, width), BF),
            pltpu.VMEM((2, 128, width), BF),
            dma((3,)),
            dma((chips,)),
            dma((2 * chips,)),
            dma((2 * chips,)),
            dma((chips,)),
            dma((chips,)),
            dma((1,)),
            dma((chips, chips)),
            dma((chips, chips)),
            dma((chips, chips)),
            dma((chips,)),
            dma((chips,)),
            dma((chips,)),
            dma((part // 128 + 1,)),
            dma((part // 128 + 1,)),
            dma((part // 128 + 1,)),
        ],
        compiler_params=pltpu.CompilerParams(
            collective_id=3, has_side_effects=True, vmem_limit_bytes=60 << 20
        ),
        cost_estimate=pl.CostEstimate(
            flops=12 * chips * rows * width * part,
            bytes_accessed=40_000_000,
            transcendentals=chips * rows * part,
        ),
        name="feed_forward",
    )(hn, *gbs, w_gu, w_d)


def chunk_rows(rows):
    return max(r for r in range(16, 65, 16) if rows % r == 0)


def finish_kernel(nf, nc, *refs):
    pieces, refs = refs[: nf // 2], refs[nf // 2 - 1 :]
    sources, (outs, owns, ins, xs) = refs[:4], (refs[i : i + 4] for i in range(4, 20, 4))
    plane_send, plane_recv, local, in_sem, x_sem, first_send, second_send, out_sem = refs[20:]
    chips = nf // 2
    place, here = lax.axis_index("fsdp"), lax.axis_index("ctx")
    chip = place // 2
    lower = here < nc // 2
    depth = jnp.where(lower, here, nc - 1 - here)
    inner = jnp.where(lower, here + 1, here - 1)
    outer = jnp.where(lower, here - 1, here + 1)
    mesh_id = pl.DeviceIdType.MESH

    barrier = pltpu.get_barrier_semaphore()
    for k in range(1, chips):
        pl.semaphore_signal(
            barrier, inc=1, device_id={"fsdp": place ^ (2 * k)}, device_id_type=mesh_id
        )
    pl.semaphore_signal(barrier, inc=1, device_id={"ctx": inner}, device_id_type=mesh_id)

    @pl.when(depth > 0)
    def _():
        pl.semaphore_signal(barrier, inc=1, device_id={"ctx": outer}, device_id_type=mesh_id)
        pl.semaphore_wait(barrier, chips + 1)

    @pl.when(depth == 0)
    def _():
        pl.semaphore_wait(barrier, chips)

    def plane_copy(u, k):
        return pltpu.make_async_remote_copy(
            src_ref=sources[u].at[chip ^ k],
            dst_ref=owns[u].at[k],
            send_sem=plane_send.at[u, k],
            recv_sem=plane_recv.at[u, k],
            device_id={"fsdp": place ^ (2 * k)},
            device_id_type=mesh_id,
        )

    def local_copy(u, k):
        source = sources[u].at[chip] if u else pieces[k]
        return pltpu.make_async_copy(source, owns[u].at[k], local.at[u, k])

    for u in range(4):
        for k in range(chips):
            if u == 0 or k == 0:
                local_copy(u, k).start()
            else:
                plane_copy(u, k).start()

    units = [(0, k) for k in range(chips)] + [(u, None) for u in (1, 2, 3)]
    chunks = []
    for u, k in units:
        total = outs[u].shape[-2]
        size = chunk_rows(total)
        chunks += [(u, k, r, size) for r in range(0, total, size)]

    def views(c):
        u, k, r, size = chunks[c]
        rows = pl.ds(r, size)
        return [owns[u].at[k or 0, rows]] + [
            ref.at[rows] if k is None else ref.at[k, rows] for ref in (ins[u], xs[u], outs[u])
        ]

    def first_copy(c, across):
        own, arriving, x, _ = views(c)
        return pltpu.make_async_remote_copy(
            src_ref=own,
            dst_ref=x if across else arriving,
            send_sem=first_send.at[c],
            recv_sem=(x_sem if across else in_sem).at[c],
            device_id={"ctx": inner},
            device_id_type=mesh_id,
        )

    def second_copy(c, across):
        _, arriving, x, _ = views(c)
        return pltpu.make_async_remote_copy(
            src_ref=arriving if across else x,
            dst_ref=x,
            send_sem=second_send.at[c],
            recv_sem=x_sem.at[c],
            device_id={"ctx": outer},
            device_id_type=mesh_id,
        )

    def out_copy(c, across):
        _, arriving, x, out = views(c)
        return pltpu.make_async_copy(arriving if across else x, out, out_sem.at[c])

    def add_into(target, terms, size):
        @pl.loop(0, size // 16)
        def _(i):
            strip = pl.ds(pl.multiple_of(i * 16, 16), 16)
            target[strip, :] = sum(term[strip, :].astype(F32) for term in terms).astype(BF)

    def inward(c, level):
        u, k, r, size = chunks[c]
        own, arriving, _, _ = views(c)
        terms = [own]
        if r == 0:
            local_copy(u, k or 0).wait()
            if u >= 1:
                for j in range(1, chips):
                    plane_copy(u, j).wait_recv()
        if u >= 1:
            terms += [owns[u].at[j, pl.ds(r, size)] for j in range(1, chips)]
        if level > 0:
            first_copy(c, False).wait_recv()
            terms.append(arriving)
        if len(terms) > 1:
            add_into(own, terms, size)
        if c >= FLIGHT:
            first_copy(c - FLIGHT, False).wait_send()
        first_copy(c, level == top).start()

    def outward(c, level):
        size = chunks[c][3]
        own, arriving, x, _ = views(c)
        first_copy(c, True).wait_recv()
        if level == top:
            add_into(arriving, [own, x], size)
        out_copy(c, level == top).start()
        if level > 0:
            if c >= FLIGHT:
                second_copy(c - FLIGHT, False).wait_send()
            second_copy(c, level == top).start()

    top = nc // 2 - 1
    count = len(chunks)
    for level in range(top + 1):

        @pl.when(depth == level)
        def _():
            lag = 1 + 2 * (top - level)
            for t in range(count + lag):
                if t < count:
                    inward(t, level)
                if t >= lag:
                    outward(t - lag, level)
            for c in range(max(0, count - FLIGHT), count):
                first_copy(c, False).wait_send()
                if level > 0:
                    second_copy(c, False).wait_send()
            for c in range(count):
                out_copy(c, False).wait()

    for u in range(1, 4):
        for k in range(1, chips):
            plane_copy(u, k).wait_send()


def finish(nf, nc, pieces, sums):
    chips = nf // 2
    pieces_shape = (chips,) + pieces[0].shape
    shapes = [pieces_shape] + [x.shape[1:] for x in sums]
    count = sum(
        (shape[0] if len(shape) == 3 else 1) * (shape[-2] // chunk_rows(shape[-2]))
        for shape in shapes
    )
    anywhere = pl.BlockSpec(memory_space=pl.ANY)
    dma = pltpu.SemaphoreType.DMA
    return pl.pallas_call(
        functools.partial(finish_kernel, nf, nc),
        in_specs=[anywhere] * (chips + 3),
        out_specs=[anywhere] * 4,
        out_shape=[jax.ShapeDtypeStruct(shape, BF) for shape in shapes],
        scratch_shapes=[pltpu.VMEM(x, BF) for x in [pieces_shape] + [x.shape for x in sums]]
        + [pltpu.VMEM(shape, BF) for shape in shapes]
        + [pltpu.VMEM(shape, BF) for shape in shapes]
        + [dma((4, chips)), dma((4, chips)), dma((4, chips))]
        + [dma((count,))] * 5,
        compiler_params=pltpu.CompilerParams(
            collective_id=0, has_side_effects=True, vmem_limit_bytes=48 << 20
        ),
        cost_estimate=pl.CostEstimate(
            flops=200_000_000_000, bytes_accessed=60_000_000, transcendentals=0
        ),
        name="finish",
    )(*pieces, *sums)


def solution(mesh):
    nf, nc = mesh.shape["fsdp"], mesh.shape["ctx"]
    chips = nf // 2

    def swap(x, k):
        return lax.ppermute(x, "fsdp", [(i, i ^ k) for i in range(nf)])

    def plane_gather(x):
        if chips != 4:
            return [swap(x, 2 * k) for k in range(1, chips)]
        one, two = swap(x, 2), swap(x, 4)
        half = x.shape[0] // 2
        return [one, two, jnp.concatenate([swap(one[:half], 4), swap(two[half:], 2)], axis=0)]

    def cross(x, k):
        return lax.ppermute(x, "ctx", [(i, i ^ k) for i in range(nc)])

    def shards(
        tokens,
        attn_gain,
        w_query,
        w_key,
        w_value,
        w_out,
        ffn_gain,
        w_gate,
        w_up,
        w_down,
        block_table,
        positions,
        out_grad,
    ):
        place = lax.axis_index("fsdp")
        chip, core = place // 2, place % 2
        x = tokens[0].astype(F32)
        gb = out_grad[0]
        rows, width = x.shape
        hidden = w_gate.shape[1]
        part = hidden // chips
        shard = w_gate.shape[0]
        key_width = KV_HEADS * HEAD_DIM

        def core_sum(x):
            other = lax.dynamic_index_in_dim(x, 1 - core, 1, keepdims=False)
            mine = lax.dynamic_index_in_dim(x, core, 1, keepdims=False)
            return (mine.astype(F32) + swap(other, 1).astype(F32)).astype(BF)

        def rows_grad(left, right):
            columns = [left[:, i * shard : (i + 1) * shard] for i in range(nf)]
            even = jnp.concatenate(columns[::2], axis=1)
            odd = jnp.concatenate(columns[1::2], axis=1)
            mine = jnp.where(core == 0, even, odd)
            other = jnp.where(core == 0, odd, even)
            left = jnp.concatenate([mine, swap(other, 1)], axis=0)
            right = jnp.concatenate([right, swap(right, 1)], axis=0)
            return dot(left, right, (0, 0)).astype(BF).reshape(chips, shard, right.shape[1])


        order = chip ^ jnp.arange(chips, dtype=jnp.int32)
        both_gains = jnp.pad(jnp.stack([attn_gain, ffn_gain]), ((0, 14), (0, 0)))
        w_q, w_kv, w_o, w_gu, w_d, gains = share_weights(
            nf,
            nc,
            w_query,
            w_key,
            w_value,
            w_out,
            w_gate,
            w_up,
            order,
            w_down,
            both_gains,
        )
        w_q = w_q.reshape(width, -1)
        w_kv = w_kv.reshape(width, -1)
        gb_sent, w_kv = lax.optimization_barrier((gb, w_kv))
        if 3 in USED:
            w_o = w_o.reshape(-1, width)
        else:
            w_out, w_kv = lax.optimization_barrier((w_out, w_kv))
            w_o = lax.all_gather(w_out, "fsdp", axis=0, tiled=True)
        w_gu = w_gu.reshape(width, 2 * part)
        w_d = w_d.reshape(part, width)
        gains = gains[:, :2].astype(F32).transpose(1, 0, 2).reshape(2, width)

        half = HEAD_DIM // 2
        frequency = THETA ** (-jnp.arange(half, dtype=F32) * (2.0 / HEAD_DIM))
        angle = positions[0].astype(F32)[:, None] * frequency[None, :]
        cosine, sine = jnp.cos(angle), jnp.sin(angle)
        cos_lanes = jnp.tile(cosine, (1, 4))
        sin_lanes = jnp.tile(jnp.concatenate([-sine, sine], axis=1), (1, 2))
        blocks = 2 * nc
        stored = block_table.reshape(-1)
        number = jnp.arange(blocks, dtype=jnp.int32)
        where = jnp.sum(
            jnp.where(stored[None, :] == number[:, None], number[None, :], 0), axis=1
        )
        here = lax.axis_index("ctx")
        own = lax.dynamic_slice_in_dim(stored, 2 * here, 2)
        where = 2 * ((where // 2) ^ here) + where % 2
        table = jnp.concatenate([own, where]).astype(jnp.int32)

        inverse_one = lax.rsqrt(jnp.mean(x * x, axis=1, keepdims=True) + EPS)
        unit_one = x * inverse_one
        xn = (unit_one * gains[0][None, :]).astype(BF)
        kv = own_keys(dot(xn, w_kv, (1, 0)), cos_lanes, sin_lanes)
        q_sum = dot(xn, w_q, (1, 0))
        gb_of = [gb] + [swap(gb_sent, 2 * k) for k in range(1, chips)]
        kv = jnp.concatenate([cross(kv, k) if k else kv for k in range(nc)], axis=0)
        qr, o, ob, lse = attention_forward(table, q_sum, cos_lanes, sin_lanes, kv)
        h1 = x + dot(ob, w_o, (1, 0))
        inverse_two = lax.rsqrt(jnp.mean(h1 * h1, axis=1, keepdims=True) + EPS)
        unit_two = h1 * inverse_two
        hn = (unit_two * gains[1][None, :]).astype(BF)

        hn, gb_of = lax.optimization_barrier((hn, gb_of))

        fused = part % 128 == 0
        if fused:
            grad_hn, left, right, downs, outs = feed_forward(nf, hn, gb_of, w_gu, w_d)
            left = left.reshape(2 * chips * rows, width // 2)
            right = right.reshape(2 * chips * rows, 2 * part)
            down_sum = (downs[0].astype(F32) + downs[1].astype(F32)).astype(BF)
        else:
            dhns = []
            hn_of, act_of, dgu_of = [], [], []
            for k, hn_k in enumerate([hn] + plane_gather(hn)):
                gu = dot(hn_k, w_gu, (1, 0))
                dact = dot(gb_of[k], w_d, (1, 1))
                gate, up = gu[:, :part], gu[:, part:]
                sg = jax.nn.sigmoid(gate)
                silu = gate * sg
                act = (silu * up).astype(BF)
                dgate = (dact * up * sg * (1.0 + gate * (1.0 - sg))).astype(BF)
                dgu = jnp.concatenate([dgate, (dact * silu).astype(BF)], axis=1)
                dhn_k = dot(dgu, w_gu, (1, 1))
                dhns.append(dhn_k.astype(BF) if k else dhn_k)
                hn_of.append(hn_k)
                act_of.append(act)
                dgu_of.append(dgu)
            got = [swap(dhns[k], 2 * k) for k in range(1, chips)]
            act_of, dgu_of, got[:-1], _ = lax.optimization_barrier(
                (act_of, dgu_of, got[:-1], dhns[1:])
            )
            grad_hn = dhns[0]
            for piece in got:
                grad_hn = grad_hn + piece.astype(F32)

            gb_all = jnp.concatenate(gb_of, axis=0)
            down = dot(jnp.concatenate(act_of, axis=0), gb_all, (0, 0)).astype(BF)
            down_sum = core_sum(down.reshape((1, 2) + w_down.shape))[0]
            left = jnp.concatenate(hn_of, axis=0)
            right = jnp.concatenate(dgu_of, axis=0)

        down_sum, left, right = lax.optimization_barrier((down_sum, left, right))
        down_sum = lax.psum_scatter(down_sum, "ctx", scatter_dimension=0, tiled=True)
        if fused:
            wide = dot(left, right, (0, 0)).astype(BF).reshape(chips, shard, 2 * part)
        else:
            wide = rows_grad(left, right)
        wide = [
            lax.dynamic_index_in_dim(wide, chip ^ k, 0, keepdims=False) for k in range(chips)
        ]
        wide, grad_hn = lax.optimization_barrier((wide, grad_hn))
        wide = [swap(piece, 2 * k) if k else piece for k, piece in enumerate(wide)]

        gain_two_grad = jnp.sum(grad_hn * unit_two, axis=0)
        grad_unit = grad_hn * gains[1][None, :]
        dh1 = gb.astype(F32) + inverse_two * (
            grad_unit - unit_two * jnp.mean(grad_unit * unit_two, axis=1, keepdims=True)
        )
        dab = dh1.astype(BF)
        dob = dot(dab, w_o, (1, 1)).astype(BF)
        dq, dkv = attention_backward(table, qr, dob, o, lse, kv, cos_lanes, sin_lanes)
        xn, ob, dab, _ = lax.optimization_barrier((xn, ob, dab, dq))
        if fused:
            outs = [outs[k] for k in range(chips)]
        else:
            act_of, _ = lax.optimization_barrier((act_of, dq))
            outs = [dot(act, w_d, (1, 0)).astype(BF) for act in act_of]
        sent = outs[1:]
        own = own_key_grads(nc, dkv, cos_lanes, sin_lanes)
        own, wide, down_sum = lax.optimization_barrier((own, wide, down_sum))
        down_sum = lax.all_gather(down_sum, "ctx", axis=0, tiled=True)
        ob, dab, _ = lax.optimization_barrier((ob, dab, own))
        out_term = rows_grad(ob, dab)
        dqkv = jnp.concatenate([dq, own], axis=1)
        grad_xn = dot(dq, w_q, (1, 1)) + dot(own, w_kv, (1, 1))
        gain_one_grad = jnp.sum(grad_xn * unit_one, axis=0)
        grad_unit = grad_xn * gains[0][None, :]
        tokens_grad = dh1 + inverse_one * (
            grad_unit - unit_one * jnp.mean(grad_unit * unit_one, axis=1, keepdims=True)
        )
        qkv_term = rows_grad(xn, dqkv)

        gains_of = jnp.stack([gain_one_grad, gain_two_grad]).reshape(2, chips, 2, shard)
        other = lax.dynamic_index_in_dim(gains_of, 1 - core, 2, keepdims=False)
        mine = lax.dynamic_index_in_dim(gains_of, core, 2, keepdims=False)
        gains_of = (mine + swap(other, 1)).transpose(1, 0, 2).reshape(chips, 1, 2 * shard)
        gains_of = jnp.pad(gains_of.astype(BF), ((0, 0), (0, 15), (0, 0)))
        wide, down_sum, out_term, qkv_term, outs[0], sent = lax.optimization_barrier(
            (wide, down_sum, out_term, qkv_term, outs[0], sent)
        )
        gu_sum, out_sum, qkv_sum, gain_sum = finish(
            nf, nc, wide, [out_term, qkv_term, gains_of]
        )
        h1, gain_sum = lax.optimization_barrier((h1, gain_sum))
        branch = h1 + outs[0].astype(F32)
        for k in range(1, chips):
            branch = branch + swap(sent[k - 1], 2 * k).astype(F32)
        layer_out = branch.astype(BF)
        qkv_sum = qkv_sum.astype(F32)
        gain_sum = gain_sum[0].reshape(2, shard).astype(F32)
        gate_grad, up_grad = place_columns(order, gu_sum)
        query_width = HEADS * HEAD_DIM
        return (
            layer_out.reshape(1, rows, width),
            tokens_grad.reshape(1, rows, width),
            gain_sum[0],
            qkv_sum[:, :query_width],
            qkv_sum[:, query_width : query_width + key_width],
            qkv_sum[:, query_width + key_width :],
            out_sum.astype(F32),
            gain_sum[1],
            gate_grad,
            up_grad,
            down_sum.astype(F32),
        )

    weight = P("fsdp", None)
    activation = P("fsdp", "ctx", None)
    return jax.shard_map(
        shards,
        mesh=mesh,
        in_specs=(
            activation,
            P("fsdp"),
            weight,
            weight,
            weight,
            weight,
            P("fsdp"),
            weight,
            weight,
            weight,
            P(),
            P("fsdp", "ctx"),
            activation,
        ),
        out_specs=(
            activation,
            activation,
            P("fsdp"),
            weight,
            weight,
            weight,
            weight,
            P("fsdp"),
            weight,
            weight,
            weight,
        ),
        check_vma=False,
    )
```

```python
import functools

import jax
import jax.numpy as jnp
from jax import lax
from jax.experimental import pallas as pl
from jax.experimental.pallas import tpu as pltpu
from jax.sharding import PartitionSpec as P

HEADS = 32
KV_HEADS = 4
HEAD_DIM = 64
GROUP = HEADS // KV_HEADS
PAIRS = GROUP // 2
LANES = 2 * HEAD_DIM
STACK = PAIRS * LANES

EPS = 1e-05
THETA = 10000.0
NEG = -1e30
FLIGHT = 2
BF = jnp.bfloat16
F32 = jnp.float32


def dot(left, right, contract, out=F32):
    return lax.dot_general(
        left, right, ((contract[:1], contract[1:]), ((), ())), preferred_element_type=out
    )


def swap_halves(z):
    lane = lax.broadcasted_iota(jnp.int32, z.shape, 1)
    first = (lane % HEAD_DIM) < (HEAD_DIM // 2)
    return jnp.where(
        first,
        pltpu.roll(z, LANES - HEAD_DIM // 2, 1),
        pltpu.roll(z, HEAD_DIM // 2, 1),
    )


def split_heads(rows):
    lane = lax.broadcasted_iota(jnp.int32, rows.shape, 1)
    zero = jnp.zeros_like(rows)
    return jnp.concatenate(
        [jnp.where(lane < HEAD_DIM, rows, zero), jnp.where(lane >= HEAD_DIM, rows, zero)], axis=0
    )


def join_heads(columns):
    half = columns.shape[1] // 2
    sub = lax.broadcasted_iota(jnp.int32, (LANES, half), 0)
    return jnp.where(sub < HEAD_DIM, columns[:, :half], columns[:, half:]).T


def stack_pairs(ref, rows):
    return jnp.concatenate([ref[rows, p * LANES : (p + 1) * LANES] for p in range(PAIRS)], axis=0)


def two_blocks(ref, table, j, block):
    parts = [
        ref[pl.ds(pl.multiple_of(table[2 + 2 * j + i] * block, block), block), :] for i in range(2)
    ]
    return jnp.concatenate(parts, axis=0)


def causal(scores, j, own, block):
    key = lax.broadcasted_iota(jnp.int32, scores.shape, 0) + j * (2 * block)
    query = lax.broadcasted_iota(jnp.int32, scores.shape, 1) % block + own * block
    return jnp.where(key <= query, scores, NEG)


def head_twice(pair, group):
    wide = pair.astype(F32)
    lane = lax.broadcasted_iota(jnp.int32, wide.shape, 1)
    keep = (lane < HEAD_DIM) == (group % 2 == 0)
    return jnp.where(keep, wide, pltpu.roll(wide, HEAD_DIM, 1)).astype(BF)


def attention_forward_kernel(
    table,
    q_ref,
    cos_ref,
    sin_ref,
    k_pair,
    v_pair,
    qr_ref,
    o_ref,
    ob_ref,
    lse_ref,
    qm,
    m,
    l,
    acc,
    k_ref,
    v_ref,
):
    block = q_ref.shape[0] // 2
    group = pl.program_id(0)
    k_ref[...] = head_twice(k_pair[...], group)
    v_ref[...] = head_twice(v_pair[...], group)
    for h in range(2):
        rows = slice(h * block, (h + 1) * block)
        cosine, sine = cos_ref[rows, :], sin_ref[rows, :]
        for p in range(PAIRS):
            lanes = slice(p * LANES, (p + 1) * LANES)
            z = q_ref[rows, lanes]
            qr_ref[rows, lanes] = (z * cosine + swap_halves(z) * sine).astype(BF)
        scaled = stack_pairs(qr_ref, rows).astype(F32) * (HEAD_DIM**-0.5)
        qm[...] = split_heads(scaled).astype(BF)
        m[...] = jnp.full_like(m, NEG)
        l[...] = jnp.zeros_like(l)
        acc[...] = jnp.zeros_like(acc)
        own = table[h]

        def step(j, masked):
            keys = two_blocks(k_ref, table, j, block)
            values = two_blocks(v_ref, table, j, block)
            s = dot(keys, qm[...], (1, 1))
            if masked:
                s = causal(s, j, own, block)
            before = m[...]
            now = jnp.maximum(before, jnp.max(s, axis=0, keepdims=True))
            p = jnp.exp(s - now)
            decay = jnp.exp(before - now)
            l[...] = l[...] * decay + jnp.sum(p, axis=0, keepdims=True)
            acc[...] = acc[...] * decay + dot(values, p.astype(BF), (0, 0))
            m[...] = now

        last = own // 2

        @pl.loop(0, last)
        def _(j):
            step(j, False)

        step(last, True)
        lse_ref[0, h : h + 1, :] = m[...] + jnp.log(l[...])
        o = join_heads(acc[...] / l[...])
        for p in range(PAIRS):
            lanes = slice(p * LANES, (p + 1) * LANES)
            piece = o[p * block : (p + 1) * block, :]
            o_ref[rows, lanes] = piece
            ob_ref[rows, lanes] = piece.astype(BF)


def attention_forward(table, q, cosine, sine, kv):
    rows, length = q.shape[0], kv.shape[0]
    query_width = HEADS * HEAD_DIM
    columns = pl.BlockSpec((rows, STACK), lambda g, t: (0, g))
    whole = pl.BlockSpec((rows, LANES), lambda g, t: (0, 0))
    key_pair = pl.BlockSpec((length, LANES), lambda g, t: (0, g // 2))
    value_pair = pl.BlockSpec((length, LANES), lambda g, t: (0, KV_HEADS // 2 + g // 2))
    wide = GROUP * (rows // 2)
    return pl.pallas_call(
        attention_forward_kernel,
        grid_spec=pltpu.PrefetchScalarGridSpec(
            num_scalar_prefetch=1,
            grid=(KV_HEADS,),
            in_specs=[columns, whole, whole, key_pair, value_pair],
            out_specs=[
                columns,
                columns,
                columns,
                pl.BlockSpec((1, 2, wide), lambda g, t: (g, 0, 0)),
            ],
            scratch_shapes=[
                pltpu.VMEM((wide, LANES), BF),
                pltpu.VMEM((1, wide), F32),
                pltpu.VMEM((1, wide), F32),
                pltpu.VMEM((LANES, wide), F32),
                pltpu.VMEM((length, LANES), BF),
                pltpu.VMEM((length, LANES), BF),
            ],
        ),
        out_shape=[
            jax.ShapeDtypeStruct((rows, query_width), BF),
            jax.ShapeDtypeStruct((rows, query_width), F32),
            jax.ShapeDtypeStruct((rows, query_width), BF),
            jax.ShapeDtypeStruct((KV_HEADS, 2, wide), F32),
        ],
        compiler_params=pltpu.CompilerParams(vmem_limit_bytes=32 << 20),
        cost_estimate=pl.CostEstimate(
            flops=8 * HEADS * rows * length * HEAD_DIM,
            bytes_accessed=16 * rows * HEADS * HEAD_DIM,
            transcendentals=HEADS * rows * length,
        ),
        name="attention_forward",
    )(table, q, cosine, sine, kv, kv)


def attention_backward_kernel(
    table,
    qr_ref,
    do_ref,
    o_ref,
    lse_ref,
    k_pair,
    v_pair,
    cos_ref,
    sin_ref,
    dq_ref,
    dkv_ref,
    qm,
    dom,
    dqt,
    k_ref,
    v_ref,
    dk_ref,
    dv_ref,
):
    block = qr_ref.shape[0] // 2
    group = pl.program_id(0)
    k_ref[...] = head_twice(k_pair[...], group)
    v_ref[...] = head_twice(v_pair[...], group)
    dk_ref[...] = jnp.zeros_like(dk_ref)
    dv_ref[...] = jnp.zeros_like(dv_ref)
    for h in range(2):
        rows = slice(h * block, (h + 1) * block)
        scaled = stack_pairs(qr_ref, rows).astype(F32) * (HEAD_DIM**-0.5)
        qm[...] = split_heads(scaled).astype(BF)
        grads = stack_pairs(do_ref, rows).astype(F32)
        dom[...] = split_heads(grads).astype(BF)
        product = (grads * stack_pairs(o_ref, rows)).T
        inner = jnp.concatenate(
            [
                jnp.sum(product[:HEAD_DIM], axis=0, keepdims=True),
                jnp.sum(product[HEAD_DIM:], axis=0, keepdims=True),
            ],
            axis=1,
        )
        lse = lse_ref[0, h : h + 1, :]
        dqt[...] = jnp.zeros_like(dqt)
        own = table[h]

        def step(j, masked):
            keys = two_blocks(k_ref, table, j, block)
            values = two_blocks(v_ref, table, j, block)
            s = dot(keys, qm[...], (1, 1))
            if masked:
                s = causal(s, j, own, block)
            p = jnp.exp(s - lse)
            dp = dot(values, dom[...], (1, 1))
            ds = (p * (dp - inner)).astype(BF)
            dv = dot(p.astype(BF), dom[...], (1, 0))
            dk = dot(ds, qm[...], (1, 0))
            dqt[...] += dot(keys, ds, (0, 0))
            for i in range(2):
                at = pl.ds(pl.multiple_of(table[2 + 2 * j + i] * block, block), block)
                dk_ref[at, :] += dk[i * block : (i + 1) * block]
                dv_ref[at, :] += dv[i * block : (i + 1) * block]

        last = own // 2

        @pl.loop(0, last)
        def _(j):
            step(j, False)

        step(last, True)
        cosine, sine = cos_ref[rows, :], sin_ref[rows, :]
        dq = join_heads(dqt[...] * (HEAD_DIM**-0.5))
        for p in range(PAIRS):
            z = dq[p * block : (p + 1) * block, :]
            dq_ref[rows, p * LANES : (p + 1) * LANES] = (
                z * cosine - swap_halves(z) * sine
            ).astype(BF)
    lane = lax.broadcasted_iota(jnp.int32, dk_ref.shape, 1)
    keep = (lane < HEAD_DIM) == (group % 2 == 0)
    for i, ref in enumerate((dk_ref, dv_ref)):
        both = ref[...] + pltpu.roll(ref[...], HEAD_DIM, 1)
        dkv_ref[i] = jnp.where(keep, both, dkv_ref[i].astype(F32)).astype(BF)


def attention_backward(table, qr, grads, o, lse, kv, cosine, sine):
    rows, length = qr.shape[0], kv.shape[0]
    columns = pl.BlockSpec((rows, STACK), lambda g, t: (0, g))
    whole = pl.BlockSpec((rows, LANES), lambda g, t: (0, 0))
    key_pair = pl.BlockSpec((length, LANES), lambda g, t: (0, g // 2))
    value_pair = pl.BlockSpec((length, LANES), lambda g, t: (0, KV_HEADS // 2 + g // 2))
    wide = GROUP * (rows // 2)
    return pl.pallas_call(
        attention_backward_kernel,
        grid_spec=pltpu.PrefetchScalarGridSpec(
            num_scalar_prefetch=1,
            grid=(KV_HEADS,),
            in_specs=[
                columns,
                columns,
                columns,
                pl.BlockSpec((1, 2, wide), lambda g, t: (g, 0, 0)),
                key_pair,
                value_pair,
                whole,
                whole,
            ],
            out_specs=[columns, pl.BlockSpec((2, length, LANES), lambda g, t: (0, 0, g // 2))],
            scratch_shapes=[
                pltpu.VMEM((wide, LANES), BF),
                pltpu.VMEM((wide, LANES), BF),
                pltpu.VMEM((LANES, wide), F32),
                pltpu.VMEM((length, LANES), BF),
                pltpu.VMEM((length, LANES), BF),
                pltpu.VMEM((length, LANES), F32),
                pltpu.VMEM((length, LANES), F32),
            ],
        ),
        out_shape=[
            jax.ShapeDtypeStruct(qr.shape, BF),
            jax.ShapeDtypeStruct((2, length, KV_HEADS * HEAD_DIM), BF),
        ],
        compiler_params=pltpu.CompilerParams(vmem_limit_bytes=32 << 20),
        cost_estimate=pl.CostEstimate(
            flops=20 * HEADS * rows * length * HEAD_DIM,
            bytes_accessed=16 * rows * HEADS * HEAD_DIM,
            transcendentals=HEADS * rows * length,
        ),
        name="attention_backward",
    )(table, qr, grads, o, lse, kv, kv, cosine, sine)


def own_key_grads_kernel(nc, dkv_ref, cos_ref, sin_ref, out_ref, got, send_sem, recv_sem):
    rows, width = out_ref.shape[0], out_ref.shape[1] // 2
    here = lax.axis_index("ctx")
    mesh_id = pl.DeviceIdType.MESH
    barrier = pltpu.get_barrier_semaphore()
    for k in range(1, nc):
        pl.semaphore_signal(barrier, inc=1, device_id={"ctx": here ^ k}, device_id_type=mesh_id)
    pl.semaphore_wait(barrier, nc - 1)

    def copy(k):
        source = dkv_ref.at[:, pl.ds(k * rows, rows)]
        if k == 0:
            return pltpu.make_async_copy(source, got.at[0], recv_sem.at[0])
        return pltpu.make_async_remote_copy(
            src_ref=source,
            dst_ref=got.at[k],
            send_sem=send_sem.at[k],
            recv_sem=recv_sem.at[k],
            device_id={"ctx": here ^ k},
            device_id_type=mesh_id,
        )

    for k in reversed(range(nc)):
        copy(k).start()
    for k in range(nc):
        copy(k).wait()

    def total(i, lanes):
        return sum(got[k, i, :, lanes].astype(F32) for k in range(nc))

    for p in range(width // LANES):
        lanes = slice(p * LANES, (p + 1) * LANES)
        z = total(0, lanes)
        out_ref[:, lanes] = (z * cos_ref[...] - swap_halves(z) * sin_ref[...]).astype(BF)
        out_ref[:, width + p * LANES : width + (p + 1) * LANES] = total(1, lanes).astype(BF)


def own_key_grads(nc, dkv, cosine, sine):
    rows, width = dkv.shape[1] // nc, dkv.shape[2]
    vmem = pl.BlockSpec(memory_space=pltpu.VMEM)
    return pl.pallas_call(
        functools.partial(own_key_grads_kernel, nc),
        in_specs=[pl.BlockSpec(memory_space=pl.ANY), vmem, vmem],
        out_specs=vmem,
        out_shape=jax.ShapeDtypeStruct((rows, 2 * width), BF),
        scratch_shapes=[
            pltpu.VMEM((nc, 2, rows, width), BF),
            pltpu.SemaphoreType.DMA((nc,)),
            pltpu.SemaphoreType.DMA((nc,)),
        ],
        compiler_params=pltpu.CompilerParams(collective_id=2, has_side_effects=True),
        name="own_key_grads",
    )(dkv, cosine, sine)


def share_kernel(nf, nc, low, size, raw, *refs):
    count = 2 if raw else 1
    w_query, w_key, w_value, w_out, *halves, down, gains, tokens, cosine, sine = refs[: 9 + count]
    refs = refs[9 + count :]
    query, key_value, out, wide, downs, all_gains, kv_all = refs[:7]
    query_own, key_value_own, out_own, wide_own, down_own, gains_own = refs[7:13]
    (local, plane_send, plane_recv, along_send, along_recv, core_send, core_recv) = refs[13:20]
    (gain_send, gain_recv, down_sem, gather_send, gather_recv, gather_core) = refs[20:26]
    w_kv, gains_v, xn, kv, kv_load, kv_send, kv_recv = refs[26:]
    chips = nf // 2
    place, here = lax.axis_index("fsdp"), lax.axis_index("ctx")
    chip, core = place // 2, place % 2
    mesh_id = pl.DeviceIdType.MESH
    shard, columns = wide.shape[1:]
    part = columns // 2
    key_width = w_key.shape[1]
    gathered = [
        (w_query, query, query_own, pl.ds(0, w_query.shape[1])),
        (w_key, key_value, key_value_own, pl.ds(0, key_width)),
        (w_value, key_value, key_value_own, pl.ds(key_width, key_width)),
        (w_out, out, out_own, pl.ds(0, w_out.shape[1])),
    ]

    barrier = pltpu.get_barrier_semaphore()

    def greet(target):
        pl.semaphore_signal(barrier, inc=1, device_id=target, device_id_type=mesh_id)

    for j in range(1, nf):
        greet({"fsdp": place ^ j})
    for pos in range(nc):

        @pl.when(here == pos)
        def _():
            for i in range(nc):
                if i != pos:
                    greet({"ctx": i})

    pl.semaphore_wait(barrier, nf - 1 + nc - 1)

    def remote(source, target, sends, recvs, where):
        return pltpu.make_async_remote_copy(
            src_ref=source,
            dst_ref=target,
            send_sem=sends,
            recv_sem=recvs,
            device_id=where,
            device_id_type=mesh_id,
        )

    def piece(k, h, rows):
        if raw:
            at = pl.ds(pl.multiple_of((chip ^ k) * part, 128), part)
            return halves[h].at[rows, at]
        return halves[0].at[k, rows]

    def side(h):
        return pl.ds(h * part, part) if raw else pl.ds(0, columns)

    def rows_of(share):
        return pl.ds(low + share * size, size)

    def plane_copy(k, kind, h):
        rows = rows_of(here) if kind else pl.ds(0, low)
        return remote(
            piece(k, h, rows),
            wide.at[place, rows, side(h)],
            plane_send.at[kind, k, h],
            plane_recv.at[kind, k, h],
            {"fsdp": place ^ (2 * k)},
        )

    def along_copy(k, share, up, target):
        block = wide.at[place ^ (2 * k), rows_of(share)]
        return remote(
            block, block, along_send.at[up, share, k], along_recv.at[share, k], {"ctx": target}
        )

    def core_copy(k, share):
        rows = rows_of(share) if share < nc else pl.ds(0, low)
        block = wide.at[place ^ (2 * k), rows]
        return remote(
            block, block, core_send.at[k, share], core_recv.at[k, share], {"fsdp": place ^ 1}
        )

    def own_core_copy(h):
        return remote(
            piece(0, h, pl.ds(0, shard)),
            wide.at[place, :, side(h)],
            core_send.at[0, h],
            core_recv.at[0, h],
            {"fsdp": place ^ 1},
        )

    half = shard // 2
    relayed = chips == 4

    def gather_copy(u, k, relay=0):
        source, target, _, at = gathered[u]
        if relay:
            owner, rows = place ^ (2 * (3 - k)), pl.ds((2 - k) * half, half)
            source = target.at[owner, rows, at]
        else:
            owner, rows = place, pl.ds(0, shard)
        number = 2 * k + relay
        return remote(
            source,
            target.at[owner, rows, at],
            gather_send.at[u, number],
            gather_recv.at[u, number],
            {"fsdp": place ^ (2 * k)},
        )

    def gather_core_copy(u, k):
        source, target, _, at = gathered[u]
        block = target.at[place ^ (2 * k), :, at]
        return remote(
            block if k else source,
            block,
            gather_core.at[0, u, k],
            gather_core.at[1, u, k],
            {"fsdp": place ^ 1},
        )

    def down_copy():
        return remote(down, downs.at[core], down_sem.at[0], down_sem.at[1], {"fsdp": place ^ 1})

    def gain_copy(j):
        return remote(
            gains, all_gains.at[place], gain_send.at[j], gain_recv.at[j], {"fsdp": place ^ j}
        )

    direct = (1, 2) if relayed else tuple(range(1, chips))
    for k in range(1, chips):
        for h in range(count):
            plane_copy(k, 1, h).start()
    for j in range(1, nf):
        gain_copy(j).start()
    for h in range(count):
        own_core_copy(h).start()
    for u in range(4):
        gather_core_copy(u, 0).start()
    down_copy().start()
    own = [(source, stage.at[:, at], None) for source, _, stage, at in gathered]
    own += [(piece(0, h, pl.ds(0, shard)), wide_own.at[:, side(h)], None) for h in range(count)]
    own += [(down, down_own, downs.at[core]), (gains, gains_own, all_gains.at[place])]
    back = [
        (query_own, query.at[place]),
        (key_value_own, key_value.at[place]),
        (out_own, out.at[place]),
        (wide_own, wide.at[place]),
        (down_own, downs.at[core]),
        (gains_own, all_gains.at[place]),
    ]
    for i, (source, stage, _) in enumerate(own):
        pltpu.make_async_copy(source, stage, local.at[0, i]).start()
    for i, (source, stage, _) in enumerate(own):
        pltpu.make_async_copy(source, stage, local.at[0, i]).wait()
    for i, (stage, target) in enumerate(back):
        pltpu.make_async_copy(stage, target, local.at[1, i]).start()

    for k in range(1, chips):
        for h in range(count):
            plane_copy(k, 1, h).wait_send()
    for u in (1, 2, 0, 3):
        for k in direct:
            gather_copy(u, k).start()

    def kv_copy(k):
        if k == 0:
            return pltpu.make_async_copy(kv, kv_all.at[0], kv_recv.at[0])
        return remote(kv, kv_all.at[k], kv_send.at[k], kv_recv.at[k], {"ctx": here ^ k})

    def make_kv():
        for i in (len(back) - 1, 1):
            stage, target = back[i]
            pltpu.make_async_copy(stage, target, local.at[1, i]).wait()
        for j in range(1, nf):
            gain_copy(j).wait_recv()
        for u in (1, 2):
            if relayed:
                for k in direct:
                    gather_copy(u, k, 1).wait_recv()
                gather_core_copy(u, 3).start()
            for k in range(chips):
                gather_core_copy(u, k).wait_recv()
        loads = [
            pltpu.make_async_copy(key_value, w_kv, kv_load.at[0]),
            pltpu.make_async_copy(all_gains, gains_v, kv_load.at[1]),
        ]
        for copy in loads:
            copy.start()
        for copy in loads:
            copy.wait()
        for i in range(0, xn.shape[0], 16):
            x = tokens[i : i + 16, :].astype(F32)
            unit = x * lax.rsqrt(jnp.mean(x * x, axis=1, keepdims=True) + EPS)
            for f in range(nf):
                lanes = slice(f * shard, (f + 1) * shard)
                gain = gains_v[f, 0:1, :].astype(F32)
                xn[i : i + 16, lanes] = (unit[:, lanes] * gain).astype(BF)
        total = sum(
            dot(xn[:, f * shard : (f + 1) * shard], w_kv[f], (1, 0)) for f in range(nf)
        )
        for p in range(0, key_width, LANES):
            z = total[:, p : p + LANES]
            kv[:, p : p + LANES] = (z * cosine[...] + swap_halves(z) * sine[...]).astype(BF)
        kv[:, key_width:] = total[:, key_width:].astype(BF)
        for k in reversed(range(nc)):
            kv_copy(k).start()

    for pos in range(nc):

        @pl.when(here == pos)
        def _():
            def pass_on(k, share):
                if share <= pos < nc - 1:
                    along_copy(k, share, 1, pos + 1).start()
                if share >= pos > 0:
                    along_copy(k, share, 0, pos - 1).start()
                core_copy(k, share).start()

            for k in range(1, chips):
                for h in range(count):
                    plane_copy(k, 1, h).wait_recv()
                pass_on(k, pos)
            if low:
                for k in range(1, chips):
                    for h in range(count):
                        plane_copy(k, 0, h).start()
            def gather_on(u):
                for k in direct:
                    gather_copy(u, k).wait_recv()
                    if relayed:
                        gather_copy(u, 3 - k, 1).start()
                    gather_core_copy(u, k).start()

            groups = [(), (1, 2), (0, 3)]
            for d in range(1, max(nc, len(groups))):
                for share in (pos - d, pos + d):
                    if 0 <= share < nc:
                        for k in range(1, chips):
                            along_copy(k, share, 0, 0).wait_recv()
                            pass_on(k, share)
                for u in groups[d] if d < len(groups) else ():
                    if u == 3:
                        make_kv()
                    gather_on(u)
            if low:
                for k in range(1, chips):
                    for h in range(count):
                        plane_copy(k, 0, h).wait_recv()
                    core_copy(k, nc).start()
            if relayed:
                for u in (0, 3):
                    for k in direct:
                        gather_copy(u, k, 1).wait_recv()
                    gather_core_copy(u, 3).start()
            for k in range(1, chips):
                for share in range(nc):
                    if share <= pos < nc - 1:
                        along_copy(k, share, 1, pos + 1).wait_send()
                    if share >= pos > 0:
                        along_copy(k, share, 0, pos - 1).wait_send()

    for h in range(count):
        own_core_copy(h).wait()
    for k in range(1, chips):
        for share in range(nc + 1 if low else nc):
            core_copy(k, share).wait()
        if low:
            for h in range(count):
                plane_copy(k, 0, h).wait_send()
    for j in range(1, nf):
        gain_copy(j).wait_send()
    for k in range(nc):
        kv_copy(k).wait()
    for u in range(4):
        for k in direct:
            gather_copy(u, k).wait_send()
            if relayed:
                gather_copy(u, k, 1).wait_send()
        for k in range(chips):
            gather_core_copy(u, k).wait_send()
            if u in (0, 3):
                gather_core_copy(u, k).wait_recv()
    down_copy().wait()
    for i, (stage, target) in enumerate(back):
        if i not in (len(back) - 1, 1):
            pltpu.make_async_copy(stage, target, local.at[1, i]).wait()


def share_weights(
    nf,
    nc,
    w_query,
    w_key,
    w_value,
    w_out,
    w_gate,
    w_up,
    order,
    down,
    gains,
    tokens,
    cosine,
    sine,
):
    chips = nf // 2
    shard, hidden = w_gate.shape
    part = hidden // chips
    size = shard // nc
    low = shard - nc * size
    raw = part % 128 == 0
    halves = [w_gate, w_up]
    if not raw:
        both = [w.reshape(shard, chips, part).transpose(1, 0, 2) for w in halves]
        halves = [jnp.take(jnp.concatenate(both, axis=2), order, axis=0)]
    anywhere = pl.BlockSpec(memory_space=pl.ANY)
    dma = pltpu.SemaphoreType.DMA
    kv_shape = (tokens.shape[0], 2 * w_key.shape[1])
    widths = [w_query.shape[1], 2 * w_key.shape[1], w_out.shape[1], 2 * part]
    return pl.pallas_call(
        functools.partial(share_kernel, nf, nc, low, size, raw),
        in_specs=[anywhere] * (6 + len(halves)) + [pl.BlockSpec(memory_space=pltpu.VMEM)] * 3,
        out_specs=[anywhere] * 7,
        out_shape=[jax.ShapeDtypeStruct((nf, shard, width), BF) for width in widths]
        + [
            jax.ShapeDtypeStruct((2,) + down.shape, BF),
            jax.ShapeDtypeStruct((nf,) + gains.shape, BF),
            jax.ShapeDtypeStruct((nc,) + kv_shape, BF),
        ],
        scratch_shapes=[pltpu.VMEM((shard, width), BF) for width in widths]
        + [
            pltpu.VMEM(down.shape, BF),
            pltpu.VMEM(gains.shape, BF),
            dma((2, 8)),
            dma((2, chips, 2)),
            dma((2, chips, 2)),
            dma((2, nc, chips)),
            dma((nc, chips)),
            dma((chips, nc + 1)),
            dma((chips, nc + 1)),
            dma((nf,)),
            dma((nf,)),
            dma((2,)),
            dma((4, 2 * chips)),
            dma((4, 2 * chips)),
            dma((2, 4, chips)),
            pltpu.VMEM((nf, shard, widths[1]), BF),
            pltpu.VMEM((nf,) + gains.shape, BF),
            pltpu.VMEM(tokens.shape, BF),
            pltpu.VMEM(kv_shape, BF),
            dma((2,)),
            dma((nc,)),
            dma((nc,)),
        ],
        compiler_params=pltpu.CompilerParams(
            collective_id=1, has_side_effects=True, vmem_limit_bytes=56 << 20
        ),
        name="share_weights",
    )(w_query, w_key, w_value, w_out, *halves, down, gains, tokens, cosine, sine)


def place_columns_kernel(order, both_ref, gate_ref, up_ref):
    part = gate_ref.shape[1]
    gate_ref[...] = both_ref[0, :, :part].astype(F32)
    up_ref[...] = both_ref[0, :, part:].astype(F32)


def place_columns(order, both):
    parts, shard, part = both.shape[0], both.shape[1], both.shape[2] // 2
    out = jax.ShapeDtypeStruct((shard, parts * part), F32)
    if part % 128:
        both = jnp.take(both, order, axis=0).transpose(1, 0, 2).astype(F32)
        return [both[:, :, i * part : (i + 1) * part].reshape(out.shape) for i in range(2)]
    columns = pl.BlockSpec((shard, part), lambda k, t: (0, t[k]))
    return pl.pallas_call(
        place_columns_kernel,
        grid_spec=pltpu.PrefetchScalarGridSpec(
            num_scalar_prefetch=1,
            grid=(parts,),
            in_specs=[pl.BlockSpec((1, shard, 2 * part), lambda k, t: (k, 0, 0))],
            out_specs=[columns, columns],
        ),
        out_shape=[out, out],
        name="place_columns",
    )(order, both)


def feed_forward_kernel(nf, *refs):
    chips = nf // 2
    hn, *gbs, w_gu, w_d, grad, left, right, downs, outs = refs[: chips + 8]
    w_gu_v, w_d_v, hn_v, gb_v, dact_v, act_v, dgu_v, sent, got, outs_v = refs[chips + 8 : chips + 18]
    tiles, *sems = refs[chips + 18 :]
    load, load_gb, hn_send, hn_recv, dhn_send, dhn_recv, store = sems[:7]
    left_local, left_send, left_recv, right_local, right_send, right_recv = sems[7:13]
    down_local, down_send, down_recv = sems[13:]
    place = lax.axis_index("fsdp")
    core = place % 2
    rows, width = hn.shape
    part = w_d.shape[0]
    shard = width // nf
    half = rows // 2
    relayed = chips == 4
    direct = (1, 2) if relayed else tuple(range(1, chips))
    mesh_id = pl.DeviceIdType.MESH

    barrier = pltpu.get_barrier_semaphore()
    for j in [1] + [2 * k for k in range(1, chips)]:
        pl.semaphore_signal(
            barrier, inc=1, device_id={"fsdp": place ^ j}, device_id_type=mesh_id
        )
    pl.semaphore_wait(barrier, chips)

    def remote(source, target, sends, recvs, step):
        return pltpu.make_async_remote_copy(
            src_ref=source,
            dst_ref=target,
            send_sem=sends,
            recv_sem=recvs,
            device_id={"fsdp": place ^ step},
            device_id_type=mesh_id,
        )

    def hn_copy(k, relay=0):
        at = 2 * k + relay
        if relay:
            lines = pl.ds((2 - k) * half, half)
            source, target = hn_v.at[3 - k, lines], hn_v.at[3, lines]
        else:
            source, target = hn, hn_v.at[k]
        return remote(source, target, hn_send.at[at], hn_recv.at[at], 2 * k)

    def dhn_copy(k):
        return remote(sent.at[k - 1], got.at[k - 1], dhn_send.at[k], dhn_recv.at[k], 2 * k)

    def left_copy(k, j, other):
        number = 1 - core if other else core
        columns = pl.ds(pl.multiple_of((2 * j + number) * shard, shard), shard)
        source = hn_v.at[k, :, columns]
        target = left.at[other, k, :, pl.ds(j * shard, shard)]
        if other:
            return remote(source, target, left_send.at[k, j], left_recv.at[k, j], 1)
        return pltpu.make_async_copy(source, target, left_local.at[k, j])

    def right_copy(k, other):
        if other:
            return remote(dgu_v.at[k], right.at[1, k], right_send.at[k], right_recv.at[k], 1)
        return pltpu.make_async_copy(dgu_v.at[k], right.at[0, k], right_local.at[k])

    loads = [
        pltpu.make_async_copy(w_d, w_d_v, load.at[0]),
        pltpu.make_async_copy(hn, hn_v.at[0], load.at[1]),
        pltpu.make_async_copy(w_gu, w_gu_v, load.at[2]),
    ]
    gb_loads = [
        pltpu.make_async_copy(gb, gb_v.at[k], load_gb.at[k]) for k, gb in enumerate(gbs)
    ]
    store_outs = pltpu.make_async_copy(outs_v, outs, store.at[0])
    for k in direct:
        hn_copy(k).start()
    for copy in loads[:1] + gb_loads + loads[1:]:
        copy.start()

    for copy in loads[:1] + gb_loads:
        copy.wait()

    def dact_tile(start, size):
        tile = w_d_v[pl.ds(start, size), :]
        for k in range(chips):
            dact_v[k, :, pl.ds(start, size)] = dot(gb_v[k], tile, (1, 1))

    @pl.loop(0, part // 256)
    def _(i):
        dact_tile(pl.multiple_of(i * 256, 256), 256)

    if part % 256:
        dact_tile(part - 128, 128)

    def forward(k):
        for j in range(chips):
            left_copy(k, j, 1).start()
            left_copy(k, j, 0).start()

        def tile(start, size):
            one, two = pl.ds(start, size), pl.ds(pl.multiple_of(part + start, 128), size)
            gate = dot(hn_v[k], w_gu_v[:, one], (1, 0))
            up = dot(hn_v[k], w_gu_v[:, two], (1, 0))
            dact = dact_v[k, :, one]
            sg = jax.nn.sigmoid(gate)
            silu = gate * sg
            act_v[k, :, one] = (silu * up).astype(BF)
            dgu_v[k, :, one] = (dact * up * sg * (1.0 + gate * (1.0 - sg))).astype(BF)
            dgu_v[k, :, two] = (dact * silu).astype(BF)

        @pl.loop(0, part // 256)
        def _(i):
            tile(pl.multiple_of(i * 256, 256), 256)

        if part % 256:
            tile(part - 128, 128)

        right_copy(k, 1).start()
        right_copy(k, 0).start()

    def backward(k):
        @pl.loop(0, width // 256)
        def _(i):
            lines = pl.ds(pl.multiple_of(i * 256, 256), 256)
            dhn = dot(dgu_v[k], w_gu_v[lines, :], (1, 1))
            if k:
                sent[k - 1, :, lines] = dhn.astype(BF)
            else:
                grad[:, lines] = dhn

        if k:
            dhn_copy(k).start()

    for copy in loads[1:]:
        copy.wait()
    forward(0)
    for k in direct:
        hn_copy(k).wait_recv()
        if relayed:
            hn_copy(3 - k, 1).start()
    for k in range(1, chips):
        if relayed and k == 3:
            for i in direct:
                hn_copy(i, 1).wait_recv()
        forward(k)
        backward(k)
    backward(0)

    @pl.loop(0, width // 256)
    def _(i):
        columns = pl.ds(pl.multiple_of(i * 256, 256), 256)
        for k in range(chips):
            outs_v[k, :, columns] = dot(act_v[k], w_d_v[:, columns], (1, 0)).astype(BF)

    store_outs.start()

    lower = part // 2
    spans = []
    for start in range(0, part, 128):
        cuts = sorted({start, min(max(lower, start), start + 128), start + 128})
        spans += [(start, a, b) for a, b in zip(cuts, cuts[1:])]

    def span_copies(n):
        start, a, b = spans[n]
        number = int(a >= lower)
        source = tiles.at[(start // 128) % 2, pl.ds(a - start, b - a)]
        at = pl.ds(a - number * lower, b - a)

        def keep():
            return pltpu.make_async_copy(source, downs.at[0, at], down_local.at[n])

        def send():
            return remote(source, downs.at[1, at], down_send.at[n], down_recv.at[n], 1)

        return number, keep, send

    def each_span(chosen, go):
        for n in chosen:
            number, keep, send = span_copies(n)

            @pl.when(core == number)
            def _():
                keep().start() if go else keep().wait()

            @pl.when(core != number)
            def _():
                send().start() if go else send().wait_send()

    for start in range(0, part, 128):
        before = [n for n, span in enumerate(spans) if span[0] == start - 256]
        each_span(before, False)
        tile = sum(
            dot(act_v[k, :, start : start + 128], gb_v[k], (0, 0)) for k in range(chips)
        )
        tiles[(start // 128) % 2] = tile.astype(BF)
        each_span([n for n, span in enumerate(spans) if span[0] == start], True)
    each_span([n for n, span in enumerate(spans) if span[0] >= part - 256], False)
    for n in range(len(spans)):
        number, _, send = span_copies(n)

        @pl.when(core == number)
        def _():
            send().wait_recv()

    for k in range(1, chips):
        dhn_copy(k).wait_recv()

    @pl.loop(0, rows // 16)
    def _(i):
        lines = pl.ds(pl.multiple_of(i * 16, 16), 16)
        grad[lines, :] += sum(got[k, lines, :].astype(F32) for k in range(chips - 1))

    store_outs.wait()
    for k in range(chips):
        for j in range(chips):
            left_copy(k, j, 0).wait()
            left_copy(k, j, 1).wait()
        right_copy(k, 0).wait()
        right_copy(k, 1).wait()
        if k:
            dhn_copy(k).wait_send()
    for k in direct:
        hn_copy(k).wait_send()
        if relayed:
            hn_copy(k, 1).wait_send()


def feed_forward(nf, hn, gbs, w_gu, w_d):
    chips = nf // 2
    rows, width = hn.shape
    part = w_d.shape[0]
    anywhere = pl.BlockSpec(memory_space=pl.ANY)
    dma = pltpu.SemaphoreType.DMA
    shape = jax.ShapeDtypeStruct
    return pl.pallas_call(
        functools.partial(feed_forward_kernel, nf),
        in_specs=[anywhere] * (chips + 3),
        out_specs=[pl.BlockSpec(memory_space=pltpu.VMEM)] + [anywhere] * 4,
        out_shape=[
            shape((rows, width), F32),
            shape((2, chips, rows, width // 2), BF),
            shape((2, chips, rows, 2 * part), BF),
            shape((2, part // 2, width), BF),
            shape((chips, rows, width), BF),
        ],
        scratch_shapes=[
            pltpu.VMEM((width, 2 * part), BF),
            pltpu.VMEM((part, width), BF),
            pltpu.VMEM((chips, rows, width), BF),
            pltpu.VMEM((chips, rows, width), BF),
            pltpu.VMEM((chips, rows, part), F32),
            pltpu.VMEM((chips, rows, part), BF),
            pltpu.VMEM((chips, rows, 2 * part), BF),
            pltpu.VMEM((chips - 1, rows, width), BF),
            pltpu.VMEM((chips - 1, rows, width), BF),
            pltpu.VMEM((chips, rows, width), BF),
            pltpu.VMEM((2, 128, width), BF),
            dma((3,)),
            dma((chips,)),
            dma((2 * chips,)),
            dma((2 * chips,)),
            dma((chips,)),
            dma((chips,)),
            dma((1,)),
            dma((chips, chips)),
            dma((chips, chips)),
            dma((chips, chips)),
            dma((chips,)),
            dma((chips,)),
            dma((chips,)),
            dma((part // 128 + 1,)),
            dma((part // 128 + 1,)),
            dma((part // 128 + 1,)),
        ],
        compiler_params=pltpu.CompilerParams(
            collective_id=3, has_side_effects=True, vmem_limit_bytes=60 << 20
        ),
        cost_estimate=pl.CostEstimate(
            flops=12 * chips * rows * width * part,
            bytes_accessed=40_000_000,
            transcendentals=chips * rows * part,
        ),
        name="feed_forward",
    )(hn, *gbs, w_gu, w_d)


def chunk_rows(rows):
    return max(r for r in range(16, 65, 16) if rows % r == 0)


def finish_kernel(nf, nc, *refs):
    pieces, refs = refs[: nf // 2], refs[nf // 2 - 1 :]
    sources, (outs, owns, ins, xs) = refs[:4], (refs[i : i + 4] for i in range(4, 20, 4))
    plane_send, plane_recv, local, in_sem, x_sem, first_send, second_send, out_sem = refs[20:]
    chips = nf // 2
    place, here = lax.axis_index("fsdp"), lax.axis_index("ctx")
    chip = place // 2
    lower = here < nc // 2
    depth = jnp.where(lower, here, nc - 1 - here)
    inner = jnp.where(lower, here + 1, here - 1)
    outer = jnp.where(lower, here - 1, here + 1)
    mesh_id = pl.DeviceIdType.MESH

    barrier = pltpu.get_barrier_semaphore()
    for k in range(1, chips):
        pl.semaphore_signal(
            barrier, inc=1, device_id={"fsdp": place ^ (2 * k)}, device_id_type=mesh_id
        )
    pl.semaphore_signal(barrier, inc=1, device_id={"ctx": inner}, device_id_type=mesh_id)

    @pl.when(depth > 0)
    def _():
        pl.semaphore_signal(barrier, inc=1, device_id={"ctx": outer}, device_id_type=mesh_id)
        pl.semaphore_wait(barrier, chips + 1)

    @pl.when(depth == 0)
    def _():
        pl.semaphore_wait(barrier, chips)

    def plane_copy(u, k):
        return pltpu.make_async_remote_copy(
            src_ref=sources[u].at[chip ^ k],
            dst_ref=owns[u].at[k],
            send_sem=plane_send.at[u, k],
            recv_sem=plane_recv.at[u, k],
            device_id={"fsdp": place ^ (2 * k)},
            device_id_type=mesh_id,
        )

    def local_copy(u, k):
        source = sources[u].at[chip] if u else pieces[k]
        return pltpu.make_async_copy(source, owns[u].at[k], local.at[u, k])

    for u in range(4):
        for k in range(chips):
            if u == 0 or k == 0:
                local_copy(u, k).start()
            else:
                plane_copy(u, k).start()

    units = [(0, k) for k in range(chips)] + [(u, None) for u in (1, 2, 3)]
    chunks = []
    for u, k in units:
        total = outs[u].shape[-2]
        size = chunk_rows(total)
        chunks += [(u, k, r, size) for r in range(0, total, size)]

    def views(c):
        u, k, r, size = chunks[c]
        rows = pl.ds(r, size)
        return [owns[u].at[k or 0, rows]] + [
            ref.at[rows] if k is None else ref.at[k, rows] for ref in (ins[u], xs[u], outs[u])
        ]

    def first_copy(c, across):
        own, arriving, x, _ = views(c)
        return pltpu.make_async_remote_copy(
            src_ref=own,
            dst_ref=x if across else arriving,
            send_sem=first_send.at[c],
            recv_sem=(x_sem if across else in_sem).at[c],
            device_id={"ctx": inner},
            device_id_type=mesh_id,
        )

    def second_copy(c, across):
        _, arriving, x, _ = views(c)
        return pltpu.make_async_remote_copy(
            src_ref=arriving if across else x,
            dst_ref=x,
            send_sem=second_send.at[c],
            recv_sem=x_sem.at[c],
            device_id={"ctx": outer},
            device_id_type=mesh_id,
        )

    def out_copy(c, across):
        _, arriving, x, out = views(c)
        return pltpu.make_async_copy(arriving if across else x, out, out_sem.at[c])

    def add_into(target, terms, size):
        @pl.loop(0, size // 16)
        def _(i):
            strip = pl.ds(pl.multiple_of(i * 16, 16), 16)
            target[strip, :] = sum(term[strip, :].astype(F32) for term in terms).astype(BF)

    def inward(c, level):
        u, k, r, size = chunks[c]
        own, arriving, _, _ = views(c)
        terms = [own]
        if r == 0:
            local_copy(u, k or 0).wait()
            if u >= 1:
                for j in range(1, chips):
                    plane_copy(u, j).wait_recv()
        if u >= 1:
            terms += [owns[u].at[j, pl.ds(r, size)] for j in range(1, chips)]
        if level > 0:
            first_copy(c, False).wait_recv()
            terms.append(arriving)
        if len(terms) > 1:
            add_into(own, terms, size)
        if c >= FLIGHT:
            first_copy(c - FLIGHT, False).wait_send()
        first_copy(c, level == top).start()

    def outward(c, level):
        size = chunks[c][3]
        own, arriving, x, _ = views(c)
        first_copy(c, True).wait_recv()
        if level == top:
            add_into(arriving, [own, x], size)
        out_copy(c, level == top).start()
        if level > 0:
            if c >= FLIGHT:
                second_copy(c - FLIGHT, False).wait_send()
            second_copy(c, level == top).start()

    top = nc // 2 - 1
    count = len(chunks)
    for level in range(top + 1):

        @pl.when(depth == level)
        def _():
            lag = 1 + 2 * (top - level)
            for t in range(count + lag):
                if t < count:
                    inward(t, level)
                if t >= lag:
                    outward(t - lag, level)
            for c in range(max(0, count - FLIGHT), count):
                first_copy(c, False).wait_send()
                if level > 0:
                    second_copy(c, False).wait_send()
            for c in range(count):
                out_copy(c, False).wait()

    for u in range(1, 4):
        for k in range(1, chips):
            plane_copy(u, k).wait_send()


def finish(nf, nc, pieces, sums):
    chips = nf // 2
    pieces_shape = (chips,) + pieces[0].shape
    shapes = [pieces_shape] + [x.shape[1:] for x in sums]
    count = sum(
        (shape[0] if len(shape) == 3 else 1) * (shape[-2] // chunk_rows(shape[-2]))
        for shape in shapes
    )
    anywhere = pl.BlockSpec(memory_space=pl.ANY)
    dma = pltpu.SemaphoreType.DMA
    return pl.pallas_call(
        functools.partial(finish_kernel, nf, nc),
        in_specs=[anywhere] * (chips + 3),
        out_specs=[anywhere] * 4,
        out_shape=[jax.ShapeDtypeStruct(shape, BF) for shape in shapes],
        scratch_shapes=[pltpu.VMEM(x, BF) for x in [pieces_shape] + [x.shape for x in sums]]
        + [pltpu.VMEM(shape, BF) for shape in shapes]
        + [pltpu.VMEM(shape, BF) for shape in shapes]
        + [dma((4, chips)), dma((4, chips)), dma((4, chips))]
        + [dma((count,))] * 5,
        compiler_params=pltpu.CompilerParams(
            collective_id=0, has_side_effects=True, vmem_limit_bytes=48 << 20
        ),
        cost_estimate=pl.CostEstimate(
            flops=200_000_000_000, bytes_accessed=60_000_000, transcendentals=0
        ),
        name="finish",
    )(*pieces, *sums)


def solution(mesh):
    nf, nc = mesh.shape["fsdp"], mesh.shape["ctx"]
    chips = nf // 2

    def swap(x, k):
        return lax.ppermute(x, "fsdp", [(i, i ^ k) for i in range(nf)])

    def plane_gather(x):
        if chips != 4:
            return [swap(x, 2 * k) for k in range(1, chips)]
        one, two = swap(x, 2), swap(x, 4)
        half = x.shape[0] // 2
        return [one, two, jnp.concatenate([swap(one[:half], 4), swap(two[half:], 2)], axis=0)]

    def cross(x, k):
        return lax.ppermute(x, "ctx", [(i, i ^ k) for i in range(nc)])

    def shards(
        tokens,
        attn_gain,
        w_query,
        w_key,
        w_value,
        w_out,
        ffn_gain,
        w_gate,
        w_up,
        w_down,
        block_table,
        positions,
        out_grad,
    ):
        place = lax.axis_index("fsdp")
        chip, core = place // 2, place % 2
        x = tokens[0].astype(F32)
        gb = out_grad[0]
        rows, width = x.shape
        hidden = w_gate.shape[1]
        part = hidden // chips
        shard = w_gate.shape[0]
        key_width = KV_HEADS * HEAD_DIM

        def core_sum(x):
            other = lax.dynamic_index_in_dim(x, 1 - core, 1, keepdims=False)
            mine = lax.dynamic_index_in_dim(x, core, 1, keepdims=False)
            return (mine.astype(F32) + swap(other, 1).astype(F32)).astype(BF)

        def rows_grad(left, right):
            columns = [left[:, i * shard : (i + 1) * shard] for i in range(nf)]
            even = jnp.concatenate(columns[::2], axis=1)
            odd = jnp.concatenate(columns[1::2], axis=1)
            mine = jnp.where(core == 0, even, odd)
            other = jnp.where(core == 0, odd, even)
            left = jnp.concatenate([mine, swap(other, 1)], axis=0)
            right = jnp.concatenate([right, swap(right, 1)], axis=0)
            return dot(left, right, (0, 0)).astype(BF).reshape(chips, shard, right.shape[1])


        half = HEAD_DIM // 2
        frequency = THETA ** (-jnp.arange(half, dtype=F32) * (2.0 / HEAD_DIM))
        angle = positions[0].astype(F32)[:, None] * frequency[None, :]
        cosine, sine = jnp.cos(angle), jnp.sin(angle)
        cos_lanes = jnp.tile(cosine, (1, 4))
        sin_lanes = jnp.tile(jnp.concatenate([-sine, sine], axis=1), (1, 2))
        blocks = 2 * nc
        stored = block_table.reshape(-1)
        number = jnp.arange(blocks, dtype=jnp.int32)
        where = jnp.sum(
            jnp.where(stored[None, :] == number[:, None], number[None, :], 0), axis=1
        )
        here = lax.axis_index("ctx")
        own = lax.dynamic_slice_in_dim(stored, 2 * here, 2)
        where = 2 * ((where // 2) ^ here) + where % 2
        table = jnp.concatenate([own, where]).astype(jnp.int32)

        order = chip ^ jnp.arange(chips, dtype=jnp.int32)
        both_gains = jnp.pad(jnp.stack([attn_gain, ffn_gain]), ((0, 14), (0, 0)))
        w_q, w_kv, w_o, w_gu, w_d, gains, kv = share_weights(
            nf,
            nc,
            w_query,
            w_key,
            w_value,
            w_out,
            w_gate,
            w_up,
            order,
            w_down,
            both_gains,
            tokens[0],
            cos_lanes,
            sin_lanes,
        )
        w_q = w_q.reshape(width, -1)
        w_kv = w_kv.reshape(width, -1)
        gb_sent, w_kv = lax.optimization_barrier((gb, w_kv))
        w_o = w_o.reshape(-1, width)
        w_gu = w_gu.reshape(width, 2 * part)
        w_d = w_d.reshape(part, width)
        gains = gains[:, :2].astype(F32).transpose(1, 0, 2).reshape(2, width)

        inverse_one = lax.rsqrt(jnp.mean(x * x, axis=1, keepdims=True) + EPS)
        unit_one = x * inverse_one
        xn = (unit_one * gains[0][None, :]).astype(BF)
        q_sum = dot(xn, w_q, (1, 0))
        gb_of = [gb] + [swap(gb_sent, 2 * k) for k in range(1, chips)]
        kv = kv.reshape(nc * rows, 2 * key_width)
        qr, o, ob, lse = attention_forward(table, q_sum, cos_lanes, sin_lanes, kv)
        h1 = x + dot(ob, w_o, (1, 0))
        inverse_two = lax.rsqrt(jnp.mean(h1 * h1, axis=1, keepdims=True) + EPS)
        unit_two = h1 * inverse_two
        hn = (unit_two * gains[1][None, :]).astype(BF)

        hn, gb_of = lax.optimization_barrier((hn, gb_of))

        fused = part % 128 == 0
        if fused:
            grad_hn, left, right, downs, outs = feed_forward(nf, hn, gb_of, w_gu, w_d)
            left = left.reshape(2 * chips * rows, width // 2)
            right = right.reshape(2 * chips * rows, 2 * part)
            down_sum = (downs[0].astype(F32) + downs[1].astype(F32)).astype(BF)
        else:
            dhns = []
            hn_of, act_of, dgu_of = [], [], []
            for k, hn_k in enumerate([hn] + plane_gather(hn)):
                gu = dot(hn_k, w_gu, (1, 0))
                dact = dot(gb_of[k], w_d, (1, 1))
                gate, up = gu[:, :part], gu[:, part:]
                sg = jax.nn.sigmoid(gate)
                silu = gate * sg
                act = (silu * up).astype(BF)
                dgate = (dact * up * sg * (1.0 + gate * (1.0 - sg))).astype(BF)
                dgu = jnp.concatenate([dgate, (dact * silu).astype(BF)], axis=1)
                dhn_k = dot(dgu, w_gu, (1, 1))
                dhns.append(dhn_k.astype(BF) if k else dhn_k)
                hn_of.append(hn_k)
                act_of.append(act)
                dgu_of.append(dgu)
            got = [swap(dhns[k], 2 * k) for k in range(1, chips)]
            act_of, dgu_of, got[:-1], _ = lax.optimization_barrier(
                (act_of, dgu_of, got[:-1], dhns[1:])
            )
            grad_hn = dhns[0]
            for piece in got:
                grad_hn = grad_hn + piece.astype(F32)

            gb_all = jnp.concatenate(gb_of, axis=0)
            down = dot(jnp.concatenate(act_of, axis=0), gb_all, (0, 0)).astype(BF)
            down_sum = core_sum(down.reshape((1, 2) + w_down.shape))[0]
            left = jnp.concatenate(hn_of, axis=0)
            right = jnp.concatenate(dgu_of, axis=0)

        down_sum, left, right = lax.optimization_barrier((down_sum, left, right))
        down_sum = lax.psum_scatter(down_sum, "ctx", scatter_dimension=0, tiled=True)
        if fused:
            wide = dot(left, right, (0, 0)).astype(BF).reshape(chips, shard, 2 * part)
        else:
            wide = rows_grad(left, right)
        wide = [
            lax.dynamic_index_in_dim(wide, chip ^ k, 0, keepdims=False) for k in range(chips)
        ]
        wide, grad_hn = lax.optimization_barrier((wide, grad_hn))
        wide = [swap(piece, 2 * k) if k else piece for k, piece in enumerate(wide)]

        gain_two_grad = jnp.sum(grad_hn * unit_two, axis=0)
        grad_unit = grad_hn * gains[1][None, :]
        dh1 = gb.astype(F32) + inverse_two * (
            grad_unit - unit_two * jnp.mean(grad_unit * unit_two, axis=1, keepdims=True)
        )
        dab = dh1.astype(BF)
        dob = dot(dab, w_o, (1, 1)).astype(BF)
        dq, dkv = attention_backward(table, qr, dob, o, lse, kv, cos_lanes, sin_lanes)
        xn, ob, dab, _ = lax.optimization_barrier((xn, ob, dab, dq))
        if fused:
            outs = [outs[k] for k in range(chips)]
        else:
            act_of, _ = lax.optimization_barrier((act_of, dq))
            outs = [dot(act, w_d, (1, 0)).astype(BF) for act in act_of]
        sent = outs[1:]
        own = own_key_grads(nc, dkv, cos_lanes, sin_lanes)
        own, wide, down_sum = lax.optimization_barrier((own, wide, down_sum))
        down_sum = lax.all_gather(down_sum, "ctx", axis=0, tiled=True)
        ob, dab, _ = lax.optimization_barrier((ob, dab, own))
        out_term = rows_grad(ob, dab)
        dqkv = jnp.concatenate([dq, own], axis=1)
        grad_xn = dot(dq, w_q, (1, 1)) + dot(own, w_kv, (1, 1))
        gain_one_grad = jnp.sum(grad_xn * unit_one, axis=0)
        grad_unit = grad_xn * gains[0][None, :]
        tokens_grad = dh1 + inverse_one * (
            grad_unit - unit_one * jnp.mean(grad_unit * unit_one, axis=1, keepdims=True)
        )
        qkv_term = rows_grad(xn, dqkv)

        gains_of = jnp.stack([gain_one_grad, gain_two_grad]).reshape(2, chips, 2, shard)
        other = lax.dynamic_index_in_dim(gains_of, 1 - core, 2, keepdims=False)
        mine = lax.dynamic_index_in_dim(gains_of, core, 2, keepdims=False)
        gains_of = (mine + swap(other, 1)).transpose(1, 0, 2).reshape(chips, 1, 2 * shard)
        gains_of = jnp.pad(gains_of.astype(BF), ((0, 0), (0, 15), (0, 0)))
        wide, down_sum, out_term, qkv_term, outs[0], sent = lax.optimization_barrier(
            (wide, down_sum, out_term, qkv_term, outs[0], sent)
        )
        gu_sum, out_sum, qkv_sum, gain_sum = finish(
            nf, nc, wide, [out_term, qkv_term, gains_of]
        )
        h1, gain_sum = lax.optimization_barrier((h1, gain_sum))
        branch = h1 + outs[0].astype(F32)
        for k in range(1, chips):
            branch = branch + swap(sent[k - 1], 2 * k).astype(F32)
        layer_out = branch.astype(BF)
        qkv_sum = qkv_sum.astype(F32)
        gain_sum = gain_sum[0].reshape(2, shard).astype(F32)
        gate_grad, up_grad = place_columns(order, gu_sum)
        query_width = HEADS * HEAD_DIM
        return (
            layer_out.reshape(1, rows, width),
            tokens_grad.reshape(1, rows, width),
            gain_sum[0],
            qkv_sum[:, :query_width],
            qkv_sum[:, query_width : query_width + key_width],
            qkv_sum[:, query_width + key_width :],
            out_sum.astype(F32),
            gain_sum[1],
            gate_grad,
            up_grad,
            down_sum.astype(F32),
        )

    weight = P("fsdp", None)
    activation = P("fsdp", "ctx", None)
    return jax.shard_map(
        shards,
        mesh=mesh,
        in_specs=(
            activation,
            P("fsdp"),
            weight,
            weight,
            weight,
            weight,
            P("fsdp"),
            weight,
            weight,
            weight,
            P(),
            P("fsdp", "ctx"),
            activation,
        ),
        out_specs=(
            activation,
            activation,
            P("fsdp"),
            weight,
            weight,
            weight,
            weight,
            P("fsdp"),
            weight,
            weight,
            weight,
        ),
        check_vma=False,
    )
```

```python
import functools

import jax
import jax.numpy as jnp
from jax import lax
from jax.experimental import pallas as pl
from jax.experimental.pallas import tpu as pltpu
from jax.sharding import PartitionSpec as P

HEADS = 32
KV_HEADS = 4
HEAD_DIM = 64
GROUP = HEADS // KV_HEADS
PAIRS = GROUP // 2
LANES = 2 * HEAD_DIM
STACK = PAIRS * LANES

EPS = 1e-05
THETA = 10000.0
NEG = -1e30
FLIGHT = 2
BF = jnp.bfloat16
F32 = jnp.float32


def dot(left, right, contract, out=F32):
    return lax.dot_general(
        left, right, ((contract[:1], contract[1:]), ((), ())), preferred_element_type=out
    )


def swap_halves(z):
    lane = lax.broadcasted_iota(jnp.int32, z.shape, 1)
    first = (lane % HEAD_DIM) < (HEAD_DIM // 2)
    return jnp.where(
        first,
        pltpu.roll(z, LANES - HEAD_DIM // 2, 1),
        pltpu.roll(z, HEAD_DIM // 2, 1),
    )


def split_heads(rows):
    lane = lax.broadcasted_iota(jnp.int32, rows.shape, 1)
    zero = jnp.zeros_like(rows)
    return jnp.concatenate(
        [jnp.where(lane < HEAD_DIM, rows, zero), jnp.where(lane >= HEAD_DIM, rows, zero)], axis=0
    )


def join_heads(columns):
    half = columns.shape[1] // 2
    sub = lax.broadcasted_iota(jnp.int32, (LANES, half), 0)
    return jnp.where(sub < HEAD_DIM, columns[:, :half], columns[:, half:]).T


def stack_pairs(ref, rows):
    return jnp.concatenate([ref[rows, p * LANES : (p + 1) * LANES] for p in range(PAIRS)], axis=0)


def two_blocks(ref, table, j, block):
    parts = [
        ref[pl.ds(pl.multiple_of(table[2 + 2 * j + i] * block, block), block), :] for i in range(2)
    ]
    return jnp.concatenate(parts, axis=0)


def causal(scores, j, own, block):
    key = lax.broadcasted_iota(jnp.int32, scores.shape, 0) + j * (2 * block)
    query = lax.broadcasted_iota(jnp.int32, scores.shape, 1) % block + own * block
    return jnp.where(key <= query, scores, NEG)


def head_twice(pair, group):
    wide = pair.astype(F32)
    lane = lax.broadcasted_iota(jnp.int32, wide.shape, 1)
    keep = (lane < HEAD_DIM) == (group % 2 == 0)
    return jnp.where(keep, wide, pltpu.roll(wide, HEAD_DIM, 1)).astype(BF)


def attention_forward_kernel(
    table,
    q_ref,
    cos_ref,
    sin_ref,
    k_pair,
    v_pair,
    qr_ref,
    o_ref,
    ob_ref,
    lse_ref,
    qm,
    m,
    l,
    acc,
    k_ref,
    v_ref,
):
    block = q_ref.shape[0] // 2
    group = pl.program_id(0)
    k_ref[...] = head_twice(k_pair[...], group)
    v_ref[...] = head_twice(v_pair[...], group)
    for h in range(2):
        rows = slice(h * block, (h + 1) * block)
        cosine, sine = cos_ref[rows, :], sin_ref[rows, :]
        for p in range(PAIRS):
            lanes = slice(p * LANES, (p + 1) * LANES)
            z = q_ref[rows, lanes]
            qr_ref[rows, lanes] = (z * cosine + swap_halves(z) * sine).astype(BF)
        scaled = stack_pairs(qr_ref, rows).astype(F32) * (HEAD_DIM**-0.5)
        qm[...] = split_heads(scaled).astype(BF)
        m[...] = jnp.full_like(m, NEG)
        l[...] = jnp.zeros_like(l)
        acc[...] = jnp.zeros_like(acc)
        own = table[h]

        def step(j, masked):
            keys = two_blocks(k_ref, table, j, block)
            values = two_blocks(v_ref, table, j, block)
            s = dot(keys, qm[...], (1, 1))
            if masked:
                s = causal(s, j, own, block)
            before = m[...]
            now = jnp.maximum(before, jnp.max(s, axis=0, keepdims=True))
            p = jnp.exp(s - now)
            decay = jnp.exp(before - now)
            l[...] = l[...] * decay + jnp.sum(p, axis=0, keepdims=True)
            acc[...] = acc[...] * decay + dot(values, p.astype(BF), (0, 0))
            m[...] = now

        last = own // 2

        @pl.loop(0, last)
        def _(j):
            step(j, False)

        step(last, True)
        lse_ref[0, h : h + 1, :] = m[...] + jnp.log(l[...])
        o = join_heads(acc[...] / l[...])
        for p in range(PAIRS):
            lanes = slice(p * LANES, (p + 1) * LANES)
            piece = o[p * block : (p + 1) * block, :]
            o_ref[rows, lanes] = piece
            ob_ref[rows, lanes] = piece.astype(BF)


def attention_forward(table, q, cosine, sine, kv):
    rows, length = q.shape[0], kv.shape[0]
    query_width = HEADS * HEAD_DIM
    columns = pl.BlockSpec((rows, STACK), lambda g, t: (0, g))
    whole = pl.BlockSpec((rows, LANES), lambda g, t: (0, 0))
    key_pair = pl.BlockSpec((length, LANES), lambda g, t: (0, g // 2))
    value_pair = pl.BlockSpec((length, LANES), lambda g, t: (0, KV_HEADS // 2 + g // 2))
    wide = GROUP * (rows // 2)
    return pl.pallas_call(
        attention_forward_kernel,
        grid_spec=pltpu.PrefetchScalarGridSpec(
            num_scalar_prefetch=1,
            grid=(KV_HEADS,),
            in_specs=[columns, whole, whole, key_pair, value_pair],
            out_specs=[
                columns,
                columns,
                columns,
                pl.BlockSpec((1, 2, wide), lambda g, t: (g, 0, 0)),
            ],
            scratch_shapes=[
                pltpu.VMEM((wide, LANES), BF),
                pltpu.VMEM((1, wide), F32),
                pltpu.VMEM((1, wide), F32),
                pltpu.VMEM((LANES, wide), F32),
                pltpu.VMEM((length, LANES), BF),
                pltpu.VMEM((length, LANES), BF),
            ],
        ),
        out_shape=[
            jax.ShapeDtypeStruct((rows, query_width), BF),
            jax.ShapeDtypeStruct((rows, query_width), F32),
            jax.ShapeDtypeStruct((rows, query_width), BF),
            jax.ShapeDtypeStruct((KV_HEADS, 2, wide), F32),
        ],
        compiler_params=pltpu.CompilerParams(vmem_limit_bytes=32 << 20),
        cost_estimate=pl.CostEstimate(
            flops=8 * HEADS * rows * length * HEAD_DIM,
            bytes_accessed=16 * rows * HEADS * HEAD_DIM,
            transcendentals=HEADS * rows * length,
        ),
        name="attention_forward",
    )(table, q, cosine, sine, kv, kv)


def attention_backward_kernel(
    table,
    qr_ref,
    do_ref,
    o_ref,
    lse_ref,
    k_pair,
    v_pair,
    cos_ref,
    sin_ref,
    dq_ref,
    dkv_ref,
    qm,
    dom,
    dqt,
    k_ref,
    v_ref,
    dk_ref,
    dv_ref,
):
    block = qr_ref.shape[0] // 2
    group = pl.program_id(0)
    k_ref[...] = head_twice(k_pair[...], group)
    v_ref[...] = head_twice(v_pair[...], group)
    dk_ref[...] = jnp.zeros_like(dk_ref)
    dv_ref[...] = jnp.zeros_like(dv_ref)
    for h in range(2):
        rows = slice(h * block, (h + 1) * block)
        scaled = stack_pairs(qr_ref, rows).astype(F32) * (HEAD_DIM**-0.5)
        qm[...] = split_heads(scaled).astype(BF)
        grads = stack_pairs(do_ref, rows).astype(F32)
        dom[...] = split_heads(grads).astype(BF)
        product = (grads * stack_pairs(o_ref, rows)).T
        inner = jnp.concatenate(
            [
                jnp.sum(product[:HEAD_DIM], axis=0, keepdims=True),
                jnp.sum(product[HEAD_DIM:], axis=0, keepdims=True),
            ],
            axis=1,
        )
        lse = lse_ref[0, h : h + 1, :]
        dqt[...] = jnp.zeros_like(dqt)
        own = table[h]

        def step(j, masked):
            keys = two_blocks(k_ref, table, j, block)
            values = two_blocks(v_ref, table, j, block)
            s = dot(keys, qm[...], (1, 1))
            if masked:
                s = causal(s, j, own, block)
            p = jnp.exp(s - lse)
            dp = dot(values, dom[...], (1, 1))
            ds = (p * (dp - inner)).astype(BF)
            dv = dot(p.astype(BF), dom[...], (1, 0))
            dk = dot(ds, qm[...], (1, 0))
            dqt[...] += dot(keys, ds, (0, 0))
            for i in range(2):
                at = pl.ds(pl.multiple_of(table[2 + 2 * j + i] * block, block), block)
                dk_ref[at, :] += dk[i * block : (i + 1) * block]
                dv_ref[at, :] += dv[i * block : (i + 1) * block]

        last = own // 2

        @pl.loop(0, last)
        def _(j):
            step(j, False)

        step(last, True)
        cosine, sine = cos_ref[rows, :], sin_ref[rows, :]
        dq = join_heads(dqt[...] * (HEAD_DIM**-0.5))
        for p in range(PAIRS):
            z = dq[p * block : (p + 1) * block, :]
            dq_ref[rows, p * LANES : (p + 1) * LANES] = (
                z * cosine - swap_halves(z) * sine
            ).astype(BF)
    lane = lax.broadcasted_iota(jnp.int32, dk_ref.shape, 1)
    keep = (lane < HEAD_DIM) == (group % 2 == 0)
    for i, ref in enumerate((dk_ref, dv_ref)):
        both = ref[...] + pltpu.roll(ref[...], HEAD_DIM, 1)
        dkv_ref[i] = jnp.where(keep, both, dkv_ref[i].astype(F32)).astype(BF)


def attention_backward(table, qr, grads, o, lse, kv, cosine, sine):
    rows, length = qr.shape[0], kv.shape[0]
    columns = pl.BlockSpec((rows, STACK), lambda g, t: (0, g))
    whole = pl.BlockSpec((rows, LANES), lambda g, t: (0, 0))
    key_pair = pl.BlockSpec((length, LANES), lambda g, t: (0, g // 2))
    value_pair = pl.BlockSpec((length, LANES), lambda g, t: (0, KV_HEADS // 2 + g // 2))
    wide = GROUP * (rows // 2)
    return pl.pallas_call(
        attention_backward_kernel,
        grid_spec=pltpu.PrefetchScalarGridSpec(
            num_scalar_prefetch=1,
            grid=(KV_HEADS,),
            in_specs=[
                columns,
                columns,
                columns,
                pl.BlockSpec((1, 2, wide), lambda g, t: (g, 0, 0)),
                key_pair,
                value_pair,
                whole,
                whole,
            ],
            out_specs=[columns, pl.BlockSpec((2, length, LANES), lambda g, t: (0, 0, g // 2))],
            scratch_shapes=[
                pltpu.VMEM((wide, LANES), BF),
                pltpu.VMEM((wide, LANES), BF),
                pltpu.VMEM((LANES, wide), F32),
                pltpu.VMEM((length, LANES), BF),
                pltpu.VMEM((length, LANES), BF),
                pltpu.VMEM((length, LANES), F32),
                pltpu.VMEM((length, LANES), F32),
            ],
        ),
        out_shape=[
            jax.ShapeDtypeStruct(qr.shape, BF),
            jax.ShapeDtypeStruct((2, length, KV_HEADS * HEAD_DIM), BF),
        ],
        compiler_params=pltpu.CompilerParams(vmem_limit_bytes=32 << 20),
        cost_estimate=pl.CostEstimate(
            flops=20 * HEADS * rows * length * HEAD_DIM,
            bytes_accessed=16 * rows * HEADS * HEAD_DIM,
            transcendentals=HEADS * rows * length,
        ),
        name="attention_backward",
    )(table, qr, grads, o, lse, kv, kv, cosine, sine)


def own_key_grads_kernel(nc, dkv_ref, cos_ref, sin_ref, out_ref, got, send_sem, recv_sem):
    rows, width = out_ref.shape[0], out_ref.shape[1] // 2
    here = lax.axis_index("ctx")
    mesh_id = pl.DeviceIdType.MESH
    barrier = pltpu.get_barrier_semaphore()
    for k in range(1, nc):
        pl.semaphore_signal(barrier, inc=1, device_id={"ctx": here ^ k}, device_id_type=mesh_id)
    pl.semaphore_wait(barrier, nc - 1)

    def copy(k):
        source = dkv_ref.at[:, pl.ds(k * rows, rows)]
        if k == 0:
            return pltpu.make_async_copy(source, got.at[0], recv_sem.at[0])
        return pltpu.make_async_remote_copy(
            src_ref=source,
            dst_ref=got.at[k],
            send_sem=send_sem.at[k],
            recv_sem=recv_sem.at[k],
            device_id={"ctx": here ^ k},
            device_id_type=mesh_id,
        )

    for k in reversed(range(nc)):
        copy(k).start()
    for k in range(nc):
        copy(k).wait()

    def total(i, lanes):
        return sum(got[k, i, :, lanes].astype(F32) for k in range(nc))

    for p in range(width // LANES):
        lanes = slice(p * LANES, (p + 1) * LANES)
        z = total(0, lanes)
        out_ref[:, lanes] = (z * cos_ref[...] - swap_halves(z) * sin_ref[...]).astype(BF)
        out_ref[:, width + p * LANES : width + (p + 1) * LANES] = total(1, lanes).astype(BF)


def own_key_grads(nc, dkv, cosine, sine):
    rows, width = dkv.shape[1] // nc, dkv.shape[2]
    vmem = pl.BlockSpec(memory_space=pltpu.VMEM)
    return pl.pallas_call(
        functools.partial(own_key_grads_kernel, nc),
        in_specs=[pl.BlockSpec(memory_space=pl.ANY), vmem, vmem],
        out_specs=vmem,
        out_shape=jax.ShapeDtypeStruct((rows, 2 * width), BF),
        scratch_shapes=[
            pltpu.VMEM((nc, 2, rows, width), BF),
            pltpu.SemaphoreType.DMA((nc,)),
            pltpu.SemaphoreType.DMA((nc,)),
        ],
        compiler_params=pltpu.CompilerParams(collective_id=2, has_side_effects=True),
        name="own_key_grads",
    )(dkv, cosine, sine)


def share_kernel(nf, nc, low, size, raw, *refs):
    count = 2 if raw else 1
    w_query, w_key, w_value, w_out, *halves, down, gains, tokens, cosine, sine = refs[: 9 + count]
    refs = refs[9 + count :]
    query, key_value, out, wide, downs, all_gains, kv_all = refs[:7]
    query_own, key_value_own, out_own, wide_own, down_own, gains_own = refs[7:13]
    (local, plane_send, plane_recv, along_send, along_recv, core_send, core_recv) = refs[13:20]
    (gain_send, gain_recv, down_sem, gather_send, gather_recv, gather_core) = refs[20:26]
    w_kv, gains_v, xn, kv, kv_load, kv_send, kv_recv = refs[26:]
    chips = nf // 2
    place, here = lax.axis_index("fsdp"), lax.axis_index("ctx")
    chip, core = place // 2, place % 2
    mesh_id = pl.DeviceIdType.MESH
    shard, columns = wide.shape[1:]
    part = columns // 2
    key_width = w_key.shape[1]
    gathered = [
        (w_query, query, query_own, pl.ds(0, w_query.shape[1])),
        (w_key, key_value, key_value_own, pl.ds(0, key_width)),
        (w_value, key_value, key_value_own, pl.ds(key_width, key_width)),
        (w_out, out, out_own, pl.ds(0, w_out.shape[1])),
    ]

    barrier = pltpu.get_barrier_semaphore()

    def greet(target):
        pl.semaphore_signal(barrier, inc=1, device_id=target, device_id_type=mesh_id)

    for j in range(1, nf):
        greet({"fsdp": place ^ j})
    for pos in range(nc):

        @pl.when(here == pos)
        def _():
            for i in range(nc):
                if i != pos:
                    greet({"ctx": i})

    pl.semaphore_wait(barrier, nf - 1 + nc - 1)

    def remote(source, target, sends, recvs, where):
        return pltpu.make_async_remote_copy(
            src_ref=source,
            dst_ref=target,
            send_sem=sends,
            recv_sem=recvs,
            device_id=where,
            device_id_type=mesh_id,
        )

    def piece(k, h, rows):
        if raw:
            at = pl.ds(pl.multiple_of((chip ^ k) * part, 128), part)
            return halves[h].at[rows, at]
        return halves[0].at[k, rows]

    def side(h):
        return pl.ds(h * part, part) if raw else pl.ds(0, columns)

    def rows_of(share):
        return pl.ds(low + share * size, size)

    def plane_copy(k, kind, h):
        rows = rows_of(here) if kind else pl.ds(0, low)
        return remote(
            piece(k, h, rows),
            wide.at[place, rows, side(h)],
            plane_send.at[kind, k, h],
            plane_recv.at[kind, k, h],
            {"fsdp": place ^ (2 * k)},
        )

    def along_copy(k, share, up, target):
        block = wide.at[place ^ (2 * k), rows_of(share)]
        return remote(
            block, block, along_send.at[up, share, k], along_recv.at[share, k], {"ctx": target}
        )

    def core_copy(k, share):
        rows = rows_of(share) if share < nc else pl.ds(0, low)
        block = wide.at[place ^ (2 * k), rows]
        return remote(
            block, block, core_send.at[k, share], core_recv.at[k, share], {"fsdp": place ^ 1}
        )

    def own_core_copy(h):
        return remote(
            piece(0, h, pl.ds(0, shard)),
            wide.at[place, :, side(h)],
            core_send.at[0, h],
            core_recv.at[0, h],
            {"fsdp": place ^ 1},
        )

    half = shard // 2
    relayed = chips == 4

    def gather_copy(u, k, relay=0):
        source, target, _, at = gathered[u]
        if relay:
            owner, rows = place ^ (2 * (3 - k)), pl.ds((2 - k) * half, half)
            source = target.at[owner, rows, at]
        else:
            owner, rows = place, pl.ds(0, shard)
        number = 2 * k + relay
        return remote(
            source,
            target.at[owner, rows, at],
            gather_send.at[u, number],
            gather_recv.at[u, number],
            {"fsdp": place ^ (2 * k)},
        )

    def gather_core_copy(u, k):
        source, target, _, at = gathered[u]
        block = target.at[place ^ (2 * k), :, at]
        return remote(
            block if k else source,
            block,
            gather_core.at[0, u, k],
            gather_core.at[1, u, k],
            {"fsdp": place ^ 1},
        )

    def down_copy():
        return remote(down, downs.at[core], down_sem.at[0], down_sem.at[1], {"fsdp": place ^ 1})

    def gain_copy(j):
        return remote(
            gains, all_gains.at[place], gain_send.at[j], gain_recv.at[j], {"fsdp": place ^ j}
        )

    direct = (1, 2) if relayed else tuple(range(1, chips))
    for k in range(1, chips):
        for h in range(count):
            plane_copy(k, 1, h).start()
    for j in range(1, nf):
        gain_copy(j).start()
    for h in range(count):
        own_core_copy(h).start()
    for u in range(4):
        gather_core_copy(u, 0).start()
    down_copy().start()
    own = [(source, stage.at[:, at], None) for source, _, stage, at in gathered]
    own += [(piece(0, h, pl.ds(0, shard)), wide_own.at[:, side(h)], None) for h in range(count)]
    own += [(down, down_own, downs.at[core]), (gains, gains_own, all_gains.at[place])]
    back = [
        (query_own, query.at[place]),
        (key_value_own, key_value.at[place]),
        (out_own, out.at[place]),
        (wide_own, wide.at[place]),
        (down_own, downs.at[core]),
        (gains_own, all_gains.at[place]),
    ]
    for i, (source, stage, _) in enumerate(own):
        pltpu.make_async_copy(source, stage, local.at[0, i]).start()
    for i, (source, stage, _) in enumerate(own):
        pltpu.make_async_copy(source, stage, local.at[0, i]).wait()
    for i, (stage, target) in enumerate(back):
        pltpu.make_async_copy(stage, target, local.at[1, i]).start()

    for k in range(1, chips):
        for h in range(count):
            plane_copy(k, 1, h).wait_send()
    for u in (1, 2, 0, 3):
        for k in direct:
            gather_copy(u, k).start()

    def kv_copy(k):
        if k == 0:
            return pltpu.make_async_copy(kv, kv_all.at[0], kv_recv.at[0])
        return remote(kv, kv_all.at[k], kv_send.at[k], kv_recv.at[k], {"ctx": here ^ k})

    def make_kv():
        for i in (len(back) - 1, 1):
            stage, target = back[i]
            pltpu.make_async_copy(stage, target, local.at[1, i]).wait()
        for j in range(1, nf):
            gain_copy(j).wait_recv()
        for u in (1, 2):
            if relayed:
                for k in direct:
                    gather_copy(u, k, 1).wait_recv()
                gather_core_copy(u, 3).start()
            for k in range(chips):
                gather_core_copy(u, k).wait_recv()
        loads = [
            pltpu.make_async_copy(key_value, w_kv, kv_load.at[0]),
            pltpu.make_async_copy(all_gains, gains_v, kv_load.at[1]),
        ]
        for copy in loads:
            copy.start()
        for copy in loads:
            copy.wait()
        for i in range(0, xn.shape[0], 16):
            x = tokens[i : i + 16, :].astype(F32)
            unit = x * lax.rsqrt(jnp.mean(x * x, axis=1, keepdims=True) + EPS)
            for f in range(nf):
                lanes = slice(f * shard, (f + 1) * shard)
                gain = gains_v[f, 0:1, :].astype(F32)
                xn[i : i + 16, lanes] = (unit[:, lanes] * gain).astype(BF)
        total = sum(
            dot(xn[:, f * shard : (f + 1) * shard], w_kv[f], (1, 0)) for f in range(nf)
        )
        for p in range(0, key_width, LANES):
            z = total[:, p : p + LANES]
            kv[:, p : p + LANES] = (z * cosine[...] + swap_halves(z) * sine[...]).astype(BF)
        kv[:, key_width:] = total[:, key_width:].astype(BF)
        for k in reversed(range(nc)):
            kv_copy(k).start()

    for pos in range(nc):

        @pl.when(here == pos)
        def _():
            def pass_on(k, share):
                if share <= pos < nc - 1:
                    along_copy(k, share, 1, pos + 1).start()
                if share >= pos > 0:
                    along_copy(k, share, 0, pos - 1).start()
                core_copy(k, share).start()

            for k in range(1, chips):
                for h in range(count):
                    plane_copy(k, 1, h).wait_recv()
                pass_on(k, pos)
            if low:
                for k in range(1, chips):
                    for h in range(count):
                        plane_copy(k, 0, h).start()
            def gather_on(u):
                for k in direct:
                    gather_copy(u, k).wait_recv()
                    if relayed:
                        gather_copy(u, 3 - k, 1).start()
                    gather_core_copy(u, k).start()

            groups = [(), (1, 2), (0, 3)]
            for d in range(1, max(nc, len(groups))):
                for share in (pos - d, pos + d):
                    if 0 <= share < nc:
                        for k in range(1, chips):
                            along_copy(k, share, 0, 0).wait_recv()
                            pass_on(k, share)
                for u in groups[d] if d < len(groups) else ():
                    if u == 3:
                        make_kv()
                    gather_on(u)
            if low:
                for k in range(1, chips):
                    for h in range(count):
                        plane_copy(k, 0, h).wait_recv()
                    core_copy(k, nc).start()
            if relayed:
                for u in (0, 3):
                    for k in direct:
                        gather_copy(u, k, 1).wait_recv()
                    gather_core_copy(u, 3).start()
            for k in range(1, chips):
                for share in range(nc):
                    if share <= pos < nc - 1:
                        along_copy(k, share, 1, pos + 1).wait_send()
                    if share >= pos > 0:
                        along_copy(k, share, 0, pos - 1).wait_send()

    for h in range(count):
        own_core_copy(h).wait()
    for k in range(1, chips):
        for share in range(nc + 1 if low else nc):
            core_copy(k, share).wait()
        if low:
            for h in range(count):
                plane_copy(k, 0, h).wait_send()
    for j in range(1, nf):
        gain_copy(j).wait_send()
    for k in range(nc):
        kv_copy(k).wait()
    for u in range(4):
        for k in direct:
            gather_copy(u, k).wait_send()
            if relayed:
                gather_copy(u, k, 1).wait_send()
        for k in range(chips):
            gather_core_copy(u, k).wait_send()
            if u in (0, 3):
                gather_core_copy(u, k).wait_recv()
    down_copy().wait()
    for i, (stage, target) in enumerate(back):
        if i not in (len(back) - 1, 1):
            pltpu.make_async_copy(stage, target, local.at[1, i]).wait()


def share_weights(
    nf,
    nc,
    w_query,
    w_key,
    w_value,
    w_out,
    w_gate,
    w_up,
    order,
    down,
    gains,
    tokens,
    cosine,
    sine,
):
    chips = nf // 2
    shard, hidden = w_gate.shape
    part = hidden // chips
    size = shard // nc
    low = shard - nc * size
    raw = part % 128 == 0
    halves = [w_gate, w_up]
    if not raw:
        both = [w.reshape(shard, chips, part).transpose(1, 0, 2) for w in halves]
        halves = [jnp.take(jnp.concatenate(both, axis=2), order, axis=0)]
    anywhere = pl.BlockSpec(memory_space=pl.ANY)
    dma = pltpu.SemaphoreType.DMA
    kv_shape = (tokens.shape[0], 2 * w_key.shape[1])
    widths = [w_query.shape[1], 2 * w_key.shape[1], w_out.shape[1], 2 * part]
    return pl.pallas_call(
        functools.partial(share_kernel, nf, nc, low, size, raw),
        in_specs=[anywhere] * (6 + len(halves)) + [pl.BlockSpec(memory_space=pltpu.VMEM)] * 3,
        out_specs=[anywhere] * 7,
        out_shape=[jax.ShapeDtypeStruct((nf, shard, width), BF) for width in widths]
        + [
            jax.ShapeDtypeStruct((2,) + down.shape, BF),
            jax.ShapeDtypeStruct((nf,) + gains.shape, BF),
            jax.ShapeDtypeStruct((nc,) + kv_shape, BF),
        ],
        scratch_shapes=[pltpu.VMEM((shard, width), BF) for width in widths]
        + [
            pltpu.VMEM(down.shape, BF),
            pltpu.VMEM(gains.shape, BF),
            dma((2, 8)),
            dma((2, chips, 2)),
            dma((2, chips, 2)),
            dma((2, nc, chips)),
            dma((nc, chips)),
            dma((chips, nc + 1)),
            dma((chips, nc + 1)),
            dma((nf,)),
            dma((nf,)),
            dma((2,)),
            dma((4, 2 * chips)),
            dma((4, 2 * chips)),
            dma((2, 4, chips)),
            pltpu.VMEM((nf, shard, widths[1]), BF),
            pltpu.VMEM((nf,) + gains.shape, BF),
            pltpu.VMEM(tokens.shape, BF),
            pltpu.VMEM(kv_shape, BF),
            dma((2,)),
            dma((nc,)),
            dma((nc,)),
        ],
        compiler_params=pltpu.CompilerParams(
            collective_id=1, has_side_effects=True, vmem_limit_bytes=56 << 20
        ),
        name="share_weights",
    )(w_query, w_key, w_value, w_out, *halves, down, gains, tokens, cosine, sine)


def place_columns_kernel(order, both_ref, gate_ref, up_ref):
    part = gate_ref.shape[1]
    gate_ref[...] = both_ref[0, :, :part].astype(F32)
    up_ref[...] = both_ref[0, :, part:].astype(F32)


def place_columns(order, both):
    parts, shard, part = both.shape[0], both.shape[1], both.shape[2] // 2
    out = jax.ShapeDtypeStruct((shard, parts * part), F32)
    if part % 128:
        both = jnp.take(both, order, axis=0).transpose(1, 0, 2).astype(F32)
        return [both[:, :, i * part : (i + 1) * part].reshape(out.shape) for i in range(2)]
    columns = pl.BlockSpec((shard, part), lambda k, t: (0, t[k]))
    return pl.pallas_call(
        place_columns_kernel,
        grid_spec=pltpu.PrefetchScalarGridSpec(
            num_scalar_prefetch=1,
            grid=(parts,),
            in_specs=[pl.BlockSpec((1, shard, 2 * part), lambda k, t: (k, 0, 0))],
            out_specs=[columns, columns],
        ),
        out_shape=[out, out],
        name="place_columns",
    )(order, both)


def feed_forward_kernel(nf, *refs):
    chips = nf // 2
    hn, *gbs, w_gu, w_d, grad, left, right, downs, outs = refs[: chips + 8]
    w_gu_v, w_d_v, hn_v, gb_v, dact_v, act_v, dgu_v, sent, got, outs_v = refs[chips + 8 : chips + 18]
    tiles, halves, half_sem, *sems = refs[chips + 18 :]
    load, load_gb, hn_send, hn_recv, dhn_send, dhn_recv, store = sems[:7]
    left_local, left_send, left_recv, right_local, right_send, right_recv = sems[7:13]
    down_local, down_send, down_recv = sems[13:]
    place = lax.axis_index("fsdp")
    core = place % 2
    rows, width = hn.shape
    part = w_d.shape[0]
    shard = width // nf
    half = rows // 2
    relayed = chips == 4
    direct = (1, 2) if relayed else tuple(range(1, chips))
    mesh_id = pl.DeviceIdType.MESH

    barrier = pltpu.get_barrier_semaphore()
    for j in [1] + [2 * k for k in range(1, chips)]:
        pl.semaphore_signal(
            barrier, inc=1, device_id={"fsdp": place ^ j}, device_id_type=mesh_id
        )
    pl.semaphore_wait(barrier, chips)

    def remote(source, target, sends, recvs, step):
        return pltpu.make_async_remote_copy(
            src_ref=source,
            dst_ref=target,
            send_sem=sends,
            recv_sem=recvs,
            device_id={"fsdp": place ^ step},
            device_id_type=mesh_id,
        )

    def hn_copy(k, relay=0):
        at = 2 * k + relay
        if relay:
            lines = pl.ds((2 - k) * half, half)
            source, target = hn_v.at[3 - k, lines], hn_v.at[3, lines]
        else:
            source, target = hn, hn_v.at[k]
        return remote(source, target, hn_send.at[at], hn_recv.at[at], 2 * k)

    def dhn_copy(k):
        return remote(sent.at[k - 1], got.at[k - 1], dhn_send.at[k], dhn_recv.at[k], 2 * k)

    def half_copy(k):
        lines = pl.ds((k - 1) * half, half)
        return remote(
            sent.at[2, lines], halves.at[k - 1], half_sem.at[0, k], half_sem.at[1, k], 2 * k
        )

    def left_copy(k, j, other):
        number = 1 - core if other else core
        columns = pl.ds(pl.multiple_of((2 * j + number) * shard, shard), shard)
        source = hn_v.at[k, :, columns]
        target = left.at[other, k, :, pl.ds(j * shard, shard)]
        if other:
            return remote(source, target, left_send.at[k, j], left_recv.at[k, j], 1)
        return pltpu.make_async_copy(source, target, left_local.at[k, j])

    def right_copy(k, other):
        if other:
            return remote(dgu_v.at[k], right.at[1, k], right_send.at[k], right_recv.at[k], 1)
        return pltpu.make_async_copy(dgu_v.at[k], right.at[0, k], right_local.at[k])

    loads = [
        pltpu.make_async_copy(w_d, w_d_v, load.at[0]),
        pltpu.make_async_copy(hn, hn_v.at[0], load.at[1]),
        pltpu.make_async_copy(w_gu, w_gu_v, load.at[2]),
    ]
    gb_loads = [
        pltpu.make_async_copy(gb, gb_v.at[k], load_gb.at[k]) for k, gb in enumerate(gbs)
    ]
    store_outs = pltpu.make_async_copy(outs_v, outs, store.at[0])
    for k in direct:
        hn_copy(k).start()
    for copy in loads[:1] + gb_loads + loads[1:]:
        copy.start()

    for copy in loads[:1] + gb_loads:
        copy.wait()

    def dact_tile(start, size):
        tile = w_d_v[pl.ds(start, size), :]
        for k in range(chips):
            dact_v[k, :, pl.ds(start, size)] = dot(gb_v[k], tile, (1, 1))

    @pl.loop(0, part // 256)
    def _(i):
        dact_tile(pl.multiple_of(i * 256, 256), 256)

    if part % 256:
        dact_tile(part - 128, 128)

    def forward(k):
        for j in range(chips):
            left_copy(k, j, 1).start()
            left_copy(k, j, 0).start()

        def tile(start, size):
            one, two = pl.ds(start, size), pl.ds(pl.multiple_of(part + start, 128), size)
            gate = dot(hn_v[k], w_gu_v[:, one], (1, 0))
            up = dot(hn_v[k], w_gu_v[:, two], (1, 0))
            dact = dact_v[k, :, one]
            sg = jax.nn.sigmoid(gate)
            silu = gate * sg
            act_v[k, :, one] = (silu * up).astype(BF)
            dgu_v[k, :, one] = (dact * up * sg * (1.0 + gate * (1.0 - sg))).astype(BF)
            dgu_v[k, :, two] = (dact * silu).astype(BF)

        @pl.loop(0, part // 256)
        def _(i):
            tile(pl.multiple_of(i * 256, 256), 256)

        if part % 256:
            tile(part - 128, 128)

        right_copy(k, 1).start()
        right_copy(k, 0).start()

    def backward(k):
        @pl.loop(0, width // 256)
        def _(i):
            lines = pl.ds(pl.multiple_of(i * 256, 256), 256)
            dhn = dot(dgu_v[k], w_gu_v[lines, :], (1, 1))
            if k:
                sent[k - 1, :, lines] = dhn.astype(BF)
            else:
                grad[:, lines] = dhn

    for copy in loads[1:]:
        copy.wait()
    forward(0)
    for k in direct:
        hn_copy(k).wait_recv()
        if relayed:
            hn_copy(3 - k, 1).start()
    if relayed:
        forward(1)
        forward(2)
        for i in direct:
            hn_copy(i, 1).wait_recv()
        forward(3)
        backward(3)
        for k in direct:
            half_copy(k).start()
        backward(1)
        backward(2)
        for k in direct:
            half_copy(k).wait_recv()

            @pl.loop(0, half // 16)
            def _(i):
                lines = pl.ds(pl.multiple_of(i * 16, 16), 16)
                into = pl.ds(pl.multiple_of((k - 1) * half + i * 16, 16), 16)
                total = sent[2 - k, into, :].astype(F32) + halves[k - 1, lines, :].astype(F32)
                sent[2 - k, into, :] = total.astype(BF)

            dhn_copy(3 - k).start()
    else:
        for k in range(1, chips):
            forward(k)
            backward(k)
            dhn_copy(k).start()
    backward(0)

    @pl.loop(0, width // 256)
    def _(i):
        columns = pl.ds(pl.multiple_of(i * 256, 256), 256)
        for k in range(chips):
            outs_v[k, :, columns] = dot(act_v[k], w_d_v[:, columns], (1, 0)).astype(BF)

    store_outs.start()

    lower = part // 2
    spans = []
    for start in range(0, part, 128):
        cuts = sorted({start, min(max(lower, start), start + 128), start + 128})
        spans += [(start, a, b) for a, b in zip(cuts, cuts[1:])]

    def span_copies(n):
        start, a, b = spans[n]
        number = int(a >= lower)
        source = tiles.at[(start // 128) % 2, pl.ds(a - start, b - a)]
        at = pl.ds(a - number * lower, b - a)

        def keep():
            return pltpu.make_async_copy(source, downs.at[0, at], down_local.at[n])

        def send():
            return remote(source, downs.at[1, at], down_send.at[n], down_recv.at[n], 1)

        return number, keep, send

    def each_span(chosen, go):
        for n in chosen:
            number, keep, send = span_copies(n)

            @pl.when(core == number)
            def _():
                keep().start() if go else keep().wait()

            @pl.when(core != number)
            def _():
                send().start() if go else send().wait_send()

    for start in range(0, part, 128):
        before = [n for n, span in enumerate(spans) if span[0] == start - 256]
        each_span(before, False)
        tile = sum(
            dot(act_v[k, :, start : start + 128], gb_v[k], (0, 0)) for k in range(chips)
        )
        tiles[(start // 128) % 2] = tile.astype(BF)
        each_span([n for n, span in enumerate(spans) if span[0] == start], True)
    each_span([n for n, span in enumerate(spans) if span[0] >= part - 256], False)
    for n in range(len(spans)):
        number, _, send = span_copies(n)

        @pl.when(core == number)
        def _():
            send().wait_recv()

    for k in direct:
        dhn_copy(k).wait_recv()

    @pl.loop(0, rows // 16)
    def _(i):
        lines = pl.ds(pl.multiple_of(i * 16, 16), 16)
        grad[lines, :] += sum(got[k - 1, lines, :].astype(F32) for k in direct)

    store_outs.wait()
    for k in range(chips):
        for j in range(chips):
            left_copy(k, j, 0).wait()
            left_copy(k, j, 1).wait()
        right_copy(k, 0).wait()
        right_copy(k, 1).wait()
    for k in direct:
        dhn_copy(k).wait_send()
        hn_copy(k).wait_send()
        if relayed:
            half_copy(k).wait_send()
            hn_copy(k, 1).wait_send()


def feed_forward(nf, hn, gbs, w_gu, w_d):
    chips = nf // 2
    rows, width = hn.shape
    part = w_d.shape[0]
    anywhere = pl.BlockSpec(memory_space=pl.ANY)
    dma = pltpu.SemaphoreType.DMA
    shape = jax.ShapeDtypeStruct
    return pl.pallas_call(
        functools.partial(feed_forward_kernel, nf),
        in_specs=[anywhere] * (chips + 3),
        out_specs=[pl.BlockSpec(memory_space=pltpu.VMEM)] + [anywhere] * 4,
        out_shape=[
            shape((rows, width), F32),
            shape((2, chips, rows, width // 2), BF),
            shape((2, chips, rows, 2 * part), BF),
            shape((2, part // 2, width), BF),
            shape((chips, rows, width), BF),
        ],
        scratch_shapes=[
            pltpu.VMEM((width, 2 * part), BF),
            pltpu.VMEM((part, width), BF),
            pltpu.VMEM((chips, rows, width), BF),
            pltpu.VMEM((chips, rows, width), BF),
            pltpu.VMEM((chips, rows, part), F32),
            pltpu.VMEM((chips, rows, part), BF),
            pltpu.VMEM((chips, rows, 2 * part), BF),
            pltpu.VMEM((chips - 1, rows, width), BF),
            pltpu.VMEM((chips - 1, rows, width), BF),
            pltpu.VMEM((chips, rows, width), BF),
            pltpu.VMEM((2, 128, width), BF),
            pltpu.VMEM((2, rows // 2, width), BF),
            dma((2, chips)),
            dma((3,)),
            dma((chips,)),
            dma((2 * chips,)),
            dma((2 * chips,)),
            dma((chips,)),
            dma((chips,)),
            dma((1,)),
            dma((chips, chips)),
            dma((chips, chips)),
            dma((chips, chips)),
            dma((chips,)),
            dma((chips,)),
            dma((chips,)),
            dma((part // 128 + 1,)),
            dma((part // 128 + 1,)),
            dma((part // 128 + 1,)),
        ],
        compiler_params=pltpu.CompilerParams(
            collective_id=3, has_side_effects=True, vmem_limit_bytes=60 << 20
        ),
        cost_estimate=pl.CostEstimate(
            flops=12 * chips * rows * width * part,
            bytes_accessed=40_000_000,
            transcendentals=chips * rows * part,
        ),
        name="feed_forward",
    )(hn, *gbs, w_gu, w_d)


def chunk_rows(rows):
    return max(r for r in range(16, 33, 16) if rows % r == 0)


def finish_kernel(nf, nc, *refs):
    pieces, refs = refs[: nf // 2], refs[nf // 2 - 1 :]
    sources, (outs, owns, ins, xs) = refs[:4], (refs[i : i + 4] for i in range(4, 20, 4))
    plane_send, plane_recv, local, in_sem, x_sem, first_send, second_send, out_sem = refs[20:]
    chips = nf // 2
    place, here = lax.axis_index("fsdp"), lax.axis_index("ctx")
    chip = place // 2
    lower = here < nc // 2
    depth = jnp.where(lower, here, nc - 1 - here)
    inner = jnp.where(lower, here + 1, here - 1)
    outer = jnp.where(lower, here - 1, here + 1)
    mesh_id = pl.DeviceIdType.MESH

    barrier = pltpu.get_barrier_semaphore()
    for k in range(1, chips):
        pl.semaphore_signal(
            barrier, inc=1, device_id={"fsdp": place ^ (2 * k)}, device_id_type=mesh_id
        )
    pl.semaphore_signal(barrier, inc=1, device_id={"ctx": inner}, device_id_type=mesh_id)

    @pl.when(depth > 0)
    def _():
        pl.semaphore_signal(barrier, inc=1, device_id={"ctx": outer}, device_id_type=mesh_id)
        pl.semaphore_wait(barrier, chips + 1)

    @pl.when(depth == 0)
    def _():
        pl.semaphore_wait(barrier, chips)

    def plane_copy(u, k):
        return pltpu.make_async_remote_copy(
            src_ref=sources[u].at[chip ^ k],
            dst_ref=owns[u].at[k],
            send_sem=plane_send.at[u, k],
            recv_sem=plane_recv.at[u, k],
            device_id={"fsdp": place ^ (2 * k)},
            device_id_type=mesh_id,
        )

    def local_copy(u, k):
        source = sources[u].at[chip] if u else pieces[k]
        return pltpu.make_async_copy(source, owns[u].at[k], local.at[u, k])

    for u in range(4):
        for k in range(chips):
            if u == 0 or k == 0:
                local_copy(u, k).start()
            else:
                plane_copy(u, k).start()

    units = [(0, k) for k in range(chips)] + [(u, None) for u in (1, 2, 3)]
    chunks = []
    for u, k in units:
        total = outs[u].shape[-2]
        size = chunk_rows(total)
        chunks += [(u, k, r, size) for r in range(0, total, size)]

    def views(c):
        u, k, r, size = chunks[c]
        rows = pl.ds(r, size)
        return [owns[u].at[k or 0, rows]] + [
            ref.at[rows] if k is None else ref.at[k, rows] for ref in (ins[u], xs[u], outs[u])
        ]

    def first_copy(c, across):
        own, arriving, x, _ = views(c)
        return pltpu.make_async_remote_copy(
            src_ref=own,
            dst_ref=x if across else arriving,
            send_sem=first_send.at[c],
            recv_sem=(x_sem if across else in_sem).at[c],
            device_id={"ctx": inner},
            device_id_type=mesh_id,
        )

    def second_copy(c, across):
        _, arriving, x, _ = views(c)
        return pltpu.make_async_remote_copy(
            src_ref=arriving if across else x,
            dst_ref=x,
            send_sem=second_send.at[c],
            recv_sem=x_sem.at[c],
            device_id={"ctx": outer},
            device_id_type=mesh_id,
        )

    def out_copy(c, across):
        _, arriving, x, out = views(c)
        return pltpu.make_async_copy(arriving if across else x, out, out_sem.at[c])

    def add_into(target, terms, size):
        @pl.loop(0, size // 16)
        def _(i):
            strip = pl.ds(pl.multiple_of(i * 16, 16), 16)
            target[strip, :] = sum(term[strip, :].astype(F32) for term in terms).astype(BF)

    def inward(c, level):
        u, k, r, size = chunks[c]
        own, arriving, _, _ = views(c)
        terms = [own]
        if r == 0:
            local_copy(u, k or 0).wait()
            if u >= 1:
                for j in range(1, chips):
                    plane_copy(u, j).wait_recv()
        if u >= 1:
            terms += [owns[u].at[j, pl.ds(r, size)] for j in range(1, chips)]
        if level > 0:
            first_copy(c, False).wait_recv()
            terms.append(arriving)
        if len(terms) > 1:
            add_into(own, terms, size)
        if c >= FLIGHT:
            first_copy(c - FLIGHT, False).wait_send()
        first_copy(c, level == top).start()

    def outward(c, level):
        size = chunks[c][3]
        own, arriving, x, _ = views(c)
        first_copy(c, True).wait_recv()
        if level == top:
            add_into(arriving, [own, x], size)
        out_copy(c, level == top).start()
        if level > 0:
            if c >= FLIGHT:
                second_copy(c - FLIGHT, False).wait_send()
            second_copy(c, level == top).start()

    top = nc // 2 - 1
    count = len(chunks)
    for level in range(top + 1):

        @pl.when(depth == level)
        def _():
            lag = 1 + 4 * (top - level)
            for t in range(count + lag):
                if t < count:
                    inward(t, level)
                if t >= lag:
                    outward(t - lag, level)
            for c in range(max(0, count - FLIGHT), count):
                first_copy(c, False).wait_send()
                if level > 0:
                    second_copy(c, False).wait_send()
            for c in range(count):
                out_copy(c, False).wait()

    for u in range(1, 4):
        for k in range(1, chips):
            plane_copy(u, k).wait_send()


def finish(nf, nc, pieces, sums):
    chips = nf // 2
    pieces_shape = (chips,) + pieces[0].shape
    shapes = [pieces_shape] + [x.shape[1:] for x in sums]
    count = sum(
        (shape[0] if len(shape) == 3 else 1) * (shape[-2] // chunk_rows(shape[-2]))
        for shape in shapes
    )
    anywhere = pl.BlockSpec(memory_space=pl.ANY)
    dma = pltpu.SemaphoreType.DMA
    return pl.pallas_call(
        functools.partial(finish_kernel, nf, nc),
        in_specs=[anywhere] * (chips + 3),
        out_specs=[anywhere] * 4,
        out_shape=[jax.ShapeDtypeStruct(shape, BF) for shape in shapes],
        scratch_shapes=[pltpu.VMEM(x, BF) for x in [pieces_shape] + [x.shape for x in sums]]
        + [pltpu.VMEM(shape, BF) for shape in shapes]
        + [pltpu.VMEM(shape, BF) for shape in shapes]
        + [dma((4, chips)), dma((4, chips)), dma((4, chips))]
        + [dma((count,))] * 5,
        compiler_params=pltpu.CompilerParams(
            collective_id=0, has_side_effects=True, vmem_limit_bytes=48 << 20
        ),
        cost_estimate=pl.CostEstimate(
            flops=200_000_000_000, bytes_accessed=60_000_000, transcendentals=0
        ),
        name="finish",
    )(*pieces, *sums)


def solution(mesh):
    nf, nc = mesh.shape["fsdp"], mesh.shape["ctx"]
    chips = nf // 2

    def swap(x, k):
        return lax.ppermute(x, "fsdp", [(i, i ^ k) for i in range(nf)])

    def plane_gather(x):
        if chips != 4:
            return [swap(x, 2 * k) for k in range(1, chips)]
        one, two = swap(x, 2), swap(x, 4)
        half = x.shape[0] // 2
        return [one, two, jnp.concatenate([swap(one[:half], 4), swap(two[half:], 2)], axis=0)]

    def cross(x, k):
        return lax.ppermute(x, "ctx", [(i, i ^ k) for i in range(nc)])

    def shards(
        tokens,
        attn_gain,
        w_query,
        w_key,
        w_value,
        w_out,
        ffn_gain,
        w_gate,
        w_up,
        w_down,
        block_table,
        positions,
        out_grad,
    ):
        place = lax.axis_index("fsdp")
        chip, core = place // 2, place % 2
        x = tokens[0].astype(F32)
        gb = out_grad[0]
        rows, width = x.shape
        hidden = w_gate.shape[1]
        part = hidden // chips
        shard = w_gate.shape[0]
        key_width = KV_HEADS * HEAD_DIM

        def core_sum(x):
            other = lax.dynamic_index_in_dim(x, 1 - core, 1, keepdims=False)
            mine = lax.dynamic_index_in_dim(x, core, 1, keepdims=False)
            return (mine.astype(F32) + swap(other, 1).astype(F32)).astype(BF)

        def rows_grad(left, right):
            columns = [left[:, i * shard : (i + 1) * shard] for i in range(nf)]
            even = jnp.concatenate(columns[::2], axis=1)
            odd = jnp.concatenate(columns[1::2], axis=1)
            mine = jnp.where(core == 0, even, odd)
            other = jnp.where(core == 0, odd, even)
            left = jnp.concatenate([mine, swap(other, 1)], axis=0)
            right = jnp.concatenate([right, swap(right, 1)], axis=0)
            return dot(left, right, (0, 0)).astype(BF).reshape(chips, shard, right.shape[1])


        half = HEAD_DIM // 2
        frequency = THETA ** (-jnp.arange(half, dtype=F32) * (2.0 / HEAD_DIM))
        angle = positions[0].astype(F32)[:, None] * frequency[None, :]
        cosine, sine = jnp.cos(angle), jnp.sin(angle)
        cos_lanes = jnp.tile(cosine, (1, 4))
        sin_lanes = jnp.tile(jnp.concatenate([-sine, sine], axis=1), (1, 2))
        blocks = 2 * nc
        stored = block_table.reshape(-1)
        number = jnp.arange(blocks, dtype=jnp.int32)
        where = jnp.sum(
            jnp.where(stored[None, :] == number[:, None], number[None, :], 0), axis=1
        )
        here = lax.axis_index("ctx")
        own = lax.dynamic_slice_in_dim(stored, 2 * here, 2)
        where = 2 * ((where // 2) ^ here) + where % 2
        table = jnp.concatenate([own, where]).astype(jnp.int32)

        order = chip ^ jnp.arange(chips, dtype=jnp.int32)
        both_gains = jnp.pad(jnp.stack([attn_gain, ffn_gain]), ((0, 14), (0, 0)))
        w_q, w_kv, w_o, w_gu, w_d, gains, kv = share_weights(
            nf,
            nc,
            w_query,
            w_key,
            w_value,
            w_out,
            w_gate,
            w_up,
            order,
            w_down,
            both_gains,
            tokens[0],
            cos_lanes,
            sin_lanes,
        )
        w_q = w_q.reshape(width, -1)
        w_kv = w_kv.reshape(width, -1)
        gb_sent, w_kv = lax.optimization_barrier((gb, w_kv))
        w_o = w_o.reshape(-1, width)
        w_gu = w_gu.reshape(width, 2 * part)
        w_d = w_d.reshape(part, width)
        gains = gains[:, :2].astype(F32).transpose(1, 0, 2).reshape(2, width)

        inverse_one = lax.rsqrt(jnp.mean(x * x, axis=1, keepdims=True) + EPS)
        unit_one = x * inverse_one
        xn = (unit_one * gains[0][None, :]).astype(BF)
        q_sum = dot(xn, w_q, (1, 0))
        gb_of = [gb] + [swap(gb_sent, 2 * k) for k in range(1, chips)]
        kv = kv.reshape(nc * rows, 2 * key_width)
        qr, o, ob, lse = attention_forward(table, q_sum, cos_lanes, sin_lanes, kv)
        h1 = x + dot(ob, w_o, (1, 0))
        inverse_two = lax.rsqrt(jnp.mean(h1 * h1, axis=1, keepdims=True) + EPS)
        unit_two = h1 * inverse_two
        hn = (unit_two * gains[1][None, :]).astype(BF)

        hn, gb_of = lax.optimization_barrier((hn, gb_of))

        fused = part % 128 == 0
        if fused:
            grad_hn, left, right, downs, outs = feed_forward(nf, hn, gb_of, w_gu, w_d)
            left = left.reshape(2 * chips * rows, width // 2)
            right = right.reshape(2 * chips * rows, 2 * part)
            down_sum = (downs[0].astype(F32) + downs[1].astype(F32)).astype(BF)
        else:
            dhns = []
            hn_of, act_of, dgu_of = [], [], []
            for k, hn_k in enumerate([hn] + plane_gather(hn)):
                gu = dot(hn_k, w_gu, (1, 0))
                dact = dot(gb_of[k], w_d, (1, 1))
                gate, up = gu[:, :part], gu[:, part:]
                sg = jax.nn.sigmoid(gate)
                silu = gate * sg
                act = (silu * up).astype(BF)
                dgate = (dact * up * sg * (1.0 + gate * (1.0 - sg))).astype(BF)
                dgu = jnp.concatenate([dgate, (dact * silu).astype(BF)], axis=1)
                dhn_k = dot(dgu, w_gu, (1, 1))
                dhns.append(dhn_k.astype(BF) if k else dhn_k)
                hn_of.append(hn_k)
                act_of.append(act)
                dgu_of.append(dgu)
            got = [swap(dhns[k], 2 * k) for k in range(1, chips)]
            act_of, dgu_of, got[:-1], _ = lax.optimization_barrier(
                (act_of, dgu_of, got[:-1], dhns[1:])
            )
            grad_hn = dhns[0]
            for piece in got:
                grad_hn = grad_hn + piece.astype(F32)

            gb_all = jnp.concatenate(gb_of, axis=0)
            down = dot(jnp.concatenate(act_of, axis=0), gb_all, (0, 0)).astype(BF)
            down_sum = core_sum(down.reshape((1, 2) + w_down.shape))[0]
            left = jnp.concatenate(hn_of, axis=0)
            right = jnp.concatenate(dgu_of, axis=0)

        down_sum, left, right = lax.optimization_barrier((down_sum, left, right))
        down_sum = lax.psum_scatter(down_sum, "ctx", scatter_dimension=0, tiled=True)
        if fused:
            wide = dot(left, right, (0, 0)).astype(BF).reshape(chips, shard, 2 * part)
        else:
            wide = rows_grad(left, right)
        wide = [
            lax.dynamic_index_in_dim(wide, chip ^ k, 0, keepdims=False) for k in range(chips)
        ]
        wide, grad_hn = lax.optimization_barrier((wide, grad_hn))
        wide = [swap(piece, 2 * k) if k else piece for k, piece in enumerate(wide)]

        gain_two_grad = jnp.sum(grad_hn * unit_two, axis=0)
        grad_unit = grad_hn * gains[1][None, :]
        dh1 = gb.astype(F32) + inverse_two * (
            grad_unit - unit_two * jnp.mean(grad_unit * unit_two, axis=1, keepdims=True)
        )
        dab = dh1.astype(BF)
        dob = dot(dab, w_o, (1, 1)).astype(BF)
        dq, dkv = attention_backward(table, qr, dob, o, lse, kv, cos_lanes, sin_lanes)
        xn, ob, dab, _ = lax.optimization_barrier((xn, ob, dab, dq))
        if fused:
            outs = [outs[k] for k in range(chips)]
        else:
            act_of, _ = lax.optimization_barrier((act_of, dq))
            outs = [dot(act, w_d, (1, 0)).astype(BF) for act in act_of]
        sent = outs[1:]
        own = own_key_grads(nc, dkv, cos_lanes, sin_lanes)
        own, wide, down_sum = lax.optimization_barrier((own, wide, down_sum))
        down_sum = lax.all_gather(down_sum, "ctx", axis=0, tiled=True)
        ob, dab, _ = lax.optimization_barrier((ob, dab, own))
        out_term = rows_grad(ob, dab)
        dqkv = jnp.concatenate([dq, own], axis=1)
        grad_xn = dot(dq, w_q, (1, 1)) + dot(own, w_kv, (1, 1))
        gain_one_grad = jnp.sum(grad_xn * unit_one, axis=0)
        grad_unit = grad_xn * gains[0][None, :]
        tokens_grad = dh1 + inverse_one * (
            grad_unit - unit_one * jnp.mean(grad_unit * unit_one, axis=1, keepdims=True)
        )
        qkv_term = rows_grad(xn, dqkv)

        gains_of = jnp.stack([gain_one_grad, gain_two_grad]).reshape(2, chips, 2, shard)
        other = lax.dynamic_index_in_dim(gains_of, 1 - core, 2, keepdims=False)
        mine = lax.dynamic_index_in_dim(gains_of, core, 2, keepdims=False)
        gains_of = (mine + swap(other, 1)).transpose(1, 0, 2).reshape(chips, 1, 2 * shard)
        gains_of = jnp.pad(gains_of.astype(BF), ((0, 0), (0, 15), (0, 0)))
        wide, down_sum, out_term, qkv_term, outs[0], sent = lax.optimization_barrier(
            (wide, down_sum, out_term, qkv_term, outs[0], sent)
        )
        gu_sum, out_sum, qkv_sum, gain_sum = finish(
            nf, nc, wide, [out_term, qkv_term, gains_of]
        )
        h1, gain_sum = lax.optimization_barrier((h1, gain_sum))
        branch = h1 + outs[0].astype(F32)
        for k in range(1, chips):
            branch = branch + swap(sent[k - 1], 2 * k).astype(F32)
        layer_out = branch.astype(BF)
        qkv_sum = qkv_sum.astype(F32)
        gain_sum = gain_sum[0].reshape(2, shard).astype(F32)
        gate_grad, up_grad = place_columns(order, gu_sum)
        query_width = HEADS * HEAD_DIM
        return (
            layer_out.reshape(1, rows, width),
            tokens_grad.reshape(1, rows, width),
            gain_sum[0],
            qkv_sum[:, :query_width],
            qkv_sum[:, query_width : query_width + key_width],
            qkv_sum[:, query_width + key_width :],
            out_sum.astype(F32),
            gain_sum[1],
            gate_grad,
            up_grad,
            down_sum.astype(F32),
        )

    weight = P("fsdp", None)
    activation = P("fsdp", "ctx", None)
    return jax.shard_map(
        shards,
        mesh=mesh,
        in_specs=(
            activation,
            P("fsdp"),
            weight,
            weight,
            weight,
            weight,
            P("fsdp"),
            weight,
            weight,
            weight,
            P(),
            P("fsdp", "ctx"),
            activation,
        ),
        out_specs=(
            activation,
            activation,
            P("fsdp"),
            weight,
            weight,
            weight,
            weight,
            P("fsdp"),
            weight,
            weight,
            weight,
        ),
        check_vma=False,
    )
```

```python
import functools

import jax
import jax.numpy as jnp
from jax import lax
from jax.experimental import pallas as pl
from jax.experimental.pallas import tpu as pltpu
from jax.sharding import PartitionSpec as P

HEADS = 32
KV_HEADS = 4
HEAD_DIM = 64
GROUP = HEADS // KV_HEADS
PAIRS = GROUP // 2
LANES = 2 * HEAD_DIM
STACK = PAIRS * LANES

EPS = 1e-05
THETA = 10000.0
NEG = -1e30
FLIGHT = 2
BF = jnp.bfloat16
F32 = jnp.float32


def dot(left, right, contract, out=F32):
    return lax.dot_general(
        left, right, ((contract[:1], contract[1:]), ((), ())), preferred_element_type=out
    )


def swap_halves(z):
    lane = lax.broadcasted_iota(jnp.int32, z.shape, 1)
    first = (lane % HEAD_DIM) < (HEAD_DIM // 2)
    return jnp.where(
        first,
        pltpu.roll(z, LANES - HEAD_DIM // 2, 1),
        pltpu.roll(z, HEAD_DIM // 2, 1),
    )


def split_heads(rows):
    lane = lax.broadcasted_iota(jnp.int32, rows.shape, 1)
    zero = jnp.zeros_like(rows)
    return jnp.concatenate(
        [jnp.where(lane < HEAD_DIM, rows, zero), jnp.where(lane >= HEAD_DIM, rows, zero)], axis=0
    )


def join_heads(columns):
    half = columns.shape[1] // 2
    sub = lax.broadcasted_iota(jnp.int32, (LANES, half), 0)
    return jnp.where(sub < HEAD_DIM, columns[:, :half], columns[:, half:]).T


def stack_pairs(ref, rows):
    return jnp.concatenate([ref[rows, p * LANES : (p + 1) * LANES] for p in range(PAIRS)], axis=0)


def two_blocks(ref, table, j, block):
    parts = [
        ref[pl.ds(pl.multiple_of(table[2 + 2 * j + i] * block, block), block), :] for i in range(2)
    ]
    return jnp.concatenate(parts, axis=0)


def causal(scores, j, own, block):
    key = lax.broadcasted_iota(jnp.int32, scores.shape, 0) + j * (2 * block)
    query = lax.broadcasted_iota(jnp.int32, scores.shape, 1) % block + own * block
    return jnp.where(key <= query, scores, NEG)


def head_twice(pair, group):
    wide = pair.astype(F32)
    lane = lax.broadcasted_iota(jnp.int32, wide.shape, 1)
    keep = (lane < HEAD_DIM) == (group % 2 == 0)
    return jnp.where(keep, wide, pltpu.roll(wide, HEAD_DIM, 1)).astype(BF)


def attention_forward_kernel(
    table,
    q_ref,
    cos_ref,
    sin_ref,
    k_pair,
    v_pair,
    qr_ref,
    o_ref,
    ob_ref,
    lse_ref,
    qm,
    m,
    l,
    acc,
    k_ref,
    v_ref,
):
    block = q_ref.shape[0] // 2
    group = pl.program_id(0)
    k_ref[...] = head_twice(k_pair[...], group)
    v_ref[...] = head_twice(v_pair[...], group)
    for h in range(2):
        rows = slice(h * block, (h + 1) * block)
        cosine, sine = cos_ref[rows, :], sin_ref[rows, :]
        for p in range(PAIRS):
            lanes = slice(p * LANES, (p + 1) * LANES)
            z = q_ref[rows, lanes]
            qr_ref[rows, lanes] = (z * cosine + swap_halves(z) * sine).astype(BF)
        scaled = stack_pairs(qr_ref, rows).astype(F32) * (HEAD_DIM**-0.5)
        qm[...] = split_heads(scaled).astype(BF)
        m[...] = jnp.full_like(m, NEG)
        l[...] = jnp.zeros_like(l)
        acc[...] = jnp.zeros_like(acc)
        own = table[h]

        def step(j, masked):
            keys = two_blocks(k_ref, table, j, block)
            values = two_blocks(v_ref, table, j, block)
            s = dot(keys, qm[...], (1, 1))
            if masked:
                s = causal(s, j, own, block)
            before = m[...]
            now = jnp.maximum(before, jnp.max(s, axis=0, keepdims=True))
            p = jnp.exp(s - now)
            decay = jnp.exp(before - now)
            l[...] = l[...] * decay + jnp.sum(p, axis=0, keepdims=True)
            acc[...] = acc[...] * decay + dot(values, p.astype(BF), (0, 0))
            m[...] = now

        last = own // 2

        @pl.loop(0, last)
        def _(j):
            step(j, False)

        step(last, True)
        lse_ref[0, h : h + 1, :] = m[...] + jnp.log(l[...])
        o = join_heads(acc[...] / l[...])
        for p in range(PAIRS):
            lanes = slice(p * LANES, (p + 1) * LANES)
            piece = o[p * block : (p + 1) * block, :]
            o_ref[rows, lanes] = piece
            ob_ref[rows, lanes] = piece.astype(BF)


def attention_forward(table, q, cosine, sine, kv):
    rows, length = q.shape[0], kv.shape[0]
    query_width = HEADS * HEAD_DIM
    columns = pl.BlockSpec((rows, STACK), lambda g, t: (0, g))
    whole = pl.BlockSpec((rows, LANES), lambda g, t: (0, 0))
    key_pair = pl.BlockSpec((length, LANES), lambda g, t: (0, g // 2))
    value_pair = pl.BlockSpec((length, LANES), lambda g, t: (0, KV_HEADS // 2 + g // 2))
    wide = GROUP * (rows // 2)
    return pl.pallas_call(
        attention_forward_kernel,
        grid_spec=pltpu.PrefetchScalarGridSpec(
            num_scalar_prefetch=1,
            grid=(KV_HEADS,),
            in_specs=[columns, whole, whole, key_pair, value_pair],
            out_specs=[
                columns,
                columns,
                columns,
                pl.BlockSpec((1, 2, wide), lambda g, t: (g, 0, 0)),
            ],
            scratch_shapes=[
                pltpu.VMEM((wide, LANES), BF),
                pltpu.VMEM((1, wide), F32),
                pltpu.VMEM((1, wide), F32),
                pltpu.VMEM((LANES, wide), F32),
                pltpu.VMEM((length, LANES), BF),
                pltpu.VMEM((length, LANES), BF),
            ],
        ),
        out_shape=[
            jax.ShapeDtypeStruct((rows, query_width), BF),
            jax.ShapeDtypeStruct((rows, query_width), F32),
            jax.ShapeDtypeStruct((rows, query_width), BF),
            jax.ShapeDtypeStruct((KV_HEADS, 2, wide), F32),
        ],
        compiler_params=pltpu.CompilerParams(vmem_limit_bytes=32 << 20),
        cost_estimate=pl.CostEstimate(
            flops=8 * HEADS * rows * length * HEAD_DIM,
            bytes_accessed=16 * rows * HEADS * HEAD_DIM,
            transcendentals=HEADS * rows * length,
        ),
        name="attention_forward",
    )(table, q, cosine, sine, kv, kv)


def attention_backward_kernel(
    table,
    qr_ref,
    do_ref,
    o_ref,
    lse_ref,
    k_pair,
    v_pair,
    cos_ref,
    sin_ref,
    dq_ref,
    dkv_ref,
    qm,
    dom,
    dqt,
    k_ref,
    v_ref,
    dk_ref,
    dv_ref,
):
    block = qr_ref.shape[0] // 2
    group = pl.program_id(0)
    k_ref[...] = head_twice(k_pair[...], group)
    v_ref[...] = head_twice(v_pair[...], group)
    dk_ref[...] = jnp.zeros_like(dk_ref)
    dv_ref[...] = jnp.zeros_like(dv_ref)
    for h in range(2):
        rows = slice(h * block, (h + 1) * block)
        scaled = stack_pairs(qr_ref, rows).astype(F32) * (HEAD_DIM**-0.5)
        qm[...] = split_heads(scaled).astype(BF)
        grads = stack_pairs(do_ref, rows).astype(F32)
        dom[...] = split_heads(grads).astype(BF)
        product = (grads * stack_pairs(o_ref, rows)).T
        inner = jnp.concatenate(
            [
                jnp.sum(product[:HEAD_DIM], axis=0, keepdims=True),
                jnp.sum(product[HEAD_DIM:], axis=0, keepdims=True),
            ],
            axis=1,
        )
        lse = lse_ref[0, h : h + 1, :]
        dqt[...] = jnp.zeros_like(dqt)
        own = table[h]

        def step(j, masked):
            keys = two_blocks(k_ref, table, j, block)
            values = two_blocks(v_ref, table, j, block)
            s = dot(keys, qm[...], (1, 1))
            if masked:
                s = causal(s, j, own, block)
            p = jnp.exp(s - lse)
            dp = dot(values, dom[...], (1, 1))
            ds = (p * (dp - inner)).astype(BF)
            dv = dot(p.astype(BF), dom[...], (1, 0))
            dk = dot(ds, qm[...], (1, 0))
            dqt[...] += dot(keys, ds, (0, 0))
            for i in range(2):
                at = pl.ds(pl.multiple_of(table[2 + 2 * j + i] * block, block), block)
                dk_ref[at, :] += dk[i * block : (i + 1) * block]
                dv_ref[at, :] += dv[i * block : (i + 1) * block]

        last = own // 2

        @pl.loop(0, last)
        def _(j):
            step(j, False)

        step(last, True)
        cosine, sine = cos_ref[rows, :], sin_ref[rows, :]
        dq = join_heads(dqt[...] * (HEAD_DIM**-0.5))
        for p in range(PAIRS):
            z = dq[p * block : (p + 1) * block, :]
            dq_ref[rows, p * LANES : (p + 1) * LANES] = (
                z * cosine - swap_halves(z) * sine
            ).astype(BF)
    lane = lax.broadcasted_iota(jnp.int32, dk_ref.shape, 1)
    keep = (lane < HEAD_DIM) == (group % 2 == 0)
    for i, ref in enumerate((dk_ref, dv_ref)):
        both = ref[...] + pltpu.roll(ref[...], HEAD_DIM, 1)
        dkv_ref[i] = jnp.where(keep, both, dkv_ref[i].astype(F32)).astype(BF)


def attention_backward(table, qr, grads, o, lse, kv, cosine, sine):
    rows, length = qr.shape[0], kv.shape[0]
    columns = pl.BlockSpec((rows, STACK), lambda g, t: (0, g))
    whole = pl.BlockSpec((rows, LANES), lambda g, t: (0, 0))
    key_pair = pl.BlockSpec((length, LANES), lambda g, t: (0, g // 2))
    value_pair = pl.BlockSpec((length, LANES), lambda g, t: (0, KV_HEADS // 2 + g // 2))
    wide = GROUP * (rows // 2)
    return pl.pallas_call(
        attention_backward_kernel,
        grid_spec=pltpu.PrefetchScalarGridSpec(
            num_scalar_prefetch=1,
            grid=(KV_HEADS,),
            in_specs=[
                columns,
                columns,
                columns,
                pl.BlockSpec((1, 2, wide), lambda g, t: (g, 0, 0)),
                key_pair,
                value_pair,
                whole,
                whole,
            ],
            out_specs=[columns, pl.BlockSpec((2, length, LANES), lambda g, t: (0, 0, g // 2))],
            scratch_shapes=[
                pltpu.VMEM((wide, LANES), BF),
                pltpu.VMEM((wide, LANES), BF),
                pltpu.VMEM((LANES, wide), F32),
                pltpu.VMEM((length, LANES), BF),
                pltpu.VMEM((length, LANES), BF),
                pltpu.VMEM((length, LANES), F32),
                pltpu.VMEM((length, LANES), F32),
            ],
        ),
        out_shape=[
            jax.ShapeDtypeStruct(qr.shape, BF),
            jax.ShapeDtypeStruct((2, length, KV_HEADS * HEAD_DIM), BF),
        ],
        compiler_params=pltpu.CompilerParams(vmem_limit_bytes=32 << 20),
        cost_estimate=pl.CostEstimate(
            flops=20 * HEADS * rows * length * HEAD_DIM,
            bytes_accessed=16 * rows * HEADS * HEAD_DIM,
            transcendentals=HEADS * rows * length,
        ),
        name="attention_backward",
    )(table, qr, grads, o, lse, kv, kv, cosine, sine)


def own_key_grads_kernel(nc, dkv_ref, cos_ref, sin_ref, out_ref, got, send_sem, recv_sem):
    rows, width = out_ref.shape[0], out_ref.shape[1] // 2
    here = lax.axis_index("ctx")
    mesh_id = pl.DeviceIdType.MESH
    barrier = pltpu.get_barrier_semaphore()
    for k in range(1, nc):
        pl.semaphore_signal(barrier, inc=1, device_id={"ctx": here ^ k}, device_id_type=mesh_id)
    pl.semaphore_wait(barrier, nc - 1)

    def copy(k):
        source = dkv_ref.at[:, pl.ds(k * rows, rows)]
        if k == 0:
            return pltpu.make_async_copy(source, got.at[0], recv_sem.at[0])
        return pltpu.make_async_remote_copy(
            src_ref=source,
            dst_ref=got.at[k],
            send_sem=send_sem.at[k],
            recv_sem=recv_sem.at[k],
            device_id={"ctx": here ^ k},
            device_id_type=mesh_id,
        )

    for k in reversed(range(nc)):
        copy(k).start()
    for k in range(nc):
        copy(k).wait()

    def total(i, lanes):
        return sum(got[k, i, :, lanes].astype(F32) for k in range(nc))

    for p in range(width // LANES):
        lanes = slice(p * LANES, (p + 1) * LANES)
        z = total(0, lanes)
        out_ref[:, lanes] = (z * cos_ref[...] - swap_halves(z) * sin_ref[...]).astype(BF)
        out_ref[:, width + p * LANES : width + (p + 1) * LANES] = total(1, lanes).astype(BF)


def own_key_grads(nc, dkv, cosine, sine):
    rows, width = dkv.shape[1] // nc, dkv.shape[2]
    vmem = pl.BlockSpec(memory_space=pltpu.VMEM)
    return pl.pallas_call(
        functools.partial(own_key_grads_kernel, nc),
        in_specs=[pl.BlockSpec(memory_space=pl.ANY), vmem, vmem],
        out_specs=vmem,
        out_shape=jax.ShapeDtypeStruct((rows, 2 * width), BF),
        scratch_shapes=[
            pltpu.VMEM((nc, 2, rows, width), BF),
            pltpu.SemaphoreType.DMA((nc,)),
            pltpu.SemaphoreType.DMA((nc,)),
        ],
        compiler_params=pltpu.CompilerParams(collective_id=2, has_side_effects=True),
        name="own_key_grads",
    )(dkv, cosine, sine)


def share_kernel(nf, nc, low, size, raw, *refs):
    count = 2 if raw else 1
    w_query, w_key, w_value, w_out, *halves, down, gains, tokens, cosine, sine = refs[: 9 + count]
    refs = refs[9 + count :]
    query, key_value, out, wide, downs, all_gains, kv_all = refs[:7]
    query_own, key_value_own, out_own, wide_own, down_own, gains_own = refs[7:13]
    (local, plane_send, plane_recv, along_send, along_recv, core_send, core_recv) = refs[13:20]
    (gain_send, gain_recv, down_sem, gather_send, gather_recv, gather_core) = refs[20:26]
    w_kv, gains_v, xn, kv, kv_load, kv_send, kv_recv = refs[26:]
    chips = nf // 2
    place, here = lax.axis_index("fsdp"), lax.axis_index("ctx")
    chip, core = place // 2, place % 2
    mesh_id = pl.DeviceIdType.MESH
    shard, columns = wide.shape[1:]
    part = columns // 2
    key_width = w_key.shape[1]
    gathered = [
        (w_query, query, query_own, pl.ds(0, w_query.shape[1])),
        (w_key, key_value, key_value_own, pl.ds(0, key_width)),
        (w_value, key_value, key_value_own, pl.ds(key_width, key_width)),
        (w_out, out, out_own, pl.ds(0, w_out.shape[1])),
    ]

    barrier = pltpu.get_barrier_semaphore()

    def greet(target):
        pl.semaphore_signal(barrier, inc=1, device_id=target, device_id_type=mesh_id)

    for j in range(1, nf):
        greet({"fsdp": place ^ j})
    for pos in range(nc):

        @pl.when(here == pos)
        def _():
            for i in range(nc):
                if i != pos:
                    greet({"ctx": i})

    pl.semaphore_wait(barrier, nf - 1 + nc - 1)

    def remote(source, target, sends, recvs, where):
        return pltpu.make_async_remote_copy(
            src_ref=source,
            dst_ref=target,
            send_sem=sends,
            recv_sem=recvs,
            device_id=where,
            device_id_type=mesh_id,
        )

    def piece(k, h, rows):
        if raw:
            at = pl.ds(pl.multiple_of((chip ^ k) * part, 128), part)
            return halves[h].at[rows, at]
        return halves[0].at[k, rows]

    def side(h):
        return pl.ds(h * part, part) if raw else pl.ds(0, columns)

    def rows_of(share):
        return pl.ds(low + share * size, size)

    def plane_copy(k, kind, h):
        rows = rows_of(here) if kind else pl.ds(0, low)
        return remote(
            piece(k, h, rows),
            wide.at[place, rows, side(h)],
            plane_send.at[kind, k, h],
            plane_recv.at[kind, k, h],
            {"fsdp": place ^ (2 * k)},
        )

    def along_copy(k, share, up, target):
        block = wide.at[place ^ (2 * k), rows_of(share)]
        return remote(
            block, block, along_send.at[up, share, k], along_recv.at[share, k], {"ctx": target}
        )

    def core_copy(k, share):
        rows = rows_of(share) if share < nc else pl.ds(0, low)
        block = wide.at[place ^ (2 * k), rows]
        return remote(
            block, block, core_send.at[k, share], core_recv.at[k, share], {"fsdp": place ^ 1}
        )

    def own_core_copy(h):
        return remote(
            piece(0, h, pl.ds(0, shard)),
            wide.at[place, :, side(h)],
            core_send.at[0, h],
            core_recv.at[0, h],
            {"fsdp": place ^ 1},
        )

    half = shard // 2
    relayed = chips == 4

    def gather_copy(u, k, relay=0):
        source, target, _, at = gathered[u]
        if relay:
            owner, rows = place ^ (2 * (3 - k)), pl.ds((2 - k) * half, half)
            source = target.at[owner, rows, at]
        else:
            owner, rows = place, pl.ds(0, shard)
        number = 2 * k + relay
        return remote(
            source,
            target.at[owner, rows, at],
            gather_send.at[u, number],
            gather_recv.at[u, number],
            {"fsdp": place ^ (2 * k)},
        )

    def gather_core_copy(u, k):
        source, target, _, at = gathered[u]
        block = target.at[place ^ (2 * k), :, at]
        return remote(
            block if k else source,
            block,
            gather_core.at[0, u, k],
            gather_core.at[1, u, k],
            {"fsdp": place ^ 1},
        )

    def down_copy():
        return remote(down, downs.at[core], down_sem.at[0], down_sem.at[1], {"fsdp": place ^ 1})

    def gain_copy(j):
        return remote(
            gains, all_gains.at[place], gain_send.at[j], gain_recv.at[j], {"fsdp": place ^ j}
        )

    direct = (1, 2) if relayed else tuple(range(1, chips))
    for k in range(1, chips):
        for h in range(count):
            plane_copy(k, 1, h).start()
    for j in range(1, nf):
        gain_copy(j).start()
    for h in range(count):
        own_core_copy(h).start()
    for u in range(4):
        gather_core_copy(u, 0).start()
    down_copy().start()
    own = [(source, stage.at[:, at], None) for source, _, stage, at in gathered]
    own += [(piece(0, h, pl.ds(0, shard)), wide_own.at[:, side(h)], None) for h in range(count)]
    own += [(down, down_own, downs.at[core]), (gains, gains_own, all_gains.at[place])]
    back = [
        (query_own, query.at[place]),
        (key_value_own, key_value.at[place]),
        (out_own, out.at[place]),
        (wide_own, wide.at[place]),
        (down_own, downs.at[core]),
        (gains_own, all_gains.at[place]),
    ]
    for i, (source, stage, _) in enumerate(own):
        pltpu.make_async_copy(source, stage, local.at[0, i]).start()
    for i, (source, stage, _) in enumerate(own):
        pltpu.make_async_copy(source, stage, local.at[0, i]).wait()
    for i, (stage, target) in enumerate(back):
        pltpu.make_async_copy(stage, target, local.at[1, i]).start()

    for k in range(1, chips):
        for h in range(count):
            plane_copy(k, 1, h).wait_send()
    for u in (1, 2, 0, 3):
        for k in direct:
            gather_copy(u, k).start()

    def kv_copy(k):
        if k == 0:
            return pltpu.make_async_copy(kv, kv_all.at[0], kv_recv.at[0])
        return remote(kv, kv_all.at[k], kv_send.at[k], kv_recv.at[k], {"ctx": here ^ k})

    def make_kv():
        for i in (len(back) - 1, 1):
            stage, target = back[i]
            pltpu.make_async_copy(stage, target, local.at[1, i]).wait()
        for j in range(1, nf):
            gain_copy(j).wait_recv()
        for u in (1, 2):
            if relayed:
                for k in direct:
                    gather_copy(u, k, 1).wait_recv()
                gather_core_copy(u, 3).start()
            for k in range(chips):
                gather_core_copy(u, k).wait_recv()
        loads = [
            pltpu.make_async_copy(key_value, w_kv, kv_load.at[0]),
            pltpu.make_async_copy(all_gains, gains_v, kv_load.at[1]),
        ]
        for copy in loads:
            copy.start()
        for copy in loads:
            copy.wait()
        for i in range(0, xn.shape[0], 16):
            x = tokens[i : i + 16, :].astype(F32)
            unit = x * lax.rsqrt(jnp.mean(x * x, axis=1, keepdims=True) + EPS)
            for f in range(nf):
                lanes = slice(f * shard, (f + 1) * shard)
                gain = gains_v[f, 0:1, :].astype(F32)
                xn[i : i + 16, lanes] = (unit[:, lanes] * gain).astype(BF)
        total = sum(
            dot(xn[:, f * shard : (f + 1) * shard], w_kv[f], (1, 0)) for f in range(nf)
        )
        for p in range(0, key_width, LANES):
            z = total[:, p : p + LANES]
            kv[:, p : p + LANES] = (z * cosine[...] + swap_halves(z) * sine[...]).astype(BF)
        kv[:, key_width:] = total[:, key_width:].astype(BF)
        for k in reversed(range(nc)):
            kv_copy(k).start()

    for pos in range(nc):

        @pl.when(here == pos)
        def _():
            def pass_on(k, share):
                if share <= pos < nc - 1:
                    along_copy(k, share, 1, pos + 1).start()
                if share >= pos > 0:
                    along_copy(k, share, 0, pos - 1).start()
                core_copy(k, share).start()

            for k in range(1, chips):
                for h in range(count):
                    plane_copy(k, 1, h).wait_recv()
                pass_on(k, pos)
            if low:
                for k in range(1, chips):
                    for h in range(count):
                        plane_copy(k, 0, h).start()
            def gather_on(u):
                for k in direct:
                    gather_copy(u, k).wait_recv()
                    if relayed:
                        gather_copy(u, 3 - k, 1).start()
                    gather_core_copy(u, k).start()

            groups = [(), (1, 2), (0, 3)]
            for d in range(1, max(nc, len(groups))):
                for share in (pos - d, pos + d):
                    if 0 <= share < nc:
                        for k in range(1, chips):
                            along_copy(k, share, 0, 0).wait_recv()
                            pass_on(k, share)
                for u in groups[d] if d < len(groups) else ():
                    if u == 3:
                        make_kv()
                    gather_on(u)
            if low:
                for k in range(1, chips):
                    for h in range(count):
                        plane_copy(k, 0, h).wait_recv()
                    core_copy(k, nc).start()
            if relayed:
                for u in (0, 3):
                    for k in direct:
                        gather_copy(u, k, 1).wait_recv()
                    gather_core_copy(u, 3).start()
            for k in range(1, chips):
                for share in range(nc):
                    if share <= pos < nc - 1:
                        along_copy(k, share, 1, pos + 1).wait_send()
                    if share >= pos > 0:
                        along_copy(k, share, 0, pos - 1).wait_send()

    for h in range(count):
        own_core_copy(h).wait()
    for k in range(1, chips):
        for share in range(nc + 1 if low else nc):
            core_copy(k, share).wait()
        if low:
            for h in range(count):
                plane_copy(k, 0, h).wait_send()
    for j in range(1, nf):
        gain_copy(j).wait_send()
    for k in range(nc):
        kv_copy(k).wait()
    for u in range(4):
        for k in direct:
            gather_copy(u, k).wait_send()
            if relayed:
                gather_copy(u, k, 1).wait_send()
        for k in range(chips):
            gather_core_copy(u, k).wait_send()
            if u in (0, 3):
                gather_core_copy(u, k).wait_recv()
    down_copy().wait()
    for i, (stage, target) in enumerate(back):
        if i not in (len(back) - 1, 1):
            pltpu.make_async_copy(stage, target, local.at[1, i]).wait()


def share_weights(
    nf,
    nc,
    w_query,
    w_key,
    w_value,
    w_out,
    w_gate,
    w_up,
    order,
    down,
    gains,
    tokens,
    cosine,
    sine,
):
    chips = nf // 2
    shard, hidden = w_gate.shape
    part = hidden // chips
    size = shard // nc
    low = shard - nc * size
    raw = part % 128 == 0
    halves = [w_gate, w_up]
    if not raw:
        both = [w.reshape(shard, chips, part).transpose(1, 0, 2) for w in halves]
        halves = [jnp.take(jnp.concatenate(both, axis=2), order, axis=0)]
    anywhere = pl.BlockSpec(memory_space=pl.ANY)
    dma = pltpu.SemaphoreType.DMA
    kv_shape = (tokens.shape[0], 2 * w_key.shape[1])
    widths = [w_query.shape[1], 2 * w_key.shape[1], w_out.shape[1], 2 * part]
    return pl.pallas_call(
        functools.partial(share_kernel, nf, nc, low, size, raw),
        in_specs=[anywhere] * (6 + len(halves)) + [pl.BlockSpec(memory_space=pltpu.VMEM)] * 3,
        out_specs=[anywhere] * 7,
        out_shape=[jax.ShapeDtypeStruct((nf, shard, width), BF) for width in widths]
        + [
            jax.ShapeDtypeStruct((2,) + down.shape, BF),
            jax.ShapeDtypeStruct((nf,) + gains.shape, BF),
            jax.ShapeDtypeStruct((nc,) + kv_shape, BF),
        ],
        scratch_shapes=[pltpu.VMEM((shard, width), BF) for width in widths]
        + [
            pltpu.VMEM(down.shape, BF),
            pltpu.VMEM(gains.shape, BF),
            dma((2, 8)),
            dma((2, chips, 2)),
            dma((2, chips, 2)),
            dma((2, nc, chips)),
            dma((nc, chips)),
            dma((chips, nc + 1)),
            dma((chips, nc + 1)),
            dma((nf,)),
            dma((nf,)),
            dma((2,)),
            dma((4, 2 * chips)),
            dma((4, 2 * chips)),
            dma((2, 4, chips)),
            pltpu.VMEM((nf, shard, widths[1]), BF),
            pltpu.VMEM((nf,) + gains.shape, BF),
            pltpu.VMEM(tokens.shape, BF),
            pltpu.VMEM(kv_shape, BF),
            dma((2,)),
            dma((nc,)),
            dma((nc,)),
        ],
        compiler_params=pltpu.CompilerParams(
            collective_id=1, has_side_effects=True, vmem_limit_bytes=56 << 20
        ),
        name="share_weights",
    )(w_query, w_key, w_value, w_out, *halves, down, gains, tokens, cosine, sine)


def place_columns_kernel(order, both_ref, gate_ref, up_ref):
    part = gate_ref.shape[1]
    gate_ref[...] = both_ref[0, :, :part].astype(F32)
    up_ref[...] = both_ref[0, :, part:].astype(F32)


def place_columns(order, both):
    parts, shard, part = both.shape[0], both.shape[1], both.shape[2] // 2
    out = jax.ShapeDtypeStruct((shard, parts * part), F32)
    if part % 128:
        both = jnp.take(both, order, axis=0).transpose(1, 0, 2).astype(F32)
        return [both[:, :, i * part : (i + 1) * part].reshape(out.shape) for i in range(2)]
    columns = pl.BlockSpec((shard, part), lambda k, t: (0, t[k]))
    return pl.pallas_call(
        place_columns_kernel,
        grid_spec=pltpu.PrefetchScalarGridSpec(
            num_scalar_prefetch=1,
            grid=(parts,),
            in_specs=[pl.BlockSpec((1, shard, 2 * part), lambda k, t: (k, 0, 0))],
            out_specs=[columns, columns],
        ),
        out_shape=[out, out],
        name="place_columns",
    )(order, both)


def feed_forward_kernel(nf, *refs):
    chips = nf // 2
    hn, *gbs, w_gu, w_d, grad, left, right, down_kept, down_got = refs[: chips + 8]
    outs, refs = refs[chips + 8 : 2 * chips + 8], refs[2 * chips + 8 :]
    w_gu_v, w_d_v, hn_v, gb_v, dact_v, act_v, dgu_v, sent, got, outs_v = refs[:10]
    tiles, halves, half_sem, *sems = refs[10:]
    load, load_gb, hn_send, hn_recv, dhn_send, dhn_recv, store = sems[:7]
    left_local, left_send, left_recv, right_local, right_send, right_recv = sems[7:13]
    down_local, down_send, down_recv = sems[13:]
    place = lax.axis_index("fsdp")
    core = place % 2
    rows, width = hn.shape
    part = w_d.shape[0]
    shard = width // nf
    half = rows // 2
    relayed = chips == 4
    direct = (1, 2) if relayed else tuple(range(1, chips))
    mesh_id = pl.DeviceIdType.MESH

    barrier = pltpu.get_barrier_semaphore()
    for j in [1] + [2 * k for k in range(1, chips)]:
        pl.semaphore_signal(
            barrier, inc=1, device_id={"fsdp": place ^ j}, device_id_type=mesh_id
        )
    pl.semaphore_wait(barrier, chips)

    def remote(source, target, sends, recvs, step):
        return pltpu.make_async_remote_copy(
            src_ref=source,
            dst_ref=target,
            send_sem=sends,
            recv_sem=recvs,
            device_id={"fsdp": place ^ step},
            device_id_type=mesh_id,
        )

    def hn_copy(k, relay=0):
        at = 2 * k + relay
        if relay:
            lines = pl.ds((2 - k) * half, half)
            source, target = hn_v.at[3 - k, lines], hn_v.at[3, lines]
        else:
            source, target = hn, hn_v.at[k]
        return remote(source, target, hn_send.at[at], hn_recv.at[at], 2 * k)

    def dhn_copy(k):
        return remote(sent.at[k - 1], got.at[k - 1], dhn_send.at[k], dhn_recv.at[k], 2 * k)

    def half_copy(k):
        lines = pl.ds((k - 1) * half, half)
        return remote(
            sent.at[2, lines], halves.at[k - 1], half_sem.at[0, k], half_sem.at[1, k], 2 * k
        )

    def left_copy(k, j, other):
        number = 1 - core if other else core
        columns = pl.ds(pl.multiple_of((2 * j + number) * shard, shard), shard)
        source = hn_v.at[k, :, columns]
        target = left.at[other, k, :, pl.ds(j * shard, shard)]
        if other:
            return remote(source, target, left_send.at[k, j], left_recv.at[k, j], 1)
        return pltpu.make_async_copy(source, target, left_local.at[k, j])

    def right_copy(k, other):
        if other:
            return remote(dgu_v.at[k], right.at[1, k], right_send.at[k], right_recv.at[k], 1)
        return pltpu.make_async_copy(dgu_v.at[k], right.at[0, k], right_local.at[k])

    loads = [
        pltpu.make_async_copy(w_d, w_d_v, load.at[0]),
        pltpu.make_async_copy(hn, hn_v.at[0], load.at[1]),
        pltpu.make_async_copy(w_gu, w_gu_v, load.at[2]),
    ]
    gb_loads = [
        pltpu.make_async_copy(gb, gb_v.at[k], load_gb.at[k]) for k, gb in enumerate(gbs)
    ]
    store_outs = [
        pltpu.make_async_copy(outs_v.at[k], out, store.at[k]) for k, out in enumerate(outs)
    ]
    for k in direct:
        hn_copy(k).start()
    for copy in loads[:1] + gb_loads + loads[1:]:
        copy.start()

    for copy in loads[:1] + gb_loads:
        copy.wait()

    def dact_tile(start, size):
        tile = w_d_v[pl.ds(start, size), :]
        for k in range(chips):
            dact_v[k, :, pl.ds(start, size)] = dot(gb_v[k], tile, (1, 1))

    @pl.loop(0, part // 256)
    def _(i):
        dact_tile(pl.multiple_of(i * 256, 256), 256)

    if part % 256:
        dact_tile(part - 128, 128)

    def forward(k):
        for j in range(chips):
            left_copy(k, j, 1).start()
            left_copy(k, j, 0).start()

        def tile(start, size):
            one, two = pl.ds(start, size), pl.ds(pl.multiple_of(part + start, 128), size)
            gate = dot(hn_v[k], w_gu_v[:, one], (1, 0))
            up = dot(hn_v[k], w_gu_v[:, two], (1, 0))
            dact = dact_v[k, :, one]
            sg = jax.nn.sigmoid(gate)
            silu = gate * sg
            act_v[k, :, one] = (silu * up).astype(BF)
            dgu_v[k, :, one] = (dact * up * sg * (1.0 + gate * (1.0 - sg))).astype(BF)
            dgu_v[k, :, two] = (dact * silu).astype(BF)

        @pl.loop(0, part // 256)
        def _(i):
            tile(pl.multiple_of(i * 256, 256), 256)

        if part % 256:
            tile(part - 128, 128)

        right_copy(k, 1).start()
        right_copy(k, 0).start()

    def backward(k):
        @pl.loop(0, width // 256)
        def _(i):
            lines = pl.ds(pl.multiple_of(i * 256, 256), 256)
            dhn = dot(dgu_v[k], w_gu_v[lines, :], (1, 1))
            if k:
                sent[k - 1, :, lines] = dhn.astype(BF)
            else:
                grad[:, lines] = dhn

    for copy in loads[1:]:
        copy.wait()
    forward(0)
    for k in direct:
        hn_copy(k).wait_recv()
        if relayed:
            hn_copy(3 - k, 1).start()
    if relayed:
        forward(1)
        forward(2)
        for i in direct:
            hn_copy(i, 1).wait_recv()
        forward(3)
        backward(3)
        for k in direct:
            half_copy(k).start()
        backward(1)
        backward(2)
        for k in direct:
            half_copy(k).wait_recv()

            @pl.loop(0, half // 16)
            def _(i):
                lines = pl.ds(pl.multiple_of(i * 16, 16), 16)
                into = pl.ds(pl.multiple_of((k - 1) * half + i * 16, 16), 16)
                total = sent[2 - k, into, :].astype(F32) + halves[k - 1, lines, :].astype(F32)
                sent[2 - k, into, :] = total.astype(BF)

            dhn_copy(3 - k).start()
    else:
        for k in range(1, chips):
            forward(k)
            backward(k)
            dhn_copy(k).start()
    backward(0)

    @pl.loop(0, width // 256)
    def _(i):
        columns = pl.ds(pl.multiple_of(i * 256, 256), 256)
        for k in range(chips):
            outs_v[k, :, columns] = dot(act_v[k], w_d_v[:, columns], (1, 0)).astype(BF)

    for copy in store_outs:
        copy.start()

    lower = part // 2
    spans = []
    for start in range(0, part, 128):
        cuts = sorted({start, min(max(lower, start), start + 128), start + 128})
        spans += [(start, a, b) for a, b in zip(cuts, cuts[1:])]

    def span_copies(n):
        start, a, b = spans[n]
        number = int(a >= lower)
        source = tiles.at[(start // 128) % 2, pl.ds(a - start, b - a)]
        at = pl.ds(a - number * lower, b - a)

        def keep():
            return pltpu.make_async_copy(source, down_kept.at[at], down_local.at[n])

        def send():
            return remote(source, down_got.at[at], down_send.at[n], down_recv.at[n], 1)

        return number, keep, send

    def each_span(chosen, go):
        for n in chosen:
            number, keep, send = span_copies(n)

            @pl.when(core == number)
            def _():
                keep().start() if go else keep().wait()

            @pl.when(core != number)
            def _():
                send().start() if go else send().wait_send()

    for start in range(0, part, 128):
        before = [n for n, span in enumerate(spans) if span[0] == start - 256]
        each_span(before, False)
        tile = sum(
            dot(act_v[k, :, start : start + 128], gb_v[k], (0, 0)) for k in range(chips)
        )
        tiles[(start // 128) % 2] = tile.astype(BF)
        each_span([n for n, span in enumerate(spans) if span[0] == start], True)
    each_span([n for n, span in enumerate(spans) if span[0] >= part - 256], False)
    for n in range(len(spans)):
        number, _, send = span_copies(n)

        @pl.when(core == number)
        def _():
            send().wait_recv()

    for k in direct:
        dhn_copy(k).wait_recv()

    @pl.loop(0, rows // 16)
    def _(i):
        lines = pl.ds(pl.multiple_of(i * 16, 16), 16)
        grad[lines, :] += sum(got[k - 1, lines, :].astype(F32) for k in direct)

    for copy in store_outs:
        copy.wait()
    for k in range(chips):
        for j in range(chips):
            left_copy(k, j, 0).wait()
            left_copy(k, j, 1).wait()
        right_copy(k, 0).wait()
        right_copy(k, 1).wait()
    for k in direct:
        dhn_copy(k).wait_send()
        hn_copy(k).wait_send()
        if relayed:
            half_copy(k).wait_send()
            hn_copy(k, 1).wait_send()


def feed_forward(nf, hn, gbs, w_gu, w_d):
    chips = nf // 2
    rows, width = hn.shape
    part = w_d.shape[0]
    anywhere = pl.BlockSpec(memory_space=pl.ANY)
    dma = pltpu.SemaphoreType.DMA
    shape = jax.ShapeDtypeStruct
    return pl.pallas_call(
        functools.partial(feed_forward_kernel, nf),
        in_specs=[anywhere] * (chips + 3),
        out_specs=[pl.BlockSpec(memory_space=pltpu.VMEM)] + [anywhere] * (chips + 4),
        out_shape=[
            shape((rows, width), F32),
            shape((2, chips, rows, width // 2), BF),
            shape((2, chips, rows, 2 * part), BF),
            shape((part // 2, width), BF),
            shape((part // 2, width), BF),
        ]
        + [shape((rows, width), BF)] * chips,
        scratch_shapes=[
            pltpu.VMEM((width, 2 * part), BF),
            pltpu.VMEM((part, width), BF),
            pltpu.VMEM((chips, rows, width), BF),
            pltpu.VMEM((chips, rows, width), BF),
            pltpu.VMEM((chips, rows, part), F32),
            pltpu.VMEM((chips, rows, part), BF),
            pltpu.VMEM((chips, rows, 2 * part), BF),
            pltpu.VMEM((chips - 1, rows, width), BF),
            pltpu.VMEM((chips - 1, rows, width), BF),
            pltpu.VMEM((chips, rows, width), BF),
            pltpu.VMEM((2, 128, width), BF),
            pltpu.VMEM((2, rows // 2, width), BF),
            dma((2, chips)),
            dma((3,)),
            dma((chips,)),
            dma((2 * chips,)),
            dma((2 * chips,)),
            dma((chips,)),
            dma((chips,)),
            dma((chips,)),
            dma((chips, chips)),
            dma((chips, chips)),
            dma((chips, chips)),
            dma((chips,)),
            dma((chips,)),
            dma((chips,)),
            dma((part // 128 + 1,)),
            dma((part // 128 + 1,)),
            dma((part // 128 + 1,)),
        ],
        compiler_params=pltpu.CompilerParams(
            collective_id=3, has_side_effects=True, vmem_limit_bytes=60 << 20
        ),
        cost_estimate=pl.CostEstimate(
            flops=12 * chips * rows * width * part,
            bytes_accessed=40_000_000,
            transcendentals=chips * rows * part,
        ),
        name="feed_forward",
    )(hn, *gbs, w_gu, w_d)


def chunk_rows(rows):
    return max(r for r in range(16, 33, 16) if rows % r == 0)


def finish_kernel(nf, nc, *refs):
    pieces, refs = refs[: nf // 2], refs[nf // 2 - 1 :]
    sources, (outs, owns, ins, xs) = refs[:4], (refs[i : i + 4] for i in range(4, 20, 4))
    plane_send, plane_recv, local, in_sem, x_sem, first_send, second_send, out_sem = refs[20:]
    chips = nf // 2
    place, here = lax.axis_index("fsdp"), lax.axis_index("ctx")
    chip = place // 2
    lower = here < nc // 2
    depth = jnp.where(lower, here, nc - 1 - here)
    inner = jnp.where(lower, here + 1, here - 1)
    outer = jnp.where(lower, here - 1, here + 1)
    mesh_id = pl.DeviceIdType.MESH

    barrier = pltpu.get_barrier_semaphore()
    for k in range(1, chips):
        pl.semaphore_signal(
            barrier, inc=1, device_id={"fsdp": place ^ (2 * k)}, device_id_type=mesh_id
        )
    pl.semaphore_signal(barrier, inc=1, device_id={"ctx": inner}, device_id_type=mesh_id)

    @pl.when(depth > 0)
    def _():
        pl.semaphore_signal(barrier, inc=1, device_id={"ctx": outer}, device_id_type=mesh_id)
        pl.semaphore_wait(barrier, chips + 1)

    @pl.when(depth == 0)
    def _():
        pl.semaphore_wait(barrier, chips)

    def plane_copy(u, k):
        return pltpu.make_async_remote_copy(
            src_ref=sources[u].at[chip ^ k],
            dst_ref=owns[u].at[k],
            send_sem=plane_send.at[u, k],
            recv_sem=plane_recv.at[u, k],
            device_id={"fsdp": place ^ (2 * k)},
            device_id_type=mesh_id,
        )

    def local_copy(u, k):
        source = sources[u].at[chip] if u else pieces[k]
        return pltpu.make_async_copy(source, owns[u].at[k], local.at[u, k])

    for u in range(4):
        for k in range(chips):
            if u == 0 or k == 0:
                local_copy(u, k).start()
            else:
                plane_copy(u, k).start()

    units = [(0, k) for k in range(chips)] + [(u, None) for u in (1, 2, 3)]
    chunks = []
    for u, k in units:
        total = outs[u].shape[-2]
        size = chunk_rows(total)
        chunks += [(u, k, r, size) for r in range(0, total, size)]

    def views(c):
        u, k, r, size = chunks[c]
        rows = pl.ds(r, size)
        return [owns[u].at[k or 0, rows]] + [
            ref.at[rows] if k is None else ref.at[k, rows] for ref in (ins[u], xs[u], outs[u])
        ]

    def first_copy(c, across):
        own, arriving, x, _ = views(c)
        return pltpu.make_async_remote_copy(
            src_ref=own,
            dst_ref=x if across else arriving,
            send_sem=first_send.at[c],
            recv_sem=(x_sem if across else in_sem).at[c],
            device_id={"ctx": inner},
            device_id_type=mesh_id,
        )

    def second_copy(c, across):
        _, arriving, x, _ = views(c)
        return pltpu.make_async_remote_copy(
            src_ref=arriving if across else x,
            dst_ref=x,
            send_sem=second_send.at[c],
            recv_sem=x_sem.at[c],
            device_id={"ctx": outer},
            device_id_type=mesh_id,
        )

    def out_copy(c, across):
        _, arriving, x, out = views(c)
        return pltpu.make_async_copy(arriving if across else x, out, out_sem.at[c])

    def add_into(target, terms, size):
        @pl.loop(0, size // 16)
        def _(i):
            strip = pl.ds(pl.multiple_of(i * 16, 16), 16)
            target[strip, :] = sum(term[strip, :].astype(F32) for term in terms).astype(BF)

    def inward(c, level):
        u, k, r, size = chunks[c]
        own, arriving, _, _ = views(c)
        terms = [own]
        if r == 0:
            local_copy(u, k or 0).wait()
            if u >= 1:
                for j in range(1, chips):
                    plane_copy(u, j).wait_recv()
        if u >= 1:
            terms += [owns[u].at[j, pl.ds(r, size)] for j in range(1, chips)]
        if level > 0:
            first_copy(c, False).wait_recv()
            terms.append(arriving)
        if len(terms) > 1:
            add_into(own, terms, size)
        if c >= FLIGHT:
            first_copy(c - FLIGHT, False).wait_send()
        first_copy(c, level == top).start()

    def outward(c, level):
        size = chunks[c][3]
        own, arriving, x, _ = views(c)
        first_copy(c, True).wait_recv()
        if level == top:
            add_into(arriving, [own, x], size)
        out_copy(c, level == top).start()
        if level > 0:
            if c >= FLIGHT:
                second_copy(c - FLIGHT, False).wait_send()
            second_copy(c, level == top).start()

    top = nc // 2 - 1
    count = len(chunks)
    for level in range(top + 1):

        @pl.when(depth == level)
        def _():
            lag = 1 + 4 * (top - level)
            for t in range(count + lag):
                if t < count:
                    inward(t, level)
                if t >= lag:
                    outward(t - lag, level)
            for c in range(max(0, count - FLIGHT), count):
                first_copy(c, False).wait_send()
                if level > 0:
                    second_copy(c, False).wait_send()
            for c in range(count):
                out_copy(c, False).wait()

    for u in range(1, 4):
        for k in range(1, chips):
            plane_copy(u, k).wait_send()


def finish(nf, nc, pieces, sums):
    chips = nf // 2
    pieces_shape = (chips,) + pieces[0].shape
    shapes = [pieces_shape] + [x.shape[1:] for x in sums]
    count = sum(
        (shape[0] if len(shape) == 3 else 1) * (shape[-2] // chunk_rows(shape[-2]))
        for shape in shapes
    )
    anywhere = pl.BlockSpec(memory_space=pl.ANY)
    dma = pltpu.SemaphoreType.DMA
    return pl.pallas_call(
        functools.partial(finish_kernel, nf, nc),
        in_specs=[anywhere] * (chips + 3),
        out_specs=[anywhere] * 4,
        out_shape=[jax.ShapeDtypeStruct(shape, BF) for shape in shapes],
        scratch_shapes=[pltpu.VMEM(x, BF) for x in [pieces_shape] + [x.shape for x in sums]]
        + [pltpu.VMEM(shape, BF) for shape in shapes]
        + [pltpu.VMEM(shape, BF) for shape in shapes]
        + [dma((4, chips)), dma((4, chips)), dma((4, chips))]
        + [dma((count,))] * 5,
        compiler_params=pltpu.CompilerParams(
            collective_id=0, has_side_effects=True, vmem_limit_bytes=48 << 20
        ),
        cost_estimate=pl.CostEstimate(
            flops=200_000_000_000, bytes_accessed=60_000_000, transcendentals=0
        ),
        name="finish",
    )(*pieces, *sums)


def solution(mesh):
    nf, nc = mesh.shape["fsdp"], mesh.shape["ctx"]
    chips = nf // 2

    def swap(x, k):
        return lax.ppermute(x, "fsdp", [(i, i ^ k) for i in range(nf)])

    def plane_gather(x):
        if chips != 4:
            return [swap(x, 2 * k) for k in range(1, chips)]
        one, two = swap(x, 2), swap(x, 4)
        half = x.shape[0] // 2
        return [one, two, jnp.concatenate([swap(one[:half], 4), swap(two[half:], 2)], axis=0)]

    def cross(x, k):
        return lax.ppermute(x, "ctx", [(i, i ^ k) for i in range(nc)])

    def shards(
        tokens,
        attn_gain,
        w_query,
        w_key,
        w_value,
        w_out,
        ffn_gain,
        w_gate,
        w_up,
        w_down,
        block_table,
        positions,
        out_grad,
    ):
        place = lax.axis_index("fsdp")
        chip, core = place // 2, place % 2
        x = tokens[0].astype(F32)
        gb = out_grad[0]
        rows, width = x.shape
        hidden = w_gate.shape[1]
        part = hidden // chips
        shard = w_gate.shape[0]
        key_width = KV_HEADS * HEAD_DIM

        def core_sum(x):
            other = lax.dynamic_index_in_dim(x, 1 - core, 1, keepdims=False)
            mine = lax.dynamic_index_in_dim(x, core, 1, keepdims=False)
            return (mine.astype(F32) + swap(other, 1).astype(F32)).astype(BF)

        def rows_grad(left, right):
            columns = [left[:, i * shard : (i + 1) * shard] for i in range(nf)]
            even = jnp.concatenate(columns[::2], axis=1)
            odd = jnp.concatenate(columns[1::2], axis=1)
            mine = jnp.where(core == 0, even, odd)
            other = jnp.where(core == 0, odd, even)
            left = jnp.concatenate([mine, swap(other, 1)], axis=0)
            right = jnp.concatenate([right, swap(right, 1)], axis=0)
            return dot(left, right, (0, 0)).astype(BF).reshape(chips, shard, right.shape[1])


        half = HEAD_DIM // 2
        frequency = THETA ** (-jnp.arange(half, dtype=F32) * (2.0 / HEAD_DIM))
        angle = positions[0].astype(F32)[:, None] * frequency[None, :]
        cosine, sine = jnp.cos(angle), jnp.sin(angle)
        cos_lanes = jnp.tile(cosine, (1, 4))
        sin_lanes = jnp.tile(jnp.concatenate([-sine, sine], axis=1), (1, 2))
        blocks = 2 * nc
        stored = block_table.reshape(-1)
        number = jnp.arange(blocks, dtype=jnp.int32)
        where = jnp.sum(
            jnp.where(stored[None, :] == number[:, None], number[None, :], 0), axis=1
        )
        here = lax.axis_index("ctx")
        own = lax.dynamic_slice_in_dim(stored, 2 * here, 2)
        where = 2 * ((where // 2) ^ here) + where % 2
        table = jnp.concatenate([own, where]).astype(jnp.int32)

        order = chip ^ jnp.arange(chips, dtype=jnp.int32)
        both_gains = jnp.pad(jnp.stack([attn_gain, ffn_gain]), ((0, 14), (0, 0)))
        w_q, w_kv, w_o, w_gu, w_d, gains, kv = share_weights(
            nf,
            nc,
            w_query,
            w_key,
            w_value,
            w_out,
            w_gate,
            w_up,
            order,
            w_down,
            both_gains,
            tokens[0],
            cos_lanes,
            sin_lanes,
        )
        w_q = w_q.reshape(width, -1)
        w_kv = w_kv.reshape(width, -1)
        gb_sent, w_kv = lax.optimization_barrier((gb, w_kv))
        w_o = w_o.reshape(-1, width)
        w_gu = w_gu.reshape(width, 2 * part)
        w_d = w_d.reshape(part, width)
        gains = gains[:, :2].astype(F32).transpose(1, 0, 2).reshape(2, width)

        inverse_one = lax.rsqrt(jnp.mean(x * x, axis=1, keepdims=True) + EPS)
        unit_one = x * inverse_one
        xn = (unit_one * gains[0][None, :]).astype(BF)
        q_sum = dot(xn, w_q, (1, 0))
        gb_of = [gb] + [swap(gb_sent, 2 * k) for k in range(1, chips)]
        kv = kv.reshape(nc * rows, 2 * key_width)
        qr, o, ob, lse = attention_forward(table, q_sum, cos_lanes, sin_lanes, kv)
        h1 = x + dot(ob, w_o, (1, 0))
        inverse_two = lax.rsqrt(jnp.mean(h1 * h1, axis=1, keepdims=True) + EPS)
        unit_two = h1 * inverse_two
        hn = (unit_two * gains[1][None, :]).astype(BF)

        hn, gb_of = lax.optimization_barrier((hn, gb_of))

        fused = part % 128 == 0
        if fused:
            grad_hn, left, right, *downs = feed_forward(nf, hn, gb_of, w_gu, w_d)
            outs = downs[2:]
            left = left.reshape(2 * chips * rows, width // 2)
            right = right.reshape(2 * chips * rows, 2 * part)
            down_sum = (downs[0].astype(F32) + downs[1].astype(F32)).astype(BF)
        else:
            dhns = []
            hn_of, act_of, dgu_of = [], [], []
            for k, hn_k in enumerate([hn] + plane_gather(hn)):
                gu = dot(hn_k, w_gu, (1, 0))
                dact = dot(gb_of[k], w_d, (1, 1))
                gate, up = gu[:, :part], gu[:, part:]
                sg = jax.nn.sigmoid(gate)
                silu = gate * sg
                act = (silu * up).astype(BF)
                dgate = (dact * up * sg * (1.0 + gate * (1.0 - sg))).astype(BF)
                dgu = jnp.concatenate([dgate, (dact * silu).astype(BF)], axis=1)
                dhn_k = dot(dgu, w_gu, (1, 1))
                dhns.append(dhn_k.astype(BF) if k else dhn_k)
                hn_of.append(hn_k)
                act_of.append(act)
                dgu_of.append(dgu)
            got = [swap(dhns[k], 2 * k) for k in range(1, chips)]
            act_of, dgu_of, got[:-1], _ = lax.optimization_barrier(
                (act_of, dgu_of, got[:-1], dhns[1:])
            )
            grad_hn = dhns[0]
            for piece in got:
                grad_hn = grad_hn + piece.astype(F32)

            gb_all = jnp.concatenate(gb_of, axis=0)
            down = dot(jnp.concatenate(act_of, axis=0), gb_all, (0, 0)).astype(BF)
            down_sum = core_sum(down.reshape((1, 2) + w_down.shape))[0]
            left = jnp.concatenate(hn_of, axis=0)
            right = jnp.concatenate(dgu_of, axis=0)

        down_sum, left, right = lax.optimization_barrier((down_sum, left, right))
        down_sum = lax.psum_scatter(down_sum, "ctx", scatter_dimension=0, tiled=True)
        if fused:
            wide = dot(left, right, (0, 0)).astype(BF).reshape(chips, shard, 2 * part)
        else:
            wide = rows_grad(left, right)
        wide = [
            lax.dynamic_index_in_dim(wide, chip ^ k, 0, keepdims=False) for k in range(chips)
        ]
        wide, grad_hn = lax.optimization_barrier((wide, grad_hn))
        wide = [swap(piece, 2 * k) if k else piece for k, piece in enumerate(wide)]

        gain_two_grad = jnp.sum(grad_hn * unit_two, axis=0)
        grad_unit = grad_hn * gains[1][None, :]
        dh1 = gb.astype(F32) + inverse_two * (
            grad_unit - unit_two * jnp.mean(grad_unit * unit_two, axis=1, keepdims=True)
        )
        dab = dh1.astype(BF)
        dob = dot(dab, w_o, (1, 1)).astype(BF)
        dq, dkv = attention_backward(table, qr, dob, o, lse, kv, cos_lanes, sin_lanes)
        xn, ob, dab, _ = lax.optimization_barrier((xn, ob, dab, dq))
        if not fused:
            act_of, _ = lax.optimization_barrier((act_of, dq))
            outs = [dot(act, w_d, (1, 0)).astype(BF) for act in act_of]
        sent = outs[1:]
        own = own_key_grads(nc, dkv, cos_lanes, sin_lanes)
        own, wide, down_sum = lax.optimization_barrier((own, wide, down_sum))
        down_sum = lax.all_gather(down_sum, "ctx", axis=0, tiled=True)
        ob, dab, _ = lax.optimization_barrier((ob, dab, own))
        out_term = rows_grad(ob, dab)
        dqkv = jnp.concatenate([dq, own], axis=1)
        grad_xn = dot(dq, w_q, (1, 1)) + dot(own, w_kv, (1, 1))
        gain_one_grad = jnp.sum(grad_xn * unit_one, axis=0)
        grad_unit = grad_xn * gains[0][None, :]
        tokens_grad = dh1 + inverse_one * (
            grad_unit - unit_one * jnp.mean(grad_unit * unit_one, axis=1, keepdims=True)
        )
        qkv_term = rows_grad(xn, dqkv)

        gains_of = jnp.stack([gain_one_grad, gain_two_grad]).reshape(2, chips, 2, shard)
        other = lax.dynamic_index_in_dim(gains_of, 1 - core, 2, keepdims=False)
        mine = lax.dynamic_index_in_dim(gains_of, core, 2, keepdims=False)
        gains_of = (mine + swap(other, 1)).transpose(1, 0, 2).reshape(chips, 1, 2 * shard)
        gains_of = jnp.pad(gains_of.astype(BF), ((0, 0), (0, 15), (0, 0)))
        wide, down_sum, out_term, qkv_term, outs[0], sent = lax.optimization_barrier(
            (wide, down_sum, out_term, qkv_term, outs[0], sent)
        )
        gu_sum, out_sum, qkv_sum, gain_sum = finish(
            nf, nc, wide, [out_term, qkv_term, gains_of]
        )
        h1, gain_sum = lax.optimization_barrier((h1, gain_sum))
        branch = h1 + outs[0].astype(F32)
        for k in range(1, chips):
            branch = branch + swap(sent[k - 1], 2 * k).astype(F32)
        layer_out = branch.astype(BF)
        qkv_sum = qkv_sum.astype(F32)
        gain_sum = gain_sum[0].reshape(2, shard).astype(F32)
        gate_grad, up_grad = place_columns(order, gu_sum)
        query_width = HEADS * HEAD_DIM
        return (
            layer_out.reshape(1, rows, width),
            tokens_grad.reshape(1, rows, width),
            gain_sum[0],
            qkv_sum[:, :query_width],
            qkv_sum[:, query_width : query_width + key_width],
            qkv_sum[:, query_width + key_width :],
            out_sum.astype(F32),
            gain_sum[1],
            gate_grad,
            up_grad,
            down_sum.astype(F32),
        )

    weight = P("fsdp", None)
    activation = P("fsdp", "ctx", None)
    return jax.shard_map(
        shards,
        mesh=mesh,
        in_specs=(
            activation,
            P("fsdp"),
            weight,
            weight,
            weight,
            weight,
            P("fsdp"),
            weight,
            weight,
            weight,
            P(),
            P("fsdp", "ctx"),
            activation,
        ),
        out_specs=(
            activation,
            activation,
            P("fsdp"),
            weight,
            weight,
            weight,
            weight,
            P("fsdp"),
            weight,
            weight,
            weight,
        ),
        check_vma=False,
    )
```

```python
import functools

import jax
import jax.numpy as jnp
from jax import lax
from jax.experimental import pallas as pl
from jax.experimental.pallas import tpu as pltpu
from jax.sharding import PartitionSpec as P

HEADS = 32
KV_HEADS = 4
HEAD_DIM = 64
GROUP = HEADS // KV_HEADS
PAIRS = GROUP // 2
LANES = 2 * HEAD_DIM
STACK = PAIRS * LANES

EPS = 1e-05
THETA = 10000.0
NEG = -1e30
FLIGHT = 2
BF = jnp.bfloat16
F32 = jnp.float32


def dot(left, right, contract, out=F32):
    return lax.dot_general(
        left, right, ((contract[:1], contract[1:]), ((), ())), preferred_element_type=out
    )


def swap_halves(z):
    lane = lax.broadcasted_iota(jnp.int32, z.shape, 1)
    first = (lane % HEAD_DIM) < (HEAD_DIM // 2)
    return jnp.where(
        first,
        pltpu.roll(z, LANES - HEAD_DIM // 2, 1),
        pltpu.roll(z, HEAD_DIM // 2, 1),
    )


def split_heads(rows):
    lane = lax.broadcasted_iota(jnp.int32, rows.shape, 1)
    zero = jnp.zeros_like(rows)
    return jnp.concatenate(
        [jnp.where(lane < HEAD_DIM, rows, zero), jnp.where(lane >= HEAD_DIM, rows, zero)], axis=0
    )


def join_heads(columns):
    half = columns.shape[1] // 2
    sub = lax.broadcasted_iota(jnp.int32, (LANES, half), 0)
    return jnp.where(sub < HEAD_DIM, columns[:, :half], columns[:, half:]).T


def stack_pairs(ref, rows):
    return jnp.concatenate([ref[rows, p * LANES : (p + 1) * LANES] for p in range(PAIRS)], axis=0)


def two_blocks(ref, table, j, block):
    parts = [
        ref[pl.ds(pl.multiple_of(table[2 + 2 * j + i] * block, block), block), :] for i in range(2)
    ]
    return jnp.concatenate(parts, axis=0)


def causal(scores, j, own, block):
    key = lax.broadcasted_iota(jnp.int32, scores.shape, 0) + j * (2 * block)
    query = lax.broadcasted_iota(jnp.int32, scores.shape, 1) % block + own * block
    return jnp.where(key <= query, scores, NEG)


def head_twice(pair, group):
    wide = pair.astype(F32)
    lane = lax.broadcasted_iota(jnp.int32, wide.shape, 1)
    keep = (lane < HEAD_DIM) == (group % 2 == 0)
    return jnp.where(keep, wide, pltpu.roll(wide, HEAD_DIM, 1)).astype(BF)


def attention_forward_kernel(
    table,
    q_ref,
    cos_ref,
    sin_ref,
    k_pair,
    v_pair,
    qr_ref,
    o_ref,
    ob_ref,
    lse_ref,
    qm,
    m,
    l,
    acc,
    k_ref,
    v_ref,
):
    block = q_ref.shape[0] // 2
    group = pl.program_id(0)
    k_ref[...] = head_twice(k_pair[...], group)
    v_ref[...] = head_twice(v_pair[...], group)
    for h in range(2):
        rows = slice(h * block, (h + 1) * block)
        cosine, sine = cos_ref[rows, :], sin_ref[rows, :]
        for p in range(PAIRS):
            lanes = slice(p * LANES, (p + 1) * LANES)
            z = q_ref[rows, lanes]
            qr_ref[rows, lanes] = (z * cosine + swap_halves(z) * sine).astype(BF)
        scaled = stack_pairs(qr_ref, rows).astype(F32) * (HEAD_DIM**-0.5)
        qm[...] = split_heads(scaled).astype(BF)
        m[...] = jnp.full_like(m, NEG)
        l[...] = jnp.zeros_like(l)
        acc[...] = jnp.zeros_like(acc)
        own = table[h]

        def step(j, masked):
            keys = two_blocks(k_ref, table, j, block)
            values = two_blocks(v_ref, table, j, block)
            s = dot(keys, qm[...], (1, 1))
            if masked:
                s = causal(s, j, own, block)
            before = m[...]
            now = jnp.maximum(before, jnp.max(s, axis=0, keepdims=True))
            p = jnp.exp(s - now)
            decay = jnp.exp(before - now)
            l[...] = l[...] * decay + jnp.sum(p, axis=0, keepdims=True)
            acc[...] = acc[...] * decay + dot(values, p.astype(BF), (0, 0))
            m[...] = now

        last = own // 2

        @pl.loop(0, last)
        def _(j):
            step(j, False)

        step(last, True)
        lse_ref[0, h : h + 1, :] = m[...] + jnp.log(l[...])
        o = join_heads(acc[...] / l[...])
        for p in range(PAIRS):
            lanes = slice(p * LANES, (p + 1) * LANES)
            piece = o[p * block : (p + 1) * block, :]
            o_ref[rows, lanes] = piece
            ob_ref[rows, lanes] = piece.astype(BF)


def attention_forward(table, q, cosine, sine, kv):
    rows, length = q.shape[0], kv.shape[0]
    query_width = HEADS * HEAD_DIM
    columns = pl.BlockSpec((rows, STACK), lambda g, t: (0, g))
    whole = pl.BlockSpec((rows, LANES), lambda g, t: (0, 0))
    key_pair = pl.BlockSpec((length, LANES), lambda g, t: (0, g // 2))
    value_pair = pl.BlockSpec((length, LANES), lambda g, t: (0, KV_HEADS // 2 + g // 2))
    wide = GROUP * (rows // 2)
    return pl.pallas_call(
        attention_forward_kernel,
        grid_spec=pltpu.PrefetchScalarGridSpec(
            num_scalar_prefetch=1,
            grid=(KV_HEADS,),
            in_specs=[columns, whole, whole, key_pair, value_pair],
            out_specs=[
                columns,
                columns,
                columns,
                pl.BlockSpec((1, 2, wide), lambda g, t: (g, 0, 0)),
            ],
            scratch_shapes=[
                pltpu.VMEM((wide, LANES), BF),
                pltpu.VMEM((1, wide), F32),
                pltpu.VMEM((1, wide), F32),
                pltpu.VMEM((LANES, wide), F32),
                pltpu.VMEM((length, LANES), BF),
                pltpu.VMEM((length, LANES), BF),
            ],
        ),
        out_shape=[
            jax.ShapeDtypeStruct((rows, query_width), BF),
            jax.ShapeDtypeStruct((rows, query_width), F32),
            jax.ShapeDtypeStruct((rows, query_width), BF),
            jax.ShapeDtypeStruct((KV_HEADS, 2, wide), F32),
        ],
        compiler_params=pltpu.CompilerParams(vmem_limit_bytes=32 << 20),
        cost_estimate=pl.CostEstimate(
            flops=8 * HEADS * rows * length * HEAD_DIM,
            bytes_accessed=16 * rows * HEADS * HEAD_DIM,
            transcendentals=HEADS * rows * length,
        ),
        name="attention_forward",
    )(table, q, cosine, sine, kv, kv)


def attention_backward_kernel(
    table,
    qr_ref,
    do_ref,
    o_ref,
    lse_ref,
    k_pair,
    v_pair,
    cos_ref,
    sin_ref,
    dq_ref,
    dkv_ref,
    qm,
    dom,
    dqt,
    k_ref,
    v_ref,
    dk_ref,
    dv_ref,
):
    block = qr_ref.shape[0] // 2
    group = pl.program_id(0)
    k_ref[...] = head_twice(k_pair[...], group)
    v_ref[...] = head_twice(v_pair[...], group)
    dk_ref[...] = jnp.zeros_like(dk_ref)
    dv_ref[...] = jnp.zeros_like(dv_ref)
    for h in range(2):
        rows = slice(h * block, (h + 1) * block)
        scaled = stack_pairs(qr_ref, rows).astype(F32) * (HEAD_DIM**-0.5)
        qm[...] = split_heads(scaled).astype(BF)
        grads = stack_pairs(do_ref, rows).astype(F32)
        dom[...] = split_heads(grads).astype(BF)
        product = (grads * stack_pairs(o_ref, rows)).T
        inner = jnp.concatenate(
            [
                jnp.sum(product[:HEAD_DIM], axis=0, keepdims=True),
                jnp.sum(product[HEAD_DIM:], axis=0, keepdims=True),
            ],
            axis=1,
        )
        lse = lse_ref[0, h : h + 1, :]
        dqt[...] = jnp.zeros_like(dqt)
        own = table[h]

        def step(j, masked):
            keys = two_blocks(k_ref, table, j, block)
            values = two_blocks(v_ref, table, j, block)
            s = dot(keys, qm[...], (1, 1))
            if masked:
                s = causal(s, j, own, block)
            p = jnp.exp(s - lse)
            dp = dot(values, dom[...], (1, 1))
            ds = (p * (dp - inner)).astype(BF)
            dv = dot(p.astype(BF), dom[...], (1, 0))
            dk = dot(ds, qm[...], (1, 0))
            dqt[...] += dot(keys, ds, (0, 0))
            for i in range(2):
                at = pl.ds(pl.multiple_of(table[2 + 2 * j + i] * block, block), block)
                dk_ref[at, :] += dk[i * block : (i + 1) * block]
                dv_ref[at, :] += dv[i * block : (i + 1) * block]

        last = own // 2

        @pl.loop(0, last)
        def _(j):
            step(j, False)

        step(last, True)
        cosine, sine = cos_ref[rows, :], sin_ref[rows, :]
        dq = join_heads(dqt[...] * (HEAD_DIM**-0.5))
        for p in range(PAIRS):
            z = dq[p * block : (p + 1) * block, :]
            dq_ref[rows, p * LANES : (p + 1) * LANES] = (
                z * cosine - swap_halves(z) * sine
            ).astype(BF)
    lane = lax.broadcasted_iota(jnp.int32, dk_ref.shape, 1)
    keep = (lane < HEAD_DIM) == (group % 2 == 0)
    for i, ref in enumerate((dk_ref, dv_ref)):
        both = ref[...] + pltpu.roll(ref[...], HEAD_DIM, 1)
        dkv_ref[i] = jnp.where(keep, both, dkv_ref[i].astype(F32)).astype(BF)


def attention_backward(table, qr, grads, o, lse, kv, cosine, sine):
    rows, length = qr.shape[0], kv.shape[0]
    columns = pl.BlockSpec((rows, STACK), lambda g, t: (0, g))
    whole = pl.BlockSpec((rows, LANES), lambda g, t: (0, 0))
    key_pair = pl.BlockSpec((length, LANES), lambda g, t: (0, g // 2))
    value_pair = pl.BlockSpec((length, LANES), lambda g, t: (0, KV_HEADS // 2 + g // 2))
    wide = GROUP * (rows // 2)
    return pl.pallas_call(
        attention_backward_kernel,
        grid_spec=pltpu.PrefetchScalarGridSpec(
            num_scalar_prefetch=1,
            grid=(KV_HEADS,),
            in_specs=[
                columns,
                columns,
                columns,
                pl.BlockSpec((1, 2, wide), lambda g, t: (g, 0, 0)),
                key_pair,
                value_pair,
                whole,
                whole,
            ],
            out_specs=[columns, pl.BlockSpec((2, length, LANES), lambda g, t: (0, 0, g // 2))],
            scratch_shapes=[
                pltpu.VMEM((wide, LANES), BF),
                pltpu.VMEM((wide, LANES), BF),
                pltpu.VMEM((LANES, wide), F32),
                pltpu.VMEM((length, LANES), BF),
                pltpu.VMEM((length, LANES), BF),
                pltpu.VMEM((length, LANES), F32),
                pltpu.VMEM((length, LANES), F32),
            ],
        ),
        out_shape=[
            jax.ShapeDtypeStruct(qr.shape, BF),
            jax.ShapeDtypeStruct((2, length, KV_HEADS * HEAD_DIM), BF),
        ],
        compiler_params=pltpu.CompilerParams(vmem_limit_bytes=32 << 20),
        cost_estimate=pl.CostEstimate(
            flops=20 * HEADS * rows * length * HEAD_DIM,
            bytes_accessed=16 * rows * HEADS * HEAD_DIM,
            transcendentals=HEADS * rows * length,
        ),
        name="attention_backward",
    )(table, qr, grads, o, lse, kv, kv, cosine, sine)


def own_key_grads_kernel(nc, dkv_ref, cos_ref, sin_ref, out_ref, got, send_sem, recv_sem):
    rows, width = out_ref.shape[0], out_ref.shape[1] // 2
    here = lax.axis_index("ctx")
    mesh_id = pl.DeviceIdType.MESH
    barrier = pltpu.get_barrier_semaphore()
    for k in range(1, nc):
        pl.semaphore_signal(barrier, inc=1, device_id={"ctx": here ^ k}, device_id_type=mesh_id)
    pl.semaphore_wait(barrier, nc - 1)

    def copy(k):
        source = dkv_ref.at[:, pl.ds(k * rows, rows)]
        if k == 0:
            return pltpu.make_async_copy(source, got.at[0], recv_sem.at[0])
        return pltpu.make_async_remote_copy(
            src_ref=source,
            dst_ref=got.at[k],
            send_sem=send_sem.at[k],
            recv_sem=recv_sem.at[k],
            device_id={"ctx": here ^ k},
            device_id_type=mesh_id,
        )

    for k in reversed(range(nc)):
        copy(k).start()
    for k in range(nc):
        copy(k).wait()

    def total(i, lanes):
        return sum(got[k, i, :, lanes].astype(F32) for k in range(nc))

    for p in range(width // LANES):
        lanes = slice(p * LANES, (p + 1) * LANES)
        z = total(0, lanes)
        out_ref[:, lanes] = (z * cos_ref[...] - swap_halves(z) * sin_ref[...]).astype(BF)
        out_ref[:, width + p * LANES : width + (p + 1) * LANES] = total(1, lanes).astype(BF)


def own_key_grads(nc, dkv, cosine, sine):
    rows, width = dkv.shape[1] // nc, dkv.shape[2]
    vmem = pl.BlockSpec(memory_space=pltpu.VMEM)
    return pl.pallas_call(
        functools.partial(own_key_grads_kernel, nc),
        in_specs=[pl.BlockSpec(memory_space=pl.ANY), vmem, vmem],
        out_specs=vmem,
        out_shape=jax.ShapeDtypeStruct((rows, 2 * width), BF),
        scratch_shapes=[
            pltpu.VMEM((nc, 2, rows, width), BF),
            pltpu.SemaphoreType.DMA((nc,)),
            pltpu.SemaphoreType.DMA((nc,)),
        ],
        compiler_params=pltpu.CompilerParams(collective_id=2, has_side_effects=True),
        name="own_key_grads",
    )(dkv, cosine, sine)


def share_kernel(nf, nc, low, size, raw, *refs):
    count = 2 if raw else 1
    w_query, w_key, w_value, w_out, *halves, down, gains, tokens, cosine, sine = refs[: 9 + count]
    refs = refs[9 + count :]
    query, key_value, out, wide, downs, all_gains, kv_all = refs[:7]
    query_own, key_value_own, out_own, wide_own, down_own, gains_own = refs[7:13]
    (local, plane_send, plane_recv, along_send, along_recv, core_send, core_recv) = refs[13:20]
    (gain_send, gain_recv, down_sem, gather_send, gather_recv, gather_core) = refs[20:26]
    w_kv, gains_v, xn, kv, kv_load, kv_send, kv_recv = refs[26:]
    chips = nf // 2
    place, here = lax.axis_index("fsdp"), lax.axis_index("ctx")
    chip, core = place // 2, place % 2
    mesh_id = pl.DeviceIdType.MESH
    shard, columns = wide.shape[1:]
    part = columns // 2
    key_width = w_key.shape[1]
    gathered = [
        (w_query, query, query_own, pl.ds(0, w_query.shape[1])),
        (w_key, key_value, key_value_own, pl.ds(0, key_width)),
        (w_value, key_value, key_value_own, pl.ds(key_width, key_width)),
        (w_out, out, out_own, pl.ds(0, w_out.shape[1])),
    ]

    barrier = pltpu.get_barrier_semaphore()

    def greet(target):
        pl.semaphore_signal(barrier, inc=1, device_id=target, device_id_type=mesh_id)

    for j in range(1, nf):
        greet({"fsdp": place ^ j})
    for pos in range(nc):

        @pl.when(here == pos)
        def _():
            for i in range(nc):
                if i != pos:
                    greet({"ctx": i})

    pl.semaphore_wait(barrier, nf - 1 + nc - 1)

    def remote(source, target, sends, recvs, where):
        return pltpu.make_async_remote_copy(
            src_ref=source,
            dst_ref=target,
            send_sem=sends,
            recv_sem=recvs,
            device_id=where,
            device_id_type=mesh_id,
        )

    def piece(k, h, rows):
        if raw:
            at = pl.ds(pl.multiple_of((chip ^ k) * part, 128), part)
            return halves[h].at[rows, at]
        return halves[0].at[k, rows]

    def side(h):
        return pl.ds(h * part, part) if raw else pl.ds(0, columns)

    def rows_of(share):
        return pl.ds(low + share * size, size)

    def plane_copy(k, kind, h):
        rows = rows_of(here) if kind else pl.ds(0, low)
        return remote(
            piece(k, h, rows),
            wide.at[place, rows, side(h)],
            plane_send.at[kind, k, h],
            plane_recv.at[kind, k, h],
            {"fsdp": place ^ (2 * k)},
        )

    def along_copy(k, share, up, target):
        block = wide.at[place ^ (2 * k), rows_of(share)]
        return remote(
            block, block, along_send.at[up, share, k], along_recv.at[share, k], {"ctx": target}
        )

    def core_copy(k, share):
        rows = rows_of(share) if share < nc else pl.ds(0, low)
        block = wide.at[place ^ (2 * k), rows]
        return remote(
            block, block, core_send.at[k, share], core_recv.at[k, share], {"fsdp": place ^ 1}
        )

    def own_core_copy(h):
        return remote(
            piece(0, h, pl.ds(0, shard)),
            wide.at[place, :, side(h)],
            core_send.at[0, h],
            core_recv.at[0, h],
            {"fsdp": place ^ 1},
        )

    half = shard // 2
    relayed = chips == 4

    def gather_copy(u, k, relay=0):
        source, target, _, at = gathered[u]
        if relay:
            owner, rows = place ^ (2 * (3 - k)), pl.ds((2 - k) * half, half)
            source = target.at[owner, rows, at]
        else:
            owner, rows = place, pl.ds(0, shard)
        number = 2 * k + relay
        return remote(
            source,
            target.at[owner, rows, at],
            gather_send.at[u, number],
            gather_recv.at[u, number],
            {"fsdp": place ^ (2 * k)},
        )

    def gather_core_copy(u, k):
        source, target, _, at = gathered[u]
        block = target.at[place ^ (2 * k), :, at]
        return remote(
            block if k else source,
            block,
            gather_core.at[0, u, k],
            gather_core.at[1, u, k],
            {"fsdp": place ^ 1},
        )

    def down_copy():
        return remote(down, downs.at[core], down_sem.at[0], down_sem.at[1], {"fsdp": place ^ 1})

    def gain_copy(j):
        return remote(
            gains, all_gains.at[place], gain_send.at[j], gain_recv.at[j], {"fsdp": place ^ j}
        )

    direct = (1, 2) if relayed else tuple(range(1, chips))
    for k in range(1, chips):
        for h in range(count):
            plane_copy(k, 1, h).start()
    for j in range(1, nf):
        gain_copy(j).start()
    for h in range(count):
        own_core_copy(h).start()
    for u in range(4):
        gather_core_copy(u, 0).start()
    down_copy().start()
    own = [(source, stage.at[:, at], None) for source, _, stage, at in gathered]
    own += [(piece(0, h, pl.ds(0, shard)), wide_own.at[:, side(h)], None) for h in range(count)]
    own += [(down, down_own, downs.at[core]), (gains, gains_own, all_gains.at[place])]
    back = [
        (query_own, query.at[place]),
        (key_value_own, key_value.at[place]),
        (out_own, out.at[place]),
        (wide_own, wide.at[place]),
        (down_own, downs.at[core]),
        (gains_own, all_gains.at[place]),
    ]
    for i, (source, stage, _) in enumerate(own):
        pltpu.make_async_copy(source, stage, local.at[0, i]).start()
    for i, (source, stage, _) in enumerate(own):
        pltpu.make_async_copy(source, stage, local.at[0, i]).wait()
    for i, (stage, target) in enumerate(back):
        pltpu.make_async_copy(stage, target, local.at[1, i]).start()

    for k in range(1, chips):
        for h in range(count):
            plane_copy(k, 1, h).wait_send()
    for u in (1, 2, 0, 3):
        for k in direct:
            gather_copy(u, k).start()

    def kv_copy(k):
        if k == 0:
            return pltpu.make_async_copy(kv, kv_all.at[0], kv_recv.at[0])
        return remote(kv, kv_all.at[k], kv_send.at[k], kv_recv.at[k], {"ctx": here ^ k})

    def make_kv():
        for i in (len(back) - 1, 1):
            stage, target = back[i]
            pltpu.make_async_copy(stage, target, local.at[1, i]).wait()
        for j in range(1, nf):
            gain_copy(j).wait_recv()
        for u in (1, 2):
            if relayed:
                for k in direct:
                    gather_copy(u, k, 1).wait_recv()
                gather_core_copy(u, 3).start()
            for k in range(chips):
                gather_core_copy(u, k).wait_recv()
        loads = [
            pltpu.make_async_copy(key_value, w_kv, kv_load.at[0]),
            pltpu.make_async_copy(all_gains, gains_v, kv_load.at[1]),
        ]
        for copy in loads:
            copy.start()
        for copy in loads:
            copy.wait()
        for i in range(0, xn.shape[0], 16):
            x = tokens[i : i + 16, :].astype(F32)
            unit = x * lax.rsqrt(jnp.mean(x * x, axis=1, keepdims=True) + EPS)
            for f in range(nf):
                lanes = slice(f * shard, (f + 1) * shard)
                gain = gains_v[f, 0:1, :].astype(F32)
                xn[i : i + 16, lanes] = (unit[:, lanes] * gain).astype(BF)
        total = sum(
            dot(xn[:, f * shard : (f + 1) * shard], w_kv[f], (1, 0)) for f in range(nf)
        )
        for p in range(0, key_width, LANES):
            z = total[:, p : p + LANES]
            kv[:, p : p + LANES] = (z * cosine[...] + swap_halves(z) * sine[...]).astype(BF)
        kv[:, key_width:] = total[:, key_width:].astype(BF)
        for k in reversed(range(nc)):
            kv_copy(k).start()

    for pos in range(nc):

        @pl.when(here == pos)
        def _():
            def pass_on(k, share):
                if share <= pos < nc - 1:
                    along_copy(k, share, 1, pos + 1).start()
                if share >= pos > 0:
                    along_copy(k, share, 0, pos - 1).start()
                core_copy(k, share).start()

            for k in range(1, chips):
                for h in range(count):
                    plane_copy(k, 1, h).wait_recv()
                pass_on(k, pos)
            if low:
                for k in range(1, chips):
                    for h in range(count):
                        plane_copy(k, 0, h).start()
            def gather_on(u):
                for k in direct:
                    gather_copy(u, k).wait_recv()
                    if relayed:
                        gather_copy(u, 3 - k, 1).start()
                    gather_core_copy(u, k).start()

            groups = [(), (1, 2), (0, 3)]
            for d in range(1, max(nc, len(groups))):
                for share in (pos - d, pos + d):
                    if 0 <= share < nc:
                        for k in range(1, chips):
                            along_copy(k, share, 0, 0).wait_recv()
                            pass_on(k, share)
                for u in groups[d] if d < len(groups) else ():
                    if u == 3:
                        make_kv()
                    gather_on(u)
            if low:
                for k in range(1, chips):
                    for h in range(count):
                        plane_copy(k, 0, h).wait_recv()
                    core_copy(k, nc).start()
            if relayed:
                for u in (0, 3):
                    for k in direct:
                        gather_copy(u, k, 1).wait_recv()
                    gather_core_copy(u, 3).start()
            for k in range(1, chips):
                for share in range(nc):
                    if share <= pos < nc - 1:
                        along_copy(k, share, 1, pos + 1).wait_send()
                    if share >= pos > 0:
                        along_copy(k, share, 0, pos - 1).wait_send()

    for h in range(count):
        own_core_copy(h).wait()
    for k in range(1, chips):
        for share in range(nc + 1 if low else nc):
            core_copy(k, share).wait()
        if low:
            for h in range(count):
                plane_copy(k, 0, h).wait_send()
    for j in range(1, nf):
        gain_copy(j).wait_send()
    for k in range(nc):
        kv_copy(k).wait()
    for u in range(4):
        for k in direct:
            gather_copy(u, k).wait_send()
            if relayed:
                gather_copy(u, k, 1).wait_send()
        for k in range(chips):
            gather_core_copy(u, k).wait_send()
            if u in (0, 3):
                gather_core_copy(u, k).wait_recv()
    down_copy().wait()
    for i, (stage, target) in enumerate(back):
        if i not in (len(back) - 1, 1):
            pltpu.make_async_copy(stage, target, local.at[1, i]).wait()


def share_weights(
    nf,
    nc,
    w_query,
    w_key,
    w_value,
    w_out,
    w_gate,
    w_up,
    order,
    down,
    gains,
    tokens,
    cosine,
    sine,
):
    chips = nf // 2
    shard, hidden = w_gate.shape
    part = hidden // chips
    size = shard // nc
    low = shard - nc * size
    raw = part % 128 == 0
    halves = [w_gate, w_up]
    if not raw:
        both = [w.reshape(shard, chips, part).transpose(1, 0, 2) for w in halves]
        halves = [jnp.take(jnp.concatenate(both, axis=2), order, axis=0)]
    anywhere = pl.BlockSpec(memory_space=pl.ANY)
    dma = pltpu.SemaphoreType.DMA
    kv_shape = (tokens.shape[0], 2 * w_key.shape[1])
    widths = [w_query.shape[1], 2 * w_key.shape[1], w_out.shape[1], 2 * part]
    return pl.pallas_call(
        functools.partial(share_kernel, nf, nc, low, size, raw),
        in_specs=[anywhere] * (6 + len(halves)) + [pl.BlockSpec(memory_space=pltpu.VMEM)] * 3,
        out_specs=[anywhere] * 7,
        out_shape=[jax.ShapeDtypeStruct((nf, shard, width), BF) for width in widths]
        + [
            jax.ShapeDtypeStruct((2,) + down.shape, BF),
            jax.ShapeDtypeStruct((nf,) + gains.shape, BF),
            jax.ShapeDtypeStruct((nc,) + kv_shape, BF),
        ],
        scratch_shapes=[pltpu.VMEM((shard, width), BF) for width in widths]
        + [
            pltpu.VMEM(down.shape, BF),
            pltpu.VMEM(gains.shape, BF),
            dma((2, 8)),
            dma((2, chips, 2)),
            dma((2, chips, 2)),
            dma((2, nc, chips)),
            dma((nc, chips)),
            dma((chips, nc + 1)),
            dma((chips, nc + 1)),
            dma((nf,)),
            dma((nf,)),
            dma((2,)),
            dma((4, 2 * chips)),
            dma((4, 2 * chips)),
            dma((2, 4, chips)),
            pltpu.VMEM((nf, shard, widths[1]), BF),
            pltpu.VMEM((nf,) + gains.shape, BF),
            pltpu.VMEM(tokens.shape, BF),
            pltpu.VMEM(kv_shape, BF),
            dma((2,)),
            dma((nc,)),
            dma((nc,)),
        ],
        compiler_params=pltpu.CompilerParams(
            collective_id=1, has_side_effects=True, vmem_limit_bytes=56 << 20
        ),
        name="share_weights",
    )(w_query, w_key, w_value, w_out, *halves, down, gains, tokens, cosine, sine)


def place_columns_kernel(order, both_ref, gate_ref, up_ref):
    part = gate_ref.shape[1]
    gate_ref[...] = both_ref[0, :, :part].astype(F32)
    up_ref[...] = both_ref[0, :, part:].astype(F32)


def place_columns(order, both):
    parts, shard, part = both.shape[0], both.shape[1], both.shape[2] // 2
    out = jax.ShapeDtypeStruct((shard, parts * part), F32)
    if part % 128:
        both = jnp.take(both, order, axis=0).transpose(1, 0, 2).astype(F32)
        return [both[:, :, i * part : (i + 1) * part].reshape(out.shape) for i in range(2)]
    columns = pl.BlockSpec((shard, part), lambda k, t: (0, t[k]))
    return pl.pallas_call(
        place_columns_kernel,
        grid_spec=pltpu.PrefetchScalarGridSpec(
            num_scalar_prefetch=1,
            grid=(parts,),
            in_specs=[pl.BlockSpec((1, shard, 2 * part), lambda k, t: (k, 0, 0))],
            out_specs=[columns, columns],
        ),
        out_shape=[out, out],
        name="place_columns",
    )(order, both)


def feed_forward_kernel(nf, *refs):
    chips = nf // 2
    hn, *gbs, w_gu, w_d, grad, left, right, down_kept, down_got = refs[: chips + 8]
    outs, refs = refs[chips + 8 : 2 * chips + 8], refs[2 * chips + 8 :]
    w_gu_v, w_d_v, hn_v, gb_v, dact_v, act_v, dgu_v, sent, got, outs_v = refs[:10]
    tiles, halves, half_sem, *sems = refs[10:]
    load, load_gb, hn_send, hn_recv, dhn_send, dhn_recv, store = sems[:7]
    left_local, left_send, left_recv, right_local, right_send, right_recv = sems[7:13]
    down_local, down_send, down_recv = sems[13:]
    place = lax.axis_index("fsdp")
    core = place % 2
    rows, width = hn.shape
    part = w_d.shape[0]
    shard = width // nf
    half = rows // 2
    relayed = chips == 4
    direct = (1, 2) if relayed else tuple(range(1, chips))
    mesh_id = pl.DeviceIdType.MESH

    barrier = pltpu.get_barrier_semaphore()
    for j in [1] + [2 * k for k in range(1, chips)]:
        pl.semaphore_signal(
            barrier, inc=1, device_id={"fsdp": place ^ j}, device_id_type=mesh_id
        )
    pl.semaphore_wait(barrier, chips)

    def remote(source, target, sends, recvs, step):
        return pltpu.make_async_remote_copy(
            src_ref=source,
            dst_ref=target,
            send_sem=sends,
            recv_sem=recvs,
            device_id={"fsdp": place ^ step},
            device_id_type=mesh_id,
        )

    def hn_copy(k, relay=0):
        at = 2 * k + relay
        if relay:
            lines = pl.ds((2 - k) * half, half)
            source, target = hn_v.at[3 - k, lines], hn_v.at[3, lines]
        else:
            source, target = hn, hn_v.at[k]
        return remote(source, target, hn_send.at[at], hn_recv.at[at], 2 * k)

    def dhn_copy(k):
        return remote(sent.at[k - 1], got.at[k - 1], dhn_send.at[k], dhn_recv.at[k], 2 * k)

    def half_copy(k):
        lines = pl.ds((k - 1) * half, half)
        return remote(
            sent.at[2, lines], halves.at[k - 1], half_sem.at[0, k], half_sem.at[1, k], 2 * k
        )

    def left_copy(k, j, other):
        number = 1 - core if other else core
        columns = pl.ds(pl.multiple_of((2 * j + number) * shard, shard), shard)
        source = hn_v.at[k, :, columns]
        target = left.at[other, k, :, pl.ds(j * shard, shard)]
        if other:
            return remote(source, target, left_send.at[k, j], left_recv.at[k, j], 1)
        return pltpu.make_async_copy(source, target, left_local.at[k, j])

    def right_copy(k, other):
        if other:
            return remote(dgu_v.at[k], right.at[1, k], right_send.at[k], right_recv.at[k], 1)
        return pltpu.make_async_copy(dgu_v.at[k], right.at[0, k], right_local.at[k])

    loads = [
        pltpu.make_async_copy(w_d, w_d_v, load.at[0]),
        pltpu.make_async_copy(hn, hn_v.at[0], load.at[1]),
        pltpu.make_async_copy(w_gu, w_gu_v, load.at[2]),
    ]
    gb_loads = [
        pltpu.make_async_copy(gb, gb_v.at[k], load_gb.at[k]) for k, gb in enumerate(gbs)
    ]
    store_outs = [
        pltpu.make_async_copy(outs_v.at[k], out, store.at[k]) for k, out in enumerate(outs)
    ]
    for k in direct:
        hn_copy(k).start()
    for copy in loads[:1] + gb_loads + loads[1:]:
        copy.start()

    for copy in loads[:1] + gb_loads:
        copy.wait()

    def dact_tile(start, size):
        tile = w_d_v[pl.ds(start, size), :]
        for k in range(chips):
            dact_v[k, :, pl.ds(start, size)] = dot(gb_v[k], tile, (1, 1))

    @pl.loop(0, part // 256)
    def _(i):
        dact_tile(pl.multiple_of(i * 256, 256), 256)

    if part % 256:
        dact_tile(part - 128, 128)

    def forward(k):
        for j in range(chips):
            left_copy(k, j, 1).start()
            left_copy(k, j, 0).start()

        def tile(start, size):
            one, two = pl.ds(start, size), pl.ds(pl.multiple_of(part + start, 128), size)
            gate = dot(hn_v[k], w_gu_v[:, one], (1, 0))
            up = dot(hn_v[k], w_gu_v[:, two], (1, 0))
            dact = dact_v[k, :, one]
            sg = jax.nn.sigmoid(gate)
            silu = gate * sg
            act_v[k, :, one] = (silu * up).astype(BF)
            dgu_v[k, :, one] = (dact * up * sg * (1.0 + gate * (1.0 - sg))).astype(BF)
            dgu_v[k, :, two] = (dact * silu).astype(BF)

        @pl.loop(0, part // 256)
        def _(i):
            tile(pl.multiple_of(i * 256, 256), 256)

        if part % 256:
            tile(part - 128, 128)

        right_copy(k, 1).start()
        right_copy(k, 0).start()

    def backward(k):
        @pl.loop(0, width // 256)
        def _(i):
            lines = pl.ds(pl.multiple_of(i * 256, 256), 256)
            dhn = dot(dgu_v[k], w_gu_v[lines, :], (1, 1))
            if k:
                sent[k - 1, :, lines] = dhn.astype(BF)
            else:
                grad[:, lines] = dhn

    for copy in loads[1:]:
        copy.wait()
    forward(0)
    for k in direct:
        hn_copy(k).wait_recv()
        if relayed:
            hn_copy(3 - k, 1).start()
    if relayed:
        forward(1)
        forward(2)
        for i in direct:
            hn_copy(i, 1).wait_recv()
        forward(3)
        backward(3)
        for k in direct:
            half_copy(k).start()
        backward(1)
        backward(2)
        for k in direct:
            half_copy(k).wait_recv()

            @pl.loop(0, half // 16)
            def _(i):
                lines = pl.ds(pl.multiple_of(i * 16, 16), 16)
                into = pl.ds(pl.multiple_of((k - 1) * half + i * 16, 16), 16)
                total = sent[2 - k, into, :].astype(F32) + halves[k - 1, lines, :].astype(F32)
                sent[2 - k, into, :] = total.astype(BF)

            dhn_copy(3 - k).start()
    else:
        for k in range(1, chips):
            forward(k)
            backward(k)
            dhn_copy(k).start()
    backward(0)

    @pl.loop(0, width // 256)
    def _(i):
        columns = pl.ds(pl.multiple_of(i * 256, 256), 256)
        for k in range(chips):
            outs_v[k, :, columns] = dot(act_v[k], w_d_v[:, columns], (1, 0)).astype(BF)

    for copy in store_outs:
        copy.start()

    lower = part // 2
    spans = []
    for start in range(0, part, 128):
        cuts = sorted({start, min(max(lower, start), start + 128), start + 128})
        spans += [(start, a, b) for a, b in zip(cuts, cuts[1:])]

    def span_copies(n):
        start, a, b = spans[n]
        number = int(a >= lower)
        source = tiles.at[(start // 128) % 2, pl.ds(a - start, b - a)]
        at = pl.ds(a - number * lower, b - a)

        def keep():
            return pltpu.make_async_copy(source, down_kept.at[at], down_local.at[n])

        def send():
            return remote(source, down_got.at[at], down_send.at[n], down_recv.at[n], 1)

        return number, keep, send

    def each_span(chosen, go):
        for n in chosen:
            number, keep, send = span_copies(n)

            @pl.when(core == number)
            def _():
                keep().start() if go else keep().wait()

            @pl.when(core != number)
            def _():
                send().start() if go else send().wait_send()

    for start in range(0, part, 128):
        before = [n for n, span in enumerate(spans) if span[0] == start - 256]
        each_span(before, False)
        tile = sum(
            dot(act_v[k, :, start : start + 128], gb_v[k], (0, 0)) for k in range(chips)
        )
        tiles[(start // 128) % 2] = tile.astype(BF)
        each_span([n for n, span in enumerate(spans) if span[0] == start], True)
    each_span([n for n, span in enumerate(spans) if span[0] >= part - 256], False)
    for n in range(len(spans)):
        number, _, send = span_copies(n)

        @pl.when(core == number)
        def _():
            send().wait_recv()

    for k in direct:
        dhn_copy(k).wait_recv()

    @pl.loop(0, rows // 16)
    def _(i):
        lines = pl.ds(pl.multiple_of(i * 16, 16), 16)
        grad[lines, :] += sum(got[k - 1, lines, :].astype(F32) for k in direct)

    for copy in store_outs:
        copy.wait()
    for k in range(chips):
        for j in range(chips):
            left_copy(k, j, 0).wait()
            left_copy(k, j, 1).wait()
        right_copy(k, 0).wait()
        right_copy(k, 1).wait()
    for k in direct:
        dhn_copy(k).wait_send()
        hn_copy(k).wait_send()
        if relayed:
            half_copy(k).wait_send()
            hn_copy(k, 1).wait_send()


def feed_forward(nf, hn, gbs, w_gu, w_d):
    chips = nf // 2
    rows, width = hn.shape
    part = w_d.shape[0]
    anywhere = pl.BlockSpec(memory_space=pl.ANY)
    dma = pltpu.SemaphoreType.DMA
    shape = jax.ShapeDtypeStruct
    return pl.pallas_call(
        functools.partial(feed_forward_kernel, nf),
        in_specs=[anywhere] * (chips + 3),
        out_specs=[pl.BlockSpec(memory_space=pltpu.VMEM)] + [anywhere] * (chips + 4),
        out_shape=[
            shape((rows, width), F32),
            shape((2, chips, rows, width // 2), BF),
            shape((2, chips, rows, 2 * part), BF),
            shape((part // 2, width), BF),
            shape((part // 2, width), BF),
        ]
        + [shape((rows, width), BF)] * chips,
        scratch_shapes=[
            pltpu.VMEM((width, 2 * part), BF),
            pltpu.VMEM((part, width), BF),
            pltpu.VMEM((chips, rows, width), BF),
            pltpu.VMEM((chips, rows, width), BF),
            pltpu.VMEM((chips, rows, part), F32),
            pltpu.VMEM((chips, rows, part), BF),
            pltpu.VMEM((chips, rows, 2 * part), BF),
            pltpu.VMEM((chips - 1, rows, width), BF),
            pltpu.VMEM((chips - 1, rows, width), BF),
            pltpu.VMEM((chips, rows, width), BF),
            pltpu.VMEM((2, 128, width), BF),
            pltpu.VMEM((2, rows // 2, width), BF),
            dma((2, chips)),
            dma((3,)),
            dma((chips,)),
            dma((2 * chips,)),
            dma((2 * chips,)),
            dma((chips,)),
            dma((chips,)),
            dma((chips,)),
            dma((chips, chips)),
            dma((chips, chips)),
            dma((chips, chips)),
            dma((chips,)),
            dma((chips,)),
            dma((chips,)),
            dma((part // 128 + 1,)),
            dma((part // 128 + 1,)),
            dma((part // 128 + 1,)),
        ],
        compiler_params=pltpu.CompilerParams(
            collective_id=3, has_side_effects=True, vmem_limit_bytes=60 << 20
        ),
        cost_estimate=pl.CostEstimate(
            flops=12 * chips * rows * width * part,
            bytes_accessed=40_000_000,
            transcendentals=chips * rows * part,
        ),
        name="feed_forward",
    )(hn, *gbs, w_gu, w_d)


def chunk_rows(rows):
    return max(r for r in range(16, 33, 16) if rows % r == 0)


def finish_kernel(nf, nc, *refs):
    pieces, refs = refs[: nf // 2], refs[nf // 2 - 1 :]
    sources, (outs, owns, ins, xs) = refs[:4], (refs[i : i + 4] for i in range(4, 20, 4))
    plane_send, plane_recv, local, in_sem, x_sem, first_send, second_send, out_sem = refs[20:]
    chips = nf // 2
    place, here = lax.axis_index("fsdp"), lax.axis_index("ctx")
    chip = place // 2
    lower = here < nc // 2
    depth = jnp.where(lower, here, nc - 1 - here)
    inner = jnp.where(lower, here + 1, here - 1)
    outer = jnp.where(lower, here - 1, here + 1)
    mesh_id = pl.DeviceIdType.MESH

    barrier = pltpu.get_barrier_semaphore()
    for k in range(1, chips):
        pl.semaphore_signal(
            barrier, inc=1, device_id={"fsdp": place ^ (2 * k)}, device_id_type=mesh_id
        )
    pl.semaphore_signal(barrier, inc=1, device_id={"ctx": inner}, device_id_type=mesh_id)

    @pl.when(depth > 0)
    def _():
        pl.semaphore_signal(barrier, inc=1, device_id={"ctx": outer}, device_id_type=mesh_id)
        pl.semaphore_wait(barrier, chips + 1)

    @pl.when(depth == 0)
    def _():
        pl.semaphore_wait(barrier, chips)

    def plane_copy(u, k):
        return pltpu.make_async_remote_copy(
            src_ref=sources[u].at[chip ^ k],
            dst_ref=owns[u].at[k],
            send_sem=plane_send.at[u, k],
            recv_sem=plane_recv.at[u, k],
            device_id={"fsdp": place ^ (2 * k)},
            device_id_type=mesh_id,
        )

    def local_copy(u, k):
        source = sources[u].at[chip] if u else pieces[k]
        return pltpu.make_async_copy(source, owns[u].at[k], local.at[u, k])

    for u in range(4):
        for k in range(chips):
            if u == 0 or k == 0:
                local_copy(u, k).start()
            else:
                plane_copy(u, k).start()

    units = [(0, k) for k in range(chips)] + [(u, None) for u in (1, 2, 3)]
    chunks = []
    for u, k in units:
        total = outs[u].shape[-2]
        size = chunk_rows(total)
        chunks += [(u, k, r, size) for r in range(0, total, size)]

    def views(c):
        u, k, r, size = chunks[c]
        rows = pl.ds(r, size)
        return [owns[u].at[k or 0, rows]] + [
            ref.at[rows] if k is None else ref.at[k, rows] for ref in (ins[u], xs[u], outs[u])
        ]

    def first_copy(c, across):
        own, arriving, x, _ = views(c)
        return pltpu.make_async_remote_copy(
            src_ref=own,
            dst_ref=x if across else arriving,
            send_sem=first_send.at[c],
            recv_sem=(x_sem if across else in_sem).at[c],
            device_id={"ctx": inner},
            device_id_type=mesh_id,
        )

    def second_copy(c, across):
        _, arriving, x, _ = views(c)
        return pltpu.make_async_remote_copy(
            src_ref=arriving if across else x,
            dst_ref=x,
            send_sem=second_send.at[c],
            recv_sem=x_sem.at[c],
            device_id={"ctx": outer},
            device_id_type=mesh_id,
        )

    def out_copy(c, across):
        _, arriving, x, out = views(c)
        return pltpu.make_async_copy(arriving if across else x, out, out_sem.at[c])

    def add_into(target, terms, size):
        @pl.loop(0, size // 16)
        def _(i):
            strip = pl.ds(pl.multiple_of(i * 16, 16), 16)
            target[strip, :] = sum(term[strip, :].astype(F32) for term in terms).astype(BF)

    def inward(c, level):
        u, k, r, size = chunks[c]
        own, arriving, _, _ = views(c)
        terms = [own]
        if r == 0:
            local_copy(u, k or 0).wait()
            if u >= 1:
                for j in range(1, chips):
                    plane_copy(u, j).wait_recv()
        if u >= 1:
            terms += [owns[u].at[j, pl.ds(r, size)] for j in range(1, chips)]
        if level > 0:
            first_copy(c, False).wait_recv()
            terms.append(arriving)
        if len(terms) > 1:
            add_into(own, terms, size)
        if c >= FLIGHT:
            first_copy(c - FLIGHT, False).wait_send()
        first_copy(c, level == top).start()

    def outward(c, level):
        size = chunks[c][3]
        own, arriving, x, _ = views(c)
        first_copy(c, True).wait_recv()
        if level == top:
            add_into(arriving, [own, x], size)
        out_copy(c, level == top).start()
        if level > 0:
            if c >= FLIGHT:
                second_copy(c - FLIGHT, False).wait_send()
            second_copy(c, level == top).start()

    top = nc // 2 - 1
    count = len(chunks)
    for level in range(top + 1):

        @pl.when(depth == level)
        def _():
            lag = 1 + 4 * (top - level)
            for t in range(count + lag):
                if t < count:
                    inward(t, level)
                if t >= lag:
                    outward(t - lag, level)
            for c in range(max(0, count - FLIGHT), count):
                first_copy(c, False).wait_send()
                if level > 0:
                    second_copy(c, False).wait_send()
            for c in range(count):
                out_copy(c, False).wait()

    for u in range(1, 4):
        for k in range(1, chips):
            plane_copy(u, k).wait_send()


def finish(nf, nc, pieces, sums):
    chips = nf // 2
    pieces_shape = (chips,) + pieces[0].shape
    shapes = [pieces_shape] + [x.shape[1:] for x in sums]
    count = sum(
        (shape[0] if len(shape) == 3 else 1) * (shape[-2] // chunk_rows(shape[-2]))
        for shape in shapes
    )
    anywhere = pl.BlockSpec(memory_space=pl.ANY)
    dma = pltpu.SemaphoreType.DMA
    return pl.pallas_call(
        functools.partial(finish_kernel, nf, nc),
        in_specs=[anywhere] * (chips + 3),
        out_specs=[anywhere] * 4,
        out_shape=[jax.ShapeDtypeStruct(shape, BF) for shape in shapes],
        scratch_shapes=[pltpu.VMEM(x, BF) for x in [pieces_shape] + [x.shape for x in sums]]
        + [pltpu.VMEM(shape, BF) for shape in shapes]
        + [pltpu.VMEM(shape, BF) for shape in shapes]
        + [dma((4, chips)), dma((4, chips)), dma((4, chips))]
        + [dma((count,))] * 5,
        compiler_params=pltpu.CompilerParams(
            collective_id=0, has_side_effects=True, vmem_limit_bytes=48 << 20
        ),
        cost_estimate=pl.CostEstimate(
            flops=200_000_000_000, bytes_accessed=60_000_000, transcendentals=0
        ),
        name="finish",
    )(*pieces, *sums)


def solution(mesh):
    nf, nc = mesh.shape["fsdp"], mesh.shape["ctx"]
    chips = nf // 2

    def swap(x, k):
        return lax.ppermute(x, "fsdp", [(i, i ^ k) for i in range(nf)])

    def plane_gather(x):
        if chips != 4:
            return [swap(x, 2 * k) for k in range(1, chips)]
        one, two = swap(x, 2), swap(x, 4)
        half = x.shape[0] // 2
        return [one, two, jnp.concatenate([swap(one[:half], 4), swap(two[half:], 2)], axis=0)]

    def cross(x, k):
        return lax.ppermute(x, "ctx", [(i, i ^ k) for i in range(nc)])

    def shards(
        tokens,
        attn_gain,
        w_query,
        w_key,
        w_value,
        w_out,
        ffn_gain,
        w_gate,
        w_up,
        w_down,
        block_table,
        positions,
        out_grad,
    ):
        place = lax.axis_index("fsdp")
        chip, core = place // 2, place % 2
        x = tokens[0].astype(F32)
        gb = out_grad[0]
        rows, width = x.shape
        hidden = w_gate.shape[1]
        part = hidden // chips
        shard = w_gate.shape[0]
        key_width = KV_HEADS * HEAD_DIM

        def core_sum(x):
            other = lax.dynamic_index_in_dim(x, 1 - core, 1, keepdims=False)
            mine = lax.dynamic_index_in_dim(x, core, 1, keepdims=False)
            return (mine.astype(F32) + swap(other, 1).astype(F32)).astype(BF)

        def rows_grad(left, right):
            columns = [left[:, i * shard : (i + 1) * shard] for i in range(nf)]
            even = jnp.concatenate(columns[::2], axis=1)
            odd = jnp.concatenate(columns[1::2], axis=1)
            mine = jnp.where(core == 0, even, odd)
            other = jnp.where(core == 0, odd, even)
            left = jnp.concatenate([mine, swap(other, 1)], axis=0)
            right = jnp.concatenate([right, swap(right, 1)], axis=0)
            return dot(left, right, (0, 0)).astype(BF).reshape(chips, shard, right.shape[1])


        half = HEAD_DIM // 2
        frequency = THETA ** (-jnp.arange(half, dtype=F32) * (2.0 / HEAD_DIM))
        angle = positions[0].astype(F32)[:, None] * frequency[None, :]
        cosine, sine = jnp.cos(angle), jnp.sin(angle)
        cos_lanes = jnp.tile(cosine, (1, 4))
        sin_lanes = jnp.tile(jnp.concatenate([-sine, sine], axis=1), (1, 2))
        blocks = 2 * nc
        stored = block_table.reshape(-1)
        number = jnp.arange(blocks, dtype=jnp.int32)
        where = jnp.sum(
            jnp.where(stored[None, :] == number[:, None], number[None, :], 0), axis=1
        )
        here = lax.axis_index("ctx")
        own = lax.dynamic_slice_in_dim(stored, 2 * here, 2)
        where = 2 * ((where // 2) ^ here) + where % 2
        table = jnp.concatenate([own, where]).astype(jnp.int32)

        order = chip ^ jnp.arange(chips, dtype=jnp.int32)
        both_gains = jnp.pad(jnp.stack([attn_gain, ffn_gain]), ((0, 14), (0, 0)))
        w_q, w_kv, w_o, w_gu, w_d, gains, kv = share_weights(
            nf,
            nc,
            w_query,
            w_key,
            w_value,
            w_out,
            w_gate,
            w_up,
            order,
            w_down,
            both_gains,
            tokens[0],
            cos_lanes,
            sin_lanes,
        )
        w_q = w_q.reshape(width, -1)
        w_kv = w_kv.reshape(width, -1)
        gb_sent, w_kv = lax.optimization_barrier((gb, w_kv))
        w_o = w_o.reshape(-1, width)
        w_gu = w_gu.reshape(width, 2 * part)
        w_d = w_d.reshape(part, width)
        gains = gains[:, :2].astype(F32).transpose(1, 0, 2).reshape(2, width)

        inverse_one = lax.rsqrt(jnp.mean(x * x, axis=1, keepdims=True) + EPS)
        unit_one = x * inverse_one
        xn = (unit_one * gains[0][None, :]).astype(BF)
        q_sum = dot(xn, w_q, (1, 0))
        gb_of = [gb] + [swap(gb_sent, 2 * k) for k in range(1, chips)]
        kv = kv.reshape(nc * rows, 2 * key_width)
        qr, o, ob, lse = attention_forward(table, q_sum, cos_lanes, sin_lanes, kv)
        h1 = x + dot(ob, w_o, (1, 0))
        inverse_two = lax.rsqrt(jnp.mean(h1 * h1, axis=1, keepdims=True) + EPS)
        unit_two = h1 * inverse_two
        hn = (unit_two * gains[1][None, :]).astype(BF)

        hn, gb_of = lax.optimization_barrier((hn, gb_of))

        fused = part % 128 == 0
        if fused:
            grad_hn, left, right, *downs = feed_forward(nf, hn, gb_of, w_gu, w_d)
            outs = downs[2:]
            left = left.reshape(2 * chips * rows, width // 2)
            right = right.reshape(2 * chips * rows, 2 * part)
            down_sum = (downs[0].astype(F32) + downs[1].astype(F32)).astype(BF)
        else:
            dhns = []
            hn_of, act_of, dgu_of = [], [], []
            for k, hn_k in enumerate([hn] + plane_gather(hn)):
                gu = dot(hn_k, w_gu, (1, 0))
                dact = dot(gb_of[k], w_d, (1, 1))
                gate, up = gu[:, :part], gu[:, part:]
                sg = jax.nn.sigmoid(gate)
                silu = gate * sg
                act = (silu * up).astype(BF)
                dgate = (dact * up * sg * (1.0 + gate * (1.0 - sg))).astype(BF)
                dgu = jnp.concatenate([dgate, (dact * silu).astype(BF)], axis=1)
                dhn_k = dot(dgu, w_gu, (1, 1))
                dhns.append(dhn_k.astype(BF) if k else dhn_k)
                hn_of.append(hn_k)
                act_of.append(act)
                dgu_of.append(dgu)
            got = [swap(dhns[k], 2 * k) for k in range(1, chips)]
            act_of, dgu_of, got[:-1], _ = lax.optimization_barrier(
                (act_of, dgu_of, got[:-1], dhns[1:])
            )
            grad_hn = dhns[0]
            for piece in got:
                grad_hn = grad_hn + piece.astype(F32)

            gb_all = jnp.concatenate(gb_of, axis=0)
            down = dot(jnp.concatenate(act_of, axis=0), gb_all, (0, 0)).astype(BF)
            down_sum = core_sum(down.reshape((1, 2) + w_down.shape))[0]
            left = jnp.concatenate(hn_of, axis=0)
            right = jnp.concatenate(dgu_of, axis=0)

        down_sum, left, right = lax.optimization_barrier((down_sum, left, right))
        down_sum = lax.psum_scatter(down_sum, "ctx", scatter_dimension=0, tiled=True)
        if fused:
            wide = dot(left, right, (0, 0)).astype(BF).reshape(chips, shard, 2 * part)
        else:
            wide = rows_grad(left, right)
        wide = [
            lax.dynamic_index_in_dim(wide, chip ^ k, 0, keepdims=False) for k in range(chips)
        ]
        wide, grad_hn = lax.optimization_barrier((wide, grad_hn))
        wide = [swap(piece, 2 * k) if k else piece for k, piece in enumerate(wide)]

        gain_two_grad = jnp.sum(grad_hn * unit_two, axis=0)
        grad_unit = grad_hn * gains[1][None, :]
        dh1 = gb.astype(F32) + inverse_two * (
            grad_unit - unit_two * jnp.mean(grad_unit * unit_two, axis=1, keepdims=True)
        )
        dab = dh1.astype(BF)
        dob = dot(dab, w_o, (1, 1)).astype(BF)
        dq, dkv = attention_backward(table, qr, dob, o, lse, kv, cos_lanes, sin_lanes)
        xn, ob, dab, _ = lax.optimization_barrier((xn, ob, dab, dq))
        if not fused:
            act_of, _ = lax.optimization_barrier((act_of, dq))
            outs = [dot(act, w_d, (1, 0)).astype(BF) for act in act_of]
        sent = outs[1:]
        own = own_key_grads(nc, dkv, cos_lanes, sin_lanes)
        own, wide, down_sum = lax.optimization_barrier((own, wide, down_sum))
        down_sum = lax.all_gather(down_sum, "ctx", axis=0, tiled=True)
        ob, dab, _ = lax.optimization_barrier((ob, dab, own))
        out_term = rows_grad(ob, dab)
        dqkv = jnp.concatenate([dq, own], axis=1)
        grad_xn = dot(dq, w_q, (1, 1)) + dot(own, w_kv, (1, 1))
        gain_one_grad = jnp.sum(grad_xn * unit_one, axis=0)
        grad_unit = grad_xn * gains[0][None, :]
        tokens_grad = dh1 + inverse_one * (
            grad_unit - unit_one * jnp.mean(grad_unit * unit_one, axis=1, keepdims=True)
        )
        qkv_term = rows_grad(xn, dqkv)

        gains_of = jnp.stack([gain_one_grad, gain_two_grad]).reshape(2, chips, 2, shard)
        other = lax.dynamic_index_in_dim(gains_of, 1 - core, 2, keepdims=False)
        mine = lax.dynamic_index_in_dim(gains_of, core, 2, keepdims=False)
        gains_of = (mine + swap(other, 1)).transpose(1, 0, 2).reshape(chips, 1, 2 * shard)
        gains_of = jnp.pad(gains_of.astype(BF), ((0, 0), (0, 15), (0, 0)))
        out_term, qkv_term, outs[0], sent = lax.optimization_barrier(
            (out_term, qkv_term, outs[0], sent)
        )
        terms = [swap(sent[k - 1], 2 * k) for k in range(1, chips)]
        wide, down_sum, out_term, qkv_term = lax.optimization_barrier(
            (wide, down_sum, out_term, qkv_term)
        )
        gu_sum, out_sum, qkv_sum, gain_sum = finish(
            nf, nc, wide, [out_term, qkv_term, gains_of]
        )
        h1, gain_sum = lax.optimization_barrier((h1, gain_sum))
        branch = h1 + outs[0].astype(F32)
        for k in range(1, chips):
            branch = branch + terms[k - 1].astype(F32)
        layer_out = branch.astype(BF)
        qkv_sum = qkv_sum.astype(F32)
        gain_sum = gain_sum[0].reshape(2, shard).astype(F32)
        gate_grad, up_grad = place_columns(order, gu_sum)
        query_width = HEADS * HEAD_DIM
        return (
            layer_out.reshape(1, rows, width),
            tokens_grad.reshape(1, rows, width),
            gain_sum[0],
            qkv_sum[:, :query_width],
            qkv_sum[:, query_width : query_width + key_width],
            qkv_sum[:, query_width + key_width :],
            out_sum.astype(F32),
            gain_sum[1],
            gate_grad,
            up_grad,
            down_sum.astype(F32),
        )

    weight = P("fsdp", None)
    activation = P("fsdp", "ctx", None)
    return jax.shard_map(
        shards,
        mesh=mesh,
        in_specs=(
            activation,
            P("fsdp"),
            weight,
            weight,
            weight,
            weight,
            P("fsdp"),
            weight,
            weight,
            weight,
            P(),
            P("fsdp", "ctx"),
            activation,
        ),
        out_specs=(
            activation,
            activation,
            P("fsdp"),
            weight,
            weight,
            weight,
            weight,
            P("fsdp"),
            weight,
            weight,
            weight,
        ),
        check_vma=False,
    )
```

```python
import functools

import jax
import jax.numpy as jnp
from jax import lax
from jax.experimental import pallas as pl
from jax.experimental.pallas import tpu as pltpu
from jax.sharding import PartitionSpec as P

HEADS = 32
KV_HEADS = 4
HEAD_DIM = 64
GROUP = HEADS // KV_HEADS
PAIRS = GROUP // 2
LANES = 2 * HEAD_DIM
STACK = PAIRS * LANES

EPS = 1e-05
THETA = 10000.0
NEG = -1e30
FLIGHT = 2
BF = jnp.bfloat16
F32 = jnp.float32


def dot(left, right, contract, out=F32):
    return lax.dot_general(
        left, right, ((contract[:1], contract[1:]), ((), ())), preferred_element_type=out
    )


def swap_halves(z):
    lane = lax.broadcasted_iota(jnp.int32, z.shape, 1)
    first = (lane % HEAD_DIM) < (HEAD_DIM // 2)
    return jnp.where(
        first,
        pltpu.roll(z, LANES - HEAD_DIM // 2, 1),
        pltpu.roll(z, HEAD_DIM // 2, 1),
    )


def split_heads(rows):
    lane = lax.broadcasted_iota(jnp.int32, rows.shape, 1)
    zero = jnp.zeros_like(rows)
    return jnp.concatenate(
        [jnp.where(lane < HEAD_DIM, rows, zero), jnp.where(lane >= HEAD_DIM, rows, zero)], axis=0
    )


def join_heads(columns):
    half = columns.shape[1] // 2
    sub = lax.broadcasted_iota(jnp.int32, (LANES, half), 0)
    return jnp.where(sub < HEAD_DIM, columns[:, :half], columns[:, half:]).T


def stack_pairs(ref, rows):
    return jnp.concatenate([ref[rows, p * LANES : (p + 1) * LANES] for p in range(PAIRS)], axis=0)


def two_blocks(ref, table, j, block):
    parts = [
        ref[pl.ds(pl.multiple_of(table[2 + 2 * j + i] * block, block), block), :] for i in range(2)
    ]
    return jnp.concatenate(parts, axis=0)


def causal(scores, j, own, block):
    key = lax.broadcasted_iota(jnp.int32, scores.shape, 0) + j * (2 * block)
    query = lax.broadcasted_iota(jnp.int32, scores.shape, 1) % block + own * block
    return jnp.where(key <= query, scores, NEG)


def head_twice(pair, group):
    wide = pair.astype(F32)
    lane = lax.broadcasted_iota(jnp.int32, wide.shape, 1)
    keep = (lane < HEAD_DIM) == (group % 2 == 0)
    return jnp.where(keep, wide, pltpu.roll(wide, HEAD_DIM, 1)).astype(BF)


def attention_forward_kernel(
    table,
    q_ref,
    cos_ref,
    sin_ref,
    k_pair,
    v_pair,
    qr_ref,
    o_ref,
    ob_ref,
    lse_ref,
    qm,
    m,
    l,
    acc,
    k_ref,
    v_ref,
):
    block = q_ref.shape[0] // 2
    group = pl.program_id(0)
    k_ref[...] = head_twice(k_pair[...], group)
    v_ref[...] = head_twice(v_pair[...], group)
    for h in range(2):
        rows = slice(h * block, (h + 1) * block)
        cosine, sine = cos_ref[rows, :], sin_ref[rows, :]
        for p in range(PAIRS):
            lanes = slice(p * LANES, (p + 1) * LANES)
            z = q_ref[rows, lanes]
            qr_ref[rows, lanes] = (z * cosine + swap_halves(z) * sine).astype(BF)
        scaled = stack_pairs(qr_ref, rows).astype(F32) * (HEAD_DIM**-0.5)
        qm[...] = split_heads(scaled).astype(BF)
        m[...] = jnp.full_like(m, NEG)
        l[...] = jnp.zeros_like(l)
        acc[...] = jnp.zeros_like(acc)
        own = table[h]

        def step(j, masked):
            keys = two_blocks(k_ref, table, j, block)
            values = two_blocks(v_ref, table, j, block)
            s = dot(keys, qm[...], (1, 1))
            if masked:
                s = causal(s, j, own, block)
            before = m[...]
            now = jnp.maximum(before, jnp.max(s, axis=0, keepdims=True))
            p = jnp.exp(s - now)
            decay = jnp.exp(before - now)
            l[...] = l[...] * decay + jnp.sum(p, axis=0, keepdims=True)
            acc[...] = acc[...] * decay + dot(values, p.astype(BF), (0, 0))
            m[...] = now

        last = own // 2

        @pl.loop(0, last)
        def _(j):
            step(j, False)

        step(last, True)
        lse_ref[0, h : h + 1, :] = m[...] + jnp.log(l[...])
        o = join_heads(acc[...] / l[...])
        for p in range(PAIRS):
            lanes = slice(p * LANES, (p + 1) * LANES)
            piece = o[p * block : (p + 1) * block, :]
            o_ref[rows, lanes] = piece
            ob_ref[rows, lanes] = piece.astype(BF)


def attention_forward(table, q, cosine, sine, kv):
    rows, length = q.shape[0], kv.shape[0]
    query_width = HEADS * HEAD_DIM
    columns = pl.BlockSpec((rows, STACK), lambda g, t: (0, g))
    whole = pl.BlockSpec((rows, LANES), lambda g, t: (0, 0))
    key_pair = pl.BlockSpec((length, LANES), lambda g, t: (0, g // 2))
    value_pair = pl.BlockSpec((length, LANES), lambda g, t: (0, KV_HEADS // 2 + g // 2))
    wide = GROUP * (rows // 2)
    return pl.pallas_call(
        attention_forward_kernel,
        grid_spec=pltpu.PrefetchScalarGridSpec(
            num_scalar_prefetch=1,
            grid=(KV_HEADS,),
            in_specs=[columns, whole, whole, key_pair, value_pair],
            out_specs=[
                columns,
                columns,
                columns,
                pl.BlockSpec((1, 2, wide), lambda g, t: (g, 0, 0)),
            ],
            scratch_shapes=[
                pltpu.VMEM((wide, LANES), BF),
                pltpu.VMEM((1, wide), F32),
                pltpu.VMEM((1, wide), F32),
                pltpu.VMEM((LANES, wide), F32),
                pltpu.VMEM((length, LANES), BF),
                pltpu.VMEM((length, LANES), BF),
            ],
        ),
        out_shape=[
            jax.ShapeDtypeStruct((rows, query_width), BF),
            jax.ShapeDtypeStruct((rows, query_width), F32),
            jax.ShapeDtypeStruct((rows, query_width), BF),
            jax.ShapeDtypeStruct((KV_HEADS, 2, wide), F32),
        ],
        compiler_params=pltpu.CompilerParams(vmem_limit_bytes=32 << 20),
        cost_estimate=pl.CostEstimate(
            flops=8 * HEADS * rows * length * HEAD_DIM,
            bytes_accessed=16 * rows * HEADS * HEAD_DIM,
            transcendentals=HEADS * rows * length,
        ),
        name="attention_forward",
    )(table, q, cosine, sine, kv, kv)


def attention_backward_kernel(
    table,
    qr_ref,
    do_ref,
    o_ref,
    lse_ref,
    k_pair,
    v_pair,
    cos_ref,
    sin_ref,
    dq_ref,
    dkv_ref,
    qm,
    dom,
    dqt,
    k_ref,
    v_ref,
    dk_ref,
    dv_ref,
):
    block = qr_ref.shape[0] // 2
    group = pl.program_id(0)
    k_ref[...] = head_twice(k_pair[...], group)
    v_ref[...] = head_twice(v_pair[...], group)
    dk_ref[...] = jnp.zeros_like(dk_ref)
    dv_ref[...] = jnp.zeros_like(dv_ref)
    for h in range(2):
        rows = slice(h * block, (h + 1) * block)
        scaled = stack_pairs(qr_ref, rows).astype(F32) * (HEAD_DIM**-0.5)
        qm[...] = split_heads(scaled).astype(BF)
        grads = stack_pairs(do_ref, rows).astype(F32)
        dom[...] = split_heads(grads).astype(BF)
        product = (grads * stack_pairs(o_ref, rows)).T
        inner = jnp.concatenate(
            [
                jnp.sum(product[:HEAD_DIM], axis=0, keepdims=True),
                jnp.sum(product[HEAD_DIM:], axis=0, keepdims=True),
            ],
            axis=1,
        )
        lse = lse_ref[0, h : h + 1, :]
        dqt[...] = jnp.zeros_like(dqt)
        own = table[h]

        def step(j, masked):
            keys = two_blocks(k_ref, table, j, block)
            values = two_blocks(v_ref, table, j, block)
            s = dot(keys, qm[...], (1, 1))
            if masked:
                s = causal(s, j, own, block)
            p = jnp.exp(s - lse)
            dp = dot(values, dom[...], (1, 1))
            ds = (p * (dp - inner)).astype(BF)
            dv = dot(p.astype(BF), dom[...], (1, 0))
            dk = dot(ds, qm[...], (1, 0))
            dqt[...] += dot(keys, ds, (0, 0))
            for i in range(2):
                at = pl.ds(pl.multiple_of(table[2 + 2 * j + i] * block, block), block)
                dk_ref[at, :] += dk[i * block : (i + 1) * block]
                dv_ref[at, :] += dv[i * block : (i + 1) * block]

        last = own // 2

        @pl.loop(0, last)
        def _(j):
            step(j, False)

        step(last, True)
        cosine, sine = cos_ref[rows, :], sin_ref[rows, :]
        dq = join_heads(dqt[...] * (HEAD_DIM**-0.5))
        for p in range(PAIRS):
            z = dq[p * block : (p + 1) * block, :]
            dq_ref[rows, p * LANES : (p + 1) * LANES] = (
                z * cosine - swap_halves(z) * sine
            ).astype(BF)
    lane = lax.broadcasted_iota(jnp.int32, dk_ref.shape, 1)
    keep = (lane < HEAD_DIM) == (group % 2 == 0)
    for i, ref in enumerate((dk_ref, dv_ref)):
        both = ref[...] + pltpu.roll(ref[...], HEAD_DIM, 1)
        dkv_ref[i] = jnp.where(keep, both, dkv_ref[i].astype(F32)).astype(BF)


def attention_backward(table, qr, grads, o, lse, kv, cosine, sine):
    rows, length = qr.shape[0], kv.shape[0]
    columns = pl.BlockSpec((rows, STACK), lambda g, t: (0, g))
    whole = pl.BlockSpec((rows, LANES), lambda g, t: (0, 0))
    key_pair = pl.BlockSpec((length, LANES), lambda g, t: (0, g // 2))
    value_pair = pl.BlockSpec((length, LANES), lambda g, t: (0, KV_HEADS // 2 + g // 2))
    wide = GROUP * (rows // 2)
    return pl.pallas_call(
        attention_backward_kernel,
        grid_spec=pltpu.PrefetchScalarGridSpec(
            num_scalar_prefetch=1,
            grid=(KV_HEADS,),
            in_specs=[
                columns,
                columns,
                columns,
                pl.BlockSpec((1, 2, wide), lambda g, t: (g, 0, 0)),
                key_pair,
                value_pair,
                whole,
                whole,
            ],
            out_specs=[columns, pl.BlockSpec((2, length, LANES), lambda g, t: (0, 0, g // 2))],
            scratch_shapes=[
                pltpu.VMEM((wide, LANES), BF),
                pltpu.VMEM((wide, LANES), BF),
                pltpu.VMEM((LANES, wide), F32),
                pltpu.VMEM((length, LANES), BF),
                pltpu.VMEM((length, LANES), BF),
                pltpu.VMEM((length, LANES), F32),
                pltpu.VMEM((length, LANES), F32),
            ],
        ),
        out_shape=[
            jax.ShapeDtypeStruct(qr.shape, BF),
            jax.ShapeDtypeStruct((2, length, KV_HEADS * HEAD_DIM), BF),
        ],
        compiler_params=pltpu.CompilerParams(vmem_limit_bytes=32 << 20),
        cost_estimate=pl.CostEstimate(
            flops=20 * HEADS * rows * length * HEAD_DIM,
            bytes_accessed=16 * rows * HEADS * HEAD_DIM,
            transcendentals=HEADS * rows * length,
        ),
        name="attention_backward",
    )(table, qr, grads, o, lse, kv, kv, cosine, sine)


def own_key_grads_kernel(nc, dkv_ref, cos_ref, sin_ref, out_ref, got, send_sem, recv_sem):
    rows, width = out_ref.shape[0], out_ref.shape[1] // 2
    here = lax.axis_index("ctx")
    mesh_id = pl.DeviceIdType.MESH
    barrier = pltpu.get_barrier_semaphore()
    for k in range(1, nc):
        pl.semaphore_signal(barrier, inc=1, device_id={"ctx": here ^ k}, device_id_type=mesh_id)
    pl.semaphore_wait(barrier, nc - 1)

    def copy(k):
        source = dkv_ref.at[:, pl.ds(k * rows, rows)]
        if k == 0:
            return pltpu.make_async_copy(source, got.at[0], recv_sem.at[0])
        return pltpu.make_async_remote_copy(
            src_ref=source,
            dst_ref=got.at[k],
            send_sem=send_sem.at[k],
            recv_sem=recv_sem.at[k],
            device_id={"ctx": here ^ k},
            device_id_type=mesh_id,
        )

    for k in reversed(range(nc)):
        copy(k).start()
    for k in range(nc):
        copy(k).wait()

    def total(i, lanes):
        return sum(got[k, i, :, lanes].astype(F32) for k in range(nc))

    for p in range(width // LANES):
        lanes = slice(p * LANES, (p + 1) * LANES)
        z = total(0, lanes)
        out_ref[:, lanes] = (z * cos_ref[...] - swap_halves(z) * sin_ref[...]).astype(BF)
        out_ref[:, width + p * LANES : width + (p + 1) * LANES] = total(1, lanes).astype(BF)


def own_key_grads(nc, dkv, cosine, sine):
    rows, width = dkv.shape[1] // nc, dkv.shape[2]
    vmem = pl.BlockSpec(memory_space=pltpu.VMEM)
    return pl.pallas_call(
        functools.partial(own_key_grads_kernel, nc),
        in_specs=[pl.BlockSpec(memory_space=pl.ANY), vmem, vmem],
        out_specs=vmem,
        out_shape=jax.ShapeDtypeStruct((rows, 2 * width), BF),
        scratch_shapes=[
            pltpu.VMEM((nc, 2, rows, width), BF),
            pltpu.SemaphoreType.DMA((nc,)),
            pltpu.SemaphoreType.DMA((nc,)),
        ],
        compiler_params=pltpu.CompilerParams(collective_id=2, has_side_effects=True),
        name="own_key_grads",
    )(dkv, cosine, sine)


def share_kernel(nf, nc, low, size, raw, *refs):
    count = 2 if raw else 1
    w_query, w_key, w_value, w_out, *halves, down, gains, tokens, cosine, sine = refs[: 9 + count]
    refs = refs[9 + count :]
    query, key_value, out, wide, downs, all_gains, kv_all = refs[:7]
    query_own, key_value_own, out_own, wide_own, down_own, gains_own = refs[7:13]
    (local, plane_send, plane_recv, along_send, along_recv, core_send, core_recv) = refs[13:20]
    (gain_send, gain_recv, down_sem, gather_send, gather_recv, gather_core) = refs[20:26]
    w_kv, gains_v, xn, kv, kv_load, kv_send, kv_recv = refs[26:]
    chips = nf // 2
    place, here = lax.axis_index("fsdp"), lax.axis_index("ctx")
    chip, core = place // 2, place % 2
    mesh_id = pl.DeviceIdType.MESH
    shard, columns = wide.shape[1:]
    part = columns // 2
    key_width = w_key.shape[1]
    gathered = [
        (w_query, query, query_own, pl.ds(0, w_query.shape[1])),
        (w_key, key_value, key_value_own, pl.ds(0, key_width)),
        (w_value, key_value, key_value_own, pl.ds(key_width, key_width)),
        (w_out, out, out_own, pl.ds(0, w_out.shape[1])),
    ]

    barrier = pltpu.get_barrier_semaphore()

    def greet(target):
        pl.semaphore_signal(barrier, inc=1, device_id=target, device_id_type=mesh_id)

    for j in range(1, nf):
        greet({"fsdp": place ^ j})
    for pos in range(nc):

        @pl.when(here == pos)
        def _():
            for i in range(nc):
                if i != pos:
                    greet({"ctx": i})

    pl.semaphore_wait(barrier, nf - 1 + nc - 1)

    def remote(source, target, sends, recvs, where):
        return pltpu.make_async_remote_copy(
            src_ref=source,
            dst_ref=target,
            send_sem=sends,
            recv_sem=recvs,
            device_id=where,
            device_id_type=mesh_id,
        )

    def piece(k, h, rows):
        if raw:
            at = pl.ds(pl.multiple_of((chip ^ k) * part, 128), part)
            return halves[h].at[rows, at]
        return halves[0].at[k, rows]

    def side(h):
        return pl.ds(h * part, part) if raw else pl.ds(0, columns)

    def rows_of(share):
        return pl.ds(low + share * size, size)

    def plane_copy(k, kind, h):
        rows = rows_of(here) if kind else pl.ds(0, low)
        return remote(
            piece(k, h, rows),
            wide.at[place, rows, side(h)],
            plane_send.at[kind, k, h],
            plane_recv.at[kind, k, h],
            {"fsdp": place ^ (2 * k)},
        )

    def along_copy(k, share, up, target):
        block = wide.at[place ^ (2 * k), rows_of(share)]
        return remote(
            block, block, along_send.at[up, share, k], along_recv.at[share, k], {"ctx": target}
        )

    def core_copy(k, share):
        rows = rows_of(share) if share < nc else pl.ds(0, low)
        block = wide.at[place ^ (2 * k), rows]
        return remote(
            block, block, core_send.at[k, share], core_recv.at[k, share], {"fsdp": place ^ 1}
        )

    def own_core_copy(h):
        return remote(
            piece(0, h, pl.ds(0, shard)),
            wide.at[place, :, side(h)],
            core_send.at[0, h],
            core_recv.at[0, h],
            {"fsdp": place ^ 1},
        )

    half = shard // 2
    relayed = chips == 4

    def gather_copy(u, k, relay=0):
        source, target, _, at = gathered[u]
        if relay:
            owner, rows = place ^ (2 * (3 - k)), pl.ds((2 - k) * half, half)
            source = target.at[owner, rows, at]
        else:
            owner, rows = place, pl.ds(0, shard)
        number = 2 * k + relay
        return remote(
            source,
            target.at[owner, rows, at],
            gather_send.at[u, number],
            gather_recv.at[u, number],
            {"fsdp": place ^ (2 * k)},
        )

    def gather_core_copy(u, k):
        source, target, _, at = gathered[u]
        block = target.at[place ^ (2 * k), :, at]
        return remote(
            block if k else source,
            block,
            gather_core.at[0, u, k],
            gather_core.at[1, u, k],
            {"fsdp": place ^ 1},
        )

    def down_copy():
        return remote(down, downs.at[core], down_sem.at[0], down_sem.at[1], {"fsdp": place ^ 1})

    def gain_copy(j):
        return remote(
            gains, all_gains.at[place], gain_send.at[j], gain_recv.at[j], {"fsdp": place ^ j}
        )

    direct = (1, 2) if relayed else tuple(range(1, chips))
    for k in range(1, chips):
        for h in range(count):
            plane_copy(k, 1, h).start()
    for j in range(1, nf):
        gain_copy(j).start()
    for h in range(count):
        own_core_copy(h).start()
    for u in range(4):
        gather_core_copy(u, 0).start()
    down_copy().start()
    own = [(source, stage.at[:, at], None) for source, _, stage, at in gathered]
    own += [(piece(0, h, pl.ds(0, shard)), wide_own.at[:, side(h)], None) for h in range(count)]
    own += [(down, down_own, downs.at[core]), (gains, gains_own, all_gains.at[place])]
    back = [
        (query_own, query.at[place]),
        (key_value_own, key_value.at[place]),
        (out_own, out.at[place]),
        (wide_own, wide.at[place]),
        (down_own, downs.at[core]),
        (gains_own, all_gains.at[place]),
    ]
    for i, (source, stage, _) in enumerate(own):
        pltpu.make_async_copy(source, stage, local.at[0, i]).start()
    for i, (source, stage, _) in enumerate(own):
        pltpu.make_async_copy(source, stage, local.at[0, i]).wait()
    for i, (stage, target) in enumerate(back):
        pltpu.make_async_copy(stage, target, local.at[1, i]).start()

    for k in range(1, chips):
        for h in range(count):
            plane_copy(k, 1, h).wait_send()
    for u in (1, 2, 0, 3):
        for k in direct:
            gather_copy(u, k).start()

    def kv_copy(k):
        if k == 0:
            return pltpu.make_async_copy(kv, kv_all.at[0], kv_recv.at[0])
        return remote(kv, kv_all.at[k], kv_send.at[k], kv_recv.at[k], {"ctx": here ^ k})

    def make_kv():
        for i in (len(back) - 1, 1):
            stage, target = back[i]
            pltpu.make_async_copy(stage, target, local.at[1, i]).wait()
        for j in range(1, nf):
            gain_copy(j).wait_recv()
        for u in (1, 2):
            if relayed:
                for k in direct:
                    gather_copy(u, k, 1).wait_recv()
                gather_core_copy(u, 3).start()
            for k in range(chips):
                gather_core_copy(u, k).wait_recv()
        loads = [
            pltpu.make_async_copy(key_value, w_kv, kv_load.at[0]),
            pltpu.make_async_copy(all_gains, gains_v, kv_load.at[1]),
        ]
        for copy in loads:
            copy.start()
        for copy in loads:
            copy.wait()
        for i in range(0, xn.shape[0], 16):
            x = tokens[i : i + 16, :].astype(F32)
            unit = x * lax.rsqrt(jnp.mean(x * x, axis=1, keepdims=True) + EPS)
            for f in range(nf):
                lanes = slice(f * shard, (f + 1) * shard)
                gain = gains_v[f, 0:1, :].astype(F32)
                xn[i : i + 16, lanes] = (unit[:, lanes] * gain).astype(BF)
        total = sum(
            dot(xn[:, f * shard : (f + 1) * shard], w_kv[f], (1, 0)) for f in range(nf)
        )
        for p in range(0, key_width, LANES):
            z = total[:, p : p + LANES]
            kv[:, p : p + LANES] = (z * cosine[...] + swap_halves(z) * sine[...]).astype(BF)
        kv[:, key_width:] = total[:, key_width:].astype(BF)
        for k in reversed(range(nc)):
            kv_copy(k).start()

    for pos in range(nc):

        @pl.when(here == pos)
        def _():
            def pass_on(k, share):
                if share <= pos < nc - 1:
                    along_copy(k, share, 1, pos + 1).start()
                if share >= pos > 0:
                    along_copy(k, share, 0, pos - 1).start()
                core_copy(k, share).start()

            for k in range(1, chips):
                for h in range(count):
                    plane_copy(k, 1, h).wait_recv()
                pass_on(k, pos)
            if low:
                for k in range(1, chips):
                    for h in range(count):
                        plane_copy(k, 0, h).start()
            def gather_on(u):
                for k in direct:
                    gather_copy(u, k).wait_recv()
                    if relayed:
                        gather_copy(u, 3 - k, 1).start()
                    gather_core_copy(u, k).start()

            groups = [(), (1, 2), (0, 3)]
            for d in range(1, max(nc, len(groups))):
                for share in (pos - d, pos + d):
                    if 0 <= share < nc:
                        for k in range(1, chips):
                            along_copy(k, share, 0, 0).wait_recv()
                            pass_on(k, share)
                for u in groups[d] if d < len(groups) else ():
                    if u == 3:
                        make_kv()
                    gather_on(u)
            if low:
                for k in range(1, chips):
                    for h in range(count):
                        plane_copy(k, 0, h).wait_recv()
                    core_copy(k, nc).start()
            if relayed:
                for u in (0, 3):
                    for k in direct:
                        gather_copy(u, k, 1).wait_recv()
                    gather_core_copy(u, 3).start()
            for k in range(1, chips):
                for share in range(nc):
                    if share <= pos < nc - 1:
                        along_copy(k, share, 1, pos + 1).wait_send()
                    if share >= pos > 0:
                        along_copy(k, share, 0, pos - 1).wait_send()

    for h in range(count):
        own_core_copy(h).wait()
    for k in range(1, chips):
        for share in range(nc + 1 if low else nc):
            core_copy(k, share).wait()
        if low:
            for h in range(count):
                plane_copy(k, 0, h).wait_send()
    for j in range(1, nf):
        gain_copy(j).wait_send()
    for k in range(nc):
        kv_copy(k).wait()
    for u in range(4):
        for k in direct:
            gather_copy(u, k).wait_send()
            if relayed:
                gather_copy(u, k, 1).wait_send()
        for k in range(chips):
            gather_core_copy(u, k).wait_send()
            if u in (0, 3):
                gather_core_copy(u, k).wait_recv()
    down_copy().wait()
    for i, (stage, target) in enumerate(back):
        if i not in (len(back) - 1, 1):
            pltpu.make_async_copy(stage, target, local.at[1, i]).wait()


def share_weights(
    nf,
    nc,
    w_query,
    w_key,
    w_value,
    w_out,
    w_gate,
    w_up,
    order,
    down,
    gains,
    tokens,
    cosine,
    sine,
):
    chips = nf // 2
    shard, hidden = w_gate.shape
    part = hidden // chips
    size = shard // nc
    low = shard - nc * size
    raw = part % 128 == 0
    halves = [w_gate, w_up]
    if not raw:
        both = [w.reshape(shard, chips, part).transpose(1, 0, 2) for w in halves]
        halves = [jnp.take(jnp.concatenate(both, axis=2), order, axis=0)]
    anywhere = pl.BlockSpec(memory_space=pl.ANY)
    dma = pltpu.SemaphoreType.DMA
    kv_shape = (tokens.shape[0], 2 * w_key.shape[1])
    widths = [w_query.shape[1], 2 * w_key.shape[1], w_out.shape[1], 2 * part]
    return pl.pallas_call(
        functools.partial(share_kernel, nf, nc, low, size, raw),
        in_specs=[anywhere] * (6 + len(halves)) + [pl.BlockSpec(memory_space=pltpu.VMEM)] * 3,
        out_specs=[anywhere] * 7,
        out_shape=[jax.ShapeDtypeStruct((nf, shard, width), BF) for width in widths]
        + [
            jax.ShapeDtypeStruct((2,) + down.shape, BF),
            jax.ShapeDtypeStruct((nf,) + gains.shape, BF),
            jax.ShapeDtypeStruct((nc,) + kv_shape, BF),
        ],
        scratch_shapes=[pltpu.VMEM((shard, width), BF) for width in widths]
        + [
            pltpu.VMEM(down.shape, BF),
            pltpu.VMEM(gains.shape, BF),
            dma((2, 8)),
            dma((2, chips, 2)),
            dma((2, chips, 2)),
            dma((2, nc, chips)),
            dma((nc, chips)),
            dma((chips, nc + 1)),
            dma((chips, nc + 1)),
            dma((nf,)),
            dma((nf,)),
            dma((2,)),
            dma((4, 2 * chips)),
            dma((4, 2 * chips)),
            dma((2, 4, chips)),
            pltpu.VMEM((nf, shard, widths[1]), BF),
            pltpu.VMEM((nf,) + gains.shape, BF),
            pltpu.VMEM(tokens.shape, BF),
            pltpu.VMEM(kv_shape, BF),
            dma((2,)),
            dma((nc,)),
            dma((nc,)),
        ],
        compiler_params=pltpu.CompilerParams(
            collective_id=1, has_side_effects=True, vmem_limit_bytes=56 << 20
        ),
        name="share_weights",
    )(w_query, w_key, w_value, w_out, *halves, down, gains, tokens, cosine, sine)


def place_columns_kernel(order, both_ref, gate_ref, up_ref):
    part = gate_ref.shape[1]
    gate_ref[...] = both_ref[0, :, :part].astype(F32)
    up_ref[...] = both_ref[0, :, part:].astype(F32)


def place_columns(order, both):
    parts, shard, part = both.shape[0], both.shape[1], both.shape[2] // 2
    out = jax.ShapeDtypeStruct((shard, parts * part), F32)
    if part % 128:
        both = jnp.take(both, order, axis=0).transpose(1, 0, 2).astype(F32)
        return [both[:, :, i * part : (i + 1) * part].reshape(out.shape) for i in range(2)]
    columns = pl.BlockSpec((shard, part), lambda k, t: (0, t[k]))
    return pl.pallas_call(
        place_columns_kernel,
        grid_spec=pltpu.PrefetchScalarGridSpec(
            num_scalar_prefetch=1,
            grid=(parts,),
            in_specs=[pl.BlockSpec((1, shard, 2 * part), lambda k, t: (k, 0, 0))],
            out_specs=[columns, columns],
        ),
        out_shape=[out, out],
        name="place_columns",
    )(order, both)


def feed_forward_kernel(nf, *refs):
    chips = nf // 2
    hn, *gbs, w_gu, w_d, grad, left, right, down_kept, down_got = refs[: chips + 8]
    outs, refs = refs[chips + 8 : 2 * chips + 8], refs[2 * chips + 8 :]
    w_gu_v, w_d_v, hn_v, gb_v, dact_v, act_v, dgu_v, sent, got, outs_v = refs[:10]
    tiles, halves, half_sem, *sems = refs[10:]
    load, load_gb, hn_send, hn_recv, dhn_send, dhn_recv, store = sems[:7]
    left_local, left_send, left_recv, right_local, right_send, right_recv = sems[7:13]
    down_local, down_send, down_recv = sems[13:]
    place = lax.axis_index("fsdp")
    core = place % 2
    rows, width = hn.shape
    part = w_d.shape[0]
    shard = width // nf
    half = rows // 2
    relayed = chips == 4
    direct = (1, 2) if relayed else tuple(range(1, chips))
    mesh_id = pl.DeviceIdType.MESH

    barrier = pltpu.get_barrier_semaphore()
    for j in [1] + [2 * k for k in range(1, chips)]:
        pl.semaphore_signal(
            barrier, inc=1, device_id={"fsdp": place ^ j}, device_id_type=mesh_id
        )
    pl.semaphore_wait(barrier, chips)

    def remote(source, target, sends, recvs, step):
        return pltpu.make_async_remote_copy(
            src_ref=source,
            dst_ref=target,
            send_sem=sends,
            recv_sem=recvs,
            device_id={"fsdp": place ^ step},
            device_id_type=mesh_id,
        )

    def hn_copy(k, relay=0):
        at = 2 * k + relay
        if relay:
            lines = pl.ds((2 - k) * half, half)
            source, target = hn_v.at[3 - k, lines], hn_v.at[3, lines]
        else:
            source, target = hn, hn_v.at[k]
        return remote(source, target, hn_send.at[at], hn_recv.at[at], 2 * k)

    def dhn_copy(k):
        return remote(sent.at[k - 1], got.at[k - 1], dhn_send.at[k], dhn_recv.at[k], 2 * k)

    def half_copy(k):
        lines = pl.ds((k - 1) * half, half)
        return remote(
            sent.at[2, lines], halves.at[k - 1], half_sem.at[0, k], half_sem.at[1, k], 2 * k
        )

    def left_copy(k, j, other):
        number = 1 - core if other else core
        columns = pl.ds(pl.multiple_of((2 * j + number) * shard, shard), shard)
        source = hn_v.at[k, :, columns]
        target = left.at[other, k, :, pl.ds(j * shard, shard)]
        if other:
            return remote(source, target, left_send.at[k, j], left_recv.at[k, j], 1)
        return pltpu.make_async_copy(source, target, left_local.at[k, j])

    def right_copy(k, other):
        if other:
            return remote(dgu_v.at[k], right.at[1, k], right_send.at[k], right_recv.at[k], 1)
        return pltpu.make_async_copy(dgu_v.at[k], right.at[0, k], right_local.at[k])

    loads = [
        pltpu.make_async_copy(w_d, w_d_v, load.at[0]),
        pltpu.make_async_copy(hn, hn_v.at[0], load.at[1]),
        pltpu.make_async_copy(w_gu, w_gu_v, load.at[2]),
    ]
    gb_loads = [
        pltpu.make_async_copy(gb, gb_v.at[k], load_gb.at[k]) for k, gb in enumerate(gbs)
    ]
    store_outs = [
        pltpu.make_async_copy(outs_v.at[k], out, store.at[k]) for k, out in enumerate(outs)
    ]
    for k in direct:
        hn_copy(k).start()
    for copy in loads[:1] + gb_loads + loads[1:]:
        copy.start()

    for copy in loads[:1] + gb_loads:
        copy.wait()

    def dact_tile(start, size):
        tile = w_d_v[pl.ds(start, size), :]
        for k in range(chips):
            dact_v[k, :, pl.ds(start, size)] = dot(gb_v[k], tile, (1, 1))

    @pl.loop(0, part // 256)
    def _(i):
        dact_tile(pl.multiple_of(i * 256, 256), 256)

    if part % 256:
        dact_tile(part - 128, 128)

    def forward(k):
        for j in range(chips):
            left_copy(k, j, 1).start()
            left_copy(k, j, 0).start()

        def tile(start, size):
            one, two = pl.ds(start, size), pl.ds(pl.multiple_of(part + start, 128), size)
            gate = dot(hn_v[k], w_gu_v[:, one], (1, 0))
            up = dot(hn_v[k], w_gu_v[:, two], (1, 0))
            dact = dact_v[k, :, one]
            sg = jax.nn.sigmoid(gate)
            silu = gate * sg
            act_v[k, :, one] = (silu * up).astype(BF)
            dgu_v[k, :, one] = (dact * up * sg * (1.0 + gate * (1.0 - sg))).astype(BF)
            dgu_v[k, :, two] = (dact * silu).astype(BF)

        @pl.loop(0, part // 256)
        def _(i):
            tile(pl.multiple_of(i * 256, 256), 256)

        if part % 256:
            tile(part - 128, 128)

        right_copy(k, 1).start()
        right_copy(k, 0).start()

    def backward(k):
        @pl.loop(0, width // 256)
        def _(i):
            lines = pl.ds(pl.multiple_of(i * 256, 256), 256)
            dhn = dot(dgu_v[k], w_gu_v[lines, :], (1, 1))
            if k:
                sent[k - 1, :, lines] = dhn.astype(BF)
            else:
                grad[:, lines] = dhn

    for copy in loads[1:]:
        copy.wait()
    forward(0)
    for k in direct:
        hn_copy(k).wait_recv()
        if relayed:
            hn_copy(3 - k, 1).start()
    if relayed:
        forward(1)
        forward(2)
        for i in direct:
            hn_copy(i, 1).wait_recv()
        forward(3)
        backward(3)
        for k in direct:
            half_copy(k).start()
        backward(1)
        backward(2)
        for k in direct:
            half_copy(k).wait_recv()

            @pl.loop(0, half // 16)
            def _(i):
                lines = pl.ds(pl.multiple_of(i * 16, 16), 16)
                into = pl.ds(pl.multiple_of((k - 1) * half + i * 16, 16), 16)
                total = sent[2 - k, into, :].astype(F32) + halves[k - 1, lines, :].astype(F32)
                sent[2 - k, into, :] = total.astype(BF)

            dhn_copy(3 - k).start()
    else:
        for k in range(1, chips):
            forward(k)
            backward(k)
            dhn_copy(k).start()
    backward(0)

    @pl.loop(0, width // 256)
    def _(i):
        columns = pl.ds(pl.multiple_of(i * 256, 256), 256)
        for k in range(chips):
            outs_v[k, :, columns] = dot(act_v[k], w_d_v[:, columns], (1, 0)).astype(BF)

    for copy in store_outs:
        copy.start()

    lower = part // 2
    spans = []
    for start in range(0, part, 128):
        cuts = sorted({start, min(max(lower, start), start + 128), start + 128})
        spans += [(start, a, b) for a, b in zip(cuts, cuts[1:])]

    def span_copies(n):
        start, a, b = spans[n]
        number = int(a >= lower)
        source = tiles.at[(start // 128) % 2, pl.ds(a - start, b - a)]
        at = pl.ds(a - number * lower, b - a)

        def keep():
            return pltpu.make_async_copy(source, down_kept.at[at], down_local.at[n])

        def send():
            return remote(source, down_got.at[at], down_send.at[n], down_recv.at[n], 1)

        return number, keep, send

    def each_span(chosen, go):
        for n in chosen:
            number, keep, send = span_copies(n)

            @pl.when(core == number)
            def _():
                keep().start() if go else keep().wait()

            @pl.when(core != number)
            def _():
                send().start() if go else send().wait_send()

    for start in range(0, part, 128):
        before = [n for n, span in enumerate(spans) if span[0] == start - 256]
        each_span(before, False)
        tile = sum(
            dot(act_v[k, :, start : start + 128], gb_v[k], (0, 0)) for k in range(chips)
        )
        tiles[(start // 128) % 2] = tile.astype(BF)
        each_span([n for n, span in enumerate(spans) if span[0] == start], True)
    each_span([n for n, span in enumerate(spans) if span[0] >= part - 256], False)
    for n in range(len(spans)):
        number, _, send = span_copies(n)

        @pl.when(core == number)
        def _():
            send().wait_recv()

    for k in direct:
        dhn_copy(k).wait_recv()

    @pl.loop(0, rows // 16)
    def _(i):
        lines = pl.ds(pl.multiple_of(i * 16, 16), 16)
        grad[lines, :] += sum(got[k - 1, lines, :].astype(F32) for k in direct)

    for copy in store_outs:
        copy.wait()
    for k in range(chips):
        for j in range(chips):
            left_copy(k, j, 0).wait()
            left_copy(k, j, 1).wait()
        right_copy(k, 0).wait()
        right_copy(k, 1).wait()
    for k in direct:
        dhn_copy(k).wait_send()
        hn_copy(k).wait_send()
        if relayed:
            half_copy(k).wait_send()
            hn_copy(k, 1).wait_send()


def feed_forward(nf, hn, gbs, w_gu, w_d):
    chips = nf // 2
    rows, width = hn.shape
    part = w_d.shape[0]
    anywhere = pl.BlockSpec(memory_space=pl.ANY)
    dma = pltpu.SemaphoreType.DMA
    shape = jax.ShapeDtypeStruct
    return pl.pallas_call(
        functools.partial(feed_forward_kernel, nf),
        in_specs=[anywhere] * (chips + 3),
        out_specs=[pl.BlockSpec(memory_space=pltpu.VMEM)] + [anywhere] * (chips + 4),
        out_shape=[
            shape((rows, width), F32),
            shape((2, chips, rows, width // 2), BF),
            shape((2, chips, rows, 2 * part), BF),
            shape((part // 2, width), BF),
            shape((part // 2, width), BF),
        ]
        + [shape((rows, width), BF)] * chips,
        scratch_shapes=[
            pltpu.VMEM((width, 2 * part), BF),
            pltpu.VMEM((part, width), BF),
            pltpu.VMEM((chips, rows, width), BF),
            pltpu.VMEM((chips, rows, width), BF),
            pltpu.VMEM((chips, rows, part), F32),
            pltpu.VMEM((chips, rows, part), BF),
            pltpu.VMEM((chips, rows, 2 * part), BF),
            pltpu.VMEM((chips - 1, rows, width), BF),
            pltpu.VMEM((chips - 1, rows, width), BF),
            pltpu.VMEM((chips, rows, width), BF),
            pltpu.VMEM((2, 128, width), BF),
            pltpu.VMEM((2, rows // 2, width), BF),
            dma((2, chips)),
            dma((3,)),
            dma((chips,)),
            dma((2 * chips,)),
            dma((2 * chips,)),
            dma((chips,)),
            dma((chips,)),
            dma((chips,)),
            dma((chips, chips)),
            dma((chips, chips)),
            dma((chips, chips)),
            dma((chips,)),
            dma((chips,)),
            dma((chips,)),
            dma((part // 128 + 1,)),
            dma((part // 128 + 1,)),
            dma((part // 128 + 1,)),
        ],
        compiler_params=pltpu.CompilerParams(
            collective_id=3, has_side_effects=True, vmem_limit_bytes=60 << 20
        ),
        cost_estimate=pl.CostEstimate(
            flops=12 * chips * rows * width * part,
            bytes_accessed=40_000_000,
            transcendentals=chips * rows * part,
        ),
        name="feed_forward",
    )(hn, *gbs, w_gu, w_d)


def chunk_rows(rows):
    return max(r for r in range(16, 17, 16) if rows % r == 0)


def finish_kernel(nf, nc, *refs):
    pieces, refs = refs[: nf // 2], refs[nf // 2 - 1 :]
    sources, (outs, owns, ins, xs) = refs[:4], (refs[i : i + 4] for i in range(4, 20, 4))
    plane_send, plane_recv, local, in_sem, x_sem, first_send, second_send, out_sem = refs[20:]
    chips = nf // 2
    place, here = lax.axis_index("fsdp"), lax.axis_index("ctx")
    chip = place // 2
    lower = here < nc // 2
    depth = jnp.where(lower, here, nc - 1 - here)
    inner = jnp.where(lower, here + 1, here - 1)
    outer = jnp.where(lower, here - 1, here + 1)
    mesh_id = pl.DeviceIdType.MESH

    barrier = pltpu.get_barrier_semaphore()
    for k in range(1, chips):
        pl.semaphore_signal(
            barrier, inc=1, device_id={"fsdp": place ^ (2 * k)}, device_id_type=mesh_id
        )
    pl.semaphore_signal(barrier, inc=1, device_id={"ctx": inner}, device_id_type=mesh_id)

    @pl.when(depth > 0)
    def _():
        pl.semaphore_signal(barrier, inc=1, device_id={"ctx": outer}, device_id_type=mesh_id)
        pl.semaphore_wait(barrier, chips + 1)

    @pl.when(depth == 0)
    def _():
        pl.semaphore_wait(barrier, chips)

    def plane_copy(u, k):
        return pltpu.make_async_remote_copy(
            src_ref=sources[u].at[chip ^ k],
            dst_ref=owns[u].at[k],
            send_sem=plane_send.at[u, k],
            recv_sem=plane_recv.at[u, k],
            device_id={"fsdp": place ^ (2 * k)},
            device_id_type=mesh_id,
        )

    def local_copy(u, k):
        source = sources[u].at[chip] if u else pieces[k]
        return pltpu.make_async_copy(source, owns[u].at[k], local.at[u, k])

    for u in range(4):
        for k in range(chips):
            if u == 0 or k == 0:
                local_copy(u, k).start()
            else:
                plane_copy(u, k).start()

    units = [(0, k) for k in range(chips)] + [(u, None) for u in (1, 2, 3)]
    chunks = []
    for u, k in units:
        total = outs[u].shape[-2]
        size = chunk_rows(total)
        chunks += [(u, k, r, size) for r in range(0, total, size)]

    def views(c):
        u, k, r, size = chunks[c]
        rows = pl.ds(r, size)
        return [owns[u].at[k or 0, rows]] + [
            ref.at[rows] if k is None else ref.at[k, rows] for ref in (ins[u], xs[u], outs[u])
        ]

    def first_copy(c, across):
        own, arriving, x, _ = views(c)
        return pltpu.make_async_remote_copy(
            src_ref=own,
            dst_ref=x if across else arriving,
            send_sem=first_send.at[c],
            recv_sem=(x_sem if across else in_sem).at[c],
            device_id={"ctx": inner},
            device_id_type=mesh_id,
        )

    def second_copy(c, across):
        _, arriving, x, _ = views(c)
        return pltpu.make_async_remote_copy(
            src_ref=arriving if across else x,
            dst_ref=x,
            send_sem=second_send.at[c],
            recv_sem=x_sem.at[c],
            device_id={"ctx": outer},
            device_id_type=mesh_id,
        )

    def out_copy(c, across):
        _, arriving, x, out = views(c)
        return pltpu.make_async_copy(arriving if across else x, out, out_sem.at[c])

    def add_into(target, terms, size):
        @pl.loop(0, size // 16)
        def _(i):
            strip = pl.ds(pl.multiple_of(i * 16, 16), 16)
            target[strip, :] = sum(term[strip, :].astype(F32) for term in terms).astype(BF)

    def inward(c, level):
        u, k, r, size = chunks[c]
        own, arriving, _, _ = views(c)
        terms = [own]
        if r == 0:
            local_copy(u, k or 0).wait()
            if u >= 1:
                for j in range(1, chips):
                    plane_copy(u, j).wait_recv()
        if u >= 1:
            terms += [owns[u].at[j, pl.ds(r, size)] for j in range(1, chips)]
        if level > 0:
            first_copy(c, False).wait_recv()
            terms.append(arriving)
        if len(terms) > 1:
            add_into(own, terms, size)
        if c >= FLIGHT:
            first_copy(c - FLIGHT, False).wait_send()
        first_copy(c, level == top).start()

    def outward(c, level):
        size = chunks[c][3]
        own, arriving, x, _ = views(c)
        first_copy(c, True).wait_recv()
        if level == top:
            add_into(arriving, [own, x], size)
        out_copy(c, level == top).start()
        if level > 0:
            if c >= FLIGHT:
                second_copy(c - FLIGHT, False).wait_send()
            second_copy(c, level == top).start()

    top = nc // 2 - 1
    count = len(chunks)
    for level in range(top + 1):

        @pl.when(depth == level)
        def _():
            lag = 3 + 6 * (top - level)
            for t in range(count + lag):
                if t < count:
                    inward(t, level)
                if t >= lag:
                    outward(t - lag, level)
            for c in range(max(0, count - FLIGHT), count):
                first_copy(c, False).wait_send()
                if level > 0:
                    second_copy(c, False).wait_send()
            for c in range(count):
                out_copy(c, False).wait()

    for u in range(1, 4):
        for k in range(1, chips):
            plane_copy(u, k).wait_send()


def finish(nf, nc, pieces, sums):
    chips = nf // 2
    pieces_shape = (chips,) + pieces[0].shape
    shapes = [pieces_shape] + [x.shape[1:] for x in sums]
    count = sum(
        (shape[0] if len(shape) == 3 else 1) * (shape[-2] // chunk_rows(shape[-2]))
        for shape in shapes
    )
    anywhere = pl.BlockSpec(memory_space=pl.ANY)
    dma = pltpu.SemaphoreType.DMA
    return pl.pallas_call(
        functools.partial(finish_kernel, nf, nc),
        in_specs=[anywhere] * (chips + 3),
        out_specs=[anywhere] * 4,
        out_shape=[jax.ShapeDtypeStruct(shape, BF) for shape in shapes],
        scratch_shapes=[pltpu.VMEM(x, BF) for x in [pieces_shape] + [x.shape for x in sums]]
        + [pltpu.VMEM(shape, BF) for shape in shapes]
        + [pltpu.VMEM(shape, BF) for shape in shapes]
        + [dma((4, chips)), dma((4, chips)), dma((4, chips))]
        + [dma((count,))] * 5,
        compiler_params=pltpu.CompilerParams(
            collective_id=0, has_side_effects=True, vmem_limit_bytes=48 << 20
        ),
        cost_estimate=pl.CostEstimate(
            flops=200_000_000_000, bytes_accessed=60_000_000, transcendentals=0
        ),
        name="finish",
    )(*pieces, *sums)


def solution(mesh):
    nf, nc = mesh.shape["fsdp"], mesh.shape["ctx"]
    chips = nf // 2

    def swap(x, k):
        return lax.ppermute(x, "fsdp", [(i, i ^ k) for i in range(nf)])

    def plane_gather(x):
        if chips != 4:
            return [swap(x, 2 * k) for k in range(1, chips)]
        one, two = swap(x, 2), swap(x, 4)
        half = x.shape[0] // 2
        return [one, two, jnp.concatenate([swap(one[:half], 4), swap(two[half:], 2)], axis=0)]

    def cross(x, k):
        return lax.ppermute(x, "ctx", [(i, i ^ k) for i in range(nc)])

    def shards(
        tokens,
        attn_gain,
        w_query,
        w_key,
        w_value,
        w_out,
        ffn_gain,
        w_gate,
        w_up,
        w_down,
        block_table,
        positions,
        out_grad,
    ):
        place = lax.axis_index("fsdp")
        chip, core = place // 2, place % 2
        x = tokens[0].astype(F32)
        gb = out_grad[0]
        rows, width = x.shape
        hidden = w_gate.shape[1]
        part = hidden // chips
        shard = w_gate.shape[0]
        key_width = KV_HEADS * HEAD_DIM

        def core_sum(x):
            other = lax.dynamic_index_in_dim(x, 1 - core, 1, keepdims=False)
            mine = lax.dynamic_index_in_dim(x, core, 1, keepdims=False)
            return (mine.astype(F32) + swap(other, 1).astype(F32)).astype(BF)

        def rows_grad(left, right):
            columns = [left[:, i * shard : (i + 1) * shard] for i in range(nf)]
            even = jnp.concatenate(columns[::2], axis=1)
            odd = jnp.concatenate(columns[1::2], axis=1)
            mine = jnp.where(core == 0, even, odd)
            other = jnp.where(core == 0, odd, even)
            left = jnp.concatenate([mine, swap(other, 1)], axis=0)
            right = jnp.concatenate([right, swap(right, 1)], axis=0)
            return dot(left, right, (0, 0)).astype(BF).reshape(chips, shard, right.shape[1])


        half = HEAD_DIM // 2
        frequency = THETA ** (-jnp.arange(half, dtype=F32) * (2.0 / HEAD_DIM))
        angle = positions[0].astype(F32)[:, None] * frequency[None, :]
        cosine, sine = jnp.cos(angle), jnp.sin(angle)
        cos_lanes = jnp.tile(cosine, (1, 4))
        sin_lanes = jnp.tile(jnp.concatenate([-sine, sine], axis=1), (1, 2))
        blocks = 2 * nc
        stored = block_table.reshape(-1)
        number = jnp.arange(blocks, dtype=jnp.int32)
        where = jnp.sum(
            jnp.where(stored[None, :] == number[:, None], number[None, :], 0), axis=1
        )
        here = lax.axis_index("ctx")
        own = lax.dynamic_slice_in_dim(stored, 2 * here, 2)
        where = 2 * ((where // 2) ^ here) + where % 2
        table = jnp.concatenate([own, where]).astype(jnp.int32)

        order = chip ^ jnp.arange(chips, dtype=jnp.int32)
        both_gains = jnp.pad(jnp.stack([attn_gain, ffn_gain]), ((0, 14), (0, 0)))
        w_q, w_kv, w_o, w_gu, w_d, gains, kv = share_weights(
            nf,
            nc,
            w_query,
            w_key,
            w_value,
            w_out,
            w_gate,
            w_up,
            order,
            w_down,
            both_gains,
            tokens[0],
            cos_lanes,
            sin_lanes,
        )
        w_q = w_q.reshape(width, -1)
        w_kv = w_kv.reshape(width, -1)
        gb_sent, w_kv = lax.optimization_barrier((gb, w_kv))
        w_o = w_o.reshape(-1, width)
        w_gu = w_gu.reshape(width, 2 * part)
        w_d = w_d.reshape(part, width)
        gains = gains[:, :2].astype(F32).transpose(1, 0, 2).reshape(2, width)

        inverse_one = lax.rsqrt(jnp.mean(x * x, axis=1, keepdims=True) + EPS)
        unit_one = x * inverse_one
        xn = (unit_one * gains[0][None, :]).astype(BF)
        q_sum = dot(xn, w_q, (1, 0))
        gb_of = [gb] + [swap(gb_sent, 2 * k) for k in range(1, chips)]
        kv = kv.reshape(nc * rows, 2 * key_width)
        qr, o, ob, lse = attention_forward(table, q_sum, cos_lanes, sin_lanes, kv)
        h1 = x + dot(ob, w_o, (1, 0))
        inverse_two = lax.rsqrt(jnp.mean(h1 * h1, axis=1, keepdims=True) + EPS)
        unit_two = h1 * inverse_two
        hn = (unit_two * gains[1][None, :]).astype(BF)

        hn, gb_of = lax.optimization_barrier((hn, gb_of))

        fused = part % 128 == 0
        if fused:
            grad_hn, left, right, *downs = feed_forward(nf, hn, gb_of, w_gu, w_d)
            outs = downs[2:]
            left = left.reshape(2 * chips * rows, width // 2)
            right = right.reshape(2 * chips * rows, 2 * part)
            down_sum = (downs[0].astype(F32) + downs[1].astype(F32)).astype(BF)
        else:
            dhns = []
            hn_of, act_of, dgu_of = [], [], []
            for k, hn_k in enumerate([hn] + plane_gather(hn)):
                gu = dot(hn_k, w_gu, (1, 0))
                dact = dot(gb_of[k], w_d, (1, 1))
                gate, up = gu[:, :part], gu[:, part:]
                sg = jax.nn.sigmoid(gate)
                silu = gate * sg
                act = (silu * up).astype(BF)
                dgate = (dact * up * sg * (1.0 + gate * (1.0 - sg))).astype(BF)
                dgu = jnp.concatenate([dgate, (dact * silu).astype(BF)], axis=1)
                dhn_k = dot(dgu, w_gu, (1, 1))
                dhns.append(dhn_k.astype(BF) if k else dhn_k)
                hn_of.append(hn_k)
                act_of.append(act)
                dgu_of.append(dgu)
            got = [swap(dhns[k], 2 * k) for k in range(1, chips)]
            act_of, dgu_of, got[:-1], _ = lax.optimization_barrier(
                (act_of, dgu_of, got[:-1], dhns[1:])
            )
            grad_hn = dhns[0]
            for piece in got:
                grad_hn = grad_hn + piece.astype(F32)

            gb_all = jnp.concatenate(gb_of, axis=0)
            down = dot(jnp.concatenate(act_of, axis=0), gb_all, (0, 0)).astype(BF)
            down_sum = core_sum(down.reshape((1, 2) + w_down.shape))[0]
            left = jnp.concatenate(hn_of, axis=0)
            right = jnp.concatenate(dgu_of, axis=0)

        down_sum, left, right = lax.optimization_barrier((down_sum, left, right))
        down_sum = lax.psum_scatter(down_sum, "ctx", scatter_dimension=0, tiled=True)
        if fused:
            wide = dot(left, right, (0, 0)).astype(BF).reshape(chips, shard, 2 * part)
        else:
            wide = rows_grad(left, right)
        wide = [
            lax.dynamic_index_in_dim(wide, chip ^ k, 0, keepdims=False) for k in range(chips)
        ]
        wide, grad_hn = lax.optimization_barrier((wide, grad_hn))
        wide = [swap(piece, 2 * k) if k else piece for k, piece in enumerate(wide)]

        gain_two_grad = jnp.sum(grad_hn * unit_two, axis=0)
        grad_unit = grad_hn * gains[1][None, :]
        dh1 = gb.astype(F32) + inverse_two * (
            grad_unit - unit_two * jnp.mean(grad_unit * unit_two, axis=1, keepdims=True)
        )
        dab = dh1.astype(BF)
        dob = dot(dab, w_o, (1, 1)).astype(BF)
        dq, dkv = attention_backward(table, qr, dob, o, lse, kv, cos_lanes, sin_lanes)
        xn, ob, dab, _ = lax.optimization_barrier((xn, ob, dab, dq))
        if not fused:
            act_of, _ = lax.optimization_barrier((act_of, dq))
            outs = [dot(act, w_d, (1, 0)).astype(BF) for act in act_of]
        sent = outs[1:]
        own = own_key_grads(nc, dkv, cos_lanes, sin_lanes)
        own, wide, down_sum = lax.optimization_barrier((own, wide, down_sum))
        down_sum = lax.all_gather(down_sum, "ctx", axis=0, tiled=True)
        ob, dab, _ = lax.optimization_barrier((ob, dab, own))
        out_term = rows_grad(ob, dab)
        dqkv = jnp.concatenate([dq, own], axis=1)
        grad_xn = dot(dq, w_q, (1, 1)) + dot(own, w_kv, (1, 1))
        gain_one_grad = jnp.sum(grad_xn * unit_one, axis=0)
        grad_unit = grad_xn * gains[0][None, :]
        tokens_grad = dh1 + inverse_one * (
            grad_unit - unit_one * jnp.mean(grad_unit * unit_one, axis=1, keepdims=True)
        )
        qkv_term = rows_grad(xn, dqkv)

        gains_of = jnp.stack([gain_one_grad, gain_two_grad]).reshape(2, chips, 2, shard)
        other = lax.dynamic_index_in_dim(gains_of, 1 - core, 2, keepdims=False)
        mine = lax.dynamic_index_in_dim(gains_of, core, 2, keepdims=False)
        gains_of = (mine + swap(other, 1)).transpose(1, 0, 2).reshape(chips, 1, 2 * shard)
        gains_of = jnp.pad(gains_of.astype(BF), ((0, 0), (0, 15), (0, 0)))
        out_term, qkv_term, outs[0], sent = lax.optimization_barrier(
            (out_term, qkv_term, outs[0], sent)
        )
        terms = [swap(sent[k - 1], 2 * k) for k in range(1, chips)]
        wide, down_sum, out_term, qkv_term = lax.optimization_barrier(
            (wide, down_sum, out_term, qkv_term)
        )
        gu_sum, out_sum, qkv_sum, gain_sum = finish(
            nf, nc, wide, [out_term, qkv_term, gains_of]
        )
        h1, gain_sum = lax.optimization_barrier((h1, gain_sum))
        branch = h1 + outs[0].astype(F32)
        for k in range(1, chips):
            branch = branch + terms[k - 1].astype(F32)
        layer_out = branch.astype(BF)
        qkv_sum = qkv_sum.astype(F32)
        gain_sum = gain_sum[0].reshape(2, shard).astype(F32)
        gate_grad, up_grad = place_columns(order, gu_sum)
        query_width = HEADS * HEAD_DIM
        return (
            layer_out.reshape(1, rows, width),
            tokens_grad.reshape(1, rows, width),
            gain_sum[0],
            qkv_sum[:, :query_width],
            qkv_sum[:, query_width : query_width + key_width],
            qkv_sum[:, query_width + key_width :],
            out_sum.astype(F32),
            gain_sum[1],
            gate_grad,
            up_grad,
            down_sum.astype(F32),
        )

    weight = P("fsdp", None)
    activation = P("fsdp", "ctx", None)
    return jax.shard_map(
        shards,
        mesh=mesh,
        in_specs=(
            activation,
            P("fsdp"),
            weight,
            weight,
            weight,
            weight,
            P("fsdp"),
            weight,
            weight,
            weight,
            P(),
            P("fsdp", "ctx"),
            activation,
        ),
        out_specs=(
            activation,
            activation,
            P("fsdp"),
            weight,
            weight,
            weight,
            weight,
            P("fsdp"),
            weight,
            weight,
            weight,
        ),
        check_vma=False,
    )
```
